32 devices in a mesh: shard: 2 (over core), ctx: 4 (over y, x), tensor: 4 (over z).
Axes of the slice: x: 2, y: 2, z: 4, core: 2. Of those that a mesh axis runs over, the one named last changes fastest.
Arguments:
- inputs: bfloat16 [2, 2048, 2048], P('shard', ('ctx', 'tensor')), may hold values from -6 to 6
- out_grad: bfloat16 [2, 2048, 2048], P('shard', ('ctx', 'tensor')), may hold values from -6 to 6
- block_order: int32 [2, 8], P('shard'), may hold values from 0 to 7, each once within a row
- gain_attn: bfloat16 [2048], P(('shard', 'ctx')), may hold values from 0.5 to 1.5
- w_query: bfloat16 [2048, 2048], P(('shard', 'ctx'), 'tensor'), may hold values from -0.125 to 0.125
- w_keyval: bfloat16 [2048, 512], P(('shard', 'ctx'), 'tensor'), may hold values from -0.125 to 0.125
- w_output: bfloat16 [2048, 2048], P(('shard', 'ctx'), 'tensor'), may hold values from -3 to 3
- gain_mlp: bfloat16 [2048], P(('shard', 'ctx')), may hold values from 0.5 to 1.5
- w_gate: bfloat16 [2048, 5632], P(('shard', 'ctx'), 'tensor'), may hold values from -0.125 to 0.125
- w_up: bfloat16 [2048, 5632], P(('shard', 'ctx'), 'tensor'), may hold values from -0.125 to 0.125
- w_down: bfloat16 [2048, 5632], P(('shard', 'ctx'), 'tensor'), may hold values from -0.078125 to 0.078125
Outputs:
- layer_out: bfloat16 [2, 2048, 2048], P('shard', ('ctx', 'tensor'))
- input_grad: float32 [2, 2048, 2048], P('shard', ('ctx', 'tensor'))
- grad_gain_attn: float32 [2048], P(('shard', 'ctx'))
- grad_query: float32 [2048, 2048], P(('shard', 'ctx'), 'tensor')
- grad_keyval: float32 [2048, 512], P(('shard', 'ctx'), 'tensor')
- grad_output: float32 [2048, 2048], P(('shard', 'ctx'), 'tensor')
- grad_gain_mlp: float32 [2048], P(('shard', 'ctx'))
- grad_gate: float32 [2048, 5632], P(('shard', 'ctx'), 'tensor')
- grad_up: float32 [2048, 5632], P(('shard', 'ctx'), 'tensor')
- grad_down: float32 [2048, 5632], P(('shard', 'ctx'), 'tensor')
The draws below stay inside these ranges and needn't reach their ends.
Inputs may be any that keep to these rules, and one draw needn't show every extreme that they name: `block_order`: each row is a permutation of the blocks of one sequence.
All inputs are finite; a program needn't handle non-finite values.
Results may differ from the reference program's by a relative error of at most 0.014.
Values may be sent and summed in bfloat16 or wider, within the bound.
A program may use at most 192 MiB of HBM per device.

```python
import jax
import jax.numpy as jnp
from jax import lax

D = 2048
H = 32
KV = 4
HD = 64
FF = 5632
BLOCK = 256
BLOCKS = 8
LEN = 2048
SEQS = 2


def levels(own_key, extent, split, low, largest):
    def one(axis_at, parts):
        steps = jax.random.uniform(jax.random.fold_in(jax.random.fold_in(own_key, 6), axis_at), (parts,), jnp.float32, low / len(split), largest / len(split))
        return jnp.repeat(jnp.exp(steps), extent[axis_at] // parts).reshape((-1,) + (1,) * (len(extent) - axis_at - 1))

    loudness = one(*split[0])
    for cut in split[1:]:
        loudness = loudness * one(*cut)
    return loudness


def noise(rng, extent, spread, most, shards=(), kind=jnp.bfloat16):
    factor_of = levels(rng, extent, shards, -0.22, 0.18) if shards else 1.0
    drawn = jax.random.normal(rng, extent, jnp.float32) * spread * factor_of
    return jnp.minimum(jnp.maximum(drawn, -most), most).astype(kind)


def setup_inputs(seed: int = 0) -> dict:
    seeds = jax.random.split(jax.random.key(seed), 12)
    return {
        "inputs": noise(seeds[0], (SEQS, LEN, D), 1.0, 6.0, ((0, 2), (1, 16))),
        "out_grad": noise(seeds[1], (SEQS, LEN, D), 1.0, 6.0, ((0, 2), (1, 16))),
        "block_order": jax.vmap(lambda own: jax.random.permutation(own, BLOCKS))(jax.random.split(seeds[2], SEQS)).reshape((SEQS, BLOCKS)).astype(jnp.int32),
        "gain_attn": jnp.clip(1.0 + 0.1 * jax.random.normal(seeds[3], (D,), jnp.float32), 0.5, 1.5).astype(jnp.bfloat16),
        "w_query": noise(seeds[4], (D, H * HD), D ** -0.5, 0.125, ((0, 8), (1, 4))),
        "w_keyval": noise(seeds[5], (D, 2 * KV * HD), D ** -0.5, 0.125, ((0, 8), (1, 4))),
        "w_output": noise(seeds[6], (D, H * HD), (4 * H * HD // (BLOCK * BLOCKS)) ** -0.5, 3.0, ((0, 8), (1, 4))),
        "gain_mlp": jnp.clip(1.0 + 0.1 * jax.random.normal(seeds[7], (D,), jnp.float32), 0.5, 1.5).astype(jnp.bfloat16),
        "w_gate": noise(seeds[8], (D, FF), D ** -0.5, 0.125, ((0, 8), (1, 4))),
        "w_up": noise(seeds[9], (D, FF), D ** -0.5, 0.125, ((0, 8), (1, 4))),
        "w_down": noise(seeds[10], (D, FF), FF ** -0.5, 0.078125, ((0, 8), (1, 4))),
    }


epsilon = 1e-05
highest = lax.Precision.HIGHEST

@jax.custom_vjp
def low(v):
    return lax.optimization_barrier(v.astype(jnp.bfloat16)).astype(jnp.float32)

@jax.custom_vjp
def low_back(v):
    return v

def low_keep(v):
    return (low(v), None)

def low_pass(kept, grad):
    return (grad,)

def back_keep(v):
    return (v, None)

def back_low(kept, grad):
    return (low(grad),)
low.defvjp(low_keep, low_pass)
low_back.defvjp(back_keep, back_low)

def rms_norm(values_in, norm_scale):
    return values_in * lax.rsqrt(lax.optimization_barrier(jnp.mean(values_in * values_in, -1, keepdims=True)) + epsilon) * norm_scale

def rotary(values_in, position):
    half_width = values_in.shape[-1] // 2
    frequency = 10000.0 ** (-jnp.arange(half_width, dtype=jnp.float32) * 2.0 / values_in.shape[-1])
    angles = position.astype(jnp.float32)[:, None] * frequency[None, :]
    cosine_table = jnp.cos(angles)[:, None, :]
    sine_table = jnp.sin(angles)[:, None, :]
    first_half = values_in[..., :half_width]
    second = values_in[..., half_width:]
    return jnp.concatenate([first_half * cosine_table - second * sine_table, second * cosine_table + first_half * sine_table], -1)

def block_layer(inputs, params, position, allowed):
    gain_attn, w_query, w_keyval, w_output, gain_mlp, w_gate, w_up, w_down = params
    length = inputs.shape[0]
    inv_root = HD ** (-0.5)
    first_normed = low(rms_norm(inputs, gain_attn))
    query_raw = low_back(jnp.dot(first_normed, w_query, precision=highest)).reshape(length, H, HD)
    keyval_raw = low_back(jnp.dot(first_normed, w_keyval, precision=highest)).reshape(length, KV, 2 * HD)
    queries = low(rotary(query_raw, position))
    keys_all = low(rotary(keyval_raw[..., :HD], position))
    values_all = low(keyval_raw[..., HD:])

    def one_head(operands):
        query_head, group_id = operands
        keys_group = lax.dynamic_index_in_dim(keys_all, group_id, 1, keepdims=False)
        values_group = lax.dynamic_index_in_dim(values_all, group_id, 1, keepdims=False)
        raw_scores = low_back(jnp.dot(query_head, keys_group.T, precision=highest) * inv_root)
        masked = jnp.where(allowed, raw_scores, -jnp.inf)
        row_max = lax.optimization_barrier(jnp.max(masked, -1, keepdims=True))
        exponent = jnp.exp(masked - row_max)
        weights = low(exponent / lax.optimization_barrier(jnp.sum(exponent, -1, keepdims=True)))
        return low_back(jnp.dot(weights, values_group, precision=highest))
    group_ids = jnp.arange(H, dtype=jnp.int32) // (H // KV)
    head_outs = lax.map(jax.checkpoint(one_head), (jnp.moveaxis(queries, 1, 0), group_ids))
    attn_out = low(jnp.moveaxis(head_outs, 0, 1).reshape(length, H * HD))
    attn_branch = low_back(jnp.dot(attn_out, w_output.T, precision=highest))
    between_rows = inputs + attn_branch
    second_normed = low(rms_norm(between_rows, gain_mlp))
    gate_act = low_back(jnp.dot(second_normed, w_gate, precision=highest))
    up_act = low_back(jnp.dot(second_normed, w_up, precision=highest))
    hidden = low(jax.nn.silu(gate_act) * up_act)
    mlp_branch = low_back(jnp.dot(hidden, w_down.T, precision=highest))
    return between_rows + mlp_branch

def reference(inputs, out_grad, block_order, gain_attn, w_query, w_keyval, w_output, gain_mlp, w_gate, w_up, w_down):
    params = tuple((weight_in.astype(jnp.float32) for weight_in in (gain_attn, w_query, w_keyval, w_output, gain_mlp, w_gate, w_up, w_down)))
    length = BLOCK * BLOCKS
    slot_index = jnp.arange(length, dtype=jnp.int32)

    def one_sequence(totals, operands):
        sequence_in, sequence_grad, order_row = operands
        block_ids = order_row[slot_index // BLOCK].astype(jnp.int32)
        position = block_ids * BLOCK + slot_index % BLOCK
        allowed = block_ids[None, :] <= block_ids[:, None]

        def forward(values_in, *weights_in):
            return block_layer(values_in, weights_in, position, allowed)
        layer_value, pullback = jax.vjp(forward, sequence_in.astype(jnp.float32), *params)
        gradients = pullback(sequence_grad.astype(jnp.float32))
        totals = tuple((running + gradient for running, gradient in zip(totals, gradients[1:])))
        return (totals, (layer_value.astype(jnp.bfloat16), gradients[0]))
    zero_init = tuple((jnp.zeros(weight_in.shape, jnp.float32) for weight_in in params))
    totals, outputs = lax.scan(one_sequence, zero_init, (inputs, out_grad, block_order))
    return (outputs[0], outputs[1], totals[0], totals[1], totals[2], totals[3], totals[4], totals[5], totals[6], totals[7])
```

```python
import functools

import jax
import jax.numpy as jnp
import numpy as np
from jax import lax
from jax.experimental import pallas as pl
from jax.experimental.pallas import tpu as pltpu
from jax.sharding import PartitionSpec as P

HD = 64
BLOCK = 256
BLOCKS = 8
ROWS = 16
CTX = 4
LINE = 4

epsilon = 1e-05
blocked = -1e30

f32 = jnp.float32
bf16 = jnp.bfloat16
MESH = pl.DeviceIdType.MESH


def nn_dot(left, right):
    return jnp.dot(left, right, preferred_element_type=f32)


def nt_dot(left, right):
    return lax.dot_general(left, right, (((1,), (1,)), ((), ())), preferred_element_type=f32)


def tn_dot(left, right):
    return lax.dot_general(left, right, (((0,), (0,)), ((), ())), preferred_element_type=f32)


class Links:
    def __init__(self, shards, send_sems, recv_sems, local_sems):
        self.shards = shards
        self.send_sems, self.recv_sems, self.local_sems = send_sems, recv_sems, local_sems
        self.s = lax.axis_index("shard")
        self.c = lax.axis_index("ctx")
        self.t = lax.axis_index("tensor")
        self.c_x = self.c + 1 - 2 * lax.rem(self.c, 2)
        self.c_y = lax.rem(self.c + 2, CTX)
        self.c_d = CTX - 1 - self.c
        self.x_dev = (self.s, self.c_x, self.t)
        self.y_dev = (self.s, self.c_y, self.t)
        self.right = (self.s, self.c, self.t + 1)
        self.left = (self.s, self.c, self.t - 1)
        self.used = 0
        self.local_used = 0
        self.sends = []
        self.locals = []

    def slots(self, count):
        first = self.used
        self.used += count
        assert self.used <= self.send_sems.shape[0]
        return first

    def plane_peer(self, step):
        index = lax.rem(self.s * CTX + self.c + step, self.shards * CTX)
        return (index // CTX, lax.rem(index, CTX), self.t)

    def core_peer(self, step):
        return (lax.rem(self.s + step, self.shards), self.c, self.t)

    def barrier(self):
        sem = pltpu.get_barrier_semaphore()
        count = self.shards * CTX - 1
        for step in range(1, count + 1):
            pl.semaphore_signal(
                sem, inc=1, device_id=self.plane_peer(step), device_id_type=MESH
            )

        @pl.when(self.t > 0)
        def _():
            pl.semaphore_signal(sem, inc=1, device_id=self.left, device_id_type=MESH)

        @pl.when(self.t < LINE - 1)
        def _():
            pl.semaphore_signal(sem, inc=1, device_id=self.right, device_id_type=MESH)

        beside = (self.t + LINE - 1) // LINE + (2 * LINE - 2 - self.t) // LINE
        pl.semaphore_wait(sem, count + beside)

    def copy(self, src, dst, device, slot):
        return pltpu.make_async_remote_copy(
            src_ref=src,
            dst_ref=dst,
            send_sem=self.send_sems.at[slot],
            recv_sem=self.recv_sems.at[slot],
            device_id=device,
            device_id_type=MESH,
        )

    def send(self, src, dst, device, slot, cond=None):
        if cond is None:
            self.copy(src, dst, device, slot).start()
        else:

            @pl.when(cond)
            def _():
                self.copy(src, dst, device, slot).start()

        self.sends.append((src, dst, device, slot, cond))

    def recv(self, dst, slot):
        self.copy(dst, dst, self.x_dev, slot).wait_recv()

    def keep(self, src, dst):
        copy = pltpu.make_async_copy(src, dst, self.local_sems.at[self.local_used])
        self.local_used += 1
        assert self.local_used <= self.local_sems.shape[0]
        copy.start()
        return copy

    def keep_later(self, src, dst):
        self.locals.append(self.keep(src, dst))

    def finish(self):
        for src, dst, device, slot, cond in self.sends:
            if cond is None:
                self.copy(src, dst, device, slot).wait_send()
            else:

                @pl.when(cond)
                def _():
                    self.copy(src, dst, device, slot).wait_send()

        for copy in self.locals:
            copy.wait()


class PlaneGather:
    def __init__(self, links, src, full):
        self.links, self.src, self.full = links, src, full
        self.rows = src.shape[0]
        self.first = links.slots(4 + 4 * (links.shards - 1))

    def block(self, s, c):
        start = pl.multiple_of((s * CTX + c) * self.rows, self.rows)
        return self.full.at[pl.ds(start, self.rows)]

    def half(self, s, c, which):
        size = self.rows // 2
        start = pl.multiple_of((s * CTX + c) * self.rows + which * size, size)
        return self.full.at[pl.ds(start, size)]

    def core_slot(self, step, part):
        return self.first + 4 + (step - 1) * 4 + part

    def core_send(self, src, c, part):
        links = self.links
        for step in range(1, links.shards):
            links.send(
                src,
                self.block(links.s, c),
                links.core_peer(step),
                self.core_slot(step, part),
            )

    def start(self):
        links = self.links
        own = self.block(links.s, links.c)
        links.send(self.src, own, links.x_dev, self.first)
        links.send(self.src, own, links.y_dev, self.first + 1)
        self.core_send(self.src, links.c, 0)
        self.local = links.keep(self.src, own)

    def forward(self):
        links = self.links
        links.recv(self.block(links.s, links.c_x), self.first)
        links.recv(self.block(links.s, links.c_y), self.first + 1)
        from_x = self.half(links.s, links.c_x, 0)
        from_y = self.half(links.s, links.c_y, 1)
        links.send(from_x, from_x, links.y_dev, self.first + 2)
        links.send(from_y, from_y, links.x_dev, self.first + 3)
        self.core_send(self.block(links.s, links.c_x), links.c_x, 1)
        self.core_send(self.block(links.s, links.c_y), links.c_y, 2)

    def diagonal(self):
        links = self.links
        links.recv(self.half(links.s, links.c_d, 0), self.first + 2)
        links.recv(self.half(links.s, links.c_d, 1), self.first + 3)
        self.core_send(self.block(links.s, links.c_d), links.c_d, 3)

    def done(self):
        links = self.links
        for step in range(1, links.shards):
            other = lax.rem(links.s + links.shards - step, links.shards)
            for part, c in enumerate((links.c, links.c_x, links.c_y, links.c_d)):
                links.recv(self.block(other, c), self.core_slot(step, part))
        self.local.wait()


class LineGather:
    def __init__(self, links, own, full, tokens):
        self.links, self.own, self.full, self.tokens = links, own, full, tokens
        self.first = links.slots(2 * (LINE - 1))

    def block(self, owner):
        return self.full.at[pl.ds(pl.multiple_of(owner * self.tokens, self.tokens), self.tokens)]

    def send(self, k):
        links = self.links
        t, u = links.t, LINE - 1 - links.t
        right, left = self.block(t - k + 1), self.block(t + k - 1)
        links.send(
            self.own if k == 1 else right,
            right,
            links.right,
            self.first + k - 1,
            jnp.logical_and(t >= k - 1, t < LINE - 1),
        )
        links.send(
            self.own if k == 1 else left,
            left,
            links.left,
            self.first + LINE - 1 + k - 1,
            jnp.logical_and(u >= k - 1, u < LINE - 1),
        )

    def recv(self, k, use=None):
        links = self.links
        t, u = links.t, LINE - 1 - links.t

        @pl.when(t >= k)
        def _():
            links.recv(self.block(t - k), self.first + k - 1)

        @pl.when(u >= k)
        def _():
            links.recv(self.block(t + k), self.first + LINE - 1 + k - 1)

        if use is not None:

            @pl.when(t >= k)
            def _():
                use(t - k)

            @pl.when(u >= k)
            def _():
                use(t + k)


class LineScatter:
    def __init__(self, links, part, tokens, to_right, to_left, from_left, from_right):
        self.links, self.part, self.tokens = links, part, tokens
        self.to_right, self.to_left = to_right, to_left
        self.from_left, self.from_right = from_left, from_right
        self.first = links.slots(2 * (LINE - 1))

    def clear(self):
        for cond, ref in (
            (self.links.t == 0, self.from_left),
            (self.links.t == LINE - 1, self.from_right),
        ):

            @pl.when(cond)
            def _():
                @pl.loop(0, self.tokens // ROWS)
                def _(i):
                    r = pl.multiple_of(i * ROWS, ROWS)
                    for k in range(LINE - 1):
                        ref[k, pl.ds(r, ROWS), :] = jnp.zeros((ROWS, ref.shape[2]), ref.dtype)

    def total(self, owner, k, out, arrived):
        @pl.loop(0, self.tokens // ROWS)
        def _(i):
            r = pl.multiple_of(i * ROWS, ROWS)
            q = pl.multiple_of(owner * self.tokens + i * ROWS, ROWS)
            summed = self.part[pl.ds(q, ROWS), :].astype(f32) + arrived[
                k, pl.ds(r, ROWS), :
            ].astype(f32)
            out[k, pl.ds(r, ROWS), :] = summed.astype(out.dtype)

    def step(self, k):
        links = self.links
        t = links.t
        slot_r, slot_l = self.first + k, self.first + LINE - 1 + k
        owner_r, owner_l = LINE - 1 - k, k

        @pl.when(t < owner_r)
        def _():
            @pl.when(t > 0)
            def _():
                links.recv(self.from_left.at[k], slot_r)

            self.total(owner_r, k, self.to_right, self.from_left)

        links.send(self.to_right.at[k], self.from_left.at[k], links.right, slot_r, t < owner_r)

        @pl.when(t > owner_l)
        def _():
            @pl.when(t < LINE - 1)
            def _():
                links.recv(self.from_right.at[k], slot_l)

            self.total(owner_l, k, self.to_left, self.from_right)

        links.send(self.to_left.at[k], self.from_right.at[k], links.left, slot_l, t > owner_l)

    def arrive(self):
        links = self.links
        t = links.t

        @pl.when(t > 0)
        def _():
            links.recv(self.from_left.at[LINE - 1 - t], self.first + LINE - 1 - t)

        @pl.when(t < LINE - 1)
        def _():
            links.recv(self.from_right.at[t], self.first + LINE - 1 + t)

    def rows(self, i):
        t = self.links.t
        r = pl.multiple_of(i * ROWS, ROWS)
        q = pl.multiple_of(t * self.tokens + i * ROWS, ROWS)
        k_l = jnp.minimum(LINE - 1 - t, LINE - 2)
        k_r = jnp.minimum(t, LINE - 2)
        return (
            self.part[pl.ds(q, ROWS), :].astype(f32)
            + self.from_left[k_l, pl.ds(r, ROWS), :].astype(f32)
            + self.from_right[k_r, pl.ds(r, ROWS), :].astype(f32)
        )


def any_spec():
    return pl.BlockSpec(memory_space=pl.ANY)


def vmem_spec():
    return pl.BlockSpec(memory_space=pltpu.VMEM)


def struct(shape, dtype):
    return jax.ShapeDtypeStruct(shape, dtype)


def forward_kernel(
    shards,
    x, og, wq, wkv, wo, wg, wu, wd, gpad, cos, sin, bias,
    wq_o, wkv_o, wo_o, wg_o, wu_o, wd_o, n1_o, og_o, n2_o, mid_o, qaug_o, kaug_o, kv_o, att_o,
    lse, gains,
    x_all, n1_all, wq_all, wkv_all, wo_all, gains_all, qaug, kv_all, kaug, v_all, scores, weights,
    attn, part, to_right, to_left, from_left, from_right, mid, n2,
    send_sems, recv_sems, local_sems,
):
    tokens, width = x.shape
    queries = tokens * LINE
    heads = qaug.shape[0]
    links = Links(shards, send_sems, recv_sems, local_sems)
    s, c, t = links.s, links.c, links.t

    gather_x = LineGather(links, x, x_all, tokens)
    gather_og = LineGather(links, og, og_o, tokens)
    gather_n2 = LineGather(links, n2, n2_o, tokens)
    small = [PlaneGather(links, *pair) for pair in ((wq, wq_all), (wkv, wkv_all), (wo, wo_all))]
    large = [PlaneGather(links, *pair) for pair in ((wg, wg_o), (wu, wu_o), (wd, wd_o))]
    scatter = LineScatter(
        links, part, tokens, to_right, to_left, from_left, from_right
    )
    plane = shards * CTX
    gain_slot = links.slots(plane - 1)
    kv_slot = links.slots(3)

    links.barrier()
    me = s * CTX + c
    for step in range(1, plane):
        links.send(gpad, gains_all.at[me], links.plane_peer(step), gain_slot + step - 1)
    own_gain = links.keep(gpad, gains_all.at[me])
    gather_x.send(1)
    own_x = links.keep(x, x_all.at[pl.ds(pl.multiple_of(t * tokens, tokens), tokens)])
    for gather in small:
        gather.start()
    scatter.clear()
    own_gain.wait()
    for step in range(1, plane):
        other = lax.rem(me + plane - step, plane)
        links.recv(gains_all.at[other], gain_slot + step - 1)
    total = gains_all[0]
    for index in range(1, plane):
        total = total + gains_all[index]
    gains[...] = total
    own_x.wait()

    def norm_block(owner):
        @pl.loop(0, tokens // ROWS)
        def _(i):
            r = pl.multiple_of(owner * tokens + i * ROWS, ROWS)
            v = x_all[pl.ds(r, ROWS), :].astype(f32)
            inverse = lax.rsqrt(jnp.mean(v * v, -1, keepdims=True) + epsilon)
            n1_all[pl.ds(r, ROWS), :] = (v * inverse * gains[0:1, :]).astype(bf16)

    norm_block(t)
    gather_x.recv(1)
    gather_x.send(2)
    for gather in small:
        gather.forward()
    norm_pair(gather_x, norm_block, 1)
    large[0].start()
    gather_x.recv(2)
    gather_x.send(3)
    for gather in small:
        gather.diagonal()
    norm_pair(gather_x, norm_block, 2)
    large[1].start()
    large[2].start()
    gather_x.recv(3)
    gather_og.send(1)
    own_og = links.keep(og, og_o.at[pl.ds(pl.multiple_of(t * tokens, tokens), tokens)])
    norm_pair(gather_x, norm_block, 3)
    for gather in small:
        gather.done()

    kv_t = nn_dot(n1_all[...], wkv_all[...]).T
    half = HD // 2
    cosine, sine = cos[...], sin[...]
    k1, k2 = kv_t[0:half], kv_t[half:HD]
    kv_all[c, 0:half, :] = (k1 * cosine - k2 * sine).astype(bf16)
    kv_all[c, half:HD, :] = (k2 * cosine + k1 * sine).astype(bf16)
    kv_all[c, HD : 2 * HD, :] = kv_t[HD:].astype(bf16)
    for step in range(1, CTX):
        peer = lax.rem(c + step, CTX)
        links.send(kv_all.at[c], kv_all.at[c], (s, peer, t), kv_slot + step - 1)

    q_t = nn_dot(n1_all[...], wq_all[...]).T
    scale = HD ** (-0.5)
    for h in range(heads):
        v1, v2 = q_t[h * HD : h * HD + half], q_t[h * HD + half : (h + 1) * HD]
        qaug[h, 0:half, :] = ((v1 * cosine - v2 * sine).astype(bf16) * scale).astype(bf16)
        qaug[h, half:HD, :] = ((v2 * cosine + v1 * sine).astype(bf16) * scale).astype(bf16)
        qaug[h, HD:, :] = bias[...]
    links.keep_later(n1_all, n1_o)
    links.keep_later(wq_all, wq_o)
    links.keep_later(wkv_all, wkv_o)
    links.keep_later(wo_all, wo_o)
    links.keep_later(qaug, qaug_o)
    for step in range(1, CTX):
        other = lax.rem(c + CTX - step, CTX)
        links.recv(kv_all.at[other], kv_slot + step - 1)
    for other in range(CTX):
        row = lax.broadcasted_iota(jnp.int32, (HD, queries), 0)
        lane = lax.broadcasted_iota(jnp.int32, (HD, queries), 1)
        mark = (row == other * (queries // BLOCK) + lane // BLOCK).astype(f32).astype(bf16)
        both = jnp.concatenate([kv_all[other, 0:HD, :], mark], 0)
        kaug[other * queries : (other + 1) * queries, :] = both.T
        v_all[:, other * queries : (other + 1) * queries] = kv_all[other, HD : 2 * HD, :]
    links.keep_later(kaug, kaug_o)
    links.keep_later(kv_all, kv_o)

    length = queries * CTX

    def head(h):
        query = qaug[h]
        top = jnp.full((1, queries), -jnp.inf, f32)
        for b in range(0, length, BLOCK):
            block_scores = nn_dot(kaug[b : b + BLOCK, :], query)
            scores[b : b + BLOCK, :] = block_scores
            top = jnp.maximum(top, jnp.max(block_scores, 0, keepdims=True))
        norm = jnp.zeros((1, queries), f32)
        for b in range(0, length, BLOCK):
            exponent = jnp.exp(scores[b : b + BLOCK, :] - top)
            norm = norm + jnp.sum(exponent, 0, keepdims=True)
            weights[b : b + BLOCK, :] = exponent.astype(bf16)
        out = nn_dot(v_all[...], weights[...]) / norm
        attn[pl.ds(pl.multiple_of(h * HD, HD), HD), :] = out.astype(bf16)
        lse[pl.ds(h, 1), :] = top + jnp.log(norm)

    pl.loop(0, heads // 2)(head)
    gather_og.recv(1)
    gather_og.send(2)
    pl.loop(heads // 2, heads)(head)
    links.keep_later(attn, att_o)

    attn_rows = attn[...].T
    for b in range(0, width, 512):
        part[:, b : b + 512] = nt_dot(attn_rows, wo_all[b : b + 512, :])
    scatter.step(0)
    gather_og.recv(2)
    gather_og.send(3)
    for gather in large:
        gather.forward()
    scatter.step(1)
    scatter.step(2)
    for gather in large:
        gather.diagonal()
    scatter.arrive()

    @pl.loop(0, tokens // ROWS)
    def _(i):
        r = pl.multiple_of(i * ROWS, ROWS)
        q = pl.multiple_of(t * tokens + i * ROWS, ROWS)
        middle = x_all[pl.ds(q, ROWS), :].astype(f32) + scatter.rows(i)
        mid[pl.ds(r, ROWS), :] = middle
        inverse = lax.rsqrt(jnp.mean(middle * middle, -1, keepdims=True) + epsilon)
        n2[pl.ds(r, ROWS), :] = (middle * inverse * gains[1:2, :]).astype(bf16)

    gather_n2.send(1)
    links.keep_later(n2, n2_o.at[pl.ds(pl.multiple_of(t * tokens, tokens), tokens)])
    links.keep_later(mid, mid_o)
    gather_og.recv(3)
    own_og.wait()
    gather_n2.recv(1)
    gather_n2.send(2)
    for gather in large:
        gather.done()
    gather_n2.recv(2)
    gather_n2.send(3)
    gather_n2.recv(3)
    links.finish()


def norm_pair(gather, norm_block, k):
    t, u = gather.links.t, LINE - 1 - gather.links.t

    @pl.when(t >= k)
    def _():
        norm_block(t - k)

    @pl.when(u >= k)
    def _():
        norm_block(t + k)


def forward_call(shards, x, og, weights_in, gpad, cos, sin, bias):
    wq, wkv, wo, wg, wu, wd = weights_in
    tokens, width = x.shape
    queries = tokens * LINE
    length = queries * CTX
    heads = wq.shape[1] // HD
    plane = shards * CTX
    full = [struct((width, w.shape[1]), bf16) for w in weights_in]
    outs = full + [
        struct((queries, width), bf16),
        struct((queries, width), bf16),
        struct((queries, width), bf16),
        struct((tokens, width), f32),
        struct((heads, 2 * HD, queries), bf16),
        struct((length, 2 * HD), bf16),
        struct((CTX, 2 * HD, queries), bf16),
        struct((heads * HD, queries), bf16),
        struct((heads, queries), f32),
        struct((2, width), f32),
    ]
    block = (LINE - 1, tokens, width)
    count = 3 * 6 + 6 * (4 + 4 * (shards - 1)) + 6 + plane - 1 + 3
    return pl.pallas_call(
        functools.partial(forward_kernel, shards),
        out_shape=outs,
        in_specs=[any_spec()] * 8 + [vmem_spec()] * 4,
        out_specs=[any_spec()] * 14 + [vmem_spec()] * 2,
        scratch_shapes=[
            pltpu.VMEM((queries, width), bf16),
            pltpu.VMEM((queries, width), bf16),
            pltpu.VMEM((width, wq.shape[1]), bf16),
            pltpu.VMEM((width, wkv.shape[1]), bf16),
            pltpu.VMEM((width, wo.shape[1]), bf16),
            pltpu.VMEM((plane, 2, width), f32),
            pltpu.VMEM((heads, 2 * HD, queries), bf16),
            pltpu.VMEM((CTX, 2 * HD, queries), bf16),
            pltpu.VMEM((length, 2 * HD), bf16),
            pltpu.VMEM((HD, length), bf16),
            pltpu.VMEM((length, queries), f32),
            pltpu.VMEM((length, queries), bf16),
            pltpu.VMEM((heads * HD, queries), bf16),
            pltpu.VMEM((queries, width), f32),
            pltpu.VMEM(block, bf16),
            pltpu.VMEM(block, bf16),
            pltpu.VMEM(block, bf16),
            pltpu.VMEM(block, bf16),
            pltpu.VMEM((tokens, width), f32),
            pltpu.VMEM((tokens, width), bf16),
            pltpu.SemaphoreType.DMA((count,)),
            pltpu.SemaphoreType.DMA((count,)),
            pltpu.SemaphoreType.DMA((32,)),
        ],
        compiler_params=pltpu.CompilerParams(
            collective_id=0, has_side_effects=True, vmem_limit_bytes=60 * 2**20
        ),
        name="forward",
    )(x, og, wq, wkv, wo, wg, wu, wd, gpad, cos, sin, bias)


def norm_backward_pass(normed_gradient, unit_rows, inverse_root_mean, norm_scale):
    unit_rows_gradient = normed_gradient * norm_scale
    scale_gradient = jnp.sum(normed_gradient * unit_rows, axis=0)
    value_gradients = inverse_root_mean * (
        unit_rows_gradient - unit_rows * jnp.mean(unit_rows_gradient * unit_rows, -1, keepdims=True)
    )
    return (scale_gradient, value_gradients)


def apply_norm(values_in):
    inverse_root_mean = lax.rsqrt(jnp.mean(values_in * values_in, -1, keepdims=True) + epsilon)
    return (values_in * inverse_root_mean, inverse_root_mean)


def body(
    inputs, out_grad, block_order, gain_attn, w_query, w_keyval, w_output, gain_mlp, w_gate, w_up, w_down
):
    shards = lax.axis_size("shard")
    x, og = inputs[0], out_grad[0]
    tokens, width = x.shape
    queries = tokens * LINE
    order = block_order[0]
    s, c = lax.axis_index("shard"), lax.axis_index("ctx")
    per = queries // BLOCK
    here = lax.dynamic_slice_in_dim(order, c * per, per)
    block_here = jnp.repeat(here, BLOCK)
    position = block_here * BLOCK + jnp.tile(jnp.arange(BLOCK, dtype=jnp.int32), per)
    half = HD // 2
    frequency = 10000.0 ** (-jnp.arange(half, dtype=f32) * 2.0 / HD)
    angles = frequency[:, None] * position.astype(f32)[None, :]
    cos, sin = jnp.cos(angles), jnp.sin(angles)
    bias = jnp.where(order[:, None] <= block_here[None, :], 0.0, blocked).astype(bf16)
    bias = jnp.concatenate([bias, jnp.zeros((HD - BLOCKS, queries), bf16)], 0)
    start = (s * CTX + c) * gain_attn.shape[0]
    gpad = lax.dynamic_update_slice(
        jnp.zeros((2, width), f32), jnp.stack([gain_attn, gain_mlp]).astype(f32), (0, start)
    )
    (wq, wkv, wo, wg, wu, wd, n1, og_all, n2, mid, qaug, kaug, kv, att, lse, gains) = forward_call(
        shards, x, og, (w_query, w_keyval, w_output, w_gate, w_up, w_down), gpad, cos, sin, bias
    )
    rs = lambda v: lax.psum_scatter(v, "tensor", scatter_dimension=0, tiled=True)
    ws = lambda v: lax.psum_scatter(
        v.astype(bf16), ("shard", "ctx"), scatter_dimension=0, tiled=True
    ).astype(f32)
    gate = nn_dot(n2, wg)
    up = nn_dot(n2, wu)
    sg = jax.nn.sigmoid(gate)
    silu = gate * sg
    hidden = (silu * up).astype(bf16)
    layer_out = (mid + rs(nt_dot(hidden, wd).astype(bf16)).astype(f32)).astype(bf16)
    dh = nn_dot(og_all, wd)
    grad_down = ws(tn_dot(og_all, hidden))
    dgate = (dh * up * sg * (1.0 + gate * (1.0 - sg))).astype(bf16)
    dup = (dh * silu).astype(bf16)
    grad_gate = ws(tn_dot(n2, dgate))
    grad_up = ws(tn_dot(n2, dup))
    dn2 = rs((nt_dot(dgate, wg) + nt_dot(dup, wu)).astype(bf16)).astype(f32)
    unit2, inv2 = apply_norm(mid)
    gm, dmid = norm_backward_pass(dn2, unit2, inv2, gains[1:2])
    dmid = dmid + og.astype(f32)
    dmid_all = lax.all_gather(dmid.astype(bf16), "tensor", axis=0, tiled=True)
    datt = nn_dot(dmid_all, wo).astype(bf16)
    grad_output = ws(nt_dot(dmid_all.T, att))
    heads = wq.shape[1] // HD
    datt_t = datt.T.reshape(heads, HD, queries)
    att_t = att.reshape(heads, HD, queries)
    k_all = kaug[:, :HD]
    v_all = jnp.moveaxis(kv[:, HD:], 1, 2).reshape(-1, HD)

    def back(acc, ops):
        q, do, o, l = ops
        p = jnp.exp(nn_dot(kaug, q) - l[None, :])
        dp = nn_dot(v_all, do)
        delta = jnp.sum(do.astype(f32) * o.astype(f32), 0, keepdims=True)
        ds = (p * (dp - delta)).astype(bf16)
        dq = tn_dot(k_all, ds) * (HD ** (-0.5))
        dk = nt_dot(ds, q[:HD])
        dv = nt_dot(p.astype(bf16), do)
        return (acc + jnp.concatenate([dk, dv], 1), dq)

    dkv, dq = lax.scan(back, jnp.zeros((k_all.shape[0], 2 * HD), f32), (qaug, datt_t, att_t, lse))
    dkv = lax.psum_scatter(dkv, "ctx", scatter_dimension=0, tiled=True)

    def unrotate(v):
        v1, v2 = v[..., :half, :], v[..., half:, :]
        return jnp.concatenate([v1 * cos + v2 * sin, v2 * cos - v1 * sin], -2)

    dkv_t = dkv.T
    dkv_raw = jnp.concatenate([unrotate(dkv_t[:HD]), dkv_t[HD:]], 0).astype(bf16).T
    dq_raw = unrotate(dq).astype(bf16).reshape(heads * HD, queries).T
    grad_query = ws(tn_dot(n1, dq_raw))
    grad_keyval = ws(tn_dot(n1, dkv_raw))
    dn1 = rs((nt_dot(dq_raw, wq) + nt_dot(dkv_raw, wkv)).astype(bf16)).astype(f32)
    unit1, inv1 = apply_norm(x.astype(f32))
    ga, dres = norm_backward_pass(dn1, unit1, inv1, gains[0:1])
    input_grad = dmid + dres
    both = lax.psum(jnp.stack([ga, gm]), ("shard", "ctx", "tensor"))
    both = lax.dynamic_slice(both, (0, start), (2, gain_attn.shape[0]))
    return (
        layer_out[None], input_grad[None], both[0], grad_query, grad_keyval, grad_output,
        both[1], grad_gate, grad_up, grad_down,
    )


def solution(mesh):
    plane = P(("shard", "ctx"), "tensor")
    gain = P(("shard", "ctx"))
    token = P("shard", ("ctx", "tensor"), None)
    return jax.shard_map(
        body,
        mesh=mesh,
        in_specs=(token, token, P("shard", None), gain, plane, plane, plane, gain, plane, plane, plane),
        out_specs=(token, token, gain, plane, plane, plane, gain, plane, plane, plane),
        check_vma=False,
    )
```

```python
import functools

import jax
import jax.numpy as jnp
import numpy as np
from jax import lax
from jax.experimental import pallas as pl
from jax.experimental.pallas import tpu as pltpu
from jax.sharding import PartitionSpec as P

HD = 64
BLOCK = 256
BLOCKS = 8
ROWS = 16
CTX = 4
LINE = 4

epsilon = 1e-05
blocked = -1e30

f32 = jnp.float32
bf16 = jnp.bfloat16
MESH = pl.DeviceIdType.MESH


def nn_dot(left, right):
    return jnp.dot(left, right, preferred_element_type=f32)


def nt_dot(left, right):
    return lax.dot_general(left, right, (((1,), (1,)), ((), ())), preferred_element_type=f32)


def tn_dot(left, right):
    return lax.dot_general(left, right, (((0,), (0,)), ((), ())), preferred_element_type=f32)


class Links:
    def __init__(self, shards, send_sems, recv_sems, local_sems):
        self.shards = shards
        self.send_sems, self.recv_sems, self.local_sems = send_sems, recv_sems, local_sems
        self.s = lax.axis_index("shard")
        self.c = lax.axis_index("ctx")
        self.t = lax.axis_index("tensor")
        self.c_x = self.c + 1 - 2 * lax.rem(self.c, 2)
        self.c_y = lax.rem(self.c + 2, CTX)
        self.c_d = CTX - 1 - self.c
        self.x_dev = (self.s, self.c_x, self.t)
        self.y_dev = (self.s, self.c_y, self.t)
        self.right = (self.s, self.c, self.t + 1)
        self.left = (self.s, self.c, self.t - 1)
        self.used = 0
        self.local_used = 0
        self.sends = []
        self.locals = []

    def slots(self, count):
        first = self.used
        self.used += count
        assert self.used <= self.send_sems.shape[0]
        return first

    def plane_peer(self, step):
        index = lax.rem(self.s * CTX + self.c + step, self.shards * CTX)
        return (index // CTX, lax.rem(index, CTX), self.t)

    def core_peer(self, step):
        return (lax.rem(self.s + step, self.shards), self.c, self.t)

    def line_peer(self, step):
        return (self.s, self.c, lax.rem(self.t + step, LINE))

    def barrier(self, whole_line=False):
        sem = pltpu.get_barrier_semaphore()
        count = self.shards * CTX - 1
        for step in range(1, count + 1):
            pl.semaphore_signal(
                sem, inc=1, device_id=self.plane_peer(step), device_id_type=MESH
            )

        if whole_line:
            for step in range(1, LINE):
                pl.semaphore_signal(
                    sem, inc=1, device_id=self.line_peer(step), device_id_type=MESH
                )
            pl.semaphore_wait(sem, count + LINE - 1)
            return

        @pl.when(self.t > 0)
        def _():
            pl.semaphore_signal(sem, inc=1, device_id=self.left, device_id_type=MESH)

        @pl.when(self.t < LINE - 1)
        def _():
            pl.semaphore_signal(sem, inc=1, device_id=self.right, device_id_type=MESH)

        beside = (self.t + LINE - 1) // LINE + (2 * LINE - 2 - self.t) // LINE
        pl.semaphore_wait(sem, count + beside)

    def copy(self, src, dst, device, slot):
        return pltpu.make_async_remote_copy(
            src_ref=src,
            dst_ref=dst,
            send_sem=self.send_sems.at[slot],
            recv_sem=self.recv_sems.at[slot],
            device_id=device,
            device_id_type=MESH,
        )

    def send(self, src, dst, device, slot, cond=None):
        if cond is None:
            self.copy(src, dst, device, slot).start()
        else:

            @pl.when(cond)
            def _():
                self.copy(src, dst, device, slot).start()

        handle = (src, dst, device, slot, cond)
        self.sends.append(handle)
        return handle

    def sent(self, handle):
        self.sends = [other for other in self.sends if other is not handle]
        self.copy(*handle[:4]).wait_send()

    def recv(self, dst, slot):
        self.copy(dst, dst, self.x_dev, slot).wait_recv()

    def keep(self, src, dst):
        copy = pltpu.make_async_copy(src, dst, self.local_sems.at[self.local_used])
        self.local_used += 1
        assert self.local_used <= self.local_sems.shape[0]
        copy.start()
        return copy

    def keep_later(self, src, dst):
        self.locals.append(self.keep(src, dst))

    def finish(self):
        for src, dst, device, slot, cond in self.sends:
            if cond is None:
                self.copy(src, dst, device, slot).wait_send()
            else:

                @pl.when(cond)
                def _():
                    self.copy(src, dst, device, slot).wait_send()

        for copy in self.locals:
            copy.wait()


class PlaneGather:
    def __init__(self, links, src, full):
        self.links, self.src, self.full = links, src, full
        self.rows = src.shape[0]
        self.first = links.slots(4 + 4 * (links.shards - 1))

    def block(self, s, c):
        start = pl.multiple_of((s * CTX + c) * self.rows, self.rows)
        return self.full.at[pl.ds(start, self.rows)]

    def half(self, s, c, which):
        size = self.rows // 2
        start = pl.multiple_of((s * CTX + c) * self.rows + which * size, size)
        return self.full.at[pl.ds(start, size)]

    def core_slot(self, step, part):
        return self.first + 4 + (step - 1) * 4 + part

    def core_send(self, src, c, part):
        links = self.links
        for step in range(1, links.shards):
            links.send(
                src,
                self.block(links.s, c),
                links.core_peer(step),
                self.core_slot(step, part),
            )

    def start(self):
        links = self.links
        own = self.block(links.s, links.c)
        links.send(self.src, own, links.x_dev, self.first)
        links.send(self.src, own, links.y_dev, self.first + 1)
        self.core_send(self.src, links.c, 0)
        self.local = links.keep(self.src, own)

    def forward(self):
        links = self.links
        links.recv(self.block(links.s, links.c_x), self.first)
        links.recv(self.block(links.s, links.c_y), self.first + 1)
        from_x = self.half(links.s, links.c_x, 0)
        from_y = self.half(links.s, links.c_y, 1)
        links.send(from_x, from_x, links.y_dev, self.first + 2)
        links.send(from_y, from_y, links.x_dev, self.first + 3)
        self.core_send(self.block(links.s, links.c_x), links.c_x, 1)
        self.core_send(self.block(links.s, links.c_y), links.c_y, 2)

    def diagonal(self):
        links = self.links
        links.recv(self.half(links.s, links.c_d, 0), self.first + 2)
        links.recv(self.half(links.s, links.c_d, 1), self.first + 3)
        self.core_send(self.block(links.s, links.c_d), links.c_d, 3)

    def done(self):
        links = self.links
        for step in range(1, links.shards):
            other = lax.rem(links.s + links.shards - step, links.shards)
            for part, c in enumerate((links.c, links.c_x, links.c_y, links.c_d)):
                links.recv(self.block(other, c), self.core_slot(step, part))
        self.local.wait()


class LineGather:
    def __init__(self, links, own, full, tokens):
        self.links, self.own, self.full, self.tokens = links, own, full, tokens
        self.first = links.slots(2 * (LINE - 1))

    def block(self, owner):
        return self.full.at[pl.ds(pl.multiple_of(owner * self.tokens, self.tokens), self.tokens)]

    def send(self, k):
        links = self.links
        t, u = links.t, LINE - 1 - links.t
        right, left = self.block(t - k + 1), self.block(t + k - 1)
        links.send(
            self.own if k == 1 else right,
            right,
            links.right,
            self.first + k - 1,
            jnp.logical_and(t >= k - 1, t < LINE - 1),
        )
        links.send(
            self.own if k == 1 else left,
            left,
            links.left,
            self.first + LINE - 1 + k - 1,
            jnp.logical_and(u >= k - 1, u < LINE - 1),
        )

    def recv(self, k, use=None):
        links = self.links
        t, u = links.t, LINE - 1 - links.t

        @pl.when(t >= k)
        def _():
            links.recv(self.block(t - k), self.first + k - 1)

        @pl.when(u >= k)
        def _():
            links.recv(self.block(t + k), self.first + LINE - 1 + k - 1)

        if use is not None:

            @pl.when(t >= k)
            def _():
                use(t - k)

            @pl.when(u >= k)
            def _():
                use(t + k)


class LineScatter:
    def __init__(self, links, part, tokens, from_left, from_right):
        self.links, self.part, self.tokens = links, part, tokens
        self.from_left, self.from_right = from_left, from_right
        self.first = links.slots(2 * (LINE - 1))

    def clear(self):
        for cond, ref in (
            (self.links.t == 0, self.from_left),
            (self.links.t == LINE - 1, self.from_right),
        ):

            @pl.when(cond)
            def _():
                @pl.loop(0, self.tokens // ROWS)
                def _(i):
                    r = pl.multiple_of(i * ROWS, ROWS)
                    for k in range(LINE - 1):
                        ref[k, pl.ds(r, ROWS), :] = jnp.zeros((ROWS, ref.shape[2]), ref.dtype)

    def total(self, owner, k, arrived):
        @pl.loop(0, self.tokens // ROWS)
        def _(i):
            r = pl.multiple_of(i * ROWS, ROWS)
            q = pl.multiple_of(owner * self.tokens + i * ROWS, ROWS)
            mine = self.part[pl.ds(q, ROWS), :].astype(f32)
            summed = mine + arrived[k, pl.ds(r, ROWS), :].astype(f32)
            arrived[k, pl.ds(r, ROWS), :] = summed.astype(arrived.dtype)

    def step(self, k):
        links = self.links
        t = links.t
        slot_r, slot_l = self.first + k, self.first + LINE - 1 + k
        owner_r, owner_l = LINE - 1 - k, k

        @pl.when(t < owner_r)
        def _():
            @pl.when(t > 0)
            def _():
                links.recv(self.from_left.at[k], slot_r)

            self.total(owner_r, k, self.from_left)

        links.send(self.from_left.at[k], self.from_left.at[k], links.right, slot_r, t < owner_r)

        @pl.when(t > owner_l)
        def _():
            @pl.when(t < LINE - 1)
            def _():
                links.recv(self.from_right.at[k], slot_l)

            self.total(owner_l, k, self.from_right)

        links.send(self.from_right.at[k], self.from_right.at[k], links.left, slot_l, t > owner_l)

    def arrive(self):
        links = self.links
        t = links.t

        @pl.when(t > 0)
        def _():
            links.recv(self.from_left.at[LINE - 1 - t], self.first + LINE - 1 - t)

        @pl.when(t < LINE - 1)
        def _():
            links.recv(self.from_right.at[t], self.first + LINE - 1 + t)

    def rows(self, i):
        t = self.links.t
        r = pl.multiple_of(i * ROWS, ROWS)
        q = pl.multiple_of(t * self.tokens + i * ROWS, ROWS)
        k_l = jnp.minimum(LINE - 1 - t, LINE - 2)
        k_r = jnp.minimum(t, LINE - 2)
        zero = jnp.zeros((ROWS, self.part.shape[1]), f32)
        return (
            self.part[pl.ds(q, ROWS), :].astype(f32)
            + jnp.where(t > 0, self.from_left[k_l, pl.ds(r, ROWS), :].astype(f32), zero)
            + jnp.where(t < LINE - 1, self.from_right[k_r, pl.ds(r, ROWS), :].astype(f32), zero)
        )


class PlaneScatter:
    def __init__(self, links, left, right, rows, core_in, x_in, y_in, x_last, y_last, out):
        self.links, self.left, self.right, self.rows = links, left, right, rows
        self.core_in, self.x_in, self.y_in = core_in, x_in, y_in
        self.x_last, self.y_last, self.out = x_last, y_last, out
        self.first = links.slots(links.shards - 1 + 6)
        self.tile = min(256, CTX * rows)

    def product(self, shard, i):
        start = pl.multiple_of(shard * (CTX * self.rows) + i * self.tile, self.tile)
        return tn_dot(self.left[:, pl.ds(start, self.tile)], self.right[...])

    def other(self, step, stage):
        links = self.links
        target = lax.rem(links.s + step, links.shards)

        @pl.loop(0, CTX * self.rows // self.tile)
        def _(i):
            r = pl.multiple_of(i * self.tile, self.tile)
            stage[pl.ds(r, self.tile), :] = self.product(target, i).astype(bf16)

        return links.send(
            stage, self.core_in.at[step - 1], links.core_peer(step), self.first + step - 1
        )

    def own(self):
        links = self.links
        for step in range(1, links.shards):
            links.recv(self.core_in.at[step - 1], self.first + step - 1)

        @pl.loop(0, CTX * self.rows // self.tile)
        def _(i):
            r = pl.multiple_of(i * self.tile, self.tile)
            summed = self.product(links.s, i)
            for step in range(1, links.shards):
                summed = summed + self.core_in[step - 1, pl.ds(r, self.tile), :].astype(f32)
            self.core_in[0, pl.ds(r, self.tile), :] = summed.astype(bf16)

    def half(self, c, which):
        size = self.rows // 2
        start = pl.multiple_of(c * self.rows + which * size, size)
        return self.core_in.at[0, pl.ds(start, size)]

    def exchange(self):
        links, first = self.links, self.first + self.links.shards - 1
        links.send(self.half(links.c_d, 0), self.x_in.at[1], links.x_dev, first)
        links.send(self.half(links.c_d, 1), self.y_in.at[1], links.y_dev, first + 1)
        links.send(self.half(links.c_x, 0), self.x_in.at[0], links.x_dev, first + 2)
        links.send(self.half(links.c_y, 1), self.y_in.at[0], links.y_dev, first + 3)

    def add(self, c, which, arrived):
        size = self.rows // 2

        @pl.loop(0, size // ROWS)
        def _(i):
            r = pl.multiple_of(i * ROWS, ROWS)
            q = pl.multiple_of(c * self.rows + which * size + i * ROWS, ROWS)
            mine = self.core_in[0, pl.ds(q, ROWS), :].astype(f32)
            summed = mine + arrived[1, pl.ds(r, ROWS), :].astype(f32)
            self.core_in[0, pl.ds(q, ROWS), :] = summed.astype(bf16)

    def fold(self):
        links, first = self.links, self.first + self.links.shards - 1
        links.recv(self.x_in.at[1], first)
        self.add(links.c_y, 0, self.x_in)
        links.send(self.half(links.c_y, 0), self.y_last, links.y_dev, first + 4)
        links.recv(self.y_in.at[1], first + 1)
        self.add(links.c_x, 1, self.y_in)
        links.send(self.half(links.c_x, 1), self.x_last, links.x_dev, first + 5)

    def total(self):
        links, first = self.links, self.first + self.links.shards - 1
        size = self.rows // 2
        links.recv(self.x_in.at[0], first + 2)
        links.recv(self.y_in.at[0], first + 3)
        links.recv(self.y_last, first + 4)
        links.recv(self.x_last, first + 5)
        for which, arrived, last in ((0, self.x_in, self.y_last), (1, self.y_in, self.x_last)):

            @pl.loop(0, size // ROWS)
            def _(i):
                r = pl.multiple_of(i * ROWS, ROWS)
                q = pl.multiple_of(links.c * self.rows + which * size + i * ROWS, ROWS)
                self.out[pl.ds(which * size + r, ROWS), :] = (
                    self.core_in[0, pl.ds(q, ROWS), :].astype(f32)
                    + arrived[0, pl.ds(r, ROWS), :].astype(f32)
                    + last[pl.ds(r, ROWS), :].astype(f32)
                )

    @staticmethod
    def scratch(shards, rows, columns):
        half = (rows // 2, columns)
        return [
            pltpu.VMEM((shards - 1, CTX * rows, columns), bf16),
            pltpu.VMEM((2,) + half, bf16),
            pltpu.VMEM((2,) + half, bf16),
            pltpu.VMEM(half, bf16),
            pltpu.VMEM(half, bf16),
            pltpu.VMEM((rows, columns), f32),
        ]


def any_spec():
    return pl.BlockSpec(memory_space=pl.ANY)


def vmem_spec():
    return pl.BlockSpec(memory_space=pltpu.VMEM)


def struct(shape, dtype):
    return jax.ShapeDtypeStruct(shape, dtype)


def forward_kernel(
    shards,
    x, og, wq, wkv, wo, wg, wu, wd, gpad, cos, sin, bias,
    wq_o, wkv_o, wo_o, wg_o, wu_o, wd_o, n1_o, og_o, n2_o, mid_o, qaug_o, kaug_o, kv_o, att_o,
    lse, gains,
    x_all, n1_all, wq_all, wkv_all, wo_all, gains_all, qaug, kv_all, kaug, v_all, scores, weights,
    attn, part, from_left, from_right, mid, n2,
    send_sems, recv_sems, local_sems,
):
    tokens, width = x.shape
    queries = tokens * LINE
    heads = qaug.shape[0]
    links = Links(shards, send_sems, recv_sems, local_sems)
    s, c, t = links.s, links.c, links.t

    gather_x = LineGather(links, x, x_all, tokens)
    gather_og = LineGather(links, og, og_o, tokens)
    gather_n2 = LineGather(links, n2, n2_o, tokens)
    small = [PlaneGather(links, *pair) for pair in ((wq, wq_all), (wkv, wkv_all), (wo, wo_all))]
    large = [PlaneGather(links, *pair) for pair in ((wg, wg_o), (wu, wu_o), (wd, wd_o))]
    scatter = LineScatter(links, part, tokens, from_left, from_right)
    plane = shards * CTX
    gain_slot = links.slots(plane - 1)
    kv_slot = links.slots(3)

    links.barrier()
    me = s * CTX + c
    for step in range(1, plane):
        links.send(gpad, gains_all.at[me], links.plane_peer(step), gain_slot + step - 1)
    own_gain = links.keep(gpad, gains_all.at[me])
    gather_x.send(1)
    own_x = links.keep(x, x_all.at[pl.ds(pl.multiple_of(t * tokens, tokens), tokens)])
    for gather in small:
        gather.start()
    scatter.clear()
    own_gain.wait()
    for step in range(1, plane):
        other = lax.rem(me + plane - step, plane)
        links.recv(gains_all.at[other], gain_slot + step - 1)
    total = gains_all[0]
    for index in range(1, plane):
        total = total + gains_all[index]
    gains[...] = total
    own_x.wait()

    def norm_block(owner):
        @pl.loop(0, tokens // ROWS)
        def _(i):
            r = pl.multiple_of(owner * tokens + i * ROWS, ROWS)
            v = x_all[pl.ds(r, ROWS), :].astype(f32)
            inverse = lax.rsqrt(jnp.mean(v * v, -1, keepdims=True) + epsilon)
            n1_all[pl.ds(r, ROWS), :] = (v * inverse * gains[0:1, :]).astype(bf16)

    norm_block(t)
    gather_x.recv(1)
    gather_x.send(2)
    for gather in small:
        gather.forward()
    norm_pair(gather_x, norm_block, 1)
    large[0].start()
    gather_x.recv(2)
    gather_x.send(3)
    for gather in small:
        gather.diagonal()
    norm_pair(gather_x, norm_block, 2)
    large[1].start()
    large[2].start()
    gather_x.recv(3)
    gather_og.send(1)
    own_og = links.keep(og, og_o.at[pl.ds(pl.multiple_of(t * tokens, tokens), tokens)])
    norm_pair(gather_x, norm_block, 3)
    for gather in small:
        gather.done()

    kv_t = nn_dot(n1_all[...], wkv_all[...]).T
    half = HD // 2
    cosine, sine = cos[...], sin[...]
    k1, k2 = kv_t[0:half], kv_t[half:HD]
    kv_all[c, 0:half, :] = (k1 * cosine - k2 * sine).astype(bf16)
    kv_all[c, half:HD, :] = (k2 * cosine + k1 * sine).astype(bf16)
    kv_all[c, HD : 2 * HD, :] = kv_t[HD:].astype(bf16)
    for step in range(1, CTX):
        peer = lax.rem(c + step, CTX)
        links.send(kv_all.at[c], kv_all.at[c], (s, peer, t), kv_slot + step - 1)

    q_t = nn_dot(n1_all[...], wq_all[...]).T
    scale = HD ** (-0.5)
    for h in range(heads):
        v1, v2 = q_t[h * HD : h * HD + half], q_t[h * HD + half : (h + 1) * HD]
        qaug[h, 0:half, :] = ((v1 * cosine - v2 * sine).astype(bf16) * scale).astype(bf16)
        qaug[h, half:HD, :] = ((v2 * cosine + v1 * sine).astype(bf16) * scale).astype(bf16)
        qaug[h, HD:, :] = bias[...]
    links.keep_later(n1_all, n1_o)
    links.keep_later(wq_all, wq_o)
    links.keep_later(wkv_all, wkv_o)
    links.keep_later(wo_all, wo_o)
    links.keep_later(qaug, qaug_o)
    for step in range(1, CTX):
        other = lax.rem(c + CTX - step, CTX)
        links.recv(kv_all.at[other], kv_slot + step - 1)
    for other in range(CTX):
        row = lax.broadcasted_iota(jnp.int32, (HD, queries), 0)
        lane = lax.broadcasted_iota(jnp.int32, (HD, queries), 1)
        mark = (row == other * (queries // BLOCK) + lane // BLOCK).astype(f32).astype(bf16)
        both = jnp.concatenate([kv_all[other, 0:HD, :], mark], 0)
        kaug[other * queries : (other + 1) * queries, :] = both.T
        v_all[:, other * queries : (other + 1) * queries] = kv_all[other, HD : 2 * HD, :]
    links.keep_later(kaug, kaug_o)
    links.keep_later(kv_all, kv_o)

    length = queries * CTX

    def head(h):
        query = qaug[h]
        top = jnp.full((1, queries), -jnp.inf, f32)
        for b in range(0, length, BLOCK):
            block_scores = nn_dot(kaug[b : b + BLOCK, :], query)
            scores[b : b + BLOCK, :] = block_scores
            top = jnp.maximum(top, jnp.max(block_scores, 0, keepdims=True))
        norm = jnp.zeros((1, queries), f32)
        for b in range(0, length, BLOCK):
            exponent = jnp.exp(scores[b : b + BLOCK, :] - top)
            norm = norm + jnp.sum(exponent, 0, keepdims=True)
            weights[b : b + BLOCK, :] = exponent.astype(bf16)
        out = nn_dot(v_all[...], weights[...]) / norm
        attn[pl.ds(pl.multiple_of(h * HD, HD), HD), :] = out.astype(bf16)
        lse[pl.ds(h, 1), :] = top + jnp.log(norm)

    pl.loop(0, heads // 2)(head)
    gather_og.recv(1)
    gather_og.send(2)
    pl.loop(heads // 2, heads)(head)
    links.keep_later(attn, att_o)

    attn_rows = attn[...].T
    for b in range(0, width, 512):
        part[:, b : b + 512] = nt_dot(attn_rows, wo_all[b : b + 512, :])
    scatter.step(0)
    gather_og.recv(2)
    gather_og.send(3)
    for gather in large:
        gather.forward()
    scatter.step(1)
    scatter.step(2)
    for gather in large:
        gather.diagonal()
    scatter.arrive()

    @pl.loop(0, tokens // ROWS)
    def _(i):
        r = pl.multiple_of(i * ROWS, ROWS)
        q = pl.multiple_of(t * tokens + i * ROWS, ROWS)
        middle = x_all[pl.ds(q, ROWS), :].astype(f32) + scatter.rows(i)
        mid[pl.ds(r, ROWS), :] = middle
        inverse = lax.rsqrt(jnp.mean(middle * middle, -1, keepdims=True) + epsilon)
        n2[pl.ds(r, ROWS), :] = (middle * inverse * gains[1:2, :]).astype(bf16)

    gather_n2.send(1)
    links.keep_later(n2, n2_o.at[pl.ds(pl.multiple_of(t * tokens, tokens), tokens)])
    links.keep_later(mid, mid_o)
    gather_og.recv(3)
    own_og.wait()
    gather_n2.recv(1)
    gather_n2.send(2)
    for gather in large:
        gather.done()
    gather_n2.recv(2)
    gather_n2.send(3)
    gather_n2.recv(3)
    links.finish()


def norm_pair(gather, norm_block, k):
    t, u = gather.links.t, LINE - 1 - gather.links.t

    @pl.when(t >= k)
    def _():
        norm_block(t - k)

    @pl.when(u >= k)
    def _():
        norm_block(t + k)


def forward_call(shards, x, og, weights_in, gpad, cos, sin, bias):
    wq, wkv, wo, wg, wu, wd = weights_in
    tokens, width = x.shape
    queries = tokens * LINE
    length = queries * CTX
    heads = wq.shape[1] // HD
    plane = shards * CTX
    full = [struct((width, w.shape[1]), bf16) for w in weights_in]
    outs = full + [
        struct((queries, width), bf16),
        struct((queries, width), bf16),
        struct((queries, width), bf16),
        struct((tokens, width), f32),
        struct((heads, 2 * HD, queries), bf16),
        struct((length, 2 * HD), bf16),
        struct((CTX, 2 * HD, queries), bf16),
        struct((heads * HD, queries), bf16),
        struct((heads, queries), f32),
        struct((2, width), f32),
    ]
    block = (LINE - 1, tokens, width)
    count = 3 * 6 + 6 * (4 + 4 * (shards - 1)) + 6 + plane - 1 + 3
    return pl.pallas_call(
        functools.partial(forward_kernel, shards),
        out_shape=outs,
        in_specs=[any_spec()] * 8 + [vmem_spec()] * 4,
        out_specs=[any_spec()] * 14 + [vmem_spec()] * 2,
        scratch_shapes=[
            pltpu.VMEM((queries, width), bf16),
            pltpu.VMEM((queries, width), bf16),
            pltpu.VMEM((width, wq.shape[1]), bf16),
            pltpu.VMEM((width, wkv.shape[1]), bf16),
            pltpu.VMEM((width, wo.shape[1]), bf16),
            pltpu.VMEM((plane, 2, width), f32),
            pltpu.VMEM((heads, 2 * HD, queries), bf16),
            pltpu.VMEM((CTX, 2 * HD, queries), bf16),
            pltpu.VMEM((length, 2 * HD), bf16),
            pltpu.VMEM((HD, length), bf16),
            pltpu.VMEM((length, queries), f32),
            pltpu.VMEM((length, queries), bf16),
            pltpu.VMEM((heads * HD, queries), bf16),
            pltpu.VMEM((queries, width), f32),
            pltpu.VMEM(block, bf16),
            pltpu.VMEM(block, bf16),
            pltpu.VMEM((tokens, width), f32),
            pltpu.VMEM((tokens, width), bf16),
            pltpu.SemaphoreType.DMA((count,)),
            pltpu.SemaphoreType.DMA((count,)),
            pltpu.SemaphoreType.DMA((32,)),
        ],
        compiler_params=pltpu.CompilerParams(
            collective_id=0, has_side_effects=True, vmem_limit_bytes=60 * 2**20
        ),
        name="forward",
    )(x, og, wq, wkv, wo, wg, wu, wd, gpad, cos, sin, bias)


def middle_kernel(
    shards, rows,
    n2_in, og_in, wg_in, wu_in, wd_in, mid_in, gains,
    out_o, dmid_o, dmid_all_o, gg_o, gu_o, gd_o, gain_sum,
    n2, og, wg, wu, wd, mid, hidden, dgate, dup, part, branch,
    left_a, right_a, left_b, right_b, dmid, dsend, layer, gain_rows,
    *rest,
):
    grads, (send_sems, recv_sems, local_sems) = rest[:-3], rest[-3:]
    tokens, width = mid.shape
    queries = n2.shape[0]
    columns = wg.shape[1]
    links = Links(shards, send_sems, recv_sems, local_sems)
    t = links.t

    loads = [
        links.keep(src, dst)
        for src, dst in (
            (n2_in, n2), (wg_in, wg), (wu_in, wu), (og_in, og), (wd_in, wd), (mid_in, mid)
        )
    ]
    scatter = LineScatter(links, part, tokens, left_a, right_a)
    scatter_out = LineScatter(links, branch, tokens, left_b, right_b)
    gather = LineGather(links, dsend, dmid_all_o, tokens)
    down = PlaneScatter(links, og, hidden, rows, *grads[0:6])
    gate = PlaneScatter(links, n2, dgate, rows, *grads[6:12])
    up = PlaneScatter(links, n2, dup, rows, *grads[12:18])
    links.barrier()
    scatter.clear()
    scatter_out.clear()
    for load in loads:
        load.wait()

    for b in range(0, columns, 256):
        e = min(b + 256, columns)
        gate_act = nn_dot(n2[...], wg[:, b:e])
        up_act = nn_dot(n2[...], wu[:, b:e])
        d_hidden = nn_dot(og[...], wd[:, b:e])
        sig = jax.nn.sigmoid(gate_act)
        silu = gate_act * sig
        hidden[:, b:e] = (silu * up_act).astype(bf16)
        dgate[:, b:e] = (d_hidden * up_act * sig * (1.0 + gate_act * (1.0 - sig))).astype(bf16)
        dup[:, b:e] = (d_hidden * silu).astype(bf16)

    @pl.loop(0, width // 512)
    def _(j):
        at = pl.ds(pl.multiple_of(j * 512, 512), 512)
        part[:, at] = (nt_dot(dgate[...], wg[at, :]) + nt_dot(dup[...], wu[at, :])).astype(bf16)

    scatter.step(0)

    @pl.loop(0, width // 512)
    def _(j):
        at = pl.ds(pl.multiple_of(j * 512, 512), 512)
        branch[:, at] = nt_dot(hidden[...], wd[at, :]).astype(bf16)

    piece = CTX * rows
    room = (width // piece) // (shards - 1)

    def others(grad, index, before):
        handles = []
        for step in range(1, shards):
            at = ((index % room) * (shards - 1) + step - 1) * piece
            if before:
                links.sent(before[step - 1])
            handles.append(grad.other(step, wd.at[pl.ds(at, piece)]))
        return handles

    held = [others(down, 0, None)]
    held.append(others(gate, 1, held[1 - room] if room <= 1 else None))
    scatter.step(1)
    down.own()
    down.exchange()
    gate.own()
    gate.exchange()
    others(up, 2, held[2 - room] if room <= 2 else None)
    scatter.step(2)
    up.own()
    up.exchange()
    scatter.arrive()
    gain_rows[...] = jnp.zeros_like(gain_rows)

    @pl.loop(0, tokens // ROWS)
    def _(i):
        r = pl.ds(pl.multiple_of(i * ROWS, ROWS), ROWS)
        q = pl.ds(pl.multiple_of(t * tokens + i * ROWS, ROWS), ROWS)
        middle = mid[r, :]
        inverse = lax.rsqrt(jnp.mean(middle * middle, -1, keepdims=True) + epsilon)
        unit = middle * inverse
        d_normed = scatter.rows(i)
        gain_rows[...] += d_normed * unit
        d_unit = d_normed * gains[1:2, :]
        back = inverse * (d_unit - unit * jnp.mean(d_unit * unit, -1, keepdims=True))
        d_middle = og[q, :].astype(f32) + back
        dmid[r, :] = d_middle
        dsend[r, :] = d_middle.astype(bf16)

    gather.send(1)
    scatter_out.step(0)
    links.keep_later(dsend, dmid_all_o.at[pl.ds(pl.multiple_of(t * tokens, tokens), tokens)])
    links.keep_later(dmid, dmid_o)
    gain_sum[...] = jnp.sum(gain_rows[...], 0, keepdims=True)
    down.fold()
    gather.recv(1)
    gather.send(2)
    scatter_out.step(1)
    gate.fold()
    gather.recv(2)
    gather.send(3)
    scatter_out.step(2)
    up.fold()
    down.total()
    links.keep_later(down.out, gd_o)
    gate.total()
    links.keep_later(gate.out, gg_o)
    scatter_out.arrive()

    @pl.loop(0, tokens // ROWS)
    def _(i):
        r = pl.ds(pl.multiple_of(i * ROWS, ROWS), ROWS)
        layer[r, :] = (mid[r, :] + scatter_out.rows(i)).astype(bf16)

    links.keep_later(layer, out_o)
    gather.recv(3)
    up.total()
    links.keep_later(up.out, gu_o)
    links.finish()


def middle_call(shards, rows, n2, og, wg, wu, wd, mid, gains):
    queries, width = n2.shape
    tokens = mid.shape[0]
    columns = wg.shape[1]
    token = (tokens, width)
    wide = (queries, columns)
    block = (LINE - 1,) + token
    outs = [
        struct(token, bf16),
        struct(token, f32),
        struct((queries, width), bf16),
        struct((rows, columns), f32),
        struct((rows, columns), f32),
        struct((rows, columns), f32),
        struct((1, width), f32),
    ]
    count = 3 * 6 + 3 * (shards - 1 + 6)
    return pl.pallas_call(
        functools.partial(middle_kernel, shards, rows),
        out_shape=outs,
        in_specs=[any_spec()] * 6 + [vmem_spec()],
        out_specs=[any_spec()] * 6 + [vmem_spec()],
        scratch_shapes=[
            pltpu.VMEM((queries, width), bf16),
            pltpu.VMEM((queries, width), bf16),
            pltpu.VMEM((width, columns), bf16),
            pltpu.VMEM((width, columns), bf16),
            pltpu.VMEM((width, columns), bf16),
            pltpu.VMEM(token, f32),
            pltpu.VMEM(wide, bf16),
            pltpu.VMEM(wide, bf16),
            pltpu.VMEM(wide, bf16),
            pltpu.VMEM((queries, width), bf16),
            pltpu.VMEM((queries, width), bf16),
            pltpu.VMEM(block, bf16),
            pltpu.VMEM(block, bf16),
            pltpu.VMEM(block, bf16),
            pltpu.VMEM(block, bf16),
            pltpu.VMEM(token, f32),
            pltpu.VMEM(token, bf16),
            pltpu.VMEM(token, bf16),
            pltpu.VMEM((ROWS, width), f32),
            *PlaneScatter.scratch(shards, rows, columns),
            *PlaneScatter.scratch(shards, rows, columns),
            *PlaneScatter.scratch(shards, rows, columns),
            pltpu.SemaphoreType.DMA((count,)),
            pltpu.SemaphoreType.DMA((count,)),
            pltpu.SemaphoreType.DMA((16,)),
        ],
        compiler_params=pltpu.CompilerParams(
            collective_id=1, has_side_effects=True, vmem_limit_bytes=63 * 2**20
        ),
        name="middle",
    )(n2, og, wg, wu, wd, mid, gains)


def backward_kernel(
    shards, rows,
    dmid_all_in, wo_in, wq_in, wkv_in, n1_in, qaug_in, kaug_in, kv_in, att_in, x_in, dmid_in,
    lse, gains, gain_mlp, cos, sin,
    in_o, gq_o, gkv_o, go_o, gain_o,
    dmid_all, wo, wq, wkv, n1, qaug, kaug, kv, att, x, dmid,
    d_out, attn_rows, v_rows, d_keys, d_values, d_query, d_query_rows, kv_send, kv_recv, d_kv, part,
    left, right, gain_rows, pair, plane_in, line_in, total, stage_o, stage_q, stage_kv,
    *rest,
):
    grads, (send_sems, recv_sems, local_sems) = rest[:-3], rest[-3:]
    tokens, width = x.shape
    queries = n1.shape[0]
    heads = qaug.shape[0]
    length = kaug.shape[0]
    half = HD // 2
    plane = shards * CTX
    links = Links(shards, send_sems, recv_sems, local_sems)
    s, c, t = links.s, links.c, links.t

    loads = [
        links.keep(src, dst)
        for src, dst in (
            (dmid_all_in, dmid_all), (wo_in, wo), (att_in, att), (kv_in, kv), (qaug_in, qaug),
            (kaug_in, kaug), (n1_in, n1), (wq_in, wq), (wkv_in, wkv), (x_in, x), (dmid_in, dmid),
        )
    ]
    scatter = LineScatter(links, part, tokens, left, right)
    g_o = PlaneScatter(links, dmid_all, attn_rows, rows, *grads[0:6])
    g_q = PlaneScatter(links, n1, d_query_rows, rows, *grads[6:12])
    g_kv = PlaneScatter(links, n1, d_kv, rows, *grads[12:18])
    kv_slot = links.slots(CTX - 1)
    plane_slot = links.slots(plane - 1)
    line_slot = links.slots(LINE - 1)
    piece = CTX * rows

    def others(grad, stage):
        for step in range(1, shards):
            grad.other(step, stage.at[pl.ds((step - 1) * piece, piece)])

    links.barrier(whole_line=True)
    scatter.clear()
    for load in loads:
        load.wait()

    d_out[...] = nn_dot(dmid_all[...], wo[...]).astype(bf16).T
    attn_rows[...] = att[...].T
    for other in range(CTX):
        v_rows[other * queries : (other + 1) * queries, :] = kv[other, HD : 2 * HD, :].T
    d_keys[...] = jnp.zeros_like(d_keys)
    d_values[...] = jnp.zeros_like(d_values)
    others(g_o, stage_o)

    def head(h):
        at = pl.ds(pl.multiple_of(h * HD, HD), HD)
        query = qaug[h]
        d_head = d_out[at, :]
        delta = jnp.sum(d_head.astype(f32) * att[at, :].astype(f32), 0, keepdims=True)
        log_sum = lse[pl.ds(h, 1), :]
        d_q = jnp.zeros((HD, queries), f32)
        for b in range(0, length, BLOCK):
            e = b + BLOCK
            probs = jnp.exp(nn_dot(kaug[b:e, :], query) - log_sum)
            d_probs = nn_dot(v_rows[b:e, :], d_head)
            d_scores = (probs * (d_probs - delta)).astype(bf16)
            d_values[b:e, :] += nt_dot(probs.astype(bf16), d_head)
            d_keys[b:e, :] += nt_dot(d_scores, query[0:HD])
            at_b = b % queries
            d_q = d_q + nn_dot(kv[b // queries, 0:HD, at_b : at_b + BLOCK], d_scores)
        d_query[at, :] = d_q * (HD ** (-0.5))

    pl.loop(0, heads // 2)(head)
    g_o.own()
    g_o.exchange()
    pl.loop(heads // 2, heads)(head)
    g_o.fold()

    for other in range(CTX):
        block = slice(other * queries, (other + 1) * queries)
        both = jnp.concatenate([d_keys[block, :], d_values[block, :]], 1)
        kv_send[other] = both.astype(bf16)
    for step in range(1, CTX):
        peer = lax.rem(c + step, CTX)
        links.send(kv_send.at[peer], kv_recv.at[step - 1], (s, peer, t), kv_slot + step - 1)

    cosine, sine = cos[...], sin[...]
    for h in range(heads):
        at = h * HD
        d1, d2 = d_query[at : at + half, :], d_query[at + half : at + HD, :]
        d_query[at : at + half, :] = d1 * cosine + d2 * sine
        d_query[at + half : at + HD, :] = d2 * cosine - d1 * sine
    d_query_rows[...] = d_query[...].astype(bf16).T
    others(g_q, stage_q)
    for step in range(1, CTX):
        links.recv(kv_recv.at[step - 1], kv_slot + step - 1)
    d_pair = kv_send[c].astype(f32)
    for step in range(1, CTX):
        d_pair = d_pair + kv_recv[step - 1].astype(f32)
    d_pair = d_pair.T
    d1, d2 = d_pair[0:half], d_pair[half:HD]
    turned = jnp.concatenate(
        [d1 * cosine + d2 * sine, d2 * cosine - d1 * sine, d_pair[HD:]], 0
    )
    d_kv[...] = turned.astype(bf16).T

    @pl.loop(0, width // 512)
    def _(j):
        at = pl.ds(pl.multiple_of(j * 512, 512), 512)
        summed = nt_dot(d_query_rows[...], wq[at, :]) + nt_dot(d_kv[...], wkv[at, :])
        part[:, at] = summed.astype(bf16)

    scatter.step(0)
    others(g_kv, stage_kv)
    g_q.own()
    g_q.exchange()
    g_kv.own()
    g_kv.exchange()
    g_o.total()
    links.keep_later(g_o.out, go_o)
    scatter.step(1)
    g_q.fold()
    g_kv.fold()
    scatter.step(2)
    g_q.total()
    links.keep_later(g_q.out, gq_o)
    g_kv.total()
    links.keep_later(g_kv.out, gkv_o)
    gain_rows[...] = jnp.zeros_like(gain_rows)
    scatter.arrive()

    @pl.loop(0, tokens // ROWS)
    def _(i):
        r = pl.ds(pl.multiple_of(i * ROWS, ROWS), ROWS)
        v = x[r, :].astype(f32)
        inverse = lax.rsqrt(jnp.mean(v * v, -1, keepdims=True) + epsilon)
        unit = v * inverse
        d_normed = scatter.rows(i)
        gain_rows[...] += d_normed * unit
        d_unit = d_normed * gains[0:1, :]
        back = inverse * (d_unit - unit * jnp.mean(d_unit * unit, -1, keepdims=True))
        dmid[r, :] = dmid[r, :] + back

    pair[0:1, :] = jnp.sum(gain_rows[...], 0, keepdims=True)
    pair[1:2, :] = gain_mlp[...]
    for step in range(1, plane):
        links.send(pair, plane_in.at[step - 1], links.plane_peer(step), plane_slot + step - 1)
    links.keep_later(dmid, in_o)
    summed = pair[...]
    for step in range(1, plane):
        links.recv(plane_in.at[step - 1], plane_slot + step - 1)
        summed = summed + plane_in[step - 1]
    total[...] = summed
    for step in range(1, LINE):
        links.send(total, line_in.at[step - 1], links.line_peer(step), line_slot + step - 1)
    for step in range(1, LINE):
        links.recv(line_in.at[step - 1], line_slot + step - 1)
        summed = summed + line_in[step - 1]
    gain_o[...] = summed
    links.finish()


def backward_call(
    shards, rows, dmid_all, wo, wq, wkv, n1, qaug, kaug, kv, att, x, dmid, lse, gains, gain_mlp,
    cos, sin,
):
    tokens, width = x.shape
    queries = n1.shape[0]
    heads = qaug.shape[0]
    length = kaug.shape[0]
    inner = heads * HD
    plane = shards * CTX
    piece = CTX * rows * (shards - 1)
    token = (tokens, width)
    block = (LINE - 1,) + token
    outs = [
        struct(token, f32),
        struct((rows, inner), f32),
        struct((rows, 2 * HD), f32),
        struct((rows, inner), f32),
        struct((2, width), f32),
    ]
    count = 6 + 3 * (shards - 1 + 6) + CTX - 1 + plane - 1 + LINE - 1
    return pl.pallas_call(
        functools.partial(backward_kernel, shards, rows),
        out_shape=outs,
        in_specs=[any_spec()] * 11 + [vmem_spec()] * 5,
        out_specs=[any_spec()] * 4 + [vmem_spec()],
        scratch_shapes=[
            pltpu.VMEM((queries, width), bf16),
            pltpu.VMEM((width, inner), bf16),
            pltpu.VMEM((width, inner), bf16),
            pltpu.VMEM((width, 2 * HD), bf16),
            pltpu.VMEM((queries, width), bf16),
            pltpu.VMEM(qaug.shape, bf16),
            pltpu.VMEM(kaug.shape, bf16),
            pltpu.VMEM(kv.shape, bf16),
            pltpu.VMEM((inner, queries), bf16),
            pltpu.VMEM(token, bf16),
            pltpu.VMEM(token, f32),
            pltpu.VMEM((inner, queries), bf16),
            pltpu.VMEM((queries, inner), bf16),
            pltpu.VMEM((length, HD), bf16),
            pltpu.VMEM((length, HD), f32),
            pltpu.VMEM((length, HD), f32),
            pltpu.VMEM((inner, queries), f32),
            pltpu.VMEM((queries, inner), bf16),
            pltpu.VMEM((CTX, queries, 2 * HD), bf16),
            pltpu.VMEM((CTX - 1, queries, 2 * HD), bf16),
            pltpu.VMEM((queries, 2 * HD), bf16),
            pltpu.VMEM((queries, width), bf16),
            pltpu.VMEM(block, bf16),
            pltpu.VMEM(block, bf16),
            pltpu.VMEM((ROWS, width), f32),
            pltpu.VMEM((2, width), f32),
            pltpu.VMEM((plane - 1, 2, width), f32),
            pltpu.VMEM((LINE - 1, 2, width), f32),
            pltpu.VMEM((2, width), f32),
            pltpu.VMEM((piece, inner), bf16),
            pltpu.VMEM((piece, inner), bf16),
            pltpu.VMEM((piece, 2 * HD), bf16),
            *PlaneScatter.scratch(shards, rows, inner),
            *PlaneScatter.scratch(shards, rows, inner),
            *PlaneScatter.scratch(shards, rows, 2 * HD),
            pltpu.SemaphoreType.DMA((count,)),
            pltpu.SemaphoreType.DMA((count,)),
            pltpu.SemaphoreType.DMA((16,)),
        ],
        compiler_params=pltpu.CompilerParams(
            collective_id=2, has_side_effects=True, vmem_limit_bytes=60 * 2**20
        ),
        name="backward",
    )(
        dmid_all, wo, wq, wkv, n1, qaug, kaug, kv, att, x, dmid, lse, gains, gain_mlp, cos, sin
    )


def body(
    inputs, out_grad, block_order, gain_attn, w_query, w_keyval, w_output, gain_mlp, w_gate, w_up, w_down
):
    shards = lax.axis_size("shard")
    x, og = inputs[0], out_grad[0]
    tokens, width = x.shape
    queries = tokens * LINE
    order = block_order[0]
    s, c = lax.axis_index("shard"), lax.axis_index("ctx")
    per = queries // BLOCK
    here = lax.dynamic_slice_in_dim(order, c * per, per)
    block_here = jnp.repeat(here, BLOCK)
    position = block_here * BLOCK + jnp.tile(jnp.arange(BLOCK, dtype=jnp.int32), per)
    half = HD // 2
    frequency = 10000.0 ** (-jnp.arange(half, dtype=f32) * 2.0 / HD)
    angles = frequency[:, None] * position.astype(f32)[None, :]
    cos, sin = jnp.cos(angles), jnp.sin(angles)
    bias = jnp.where(order[:, None] <= block_here[None, :], 0.0, blocked).astype(bf16)
    bias = jnp.concatenate([bias, jnp.zeros((HD - BLOCKS, queries), bf16)], 0)
    start = (s * CTX + c) * gain_attn.shape[0]
    gpad = lax.dynamic_update_slice(
        jnp.zeros((2, width), f32), jnp.stack([gain_attn, gain_mlp]).astype(f32), (0, start)
    )
    (wq, wkv, wo, wg, wu, wd, n1, og_all, n2, mid, qaug, kaug, kv, att, lse, gains) = forward_call(
        shards, x, og, (w_query, w_keyval, w_output, w_gate, w_up, w_down), gpad, cos, sin, bias
    )
    (layer_out, dmid, dmid_all, grad_gate, grad_up, grad_down, gm) = middle_call(
        shards, w_gate.shape[0], n2, og_all, wg, wu, wd, mid, gains
    )
    (input_grad, grad_query, grad_keyval, grad_output, both) = backward_call(
        shards, w_query.shape[0], dmid_all, wo, wq, wkv, n1, qaug, kaug, kv, att, x, dmid,
        lse, gains, gm, cos, sin,
    )
    both = lax.dynamic_slice(both, (0, start), (2, gain_attn.shape[0]))
    return (
        layer_out[None], input_grad[None], both[0], grad_query, grad_keyval, grad_output,
        both[1], grad_gate, grad_up, grad_down,
    )


def solution(mesh):
    plane = P(("shard", "ctx"), "tensor")
    gain = P(("shard", "ctx"))
    token = P("shard", ("ctx", "tensor"), None)
    return jax.shard_map(
        body,
        mesh=mesh,
        in_specs=(token, token, P("shard", None), gain, plane, plane, plane, gain, plane, plane, plane),
        out_specs=(token, token, gain, plane, plane, plane, gain, plane, plane, plane),
        check_vma=False,
    )
```

```python
import functools

import jax
import jax.numpy as jnp
import numpy as np
from jax import lax
from jax.experimental import pallas as pl
from jax.experimental.pallas import tpu as pltpu
from jax.sharding import PartitionSpec as P

HD = 64
BLOCK = 256
BLOCKS = 8
ROWS = 16
CTX = 4
LINE = 4
PIECES = 2

epsilon = 1e-05
blocked = -1e30

f32 = jnp.float32
bf16 = jnp.bfloat16
MESH = pl.DeviceIdType.MESH


def place(owner):
    return (owner + (owner + 1) // 2) % LINE if isinstance(owner, int) else lax.rem(
        owner + (owner + 1) // 2, LINE
    )


def nn_dot(left, right):
    return jnp.dot(left, right, preferred_element_type=f32)


def nt_dot(left, right):
    return lax.dot_general(left, right, (((1,), (1,)), ((), ())), preferred_element_type=f32)


def tn_dot(left, right):
    return lax.dot_general(left, right, (((0,), (0,)), ((), ())), preferred_element_type=f32)


class Links:
    def __init__(self, shards, send_sems, recv_sems, local_sems):
        self.shards = shards
        self.send_sems, self.recv_sems, self.local_sems = send_sems, recv_sems, local_sems
        self.s = lax.axis_index("shard")
        self.c = lax.axis_index("ctx")
        self.t = lax.axis_index("tensor")
        self.c_x = self.c + 1 - 2 * lax.rem(self.c, 2)
        self.c_y = lax.rem(self.c + 2, CTX)
        self.c_d = CTX - 1 - self.c
        self.x_dev = (self.s, self.c_x, self.t)
        self.y_dev = (self.s, self.c_y, self.t)
        self.right = (self.s, self.c, self.t + 1)
        self.left = (self.s, self.c, self.t - 1)
        self.used = 0
        self.local_used = 0
        self.sends = []
        self.locals = []

    def slots(self, count):
        first = self.used
        self.used += count
        assert self.used <= self.send_sems.shape[0]
        return first

    def plane_peer(self, step):
        index = lax.rem(self.s * CTX + self.c + step, self.shards * CTX)
        return (index // CTX, lax.rem(index, CTX), self.t)

    def core_peer(self, step):
        return (lax.rem(self.s + step, self.shards), self.c, self.t)

    def line_peer(self, step):
        return (self.s, self.c, lax.rem(self.t + step, LINE))

    def barrier(self, whole_line=False):
        sem = pltpu.get_barrier_semaphore()
        count = self.shards * CTX - 1
        for step in range(1, count + 1):
            pl.semaphore_signal(
                sem, inc=1, device_id=self.plane_peer(step), device_id_type=MESH
            )

        if whole_line:
            for step in range(1, LINE):
                pl.semaphore_signal(
                    sem, inc=1, device_id=self.line_peer(step), device_id_type=MESH
                )
            pl.semaphore_wait(sem, count + LINE - 1)
            return

        @pl.when(self.t > 0)
        def _():
            pl.semaphore_signal(sem, inc=1, device_id=self.left, device_id_type=MESH)

        @pl.when(self.t < LINE - 1)
        def _():
            pl.semaphore_signal(sem, inc=1, device_id=self.right, device_id_type=MESH)

        beside = (self.t + LINE - 1) // LINE + (2 * LINE - 2 - self.t) // LINE
        pl.semaphore_wait(sem, count + beside)

    def copy(self, src, dst, device, slot):
        return pltpu.make_async_remote_copy(
            src_ref=src,
            dst_ref=dst,
            send_sem=self.send_sems.at[slot],
            recv_sem=self.recv_sems.at[slot],
            device_id=device,
            device_id_type=MESH,
        )

    def send(self, src, dst, device, slot, cond=None):
        if cond is None:
            self.copy(src, dst, device, slot).start()
        else:

            @pl.when(cond)
            def _():
                self.copy(src, dst, device, slot).start()

        handle = (src, dst, device, slot, cond)
        self.sends.append(handle)
        return handle

    def sent(self, handle):
        self.sends = [other for other in self.sends if other is not handle]
        self.copy(*handle[:4]).wait_send()

    def recv(self, dst, slot):
        self.copy(dst, dst, self.x_dev, slot).wait_recv()

    def keep(self, src, dst):
        copy = pltpu.make_async_copy(src, dst, self.local_sems.at[self.local_used])
        self.local_used += 1
        assert self.local_used <= self.local_sems.shape[0]
        copy.start()
        return copy

    def keep_later(self, src, dst):
        self.locals.append(self.keep(src, dst))

    def finish(self):
        for src, dst, device, slot, cond in self.sends:
            if cond is None:
                self.copy(src, dst, device, slot).wait_send()
            else:

                @pl.when(cond)
                def _():
                    self.copy(src, dst, device, slot).wait_send()

        for copy in self.locals:
            copy.wait()


class PlaneGather:
    def __init__(self, links, src, full, stage=None):
        self.links, self.src, self.full, self.stage = links, src, full, stage
        self.rows = src.shape[0]
        self.first = links.slots(4 + 4 * (links.shards - 1))

    def block(self, s, c):
        start = pl.multiple_of((s * CTX + c) * self.rows, self.rows)
        return self.full.at[pl.ds(start, self.rows)]

    def half(self, s, c, which):
        size = self.rows // 2
        start = pl.multiple_of((s * CTX + c) * self.rows + which * size, size)
        return self.full.at[pl.ds(start, size)]

    def core_slot(self, step, part):
        return self.first + 4 + (step - 1) * 4 + part

    def core_send(self, src, c, part):
        links = self.links
        for step in range(1, links.shards):
            links.send(
                src,
                self.block(links.s, c),
                links.core_peer(step),
                self.core_slot(step, part),
            )

    def start(self):
        links = self.links
        own = self.block(links.s, links.c)
        links.send(self.src, own, links.x_dev, self.first)
        links.send(self.src, own, links.y_dev, self.first + 1)
        self.core_send(self.src, links.c, 0)
        self.local = links.keep(self.src, own if self.stage is None else self.stage)

    def settle(self):
        self.local.wait()
        self.local = self.links.keep(self.stage, self.block(self.links.s, self.links.c))

    def forward(self):
        links = self.links
        links.recv(self.block(links.s, links.c_x), self.first)
        links.recv(self.block(links.s, links.c_y), self.first + 1)
        from_x = self.half(links.s, links.c_x, 0)
        from_y = self.half(links.s, links.c_y, 1)
        links.send(from_x, from_x, links.y_dev, self.first + 2)
        links.send(from_y, from_y, links.x_dev, self.first + 3)
        self.core_send(self.block(links.s, links.c_x), links.c_x, 1)
        self.core_send(self.block(links.s, links.c_y), links.c_y, 2)

    def diagonal(self):
        links = self.links
        links.recv(self.half(links.s, links.c_d, 0), self.first + 2)
        links.recv(self.half(links.s, links.c_d, 1), self.first + 3)
        self.core_send(self.block(links.s, links.c_d), links.c_d, 3)

    def done(self):
        links = self.links
        for step in range(1, links.shards):
            other = lax.rem(links.s + links.shards - step, links.shards)
            for part, c in enumerate((links.c, links.c_x, links.c_y, links.c_d)):
                links.recv(self.block(other, c), self.core_slot(step, part))
        self.local.wait()


class LineGather:
    def __init__(self, links, own, full, tokens, pieces=1):
        self.links, self.own, self.full, self.tokens = links, own, full, tokens
        self.pieces, self.size = pieces, tokens // pieces
        self.first = links.slots(2 * (LINE - 1) * pieces)

    def block(self, owner, p):
        start = pl.multiple_of(place(owner) * self.tokens + p * self.size, self.size)
        return self.full.at[pl.ds(start, self.size)]

    def slot(self, side, k, p):
        return self.first + (side * (LINE - 1) + k - 1) * self.pieces + p

    def send(self, k, p=0):
        links = self.links
        t, u = links.t, LINE - 1 - links.t
        own = self.own.at[pl.ds(p * self.size, self.size)]
        right, left = self.block(t - k + 1, p), self.block(t + k - 1, p)
        links.send(
            own if k == 1 else right,
            right,
            links.right,
            self.slot(0, k, p),
            jnp.logical_and(t >= k - 1, t < LINE - 1),
        )
        links.send(
            own if k == 1 else left,
            left,
            links.left,
            self.slot(1, k, p),
            jnp.logical_and(u >= k - 1, u < LINE - 1),
        )

    def recv(self, k, p=0):
        links = self.links
        t, u = links.t, LINE - 1 - links.t

        @pl.when(t >= k)
        def _():
            links.recv(self.block(t - k, p), self.slot(0, k, p))

        @pl.when(u >= k)
        def _():
            links.recv(self.block(t + k, p), self.slot(1, k, p))


class LineScatter:
    def __init__(self, links, part, tokens, from_left, from_right, pieces=1):
        self.links, self.part, self.tokens = links, part, tokens
        self.from_left, self.from_right = from_left, from_right
        self.pieces, self.size = pieces, tokens // pieces
        self.first = links.slots(2 * (LINE - 1) * pieces)

    def slot(self, side, k, p):
        return self.first + (side * (LINE - 1) + k) * self.pieces + p

    def piece(self, ref, k, p):
        return ref.at[k, pl.ds(p * self.size, self.size)]

    def clear(self):
        for cond, ref in (
            (self.links.t == 0, self.from_left),
            (self.links.t == LINE - 1, self.from_right),
        ):

            @pl.when(cond)
            def _():
                @pl.loop(0, self.tokens // ROWS)
                def _(i):
                    r = pl.multiple_of(i * ROWS, ROWS)
                    for k in range(LINE - 1):
                        ref[k, pl.ds(r, ROWS), :] = jnp.zeros((ROWS, ref.shape[2]), ref.dtype)

    def total(self, owner, k, p, arrived):
        @pl.loop(0, self.size // ROWS)
        def _(i):
            r = pl.multiple_of(p * self.size + i * ROWS, ROWS)
            q = pl.multiple_of(place(owner) * self.tokens + p * self.size + i * ROWS, ROWS)
            mine = self.part[pl.ds(q, ROWS), :].astype(f32)
            summed = mine + arrived[k, pl.ds(r, ROWS), :].astype(f32)
            arrived[k, pl.ds(r, ROWS), :] = summed.astype(arrived.dtype)

    def step(self, k, p=0):
        links = self.links
        t = links.t
        slot_r, slot_l = self.slot(0, k, p), self.slot(1, k, p)
        owner_r, owner_l = LINE - 1 - k, k
        piece_r, piece_l = self.piece(self.from_left, k, p), self.piece(self.from_right, k, p)

        @pl.when(t < owner_r)
        def _():
            @pl.when(t > 0)
            def _():
                links.recv(piece_r, slot_r)

            self.total(owner_r, k, p, self.from_left)

        links.send(piece_r, piece_r, links.right, slot_r, t < owner_r)

        @pl.when(t > owner_l)
        def _():
            @pl.when(t < LINE - 1)
            def _():
                links.recv(piece_l, slot_l)

            self.total(owner_l, k, p, self.from_right)

        links.send(piece_l, piece_l, links.left, slot_l, t > owner_l)

    def arrive(self, p=0):
        links = self.links
        t = links.t

        @pl.when(t > 0)
        def _():
            links.recv(
                self.piece(self.from_left, LINE - 1 - t, p), self.slot(0, LINE - 1 - t, p)
            )

        @pl.when(t < LINE - 1)
        def _():
            links.recv(self.piece(self.from_right, t, p), self.slot(1, t, p))

    def rows(self, r):
        t = self.links.t
        q = pl.multiple_of(place(t) * self.tokens + r, ROWS)
        k_l = jnp.minimum(LINE - 1 - t, LINE - 2)
        k_r = jnp.minimum(t, LINE - 2)
        zero = jnp.zeros((ROWS, self.part.shape[1]), f32)
        return (
            self.part[pl.ds(q, ROWS), :].astype(f32)
            + jnp.where(t > 0, self.from_left[k_l, pl.ds(r, ROWS), :].astype(f32), zero)
            + jnp.where(t < LINE - 1, self.from_right[k_r, pl.ds(r, ROWS), :].astype(f32), zero)
        )

    def owned(self, p, use):
        @pl.loop(0, self.size // ROWS)
        def _(i):
            r = pl.multiple_of(p * self.size + i * ROWS, ROWS)
            use(r, self.rows(r))


def line_steps(scatter, k, hooks=()):
    for p in range(scatter.pieces):
        scatter.step(k, p)
    for hook in hooks:
        hook()


def line_finish(scatter, use, gather=None):
    for p in range(scatter.pieces):
        scatter.arrive(p)
        scatter.owned(p, use)
        if gather is not None:
            gather.send(1, p)


def line_spread(gather, k):
    for p in range(gather.pieces):
        gather.recv(k, p)
        if k < LINE - 1:
            gather.send(k + 1, p)


class PlaneScatter:
    def __init__(self, links, left, right, rows, core_in, x_in, y_in, x_last, y_last, out):
        self.links, self.left, self.right, self.rows = links, left, right, rows
        self.core_in, self.x_in, self.y_in = core_in, x_in, y_in
        self.x_last, self.y_last, self.out = x_last, y_last, out
        self.first = links.slots(links.shards - 1 + 6)
        self.tile = min(256, CTX * rows)

    def product(self, shard, i):
        start = pl.multiple_of(shard * (CTX * self.rows) + i * self.tile, self.tile)
        return tn_dot(self.left[:, pl.ds(start, self.tile)], self.right[...])

    @property
    def tiles(self):
        return CTX * self.rows // self.tile

    def other(self, step, stage, part=None):
        links = self.links
        target = lax.rem(links.s + step, links.shards)
        low, high = (0, self.tiles) if part is None else part

        @pl.loop(low, high)
        def _(i):
            r = pl.multiple_of(i * self.tile, self.tile)
            stage[pl.ds(r, self.tile), :] = self.product(target, i).astype(bf16)

        if high == self.tiles:
            return links.send(
                stage, self.core_in.at[step - 1], links.core_peer(step), self.first + step - 1
            )

    def own(self, part=None):
        links = self.links
        low, high = (0, self.tiles) if part is None else part
        if low == 0:
            for step in range(1, links.shards):
                links.recv(self.core_in.at[step - 1], self.first + step - 1)

        @pl.loop(low, high)
        def _(i):
            r = pl.multiple_of(i * self.tile, self.tile)
            summed = self.product(links.s, i)
            for step in range(1, links.shards):
                summed = summed + self.core_in[step - 1, pl.ds(r, self.tile), :].astype(f32)
            self.core_in[0, pl.ds(r, self.tile), :] = summed.astype(bf16)

    def half(self, c, which):
        size = self.rows // 2
        start = pl.multiple_of(c * self.rows + which * size, size)
        return self.core_in.at[0, pl.ds(start, size)]

    def exchange(self):
        links, first = self.links, self.first + self.links.shards - 1
        links.send(self.half(links.c_d, 0), self.x_in.at[1], links.x_dev, first)
        links.send(self.half(links.c_d, 1), self.y_in.at[1], links.y_dev, first + 1)
        links.send(self.half(links.c_x, 0), self.x_in.at[0], links.x_dev, first + 2)
        links.send(self.half(links.c_y, 1), self.y_in.at[0], links.y_dev, first + 3)

    def add(self, c, which, arrived):
        size = self.rows // 2

        @pl.loop(0, size // ROWS)
        def _(i):
            r = pl.multiple_of(i * ROWS, ROWS)
            q = pl.multiple_of(c * self.rows + which * size + i * ROWS, ROWS)
            mine = self.core_in[0, pl.ds(q, ROWS), :].astype(f32)
            summed = mine + arrived[1, pl.ds(r, ROWS), :].astype(f32)
            self.core_in[0, pl.ds(q, ROWS), :] = summed.astype(bf16)

    def fold(self):
        links, first = self.links, self.first + self.links.shards - 1
        links.recv(self.x_in.at[1], first)
        self.add(links.c_y, 0, self.x_in)
        links.send(self.half(links.c_y, 0), self.y_last, links.y_dev, first + 4)
        links.recv(self.y_in.at[1], first + 1)
        self.add(links.c_x, 1, self.y_in)
        links.send(self.half(links.c_x, 1), self.x_last, links.x_dev, first + 5)

    def total(self):
        links, first = self.links, self.first + self.links.shards - 1
        size = self.rows // 2
        links.recv(self.x_in.at[0], first + 2)
        links.recv(self.y_in.at[0], first + 3)
        links.recv(self.y_last, first + 4)
        links.recv(self.x_last, first + 5)
        for which, arrived, last in ((0, self.x_in, self.y_last), (1, self.y_in, self.x_last)):

            @pl.loop(0, size // ROWS)
            def _(i):
                r = pl.multiple_of(i * ROWS, ROWS)
                q = pl.multiple_of(links.c * self.rows + which * size + i * ROWS, ROWS)
                self.out[pl.ds(which * size + r, ROWS), :] = (
                    self.core_in[0, pl.ds(q, ROWS), :].astype(f32)
                    + arrived[0, pl.ds(r, ROWS), :].astype(f32)
                    + last[pl.ds(r, ROWS), :].astype(f32)
                )

    @staticmethod
    def scratch(shards, rows, columns):
        half = (rows // 2, columns)
        return [
            pltpu.VMEM((shards - 1, CTX * rows, columns), bf16),
            pltpu.VMEM((2,) + half, bf16),
            pltpu.VMEM((2,) + half, bf16),
            pltpu.VMEM(half, bf16),
            pltpu.VMEM(half, bf16),
            pltpu.VMEM((rows, columns), f32),
        ]


def any_spec():
    return pl.BlockSpec(memory_space=pl.ANY)


def vmem_spec():
    return pl.BlockSpec(memory_space=pltpu.VMEM)


def struct(shape, dtype):
    return jax.ShapeDtypeStruct(shape, dtype)


def forward_kernel(
    shards,
    x, og, wq, wkv, wo, wg, wu, wd, gpad, cos, sin, bias,
    wq_o, wkv_o, wo_o, wg_o, wu_o, wd_o, n1_o, og_o, n2_o, mid_o, qaug_o, kaug_o, kv_o, att_o, x_o,
    lse, gains,
    x_all, n1_all, wq_all, wkv_all, wo_all, gains_all, qaug, kv_all, kaug, v_all, scores, weights,
    attn, part, from_left, from_right, mid, n2, og_stage, wg_stage, wu_stage, wd_stage,
    send_sems, recv_sems, local_sems,
):
    tokens, width = x.shape
    queries = tokens * LINE
    heads = qaug.shape[0]
    links = Links(shards, send_sems, recv_sems, local_sems)
    s, c, t = links.s, links.c, links.t

    gather_x = LineGather(links, x, x_all, tokens)
    gather_og = LineGather(links, og, og_o, tokens)
    gather_n2 = LineGather(links, n2, n2_o, tokens, PIECES)
    small = [PlaneGather(links, *pair) for pair in ((wq, wq_all), (wkv, wkv_all), (wo, wo_all))]
    large = [
        PlaneGather(links, *three)
        for three in ((wg, wg_o, wg_stage), (wu, wu_o, wu_stage), (wd, wd_o, wd_stage))
    ]
    scatter = LineScatter(links, part, tokens, from_left, from_right, PIECES)
    plane = shards * CTX
    gain_slot = links.slots(plane - 1)
    kv_slot = links.slots(3)

    links.barrier()
    me = s * CTX + c
    for step in range(1, plane):
        links.send(gpad, gains_all.at[me], links.plane_peer(step), gain_slot + step - 1)
    own_gain = links.keep(gpad, gains_all.at[me])
    gather_x.send(1)
    own_rows = pl.ds(pl.multiple_of(place(t) * tokens, tokens), tokens)
    own_x = links.keep(x, x_all.at[own_rows])
    for gather in small:
        gather.start()
    scatter.clear()
    own_gain.wait()
    for step in range(1, plane):
        other = lax.rem(me + plane - step, plane)
        links.recv(gains_all.at[other], gain_slot + step - 1)
    total = gains_all[0]
    for index in range(1, plane):
        total = total + gains_all[index]
    gains[...] = total
    own_x.wait()

    def norm_block(owner):
        @pl.loop(0, tokens // ROWS)
        def _(i):
            r = pl.multiple_of(place(owner) * tokens + i * ROWS, ROWS)
            v = x_all[pl.ds(r, ROWS), :].astype(f32)
            inverse = lax.rsqrt(jnp.mean(v * v, -1, keepdims=True) + epsilon)
            n1_all[pl.ds(r, ROWS), :] = (v * inverse * gains[0:1, :]).astype(bf16)

    own_og = links.keep(og, og_stage)
    norm_block(t)
    gather_x.recv(1)
    gather_x.send(2)
    for gather in small:
        gather.forward()
    large[0].start()
    norm_pair(gather_x, norm_block, 1)
    gather_x.recv(2)
    gather_x.send(3)
    gather_og.send(1)
    for gather in small:
        gather.diagonal()
    norm_pair(gather_x, norm_block, 2)
    own_og.wait()
    links.keep_later(og_stage, og_o.at[own_rows])
    gather_x.recv(3)
    norm_pair(gather_x, norm_block, 3)
    for gather in small:
        gather.done()

    kv_t = nn_dot(n1_all[...], wkv_all[...]).T
    half = HD // 2
    cosine, sine = cos[...], sin[...]
    k1, k2 = kv_t[0:half], kv_t[half:HD]
    kv_all[c, 0:half, :] = (k1 * cosine - k2 * sine).astype(bf16)
    kv_all[c, half:HD, :] = (k2 * cosine + k1 * sine).astype(bf16)
    kv_all[c, HD : 2 * HD, :] = kv_t[HD:].astype(bf16)
    for step in range(1, CTX):
        peer = lax.rem(c + step, CTX)
        links.send(kv_all.at[c], kv_all.at[c], (s, peer, t), kv_slot + step - 1)
    large[0].settle()
    large[0].forward()
    large[1].start()
    large[2].start()

    q_t = nn_dot(n1_all[...], wq_all[...]).T
    scale = HD ** (-0.5)
    for h in range(heads):
        v1, v2 = q_t[h * HD : h * HD + half], q_t[h * HD + half : (h + 1) * HD]
        qaug[h, 0:half, :] = ((v1 * cosine - v2 * sine).astype(bf16) * scale).astype(bf16)
        qaug[h, half:HD, :] = ((v2 * cosine + v1 * sine).astype(bf16) * scale).astype(bf16)
        qaug[h, HD:, :] = bias[...]
    links.keep_later(n1_all, n1_o)
    links.keep_later(x_all, x_o)
    links.keep_later(wq_all, wq_o)
    links.keep_later(wkv_all, wkv_o)
    links.keep_later(wo_all, wo_o)
    links.keep_later(qaug, qaug_o)
    for step in range(1, CTX):
        other = lax.rem(c + CTX - step, CTX)
        links.recv(kv_all.at[other], kv_slot + step - 1)
    for other in range(CTX):
        row = lax.broadcasted_iota(jnp.int32, (HD, queries), 0)
        lane = lax.broadcasted_iota(jnp.int32, (HD, queries), 1)
        mark = (row == other * (queries // BLOCK) + lax.rem(lane // tokens, 2)).astype(f32).astype(bf16)
        both = jnp.concatenate([kv_all[other, 0:HD, :], mark], 0)
        kaug[other * queries : (other + 1) * queries, :] = both.T
        v_all[:, other * queries : (other + 1) * queries] = kv_all[other, HD : 2 * HD, :]
    links.keep_later(kaug, kaug_o)
    links.keep_later(kv_all, kv_o)

    length = queries * CTX

    side = queries // 2

    def head(half, h):
        lanes = slice(half * side, (half + 1) * side)
        query = qaug[h, :, lanes]
        top = jnp.full((1, side), -jnp.inf, f32)
        for b in range(0, length, BLOCK):
            block_scores = nn_dot(kaug[b : b + BLOCK, :], query)
            scores[b : b + BLOCK, :] = block_scores
            top = jnp.maximum(top, jnp.max(block_scores, 0, keepdims=True))
        norm = jnp.zeros((1, side), f32)
        for b in range(0, length, BLOCK):
            exponent = jnp.exp(scores[b : b + BLOCK, :] - top)
            norm = norm + jnp.sum(exponent, 0, keepdims=True)
            weights[b : b + BLOCK, :] = exponent.astype(bf16)
        out = nn_dot(v_all[...], weights[...]) / norm
        attn[pl.ds(pl.multiple_of(h * HD, HD), HD), lanes] = out.astype(bf16)
        lse[pl.ds(h, 1), lanes] = top + jnp.log(norm)

    def project(half):
        rows = slice(half * side, (half + 1) * side)
        attn_rows = attn[:, rows].T
        for b in range(0, width, 512):
            part[rows, b : b + 512] = nt_dot(attn_rows, wo_all[b : b + 512, :])

    pl.loop(0, heads)(functools.partial(head, 0))
    gather_og.recv(1)
    gather_og.send(2)
    project(0)
    line_steps(scatter, 0)
    large[1].settle()
    large[2].settle()
    pl.loop(0, heads)(functools.partial(head, 1))
    project(1)
    links.keep_later(attn, att_o)

    def finish_rows(r, summed):
        q = pl.multiple_of(place(t) * tokens + r, ROWS)
        middle = x_all[pl.ds(q, ROWS), :].astype(f32) + summed
        mid[pl.ds(r, ROWS), :] = middle
        inverse = lax.rsqrt(jnp.mean(middle * middle, -1, keepdims=True) + epsilon)
        n2[pl.ds(r, ROWS), :] = (middle * inverse * gains[1:2, :]).astype(bf16)

    line_steps(scatter, 1)
    gather_og.recv(2)
    gather_og.send(3)
    large[0].diagonal()
    line_steps(scatter, 2)
    large[1].forward()
    large[2].forward()
    line_finish(scatter, finish_rows, gather_n2)
    links.keep_later(n2, n2_o.at[own_rows])
    links.keep_later(mid, mid_o)
    gather_og.recv(3)
    line_spread(gather_n2, 1)
    large[1].diagonal()
    large[2].diagonal()
    line_spread(gather_n2, 2)
    for gather in large:
        gather.done()
    line_spread(gather_n2, 3)
    links.finish()


def norm_pair(gather, norm_block, k):
    t, u = gather.links.t, LINE - 1 - gather.links.t

    @pl.when(t >= k)
    def _():
        norm_block(t - k)

    @pl.when(u >= k)
    def _():
        norm_block(t + k)


def forward_call(shards, x, og, weights_in, gpad, cos, sin, bias):
    wq, wkv, wo, wg, wu, wd = weights_in
    tokens, width = x.shape
    queries = tokens * LINE
    length = queries * CTX
    heads = wq.shape[1] // HD
    plane = shards * CTX
    full = [struct((width, w.shape[1]), bf16) for w in weights_in]
    outs = full + [
        struct((queries, width), bf16),
        struct((queries, width), bf16),
        struct((queries, width), bf16),
        struct((tokens, width), f32),
        struct((heads, 2 * HD, queries), bf16),
        struct((length, 2 * HD), bf16),
        struct((CTX, 2 * HD, queries), bf16),
        struct((heads * HD, queries), bf16),
        struct((queries, width), bf16),
        struct((heads, queries), f32),
        struct((2, width), f32),
    ]
    block = (LINE - 1, tokens, width)
    count = 12 * (1 + PIECES) + 6 * (4 + 4 * (shards - 1)) + plane - 1 + 3
    return pl.pallas_call(
        functools.partial(forward_kernel, shards),
        out_shape=outs,
        in_specs=[any_spec()] * 8 + [vmem_spec()] * 4,
        out_specs=[any_spec()] * 15 + [vmem_spec()] * 2,
        scratch_shapes=[
            pltpu.VMEM((queries, width), bf16),
            pltpu.VMEM((queries, width), bf16),
            pltpu.VMEM((width, wq.shape[1]), bf16),
            pltpu.VMEM((width, wkv.shape[1]), bf16),
            pltpu.VMEM((width, wo.shape[1]), bf16),
            pltpu.VMEM((plane, 2, width), f32),
            pltpu.VMEM((heads, 2 * HD, queries), bf16),
            pltpu.VMEM((CTX, 2 * HD, queries), bf16),
            pltpu.VMEM((length, 2 * HD), bf16),
            pltpu.VMEM((HD, length), bf16),
            pltpu.VMEM((length, queries // 2), f32),
            pltpu.VMEM((length, queries // 2), bf16),
            pltpu.VMEM((heads * HD, queries), bf16),
            pltpu.VMEM((queries, width), f32),
            pltpu.VMEM(block, bf16),
            pltpu.VMEM(block, bf16),
            pltpu.VMEM((tokens, width), f32),
            pltpu.VMEM((tokens, width), bf16),
            pltpu.VMEM((tokens, width), bf16),
            pltpu.VMEM(wg.shape, bf16),
            pltpu.VMEM(wu.shape, bf16),
            pltpu.VMEM(wd.shape, bf16),
            pltpu.SemaphoreType.DMA((count,)),
            pltpu.SemaphoreType.DMA((count,)),
            pltpu.SemaphoreType.DMA((32,)),
        ],
        compiler_params=pltpu.CompilerParams(
            collective_id=0, has_side_effects=True, vmem_limit_bytes=60 * 2**20
        ),
        name="forward",
    )(x, og, wq, wkv, wo, wg, wu, wd, gpad, cos, sin, bias)


def middle_kernel(
    shards, rows,
    n2_in, og_in, wg_in, wu_in, wd_in, mid_in, gains,
    dmid_o, dmid_all_o, gg_o, gd_o, branch_o, gu_part_o, gain_sum,
    n2, og, wg, wu, wd, mid, hidden, dgate, dup, part, branch,
    left, right, dmid, dsend, gain_rows, up_in,
    *rest,
):
    grads, (send_sems, recv_sems, local_sems) = rest[:-3], rest[-3:]
    tokens, width = mid.shape
    queries = n2.shape[0]
    columns = wg.shape[1]
    side = queries // 2
    links = Links(shards, send_sems, recv_sems, local_sems)
    t = links.t
    own_rows = pl.ds(pl.multiple_of(place(t) * tokens, tokens), tokens)

    spans = [slice(b, min(b + 256, columns)) for b in range(0, columns, 256)]
    sides = [slice(0, side), slice(side, queries)]
    loads = {"n2": links.keep(n2_in.at[sides[0]], n2.at[sides[0]])}
    for index, span in enumerate(spans):
        loads["g", index] = links.keep(wg_in.at[:, span], wg.at[:, span])
        loads["u", index] = links.keep(wu_in.at[:, span], wu.at[:, span])
        if index == 0:
            loads["og"] = links.keep(og_in.at[sides[0]], og.at[sides[0]])
        loads["d", index] = links.keep(wd_in.at[:, span], wd.at[:, span])
    loads["n2b"] = links.keep(n2_in.at[sides[1]], n2.at[sides[1]])
    loads["ogb"] = links.keep(og_in.at[sides[1]], og.at[sides[1]])
    loads["mid"] = links.keep(mid_in, mid)
    scatter = LineScatter(links, part, tokens, left, right, PIECES)
    gather = LineGather(links, dsend, dmid_all_o, tokens, PIECES)
    down = PlaneScatter(links, og, hidden, rows, *grads[0:6])
    gate = PlaneScatter(links, n2, dgate, rows, *grads[6:12])
    up = PlaneScatter(links, n2, dup, rows, up_in, None, None, None, None, None)
    links.barrier()
    scatter.clear()

    def feed_forward(half):
        at = sides[half]
        for index, span in enumerate(spans):
            if half == 0:
                if index == 0:
                    loads["n2"].wait()
                loads["g", index].wait()
                loads["u", index].wait()
            gate_act = nn_dot(n2[at, :], wg[:, span])
            up_act = nn_dot(n2[at, :], wu[:, span])
            if half == 0:
                if index == 0:
                    loads["og"].wait()
                loads["d", index].wait()
            d_hidden = nn_dot(og[at, :], wd[:, span])
            sig = jax.nn.sigmoid(gate_act)
            silu = gate_act * sig
            hidden[at, span] = (silu * up_act).astype(bf16)
            d_gate = d_hidden * up_act * sig * (1.0 + gate_act * (1.0 - sig))
            dgate[at, span] = d_gate.astype(bf16)
            dup[at, span] = (d_hidden * silu).astype(bf16)

        @pl.loop(0, width // 512)
        def _(j):
            of = pl.ds(pl.multiple_of(j * 512, 512), 512)
            summed = nt_dot(dgate[at, :], wg[of, :]) + nt_dot(dup[at, :], wu[of, :])
            part[at, of] = summed.astype(bf16)

    feed_forward(0)
    line_steps(scatter, 0)
    loads["n2b"].wait()
    loads["ogb"].wait()
    feed_forward(1)
    line_steps(scatter, 1)

    @pl.loop(0, width // 512)
    def _(j):
        of = pl.ds(pl.multiple_of(j * 512, 512), 512)
        branch[:, of] = nt_dot(hidden[...], wd[of, :]).astype(bf16)

    links.keep_later(branch, branch_o)

    piece = CTX * rows

    def others(grad, room):
        for step in range(1, shards):
            grad.other(step, room.at[pl.ds((step - 1) * piece, piece)])

    others(down, wd)
    line_steps(scatter, 2)
    others(gate, wg)
    down.own()
    down.exchange()
    loads["mid"].wait()
    gain_rows[...] = jnp.zeros_like(gain_rows)

    def finish_rows(r, d_normed):
        at = pl.ds(r, ROWS)
        q = pl.ds(pl.multiple_of(place(t) * tokens + r, ROWS), ROWS)
        middle = mid[at, :]
        inverse = lax.rsqrt(jnp.mean(middle * middle, -1, keepdims=True) + epsilon)
        unit = middle * inverse
        gain_rows[...] += d_normed * unit
        d_unit = d_normed * gains[1:2, :]
        back = inverse * (d_unit - unit * jnp.mean(d_unit * unit, -1, keepdims=True))
        d_middle = og[q, :].astype(f32) + back
        dmid[at, :] = d_middle
        dsend[at, :] = d_middle.astype(bf16)

    line_finish(scatter, finish_rows, gather)
    links.keep_later(dsend, dmid_all_o.at[own_rows])
    links.keep_later(dmid, dmid_o)
    gate.own()
    gate.exchange()
    others(up, wu)
    gain_sum[...] = jnp.sum(gain_rows[...], 0, keepdims=True)
    line_spread(gather, 1)
    up.own()
    links.keep_later(up_in.at[0], gu_part_o)
    line_spread(gather, 2)
    down.fold()
    line_spread(gather, 3)
    gate.fold()
    down.total()
    links.keep_later(down.out, gd_o)
    gate.total()
    links.keep_later(gate.out, gg_o)
    links.finish()


def middle_call(shards, rows, n2, og, wg, wu, wd, mid, gains):
    queries, width = n2.shape
    tokens = mid.shape[0]
    columns = wg.shape[1]
    token = (tokens, width)
    wide = (queries, columns)
    block = (LINE - 1,) + token
    outs = [
        struct(token, f32),
        struct((queries, width), bf16),
        struct((rows, columns), f32),
        struct((rows, columns), f32),
        struct((queries, width), bf16),
        struct((CTX * rows, columns), bf16),
        struct((1, width), f32),
    ]
    count = 12 * PIECES + 3 * (shards - 1 + 6)
    return pl.pallas_call(
        functools.partial(middle_kernel, shards, rows),
        out_shape=outs,
        in_specs=[any_spec()] * 6 + [vmem_spec()],
        out_specs=[any_spec()] * 6 + [vmem_spec()],
        scratch_shapes=[
            pltpu.VMEM((queries, width), bf16),
            pltpu.VMEM((queries, width), bf16),
            pltpu.VMEM((width, columns), bf16),
            pltpu.VMEM((width, columns), bf16),
            pltpu.VMEM((width, columns), bf16),
            pltpu.VMEM(token, f32),
            pltpu.VMEM(wide, bf16),
            pltpu.VMEM(wide, bf16),
            pltpu.VMEM(wide, bf16),
            pltpu.VMEM((queries, width), bf16),
            pltpu.VMEM((queries, width), bf16),
            pltpu.VMEM(block, bf16),
            pltpu.VMEM(block, bf16),
            pltpu.VMEM(token, f32),
            pltpu.VMEM(token, bf16),
            pltpu.VMEM((ROWS, width), f32),
            pltpu.VMEM((shards - 1, CTX * rows, columns), bf16),
            *PlaneScatter.scratch(shards, rows, columns),
            *PlaneScatter.scratch(shards, rows, columns),
            pltpu.SemaphoreType.DMA((count,)),
            pltpu.SemaphoreType.DMA((count,)),
            pltpu.SemaphoreType.DMA((40,)),
        ],
        compiler_params=pltpu.CompilerParams(
            collective_id=1, has_side_effects=True, vmem_limit_bytes=63 * 2**20
        ),
        name="middle",
    )(n2, og, wg, wu, wd, mid, gains)


def backward_kernel(
    shards, rows,
    dmid_all_in, wo_in, wq_in, wkv_in, n1_in, qaug_in, kaug_in, kv_in, att_in, x_in, dmid_in,
    branch_in, gu_part_in, mid_in, lse, gains, gain_mlp, cos, sin,
    in_o, gq_o, gkv_o, go_o, gu_o, out_o, gain_o,
    dmid_all, wo, wq, wkv, n1, qaug, kaug, kv, att, x, dmid,
    d_out, attn_rows, v_rows, d_keys, d_values, d_query, d_query_rows, kv_send, kv_recv, d_kv, part,
    left, right, gain_rows, pair, plane_in, line_in, total, stage_o, stage_q, stage_kv,
    branch, left_b, right_b, mid, layer,
    *rest,
):
    grads, (send_sems, recv_sems, local_sems) = rest[:-3], rest[-3:]
    tokens, width = dmid.shape
    queries = n1.shape[0]
    heads = qaug.shape[0]
    length = kaug.shape[0]
    half = HD // 2
    plane = shards * CTX
    links = Links(shards, send_sems, recv_sems, local_sems)
    s, c, t = links.s, links.c, links.t

    scatter = LineScatter(links, part, tokens, left, right, PIECES)
    scatter_out = LineScatter(links, branch, tokens, left_b, right_b)
    g_o = PlaneScatter(links, dmid_all, attn_rows, rows, *grads[0:6])
    g_q = PlaneScatter(links, n1, d_query_rows, rows, *grads[6:12])
    g_kv = PlaneScatter(links, n1, d_kv, rows, *grads[12:18])
    g_u = PlaneScatter(links, None, None, rows, *grads[18:24])
    kv_slot = links.slots(CTX - 1)
    plane_slot = links.slots(plane - 1)
    line_slot = links.slots(LINE - 1)
    piece = CTX * rows
    loads = [
        links.keep(src, dst)
        for src, dst in (
            (branch_in, branch), (dmid_all_in, dmid_all), (wo_in, wo), (gu_part_in, g_u.core_in.at[0]),
            (att_in, att), (kv_in, kv), (qaug_in, qaug), (kaug_in, kaug), (n1_in, n1), (wq_in, wq),
            (wkv_in, wkv), (x_in, x), (dmid_in, dmid), (mid_in, mid),
        )
    ]

    def others(grad, stage):
        for step in range(1, shards):
            grad.other(step, stage.at[pl.ds((step - 1) * piece, piece)])

    links.barrier(whole_line=True)
    scatter.clear()
    scatter_out.clear()
    loads[0].wait()
    scatter_out.step(0)
    for load in loads[1:3]:
        load.wait()
    d_out[...] = nn_dot(dmid_all[...], wo[...]).astype(bf16).T
    loads[3].wait()
    g_u.exchange()
    for load in loads[4:8]:
        load.wait()
    attn_rows[...] = att[...].T
    for other in range(CTX):
        v_rows[other * queries : (other + 1) * queries, :] = kv[other, HD : 2 * HD, :].T
    d_keys[...] = jnp.zeros_like(d_keys)
    d_values[...] = jnp.zeros_like(d_values)
    others(g_o, stage_o)

    def head(h):
        at = pl.ds(pl.multiple_of(h * HD, HD), HD)
        query = qaug[h]
        d_head = d_out[at, :]
        delta = jnp.sum(d_head.astype(f32) * att[at, :].astype(f32), 0, keepdims=True)
        log_sum = lse[pl.ds(h, 1), :]
        d_q = jnp.zeros((HD, queries), f32)
        for b in range(0, length, BLOCK):
            e = b + BLOCK
            probs = jnp.exp(nn_dot(kaug[b:e, :], query) - log_sum)
            d_probs = nn_dot(v_rows[b:e, :], d_head)
            d_scores = (probs * (d_probs - delta)).astype(bf16)
            d_values[b:e, :] += nt_dot(probs.astype(bf16), d_head)
            d_keys[b:e, :] += nt_dot(d_scores, query[0:HD])
            at_b = b % queries
            d_q = d_q + nn_dot(kv[b // queries, 0:HD, at_b : at_b + BLOCK], d_scores)
        d_query[at, :] = d_q * (HD ** (-0.5))

    quarter = heads // 4
    pl.loop(0, quarter)(head)
    g_o.own()
    g_o.exchange()
    pl.loop(quarter, 2 * quarter)(head)
    scatter_out.step(1)
    pl.loop(2 * quarter, heads)(head)

    for other in range(CTX):
        block = slice(other * queries, (other + 1) * queries)
        both = jnp.concatenate([d_keys[block, :], d_values[block, :]], 1)
        kv_send[other] = both.astype(bf16)
    for step in range(1, CTX):
        peer = lax.rem(c + step, CTX)
        links.send(kv_send.at[peer], kv_recv.at[step - 1], (s, peer, t), kv_slot + step - 1)
    scatter_out.step(2)
    for load in loads[8:]:
        load.wait()

    cosine, sine = cos[...], sin[...]
    for h in range(heads):
        at = h * HD
        d1, d2 = d_query[at : at + half, :], d_query[at + half : at + HD, :]
        d_query[at : at + half, :] = d1 * cosine + d2 * sine
        d_query[at + half : at + HD, :] = d2 * cosine - d1 * sine
    d_query_rows[...] = d_query[...].astype(bf16).T
    others(g_q, stage_q)
    for step in range(1, CTX):
        links.recv(kv_recv.at[step - 1], kv_slot + step - 1)
    d_pair = kv_send[c].astype(f32)
    for step in range(1, CTX):
        d_pair = d_pair + kv_recv[step - 1].astype(f32)
    d_pair = d_pair.T
    d1, d2 = d_pair[0:half], d_pair[half:HD]
    turned = jnp.concatenate(
        [d1 * cosine + d2 * sine, d2 * cosine - d1 * sine, d_pair[HD:]], 0
    )
    d_kv[...] = turned.astype(bf16).T

    @pl.loop(0, width // 512)
    def _(j):
        at = pl.ds(pl.multiple_of(j * 512, 512), 512)
        summed = nt_dot(d_query_rows[...], wq[at, :]) + nt_dot(d_kv[...], wkv[at, :])
        part[:, at] = summed.astype(bf16)

    line_steps(scatter, 0)
    g_u.fold()
    g_o.fold()

    gain_rows[...] = jnp.zeros_like(gain_rows)

    @pl.loop(0, queries // ROWS)
    def _(i):
        r = pl.ds(pl.multiple_of(i * ROWS, ROWS), ROWS)
        v = x[r, :].astype(f32)
        inverse = lax.rsqrt(jnp.mean(v * v, -1, keepdims=True) + epsilon)
        gain_rows[...] += part[r, :].astype(f32) * (v * inverse)

    pair[0:1, :] = jnp.sum(gain_rows[...], 0, keepdims=True)
    pair[1:2, :] = gain_mlp[...]
    for step in range(1, plane):
        links.send(pair, plane_in.at[step - 1], links.plane_peer(step), plane_slot + step - 1)
    others(g_kv, stage_kv)
    g_q.own()
    g_q.exchange()
    line_steps(scatter, 1)
    summed = pair[...]
    for step in range(1, plane):
        links.recv(plane_in.at[step - 1], plane_slot + step - 1)
        summed = summed + plane_in[step - 1]
    total[...] = summed
    for step in range(1, LINE):
        links.send(total, line_in.at[step - 1], links.line_peer(step), line_slot + step - 1)
    g_kv.own()
    g_kv.exchange()
    line_steps(scatter, 2)
    scatter_out.arrive()

    def layer_rows(r, total_rows):
        layer[pl.ds(r, ROWS), :] = (mid[pl.ds(r, ROWS), :] + total_rows).astype(bf16)

    scatter_out.owned(0, layer_rows)
    links.keep_later(layer, out_o)
    g_o.total()
    links.keep_later(g_o.out, go_o)
    g_q.fold()
    g_kv.fold()

    def finish_rows(r, d_normed):
        at = pl.ds(r, ROWS)
        q = pl.ds(pl.multiple_of(place(t) * tokens + r, ROWS), ROWS)
        v = x[q, :].astype(f32)
        inverse = lax.rsqrt(jnp.mean(v * v, -1, keepdims=True) + epsilon)
        unit = v * inverse
        d_unit = d_normed * gains[0:1, :]
        back = inverse * (d_unit - unit * jnp.mean(d_unit * unit, -1, keepdims=True))
        dmid[at, :] = dmid[at, :] + back

    line_finish(scatter, finish_rows)
    links.keep_later(dmid, in_o)
    g_u.total()
    links.keep_later(g_u.out, gu_o)
    g_q.total()
    links.keep_later(g_q.out, gq_o)
    g_kv.total()
    links.keep_later(g_kv.out, gkv_o)
    for step in range(1, LINE):
        links.recv(line_in.at[step - 1], line_slot + step - 1)
        summed = summed + line_in[step - 1]
    gain_o[...] = summed
    links.finish()


def backward_call(
    shards, rows, dmid_all, wo, wq, wkv, n1, qaug, kaug, kv, att, x, dmid, branch, gu_part, mid,
    lse, gains, gain_mlp, cos, sin,
):
    tokens, width = dmid.shape
    queries = n1.shape[0]
    heads = qaug.shape[0]
    length = kaug.shape[0]
    inner = heads * HD
    columns = gu_part.shape[1]
    plane = shards * CTX
    piece = CTX * rows * (shards - 1)
    token = (tokens, width)
    block = (LINE - 1,) + token
    outs = [
        struct(token, f32),
        struct((rows, inner), f32),
        struct((rows, 2 * HD), f32),
        struct((rows, inner), f32),
        struct((rows, columns), f32),
        struct(token, bf16),
        struct((2, width), f32),
    ]
    count = 6 + 6 * PIECES + 4 * (shards - 1 + 6) + CTX - 1 + plane - 1 + LINE - 1
    return pl.pallas_call(
        functools.partial(backward_kernel, shards, rows),
        out_shape=outs,
        in_specs=[any_spec()] * 14 + [vmem_spec()] * 5,
        out_specs=[any_spec()] * 6 + [vmem_spec()],
        scratch_shapes=[
            pltpu.VMEM((queries, width), bf16),
            pltpu.VMEM((width, inner), bf16),
            pltpu.VMEM((width, inner), bf16),
            pltpu.VMEM((width, 2 * HD), bf16),
            pltpu.VMEM((queries, width), bf16),
            pltpu.VMEM(qaug.shape, bf16),
            pltpu.VMEM(kaug.shape, bf16),
            pltpu.VMEM(kv.shape, bf16),
            pltpu.VMEM((inner, queries), bf16),
            pltpu.VMEM((queries, width), bf16),
            pltpu.VMEM(token, f32),
            pltpu.VMEM((inner, queries), bf16),
            pltpu.VMEM((queries, inner), bf16),
            pltpu.VMEM((length, HD), bf16),
            pltpu.VMEM((length, HD), f32),
            pltpu.VMEM((length, HD), f32),
            pltpu.VMEM((inner, queries), f32),
            pltpu.VMEM((queries, inner), bf16),
            pltpu.VMEM((CTX, queries, 2 * HD), bf16),
            pltpu.VMEM((CTX - 1, queries, 2 * HD), bf16),
            pltpu.VMEM((queries, 2 * HD), bf16),
            pltpu.VMEM((queries, width), bf16),
            pltpu.VMEM(block, bf16),
            pltpu.VMEM(block, bf16),
            pltpu.VMEM((ROWS, width), f32),
            pltpu.VMEM((2, width), f32),
            pltpu.VMEM((plane - 1, 2, width), f32),
            pltpu.VMEM((LINE - 1, 2, width), f32),
            pltpu.VMEM((2, width), f32),
            pltpu.VMEM((piece, inner), bf16),
            pltpu.VMEM((piece, inner), bf16),
            pltpu.VMEM((piece, 2 * HD), bf16),
            pltpu.VMEM((queries, width), bf16),
            pltpu.VMEM(block, bf16),
            pltpu.VMEM(block, bf16),
            pltpu.VMEM(token, f32),
            pltpu.VMEM(token, bf16),
            *PlaneScatter.scratch(shards, rows, inner),
            *PlaneScatter.scratch(shards, rows, inner),
            *PlaneScatter.scratch(shards, rows, 2 * HD),
            *PlaneScatter.scratch(1 + 1, rows, columns),
            pltpu.SemaphoreType.DMA((count,)),
            pltpu.SemaphoreType.DMA((count,)),
            pltpu.SemaphoreType.DMA((32,)),
        ],
        compiler_params=pltpu.CompilerParams(
            collective_id=2, has_side_effects=True, vmem_limit_bytes=60 * 2**20
        ),
        name="backward",
    )(
        dmid_all, wo, wq, wkv, n1, qaug, kaug, kv, att, x, dmid, branch, gu_part, mid,
        lse, gains, gain_mlp, cos, sin,
    )


def body(
    inputs, out_grad, block_order, gain_attn, w_query, w_keyval, w_output, gain_mlp, w_gate, w_up, w_down
):
    shards = lax.axis_size("shard")
    x, og = inputs[0], out_grad[0]
    tokens, width = x.shape
    queries = tokens * LINE
    order = block_order[0]
    s, c = lax.axis_index("shard"), lax.axis_index("ctx")
    per = queries // BLOCK
    owners = [owner for at in range(LINE) for owner in range(LINE) if place(owner) == at]
    slots = np.concatenate([owner * tokens + np.arange(tokens) for owner in owners])
    here = lax.dynamic_slice_in_dim(order, c * per, per)
    block_here = sum(jnp.where(slots // BLOCK == i, here[i], 0) for i in range(per))
    position = block_here * BLOCK + (slots % BLOCK).astype(np.int32)
    half = HD // 2
    frequency = 10000.0 ** (-jnp.arange(half, dtype=f32) * 2.0 / HD)
    angles = frequency[:, None] * position.astype(f32)[None, :]
    cos, sin = jnp.cos(angles), jnp.sin(angles)
    bias = jnp.where(order[:, None] <= block_here[None, :], 0.0, blocked).astype(bf16)
    bias = jnp.concatenate([bias, jnp.zeros((HD - BLOCKS, queries), bf16)], 0)
    start = (s * CTX + c) * gain_attn.shape[0]
    gpad = lax.dynamic_update_slice(
        jnp.zeros((2, width), f32), jnp.stack([gain_attn, gain_mlp]).astype(f32), (0, start)
    )
    (wq, wkv, wo, wg, wu, wd, n1, og_all, n2, mid, qaug, kaug, kv, att, x_all, lse, gains) = forward_call(
        shards, x, og, (w_query, w_keyval, w_output, w_gate, w_up, w_down), gpad, cos, sin, bias
    )
    (dmid, dmid_all, grad_gate, grad_down, branch, gu_part, gm) = middle_call(
        shards, w_gate.shape[0], n2, og_all, wg, wu, wd, mid, gains
    )
    (input_grad, grad_query, grad_keyval, grad_output, grad_up, layer_out, both) = backward_call(
        shards, w_query.shape[0], dmid_all, wo, wq, wkv, n1, qaug, kaug, kv, att, x_all, dmid,
        branch, gu_part, mid, lse, gains, gm, cos, sin,
    )
    both = lax.dynamic_slice(both, (0, start), (2, gain_attn.shape[0]))
    return (
        layer_out[None], input_grad[None], both[0], grad_query, grad_keyval, grad_output,
        both[1], grad_gate, grad_up, grad_down,
    )


def solution(mesh):
    plane = P(("shard", "ctx"), "tensor")
    gain = P(("shard", "ctx"))
    token = P("shard", ("ctx", "tensor"), None)
    return jax.shard_map(
        body,
        mesh=mesh,
        in_specs=(token, token, P("shard", None), gain, plane, plane, plane, gain, plane, plane, plane),
        out_specs=(token, token, gain, plane, plane, plane, gain, plane, plane, plane),
        check_vma=False,
    )
```

```python
import functools

import jax
import jax.numpy as jnp
import numpy as np
from jax import lax
from jax.experimental import pallas as pl
from jax.experimental.pallas import tpu as pltpu
from jax.sharding import PartitionSpec as P

HD = 64
BLOCK = 256
BLOCKS = 8
ROWS = 16
CTX = 4
LINE = 4
PIECES = 2

epsilon = 1e-05
blocked = -1e30

f32 = jnp.float32
bf16 = jnp.bfloat16
MESH = pl.DeviceIdType.MESH


def place(owner):
    return (owner + (owner + 1) // 2) % LINE if isinstance(owner, int) else lax.rem(
        owner + (owner + 1) // 2, LINE
    )


def nn_dot(left, right):
    return jnp.dot(left, right, preferred_element_type=f32)


def nt_dot(left, right):
    return lax.dot_general(left, right, (((1,), (1,)), ((), ())), preferred_element_type=f32)


def tn_dot(left, right):
    return lax.dot_general(left, right, (((0,), (0,)), ((), ())), preferred_element_type=f32)


class Links:
    def __init__(self, shards, send_sems, recv_sems, local_sems):
        self.shards = shards
        self.send_sems, self.recv_sems, self.local_sems = send_sems, recv_sems, local_sems
        self.s = lax.axis_index("shard")
        self.c = lax.axis_index("ctx")
        self.t = lax.axis_index("tensor")
        self.c_x = self.c + 1 - 2 * lax.rem(self.c, 2)
        self.c_y = lax.rem(self.c + 2, CTX)
        self.c_d = CTX - 1 - self.c
        self.x_dev = (self.s, self.c_x, self.t)
        self.y_dev = (self.s, self.c_y, self.t)
        self.right = (self.s, self.c, self.t + 1)
        self.left = (self.s, self.c, self.t - 1)
        self.used = 0
        self.local_used = 0
        self.sends = []
        self.locals = []

    def slots(self, count):
        first = self.used
        self.used += count
        assert self.used <= self.send_sems.shape[0]
        return first

    def plane_peer(self, step):
        index = lax.rem(self.s * CTX + self.c + step, self.shards * CTX)
        return (index // CTX, lax.rem(index, CTX), self.t)

    def core_peer(self, step):
        return (lax.rem(self.s + step, self.shards), self.c, self.t)

    def line_peer(self, step):
        return (self.s, self.c, lax.rem(self.t + step, LINE))

    def barrier(self, whole_line=False):
        sem = pltpu.get_barrier_semaphore()
        count = self.shards * CTX - 1
        for step in range(1, count + 1):
            pl.semaphore_signal(
                sem, inc=1, device_id=self.plane_peer(step), device_id_type=MESH
            )

        if whole_line:
            for step in range(1, LINE):
                pl.semaphore_signal(
                    sem, inc=1, device_id=self.line_peer(step), device_id_type=MESH
                )
            pl.semaphore_wait(sem, count + LINE - 1)
            return

        @pl.when(self.t > 0)
        def _():
            pl.semaphore_signal(sem, inc=1, device_id=self.left, device_id_type=MESH)

        @pl.when(self.t < LINE - 1)
        def _():
            pl.semaphore_signal(sem, inc=1, device_id=self.right, device_id_type=MESH)

        beside = (self.t + LINE - 1) // LINE + (2 * LINE - 2 - self.t) // LINE
        pl.semaphore_wait(sem, count + beside)

    def copy(self, src, dst, device, slot):
        return pltpu.make_async_remote_copy(
            src_ref=src,
            dst_ref=dst,
            send_sem=self.send_sems.at[slot],
            recv_sem=self.recv_sems.at[slot],
            device_id=device,
            device_id_type=MESH,
        )

    def send(self, src, dst, device, slot, cond=None):
        if cond is None:
            self.copy(src, dst, device, slot).start()
        else:

            @pl.when(cond)
            def _():
                self.copy(src, dst, device, slot).start()

        handle = (src, dst, device, slot, cond)
        self.sends.append(handle)
        return handle

    def sent(self, handle):
        self.sends = [other for other in self.sends if other is not handle]
        self.copy(*handle[:4]).wait_send()

    def recv(self, dst, slot):
        self.copy(dst, dst, self.x_dev, slot).wait_recv()

    def keep(self, src, dst):
        copy = pltpu.make_async_copy(src, dst, self.local_sems.at[self.local_used])
        self.local_used += 1
        assert self.local_used <= self.local_sems.shape[0]
        copy.start()
        return copy

    def keep_later(self, src, dst):
        self.locals.append(self.keep(src, dst))

    def finish(self):
        for src, dst, device, slot, cond in self.sends:
            if cond is None:
                self.copy(src, dst, device, slot).wait_send()
            else:

                @pl.when(cond)
                def _():
                    self.copy(src, dst, device, slot).wait_send()

        for copy in self.locals:
            copy.wait()


class PlaneGather:
    def __init__(self, links, src, full, stage=None):
        self.links, self.src, self.full, self.stage = links, src, full, stage
        self.rows = src.shape[0]
        self.first = links.slots(4 + 4 * (links.shards - 1))

    def block(self, s, c):
        start = pl.multiple_of((s * CTX + c) * self.rows, self.rows)
        return self.full.at[pl.ds(start, self.rows)]

    def half(self, s, c, which):
        size = self.rows // 2
        start = pl.multiple_of((s * CTX + c) * self.rows + which * size, size)
        return self.full.at[pl.ds(start, size)]

    def core_slot(self, step, part):
        return self.first + 4 + (step - 1) * 4 + part

    def core_send(self, src, c, part):
        links = self.links
        for step in range(1, links.shards):
            links.send(
                src,
                self.block(links.s, c),
                links.core_peer(step),
                self.core_slot(step, part),
            )

    def start(self):
        links = self.links
        own = self.block(links.s, links.c)
        links.send(self.src, own, links.x_dev, self.first)
        links.send(self.src, own, links.y_dev, self.first + 1)
        self.core_send(self.src, links.c, 0)
        self.local = links.keep(self.src, own if self.stage is None else self.stage)

    def settle(self):
        self.local.wait()
        self.local = self.links.keep(self.stage, self.block(self.links.s, self.links.c))

    def forward(self):
        links = self.links
        links.recv(self.block(links.s, links.c_x), self.first)
        links.recv(self.block(links.s, links.c_y), self.first + 1)
        from_x = self.half(links.s, links.c_x, 0)
        from_y = self.half(links.s, links.c_y, 1)
        links.send(from_x, from_x, links.y_dev, self.first + 2)
        links.send(from_y, from_y, links.x_dev, self.first + 3)
        self.core_send(self.block(links.s, links.c_x), links.c_x, 1)
        self.core_send(self.block(links.s, links.c_y), links.c_y, 2)

    def diagonal(self):
        links = self.links
        links.recv(self.half(links.s, links.c_d, 0), self.first + 2)
        links.recv(self.half(links.s, links.c_d, 1), self.first + 3)
        self.core_send(self.block(links.s, links.c_d), links.c_d, 3)

    def done(self):
        links = self.links
        for step in range(1, links.shards):
            other = lax.rem(links.s + links.shards - step, links.shards)
            for part, c in enumerate((links.c, links.c_x, links.c_y, links.c_d)):
                links.recv(self.block(other, c), self.core_slot(step, part))
        self.local.wait()


class LineGather:
    def __init__(self, links, own, full, tokens, pieces=1):
        self.links, self.own, self.full, self.tokens = links, own, full, tokens
        self.pieces, self.size = pieces, tokens // pieces
        self.first = links.slots(2 * (LINE - 1) * pieces)

    def block(self, owner, p):
        start = pl.multiple_of(place(owner) * self.tokens + p * self.size, self.size)
        return self.full.at[pl.ds(start, self.size)]

    def slot(self, side, k, p):
        return self.first + (side * (LINE - 1) + k - 1) * self.pieces + p

    def send(self, k, p=0):
        links = self.links
        t, u = links.t, LINE - 1 - links.t
        own = self.own.at[pl.ds(p * self.size, self.size)]
        right, left = self.block(t - k + 1, p), self.block(t + k - 1, p)
        links.send(
            own if k == 1 else right,
            right,
            links.right,
            self.slot(0, k, p),
            jnp.logical_and(t >= k - 1, t < LINE - 1),
        )
        links.send(
            own if k == 1 else left,
            left,
            links.left,
            self.slot(1, k, p),
            jnp.logical_and(u >= k - 1, u < LINE - 1),
        )

    def recv(self, k, p=0):
        links = self.links
        t, u = links.t, LINE - 1 - links.t

        @pl.when(t >= k)
        def _():
            links.recv(self.block(t - k, p), self.slot(0, k, p))

        @pl.when(u >= k)
        def _():
            links.recv(self.block(t + k, p), self.slot(1, k, p))


class LineScatter:
    def __init__(self, links, part, tokens, from_left, from_right, pieces=1):
        self.links, self.part, self.tokens = links, part, tokens
        self.from_left, self.from_right = from_left, from_right
        self.pieces, self.size = pieces, tokens // pieces
        self.first = links.slots(2 * (LINE - 1) * pieces)

    def slot(self, side, k, p):
        return self.first + (side * (LINE - 1) + k) * self.pieces + p

    def piece(self, ref, k, p):
        return ref.at[k, pl.ds(p * self.size, self.size)]

    def clear(self):
        for cond, ref in (
            (self.links.t == 0, self.from_left),
            (self.links.t == LINE - 1, self.from_right),
        ):

            @pl.when(cond)
            def _():
                @pl.loop(0, self.tokens // ROWS)
                def _(i):
                    r = pl.multiple_of(i * ROWS, ROWS)
                    for k in range(LINE - 1):
                        ref[k, pl.ds(r, ROWS), :] = jnp.zeros((ROWS, ref.shape[2]), ref.dtype)

    def total(self, owner, k, p, arrived):
        @pl.loop(0, self.size // ROWS)
        def _(i):
            r = pl.multiple_of(p * self.size + i * ROWS, ROWS)
            q = pl.multiple_of(place(owner) * self.tokens + p * self.size + i * ROWS, ROWS)
            mine = self.part[pl.ds(q, ROWS), :].astype(f32)
            summed = mine + arrived[k, pl.ds(r, ROWS), :].astype(f32)
            arrived[k, pl.ds(r, ROWS), :] = summed.astype(arrived.dtype)

    def stage(self, now, p=0):
        links = self.links
        t, u = links.t, LINE - 1 - links.t
        for side, behind, arrived, device in (
            (0, t, self.from_left, links.right),
            (1, u, self.from_right, links.left),
        ):
            k = now - behind
            owner = LINE - 1 - k if side == 0 else k
            piece, slot = self.piece(arrived, k, p), self.slot(side, k, p)

            @pl.when(k >= 0)
            def _():
                @pl.when(behind > 0)
                def _():
                    links.recv(piece, slot)

                self.total(owner, k, p, arrived)

            links.send(piece, piece, device, slot, k >= 0)

    def arrive(self, p=0):
        links = self.links
        t = links.t

        @pl.when(t > 0)
        def _():
            links.recv(
                self.piece(self.from_left, LINE - 1 - t, p), self.slot(0, LINE - 1 - t, p)
            )

        @pl.when(t < LINE - 1)
        def _():
            links.recv(self.piece(self.from_right, t, p), self.slot(1, t, p))

    def rows(self, r):
        t = self.links.t
        q = pl.multiple_of(place(t) * self.tokens + r, ROWS)
        k_l = jnp.minimum(LINE - 1 - t, LINE - 2)
        k_r = jnp.minimum(t, LINE - 2)
        zero = jnp.zeros((ROWS, self.part.shape[1]), f32)
        return (
            self.part[pl.ds(q, ROWS), :].astype(f32)
            + jnp.where(t > 0, self.from_left[k_l, pl.ds(r, ROWS), :].astype(f32), zero)
            + jnp.where(t < LINE - 1, self.from_right[k_r, pl.ds(r, ROWS), :].astype(f32), zero)
        )

    def owned(self, p, use):
        @pl.loop(0, self.size // ROWS)
        def _(i):
            r = pl.multiple_of(p * self.size + i * ROWS, ROWS)
            use(r, self.rows(r))


def line_steps(scatter, k, hooks=()):
    for p in range(scatter.pieces):
        scatter.stage(k, p)
    for hook in hooks:
        hook()


def line_finish(scatter, use, gather=None):
    for p in range(scatter.pieces):
        scatter.arrive(p)
        scatter.owned(p, use)
        if gather is not None:
            gather.send(1, p)


def line_spread(gather, k):
    for p in range(gather.pieces):
        gather.recv(k, p)
        if k < LINE - 1:
            gather.send(k + 1, p)


class PlaneScatter:
    def __init__(self, links, left, right, rows, core_in, x_in, y_in, x_last, y_last, out):
        self.links, self.left, self.right, self.rows = links, left, right, rows
        self.core_in, self.x_in, self.y_in = core_in, x_in, y_in
        self.x_last, self.y_last, self.out = x_last, y_last, out
        self.first = links.slots(links.shards - 1 + 6)
        self.tile = min(256, CTX * rows)

    def product(self, shard, i):
        start = pl.multiple_of(shard * (CTX * self.rows) + i * self.tile, self.tile)
        return tn_dot(self.left[:, pl.ds(start, self.tile)], self.right[...])

    @property
    def tiles(self):
        return CTX * self.rows // self.tile

    def other(self, step, stage, part=None):
        links = self.links
        target = lax.rem(links.s + step, links.shards)
        low, high = (0, self.tiles) if part is None else part

        @pl.loop(low, high)
        def _(i):
            r = pl.multiple_of(i * self.tile, self.tile)
            stage[pl.ds(r, self.tile), :] = self.product(target, i).astype(bf16)

        if high == self.tiles:
            return links.send(
                stage, self.core_in.at[step - 1], links.core_peer(step), self.first + step - 1
            )

    def own(self, part=None):
        links = self.links
        low, high = (0, self.tiles) if part is None else part
        if low == 0:
            for step in range(1, links.shards):
                links.recv(self.core_in.at[step - 1], self.first + step - 1)

        @pl.loop(low, high)
        def _(i):
            r = pl.multiple_of(i * self.tile, self.tile)
            summed = self.product(links.s, i)
            for step in range(1, links.shards):
                summed = summed + self.core_in[step - 1, pl.ds(r, self.tile), :].astype(f32)
            self.core_in[0, pl.ds(r, self.tile), :] = summed.astype(bf16)

    def half(self, c, which):
        size = self.rows // 2
        start = pl.multiple_of(c * self.rows + which * size, size)
        return self.core_in.at[0, pl.ds(start, size)]

    def exchange(self):
        links, first = self.links, self.first + self.links.shards - 1
        links.send(self.half(links.c_d, 0), self.x_in.at[1], links.x_dev, first)
        links.send(self.half(links.c_d, 1), self.y_in.at[1], links.y_dev, first + 1)
        links.send(self.half(links.c_x, 0), self.x_in.at[0], links.x_dev, first + 2)
        links.send(self.half(links.c_y, 1), self.y_in.at[0], links.y_dev, first + 3)

    def add(self, c, which, arrived):
        size = self.rows // 2

        @pl.loop(0, size // ROWS)
        def _(i):
            r = pl.multiple_of(i * ROWS, ROWS)
            q = pl.multiple_of(c * self.rows + which * size + i * ROWS, ROWS)
            mine = self.core_in[0, pl.ds(q, ROWS), :].astype(f32)
            summed = mine + arrived[1, pl.ds(r, ROWS), :].astype(f32)
            self.core_in[0, pl.ds(q, ROWS), :] = summed.astype(bf16)

    def fold(self):
        links, first = self.links, self.first + self.links.shards - 1
        links.recv(self.x_in.at[1], first)
        self.add(links.c_y, 0, self.x_in)
        links.send(self.half(links.c_y, 0), self.y_last, links.y_dev, first + 4)
        links.recv(self.y_in.at[1], first + 1)
        self.add(links.c_x, 1, self.y_in)
        links.send(self.half(links.c_x, 1), self.x_last, links.x_dev, first + 5)

    def total(self):
        links, first = self.links, self.first + self.links.shards - 1
        size = self.rows // 2
        links.recv(self.x_in.at[0], first + 2)
        links.recv(self.y_in.at[0], first + 3)
        links.recv(self.y_last, first + 4)
        links.recv(self.x_last, first + 5)
        for which, arrived, last in ((0, self.x_in, self.y_last), (1, self.y_in, self.x_last)):

            @pl.loop(0, size // ROWS)
            def _(i):
                r = pl.multiple_of(i * ROWS, ROWS)
                q = pl.multiple_of(links.c * self.rows + which * size + i * ROWS, ROWS)
                self.out[pl.ds(which * size + r, ROWS), :] = (
                    self.core_in[0, pl.ds(q, ROWS), :].astype(f32)
                    + arrived[0, pl.ds(r, ROWS), :].astype(f32)
                    + last[pl.ds(r, ROWS), :].astype(f32)
                )

    @staticmethod
    def scratch(shards, rows, columns):
        half = (rows // 2, columns)
        return [
            pltpu.VMEM((shards - 1, CTX * rows, columns), bf16),
            pltpu.VMEM((2,) + half, bf16),
            pltpu.VMEM((2,) + half, bf16),
            pltpu.VMEM(half, bf16),
            pltpu.VMEM(half, bf16),
            pltpu.VMEM((rows, columns), f32),
        ]


def any_spec():
    return pl.BlockSpec(memory_space=pl.ANY)


def vmem_spec():
    return pl.BlockSpec(memory_space=pltpu.VMEM)


def struct(shape, dtype):
    return jax.ShapeDtypeStruct(shape, dtype)


def forward_kernel(
    shards,
    x, og, wq, wkv, wo, wg, wu, wd, gpad, frequency, order,
    wq_o, wkv_o, wo_o, wg_o, wu_o, wd_o, n1_o, og_o, n2_o, mid_o, qaug_o, kaug_o, kv_o, att_o, x_o,
    lse, gains, cos, sin,
    x_all, n1_all, wq_all, wkv_all, wo_all, gains_all, qaug, kv_all, kaug, v_all, scores, weights,
    attn, part, from_left, from_right, mid, n2, og_stage, wg_stage, wu_stage, wd_stage,
    send_sems, recv_sems, local_sems,
):
    tokens, width = x.shape
    queries = tokens * LINE
    heads = qaug.shape[0]
    links = Links(shards, send_sems, recv_sems, local_sems)
    s, c, t = links.s, links.c, links.t

    gather_x = LineGather(links, x, x_all, tokens)
    gather_og = LineGather(links, og, og_o, tokens)
    gather_n2 = LineGather(links, n2, n2_o, tokens, PIECES)
    small = [PlaneGather(links, *pair) for pair in ((wq, wq_all), (wkv, wkv_all), (wo, wo_all))]
    large = [
        PlaneGather(links, *three)
        for three in ((wg, wg_o, wg_stage), (wu, wu_o, wu_stage), (wd, wd_o, wd_stage))
    ]
    scatter = LineScatter(links, part, tokens, from_left, from_right, PIECES)
    plane = shards * CTX
    gain_slot = links.slots(plane - 1)
    kv_slot = links.slots(3)

    links.barrier()
    me = s * CTX + c
    for step in range(1, plane):
        links.send(gpad, gains_all.at[me], links.plane_peer(step), gain_slot + step - 1)
    own_gain = links.keep(gpad, gains_all.at[me])
    gather_x.send(1)
    own_rows = pl.ds(pl.multiple_of(place(t) * tokens, tokens), tokens)
    own_x = links.keep(x, x_all.at[own_rows])
    for gather in small:
        gather.start()
    scatter.clear()

    per = queries // BLOCK
    lane = lax.broadcasted_iota(jnp.int32, (1, queries), 1)
    owner = jnp.zeros((1, queries), jnp.int32)
    for index in range(LINE):
        owner = jnp.where(lane // tokens == place(index), index, owner)
    slot = owner * tokens + lax.rem(lane, tokens)
    block_here = jnp.zeros((1, queries), jnp.int32)
    for index in range(per):
        block_here = jnp.where(slot // BLOCK == index, order[c * per + index], block_here)
    position = (block_here * BLOCK + lax.rem(slot, BLOCK)).astype(f32)
    angles = frequency[...] * position
    cos[...] = jnp.cos(angles)
    sin[...] = jnp.sin(angles)
    row = lax.broadcasted_iota(jnp.int32, (HD, queries), 0)
    bias = jnp.zeros((HD, queries), f32)
    for index in range(BLOCKS):
        barred = jnp.logical_and(row == index, order[index] > block_here)
        bias = jnp.where(barred, blocked, bias)
    bias = bias.astype(bf16)
    for h in range(heads):
        qaug[h, HD:, :] = bias

    own_gain.wait()
    for step in range(1, plane):
        other = lax.rem(me + plane - step, plane)
        links.recv(gains_all.at[other], gain_slot + step - 1)
    total = gains_all[0]
    for index in range(1, plane):
        total = total + gains_all[index]
    gains[...] = total
    own_x.wait()

    def norm_block(owner):
        @pl.loop(0, tokens // ROWS)
        def _(i):
            r = pl.multiple_of(place(owner) * tokens + i * ROWS, ROWS)
            v = x_all[pl.ds(r, ROWS), :].astype(f32)
            inverse = lax.rsqrt(jnp.mean(v * v, -1, keepdims=True) + epsilon)
            n1_all[pl.ds(r, ROWS), :] = (v * inverse * gains[0:1, :]).astype(bf16)

    own_og = links.keep(og, og_stage)
    norm_block(t)
    gather_x.recv(1)
    gather_x.send(2)
    for gather in small:
        gather.forward()
    large[0].start()
    norm_pair(gather_x, norm_block, 1)
    gather_x.recv(2)
    gather_x.send(3)
    gather_og.send(1)
    for gather in small:
        gather.diagonal()
    norm_pair(gather_x, norm_block, 2)
    own_og.wait()
    links.keep_later(og_stage, og_o.at[own_rows])
    gather_x.recv(3)
    norm_pair(gather_x, norm_block, 3)
    for gather in small:
        gather.done()

    kv_t = nn_dot(n1_all[...], wkv_all[...]).T
    half = HD // 2
    cosine, sine = cos[...], sin[...]
    k1, k2 = kv_t[0:half], kv_t[half:HD]
    kv_all[c, 0:half, :] = (k1 * cosine - k2 * sine).astype(bf16)
    kv_all[c, half:HD, :] = (k2 * cosine + k1 * sine).astype(bf16)
    kv_all[c, HD : 2 * HD, :] = kv_t[HD:].astype(bf16)
    for step in range(1, CTX):
        peer = lax.rem(c + step, CTX)
        links.send(kv_all.at[c], kv_all.at[c], (s, peer, t), kv_slot + step - 1)
    large[0].settle()
    large[0].forward()
    large[1].start()
    large[2].start()

    q_t = nn_dot(n1_all[...], wq_all[...]).T
    scale = HD ** (-0.5)
    for h in range(heads):
        v1, v2 = q_t[h * HD : h * HD + half], q_t[h * HD + half : (h + 1) * HD]
        qaug[h, 0:half, :] = ((v1 * cosine - v2 * sine).astype(bf16) * scale).astype(bf16)
        qaug[h, half:HD, :] = ((v2 * cosine + v1 * sine).astype(bf16) * scale).astype(bf16)
    links.keep_later(n1_all, n1_o)
    links.keep_later(x_all, x_o)
    links.keep_later(wq_all, wq_o)
    links.keep_later(wkv_all, wkv_o)
    links.keep_later(wo_all, wo_o)
    links.keep_later(qaug, qaug_o)
    for step in range(1, CTX):
        other = lax.rem(c + CTX - step, CTX)
        links.recv(kv_all.at[other], kv_slot + step - 1)
    for other in range(CTX):
        row = lax.broadcasted_iota(jnp.int32, (HD, queries), 0)
        lane = lax.broadcasted_iota(jnp.int32, (HD, queries), 1)
        mark = (row == other * (queries // BLOCK) + lax.rem(lane // tokens, 2)).astype(f32).astype(bf16)
        both = jnp.concatenate([kv_all[other, 0:HD, :], mark], 0)
        kaug[other * queries : (other + 1) * queries, :] = both.T
        v_all[:, other * queries : (other + 1) * queries] = kv_all[other, HD : 2 * HD, :]
    links.keep_later(kaug, kaug_o)
    links.keep_later(kv_all, kv_o)

    length = queries * CTX

    side = queries // 2

    def head(half, h):
        lanes = slice(half * side, (half + 1) * side)
        query = qaug[h, :, lanes]
        top = jnp.full((1, side), -jnp.inf, f32)
        for b in range(0, length, BLOCK):
            block_scores = nn_dot(kaug[b : b + BLOCK, :], query)
            scores[b : b + BLOCK, :] = block_scores
            top = jnp.maximum(top, jnp.max(block_scores, 0, keepdims=True))
        norm = jnp.zeros((1, side), f32)
        for b in range(0, length, BLOCK):
            exponent = jnp.exp(scores[b : b + BLOCK, :] - top)
            norm = norm + jnp.sum(exponent, 0, keepdims=True)
            weights[b : b + BLOCK, :] = exponent.astype(bf16)
        out = nn_dot(v_all[...], weights[...]) / norm
        attn[pl.ds(pl.multiple_of(h * HD, HD), HD), lanes] = out.astype(bf16)
        lse[pl.ds(h, 1), lanes] = top + jnp.log(norm)

    def project(half):
        rows = slice(half * side, (half + 1) * side)
        attn_rows = attn[:, rows].T
        for b in range(0, width, 512):
            part[rows, b : b + 512] = nt_dot(attn_rows, wo_all[b : b + 512, :])

    gather_og.recv(1)
    gather_og.send(2)
    pl.loop(0, heads)(functools.partial(head, 0))
    gather_og.recv(2)
    gather_og.send(3)
    project(0)
    line_steps(scatter, 0)
    large[1].settle()
    large[2].settle()
    pl.loop(0, heads)(functools.partial(head, 1))
    project(1)
    links.keep_later(attn, att_o)

    def finish_rows(r, summed):
        q = pl.multiple_of(place(t) * tokens + r, ROWS)
        middle = x_all[pl.ds(q, ROWS), :].astype(f32) + summed
        mid[pl.ds(r, ROWS), :] = middle
        inverse = lax.rsqrt(jnp.mean(middle * middle, -1, keepdims=True) + epsilon)
        n2[pl.ds(r, ROWS), :] = (middle * inverse * gains[1:2, :]).astype(bf16)

    line_steps(scatter, 1)
    large[0].diagonal()
    line_steps(scatter, 2)
    line_finish(scatter, finish_rows, gather_n2)
    links.keep_later(n2, n2_o.at[own_rows])
    links.keep_later(mid, mid_o)
    large[1].forward()
    large[2].forward()
    line_spread(gather_n2, 1)
    line_spread(gather_n2, 2)
    large[1].diagonal()
    large[2].diagonal()
    gather_og.recv(3)
    line_spread(gather_n2, 3)
    for gather in large:
        gather.done()
    links.finish()


def norm_pair(gather, norm_block, k):
    t, u = gather.links.t, LINE - 1 - gather.links.t

    @pl.when(t >= k)
    def _():
        norm_block(t - k)

    @pl.when(u >= k)
    def _():
        norm_block(t + k)


def forward_call(shards, x, og, weights_in, gpad, frequency, order):
    wq, wkv, wo, wg, wu, wd = weights_in
    tokens, width = x.shape
    queries = tokens * LINE
    length = queries * CTX
    heads = wq.shape[1] // HD
    plane = shards * CTX
    full = [struct((width, w.shape[1]), bf16) for w in weights_in]
    outs = full + [
        struct((queries, width), bf16),
        struct((queries, width), bf16),
        struct((queries, width), bf16),
        struct((tokens, width), f32),
        struct((heads, 2 * HD, queries), bf16),
        struct((length, 2 * HD), bf16),
        struct((CTX, 2 * HD, queries), bf16),
        struct((heads * HD, queries), bf16),
        struct((queries, width), bf16),
        struct((heads, queries), f32),
        struct((2, width), f32),
        struct((HD // 2, queries), f32),
        struct((HD // 2, queries), f32),
    ]
    block = (LINE - 1, tokens, width)
    count = 12 * (1 + PIECES) + 6 * (4 + 4 * (shards - 1)) + plane - 1 + 3
    return pl.pallas_call(
        functools.partial(forward_kernel, shards),
        out_shape=outs,
        in_specs=[any_spec()] * 8
        + [vmem_spec()] * 2
        + [pl.BlockSpec(memory_space=pltpu.SMEM)],
        out_specs=[any_spec()] * 15 + [vmem_spec()] * 4,
        scratch_shapes=[
            pltpu.VMEM((queries, width), bf16),
            pltpu.VMEM((queries, width), bf16),
            pltpu.VMEM((width, wq.shape[1]), bf16),
            pltpu.VMEM((width, wkv.shape[1]), bf16),
            pltpu.VMEM((width, wo.shape[1]), bf16),
            pltpu.VMEM((plane, 2, width), f32),
            pltpu.VMEM((heads, 2 * HD, queries), bf16),
            pltpu.VMEM((CTX, 2 * HD, queries), bf16),
            pltpu.VMEM((length, 2 * HD), bf16),
            pltpu.VMEM((HD, length), bf16),
            pltpu.VMEM((length, queries // 2), f32),
            pltpu.VMEM((length, queries // 2), bf16),
            pltpu.VMEM((heads * HD, queries), bf16),
            pltpu.VMEM((queries, width), f32),
            pltpu.VMEM(block, bf16),
            pltpu.VMEM(block, bf16),
            pltpu.VMEM((tokens, width), f32),
            pltpu.VMEM((tokens, width), bf16),
            pltpu.VMEM((tokens, width), bf16),
            pltpu.VMEM(wg.shape, bf16),
            pltpu.VMEM(wu.shape, bf16),
            pltpu.VMEM(wd.shape, bf16),
            pltpu.SemaphoreType.DMA((count,)),
            pltpu.SemaphoreType.DMA((count,)),
            pltpu.SemaphoreType.DMA((32,)),
        ],
        compiler_params=pltpu.CompilerParams(
            collective_id=0, has_side_effects=True, vmem_limit_bytes=60 * 2**20
        ),
        name="forward",
    )(x, og, wq, wkv, wo, wg, wu, wd, gpad, frequency, order)


def middle_kernel(
    shards, rows,
    n2_in, og_in, wg_in, wu_in, wd_in, mid_in, gains,
    dmid_o, dmid_all_o, gg_o, gd_o, branch_o, gu_part_o, gain_sum,
    n2, og, wg, wu, wd, mid, hidden, dgate, dup, part, branch,
    left, right, dmid, dsend, gain_rows, up_in,
    *rest,
):
    grads, (send_sems, recv_sems, local_sems) = rest[:-3], rest[-3:]
    tokens, width = mid.shape
    queries = n2.shape[0]
    columns = wg.shape[1]
    side = queries // 2
    links = Links(shards, send_sems, recv_sems, local_sems)
    t = links.t
    own_rows = pl.ds(pl.multiple_of(place(t) * tokens, tokens), tokens)

    sides = [slice(0, side), slice(side, queries)]
    full, rest_columns = columns // 256, columns % 256
    weights = ((wg_in, wg), (wu_in, wu), (wd_in, wd))

    def fetch(j, start, size, index):
        src, dst = weights[j]
        of = pl.ds(start, size)
        sem = local_sems.at[3 * index + j]
        return pltpu.make_async_copy(src.at[:, of], dst.at[:, of], sem)

    links.local_used = 3 * (full + 1)
    load_n2 = links.keep(n2_in.at[sides[0]], n2.at[sides[0]])
    for index in range(full):
        for j in range(3):
            fetch(j, index * 256, 256, index).start()
        if index == 0:
            load_og = links.keep(og_in.at[sides[0]], og.at[sides[0]])
    if rest_columns:
        for j in range(3):
            fetch(j, full * 256, rest_columns, full).start()
    load_n2b = links.keep(n2_in.at[sides[1]], n2.at[sides[1]])
    load_ogb = links.keep(og_in.at[sides[1]], og.at[sides[1]])
    load_mid = links.keep(mid_in, mid)
    scatter = LineScatter(links, part, tokens, left, right, PIECES)
    gather = LineGather(links, dsend, dmid_all_o, tokens, PIECES)
    down = PlaneScatter(links, og, hidden, rows, *grads[0:6])
    gate = PlaneScatter(links, n2, dgate, rows, *grads[6:12])
    up = PlaneScatter(links, n2, dup, rows, up_in, None, None, None, None, None)
    links.barrier()
    scatter.clear()

    def feed_forward(half):
        at = sides[half]

        def tile(start, size, index):
            of = pl.ds(start, size)
            if half == 0:
                fetch(0, start, size, index).wait()
                fetch(1, start, size, index).wait()
            gate_act = nn_dot(n2[at, :], wg[:, of])
            up_act = nn_dot(n2[at, :], wu[:, of])
            if half == 0:
                fetch(2, start, size, index).wait()
            d_hidden = nn_dot(og[at, :], wd[:, of])
            sig = jax.nn.sigmoid(gate_act)
            silu = gate_act * sig
            hidden[at, of] = (silu * up_act).astype(bf16)
            d_gate = d_hidden * up_act * sig * (1.0 + gate_act * (1.0 - sig))
            dgate[at, of] = d_gate.astype(bf16)
            dup[at, of] = (d_hidden * silu).astype(bf16)

        @pl.loop(0, full)
        def _(index):
            tile(pl.multiple_of(index * 256, 256), 256, index)

        if rest_columns:
            tile(full * 256, rest_columns, full)

        @pl.loop(0, width // 512)
        def _(j):
            of = pl.ds(pl.multiple_of(j * 512, 512), 512)
            summed = nt_dot(dgate[at, :], wg[of, :]) + nt_dot(dup[at, :], wu[of, :])
            part[at, of] = summed.astype(bf16)

    piece = CTX * rows

    def others(grad, room):
        for step in range(1, shards):
            grad.other(step, room.at[pl.ds((step - 1) * piece, piece)])

    load_n2.wait()
    load_og.wait()
    feed_forward(0)
    line_steps(scatter, 0)
    load_n2b.wait()
    load_ogb.wait()
    feed_forward(1)
    line_steps(scatter, 1)
    others(gate, wg)
    others(up, wu)
    gate.own()
    gate.exchange()
    line_steps(scatter, 2)

    @pl.loop(0, width // 512)
    def _(j):
        of = pl.ds(pl.multiple_of(j * 512, 512), 512)
        branch[:, of] = nt_dot(hidden[...], wd[of, :]).astype(bf16)

    links.keep_later(branch, branch_o)
    others(down, wd)
    load_mid.wait()
    gain_rows[...] = jnp.zeros_like(gain_rows)

    def finish_rows(r, d_normed):
        at = pl.ds(r, ROWS)
        q = pl.ds(pl.multiple_of(place(t) * tokens + r, ROWS), ROWS)
        middle = mid[at, :]
        inverse = lax.rsqrt(jnp.mean(middle * middle, -1, keepdims=True) + epsilon)
        unit = middle * inverse
        gain_rows[...] += d_normed * unit
        d_unit = d_normed * gains[1:2, :]
        back = inverse * (d_unit - unit * jnp.mean(d_unit * unit, -1, keepdims=True))
        d_middle = og[q, :].astype(f32) + back
        dmid[at, :] = d_middle
        dsend[at, :] = d_middle.astype(bf16)

    line_finish(scatter, finish_rows, gather)
    down.own()
    down.exchange()
    links.keep_later(dsend, dmid_all_o.at[own_rows])
    links.keep_later(dmid, dmid_o)
    line_spread(gather, 1)
    up.own()
    links.keep_later(up_in.at[0], gu_part_o)
    gain_sum[...] = jnp.sum(gain_rows[...], 0, keepdims=True)
    gate.fold()
    line_spread(gather, 2)
    down.fold()
    line_spread(gather, 3)
    gate.total()
    links.keep_later(gate.out, gg_o)
    down.total()
    links.keep_later(down.out, gd_o)
    links.finish()


def middle_call(shards, rows, n2, og, wg, wu, wd, mid, gains):
    queries, width = n2.shape
    tokens = mid.shape[0]
    columns = wg.shape[1]
    token = (tokens, width)
    wide = (queries, columns)
    block = (LINE - 1,) + token
    outs = [
        struct(token, f32),
        struct((queries, width), bf16),
        struct((rows, columns), f32),
        struct((rows, columns), f32),
        struct((queries, width), bf16),
        struct((CTX * rows, columns), bf16),
        struct((1, width), f32),
    ]
    count = 12 * PIECES + 3 * (shards - 1 + 6)
    return pl.pallas_call(
        functools.partial(middle_kernel, shards, rows),
        out_shape=outs,
        in_specs=[any_spec()] * 6 + [vmem_spec()],
        out_specs=[any_spec()] * 6 + [vmem_spec()],
        scratch_shapes=[
            pltpu.VMEM((queries, width), bf16),
            pltpu.VMEM((queries, width), bf16),
            pltpu.VMEM((width, columns), bf16),
            pltpu.VMEM((width, columns), bf16),
            pltpu.VMEM((width, columns), bf16),
            pltpu.VMEM(token, f32),
            pltpu.VMEM(wide, bf16),
            pltpu.VMEM(wide, bf16),
            pltpu.VMEM(wide, bf16),
            pltpu.VMEM((queries, width), bf16),
            pltpu.VMEM((queries, width), bf16),
            pltpu.VMEM(block, bf16),
            pltpu.VMEM(block, bf16),
            pltpu.VMEM(token, f32),
            pltpu.VMEM(token, bf16),
            pltpu.VMEM((ROWS, width), f32),
            pltpu.VMEM((shards - 1, CTX * rows, columns), bf16),
            *PlaneScatter.scratch(shards, rows, columns),
            *PlaneScatter.scratch(shards, rows, columns),
            pltpu.SemaphoreType.DMA((count,)),
            pltpu.SemaphoreType.DMA((count,)),
            pltpu.SemaphoreType.DMA((40,)),
        ],
        compiler_params=pltpu.CompilerParams(
            collective_id=1, has_side_effects=True, vmem_limit_bytes=63 * 2**20
        ),
        name="middle",
    )(n2, og, wg, wu, wd, mid, gains)


def backward_kernel(
    shards, rows,
    dmid_all_in, wo_in, wq_in, wkv_in, n1_in, qaug_in, kaug_in, kv_in, att_in, x_in, dmid_in,
    branch_in, gu_part_in, mid_in, lse, gains, gain_mlp, cos, sin,
    in_o, gq_o, gkv_o, go_o, gu_o, out_o, gain_o,
    dmid_all, wo, wq, wkv, n1, qaug, kaug, kv, att, x, dmid,
    d_out, attn_rows, v_rows, d_keys, d_values, d_query, d_query_rows, kv_send, kv_recv, d_kv, part,
    left, right, gain_rows, pair, plane_in, line_in, total, stage_o, stage_q, stage_kv,
    branch, left_b, right_b, mid, layer,
    *rest,
):
    grads, (send_sems, recv_sems, local_sems) = rest[:-3], rest[-3:]
    tokens, width = dmid.shape
    queries = n1.shape[0]
    heads = qaug.shape[0]
    length = kaug.shape[0]
    half = HD // 2
    plane = shards * CTX
    links = Links(shards, send_sems, recv_sems, local_sems)
    s, c, t = links.s, links.c, links.t

    scatter = LineScatter(links, part, tokens, left, right, PIECES)
    scatter_out = LineScatter(links, branch, tokens, left_b, right_b)
    g_o = PlaneScatter(links, dmid_all, attn_rows, rows, *grads[0:6])
    g_q = PlaneScatter(links, n1, d_query_rows, rows, *grads[6:12])
    g_kv = PlaneScatter(links, n1, d_kv, rows, *grads[12:18])
    g_u = PlaneScatter(links, None, None, rows, *grads[18:24])
    kv_slot = links.slots(CTX - 1)
    plane_slot = links.slots(plane - 1)
    line_slot = links.slots(LINE - 1)
    piece = CTX * rows
    loads = [
        links.keep(src, dst)
        for src, dst in (
            (branch_in, branch), (dmid_all_in, dmid_all), (wo_in, wo), (gu_part_in, g_u.core_in.at[0]),
            (att_in, att), (kv_in, kv), (qaug_in, qaug), (kaug_in, kaug), (n1_in, n1), (wq_in, wq),
            (wkv_in, wkv), (x_in, x), (dmid_in, dmid), (mid_in, mid),
        )
    ]

    def others(grad, stage):
        for step in range(1, shards):
            grad.other(step, stage.at[pl.ds((step - 1) * piece, piece)])

    links.barrier(whole_line=True)
    scatter.clear()
    scatter_out.clear()
    loads[0].wait()
    scatter_out.stage(0)
    for load in loads[1:3]:
        load.wait()
    d_out[...] = nn_dot(dmid_all[...], wo[...]).astype(bf16).T
    loads[3].wait()
    g_u.exchange()
    for load in loads[4:8]:
        load.wait()
    attn_rows[...] = att[...].T
    others(g_o, stage_o)
    for other in range(CTX):
        v_rows[other * queries : (other + 1) * queries, :] = kv[other, HD : 2 * HD, :].T
    d_keys[...] = jnp.zeros_like(d_keys)
    d_values[...] = jnp.zeros_like(d_values)
    g_o.own()
    g_o.exchange()

    def head(h):
        at = pl.ds(pl.multiple_of(h * HD, HD), HD)
        query = qaug[h]
        d_head = d_out[at, :]
        delta = jnp.sum(d_head.astype(f32) * att[at, :].astype(f32), 0, keepdims=True)
        log_sum = lse[pl.ds(h, 1), :]
        d_q = jnp.zeros((HD, queries), f32)
        for b in range(0, length, BLOCK):
            e = b + BLOCK
            probs = jnp.exp(nn_dot(kaug[b:e, :], query) - log_sum)
            d_probs = nn_dot(v_rows[b:e, :], d_head)
            d_scores = (probs * (d_probs - delta)).astype(bf16)
            d_values[b:e, :] += nt_dot(probs.astype(bf16), d_head)
            d_keys[b:e, :] += nt_dot(d_scores, query[0:HD])
            at_b = b % queries
            d_q = d_q + nn_dot(kv[b // queries, 0:HD, at_b : at_b + BLOCK], d_scores)
        d_query[at, :] = d_q * (HD ** (-0.5))

    pl.loop(0, heads // 2)(head)
    scatter_out.stage(1)
    pl.loop(heads // 2, heads)(head)

    for other in range(CTX):
        block = slice(other * queries, (other + 1) * queries)
        both = jnp.concatenate([d_keys[block, :], d_values[block, :]], 1)
        kv_send[other] = both.astype(bf16)
    for step in range(1, CTX):
        peer = lax.rem(c + step, CTX)
        links.send(kv_send.at[peer], kv_recv.at[step - 1], (s, peer, t), kv_slot + step - 1)
    scatter_out.stage(2)
    for load in loads[8:]:
        load.wait()

    cosine, sine = cos[...], sin[...]
    for h in range(heads):
        at = h * HD
        d1, d2 = d_query[at : at + half, :], d_query[at + half : at + HD, :]
        d_query[at : at + half, :] = d1 * cosine + d2 * sine
        d_query[at + half : at + HD, :] = d2 * cosine - d1 * sine
    d_query_rows[...] = d_query[...].astype(bf16).T
    others(g_q, stage_q)
    for step in range(1, CTX):
        links.recv(kv_recv.at[step - 1], kv_slot + step - 1)
    d_pair = kv_send[c].astype(f32)
    for step in range(1, CTX):
        d_pair = d_pair + kv_recv[step - 1].astype(f32)
    d_pair = d_pair.T
    d1, d2 = d_pair[0:half], d_pair[half:HD]
    turned = jnp.concatenate(
        [d1 * cosine + d2 * sine, d2 * cosine - d1 * sine, d_pair[HD:]], 0
    )
    d_kv[...] = turned.astype(bf16).T

    @pl.loop(0, width // 512)
    def _(j):
        at = pl.ds(pl.multiple_of(j * 512, 512), 512)
        summed = nt_dot(d_query_rows[...], wq[at, :]) + nt_dot(d_kv[...], wkv[at, :])
        part[:, at] = summed.astype(bf16)

    line_steps(scatter, 0)
    g_u.fold()
    g_o.fold()

    gain_rows[...] = jnp.zeros_like(gain_rows)

    @pl.loop(0, queries // ROWS)
    def _(i):
        r = pl.ds(pl.multiple_of(i * ROWS, ROWS), ROWS)
        v = x[r, :].astype(f32)
        inverse = lax.rsqrt(jnp.mean(v * v, -1, keepdims=True) + epsilon)
        gain_rows[...] += part[r, :].astype(f32) * (v * inverse)

    pair[0:1, :] = jnp.sum(gain_rows[...], 0, keepdims=True)
    pair[1:2, :] = gain_mlp[...]
    for step in range(1, plane):
        links.send(pair, plane_in.at[step - 1], links.plane_peer(step), plane_slot + step - 1)
    others(g_kv, stage_kv)
    g_q.own()
    g_q.exchange()
    line_steps(scatter, 1)
    summed = pair[...]
    for step in range(1, plane):
        links.recv(plane_in.at[step - 1], plane_slot + step - 1)
        summed = summed + plane_in[step - 1]
    total[...] = summed
    for step in range(1, LINE):
        links.send(total, line_in.at[step - 1], links.line_peer(step), line_slot + step - 1)
    g_kv.own()
    g_kv.exchange()
    line_steps(scatter, 2)
    scatter_out.arrive()

    def layer_rows(r, total_rows):
        layer[pl.ds(r, ROWS), :] = (mid[pl.ds(r, ROWS), :] + total_rows).astype(bf16)

    scatter_out.owned(0, layer_rows)
    links.keep_later(layer, out_o)
    g_o.total()
    links.keep_later(g_o.out, go_o)
    g_q.fold()
    g_kv.fold()

    def finish_rows(r, d_normed):
        at = pl.ds(r, ROWS)
        q = pl.ds(pl.multiple_of(place(t) * tokens + r, ROWS), ROWS)
        v = x[q, :].astype(f32)
        inverse = lax.rsqrt(jnp.mean(v * v, -1, keepdims=True) + epsilon)
        unit = v * inverse
        d_unit = d_normed * gains[0:1, :]
        back = inverse * (d_unit - unit * jnp.mean(d_unit * unit, -1, keepdims=True))
        dmid[at, :] = dmid[at, :] + back

    line_finish(scatter, finish_rows)
    links.keep_later(dmid, in_o)
    g_u.total()
    links.keep_later(g_u.out, gu_o)
    g_q.total()
    links.keep_later(g_q.out, gq_o)
    g_kv.total()
    links.keep_later(g_kv.out, gkv_o)
    for step in range(1, LINE):
        links.recv(line_in.at[step - 1], line_slot + step - 1)
        summed = summed + line_in[step - 1]
    gain_o[...] = summed
    links.finish()


def backward_call(
    shards, rows, dmid_all, wo, wq, wkv, n1, qaug, kaug, kv, att, x, dmid, branch, gu_part, mid,
    lse, gains, gain_mlp, cos, sin,
):
    tokens, width = dmid.shape
    queries = n1.shape[0]
    heads = qaug.shape[0]
    length = kaug.shape[0]
    inner = heads * HD
    columns = gu_part.shape[1]
    plane = shards * CTX
    piece = CTX * rows * (shards - 1)
    token = (tokens, width)
    block = (LINE - 1,) + token
    outs = [
        struct(token, f32),
        struct((rows, inner), f32),
        struct((rows, 2 * HD), f32),
        struct((rows, inner), f32),
        struct((rows, columns), f32),
        struct(token, bf16),
        struct((2, width), f32),
    ]
    count = 6 + 6 * PIECES + 4 * (shards - 1 + 6) + CTX - 1 + plane - 1 + LINE - 1
    return pl.pallas_call(
        functools.partial(backward_kernel, shards, rows),
        out_shape=outs,
        in_specs=[any_spec()] * 14 + [vmem_spec()] * 5,
        out_specs=[any_spec()] * 6 + [vmem_spec()],
        scratch_shapes=[
            pltpu.VMEM((queries, width), bf16),
            pltpu.VMEM((width, inner), bf16),
            pltpu.VMEM((width, inner), bf16),
            pltpu.VMEM((width, 2 * HD), bf16),
            pltpu.VMEM((queries, width), bf16),
            pltpu.VMEM(qaug.shape, bf16),
            pltpu.VMEM(kaug.shape, bf16),
            pltpu.VMEM(kv.shape, bf16),
            pltpu.VMEM((inner, queries), bf16),
            pltpu.VMEM((queries, width), bf16),
            pltpu.VMEM(token, f32),
            pltpu.VMEM((inner, queries), bf16),
            pltpu.VMEM((queries, inner), bf16),
            pltpu.VMEM((length, HD), bf16),
            pltpu.VMEM((length, HD), f32),
            pltpu.VMEM((length, HD), f32),
            pltpu.VMEM((inner, queries), f32),
            pltpu.VMEM((queries, inner), bf16),
            pltpu.VMEM((CTX, queries, 2 * HD), bf16),
            pltpu.VMEM((CTX - 1, queries, 2 * HD), bf16),
            pltpu.VMEM((queries, 2 * HD), bf16),
            pltpu.VMEM((queries, width), bf16),
            pltpu.VMEM(block, bf16),
            pltpu.VMEM(block, bf16),
            pltpu.VMEM((ROWS, width), f32),
            pltpu.VMEM((2, width), f32),
            pltpu.VMEM((plane - 1, 2, width), f32),
            pltpu.VMEM((LINE - 1, 2, width), f32),
            pltpu.VMEM((2, width), f32),
            pltpu.VMEM((piece, inner), bf16),
            pltpu.VMEM((piece, inner), bf16),
            pltpu.VMEM((piece, 2 * HD), bf16),
            pltpu.VMEM((queries, width), bf16),
            pltpu.VMEM(block, bf16),
            pltpu.VMEM(block, bf16),
            pltpu.VMEM(token, f32),
            pltpu.VMEM(token, bf16),
            *PlaneScatter.scratch(shards, rows, inner),
            *PlaneScatter.scratch(shards, rows, inner),
            *PlaneScatter.scratch(shards, rows, 2 * HD),
            *PlaneScatter.scratch(1 + 1, rows, columns),
            pltpu.SemaphoreType.DMA((count,)),
            pltpu.SemaphoreType.DMA((count,)),
            pltpu.SemaphoreType.DMA((32,)),
        ],
        compiler_params=pltpu.CompilerParams(
            collective_id=2, has_side_effects=True, vmem_limit_bytes=60 * 2**20
        ),
        name="backward",
    )(
        dmid_all, wo, wq, wkv, n1, qaug, kaug, kv, att, x, dmid, branch, gu_part, mid,
        lse, gains, gain_mlp, cos, sin,
    )


def body(
    inputs, out_grad, block_order, gain_attn, w_query, w_keyval, w_output, gain_mlp, w_gate, w_up, w_down
):
    shards = lax.axis_size("shard")
    x, og = inputs[0], out_grad[0]
    tokens, width = x.shape
    s, c = lax.axis_index("shard"), lax.axis_index("ctx")
    frequency = 10000.0 ** (-jnp.arange(HD // 2, dtype=f32)[:, None] * 2.0 / HD)
    own = gain_attn.shape[0]
    start = (s * CTX + c) * own
    lane = lax.broadcasted_iota(jnp.int32, (2, width), 1)
    row = lax.broadcasted_iota(jnp.int32, (2, width), 0)
    spread = lambda gain: jnp.broadcast_to(gain.astype(f32), (width // own, own)).reshape(1, width)
    gpad = jnp.where(row == 0, spread(gain_attn), spread(gain_mlp))
    gpad = jnp.where(lane // own == s * CTX + c, gpad, 0.0)
    (wq, wkv, wo, wg, wu, wd, n1, og_all, n2, mid, qaug, kaug, kv, att, x_all, lse, gains, cos, sin) = forward_call(
        shards, x, og, (w_query, w_keyval, w_output, w_gate, w_up, w_down), gpad, frequency,
        block_order[0],
    )
    (dmid, dmid_all, grad_gate, grad_down, branch, gu_part, gm) = middle_call(
        shards, w_gate.shape[0], n2, og_all, wg, wu, wd, mid, gains
    )
    (input_grad, grad_query, grad_keyval, grad_output, grad_up, layer_out, both) = backward_call(
        shards, w_query.shape[0], dmid_all, wo, wq, wkv, n1, qaug, kaug, kv, att, x_all, dmid,
        branch, gu_part, mid, lse, gains, gm, cos, sin,
    )
    both = lax.dynamic_slice(both, (0, start), (2, gain_attn.shape[0]))
    return (
        layer_out[None], input_grad[None], both[0], grad_query, grad_keyval, grad_output,
        both[1], grad_gate, grad_up, grad_down,
    )


def solution(mesh):
    plane = P(("shard", "ctx"), "tensor")
    gain = P(("shard", "ctx"))
    token = P("shard", ("ctx", "tensor"), None)
    return jax.shard_map(
        body,
        mesh=mesh,
        in_specs=(token, token, P("shard", None), gain, plane, plane, plane, gain, plane, plane, plane),
        out_specs=(token, token, gain, plane, plane, plane, gain, plane, plane, plane),
        check_vma=False,
    )
```

```python
import functools

import jax
import jax.numpy as jnp
import numpy as np
from jax import lax
from jax.experimental import pallas as pl
from jax.experimental.pallas import tpu as pltpu
from jax.sharding import PartitionSpec as P

HD = 64
BLOCK = 256
BLOCKS = 8
ROWS = 16
CTX = 4
LINE = 4
PIECES = 2

epsilon = 1e-05
blocked = -1e30

f32 = jnp.float32
bf16 = jnp.bfloat16
MESH = pl.DeviceIdType.MESH


def place(owner):
    return (owner + (owner + 1) // 2) % LINE if isinstance(owner, int) else lax.rem(
        owner + (owner + 1) // 2, LINE
    )


def nn_dot(left, right):
    return jnp.dot(left, right, preferred_element_type=f32)


def nt_dot(left, right):
    return lax.dot_general(left, right, (((1,), (1,)), ((), ())), preferred_element_type=f32)


def tn_dot(left, right):
    return lax.dot_general(left, right, (((0,), (0,)), ((), ())), preferred_element_type=f32)


class Links:
    def __init__(self, shards, send_sems, recv_sems, local_sems):
        self.shards = shards
        self.send_sems, self.recv_sems, self.local_sems = send_sems, recv_sems, local_sems
        self.s = lax.axis_index("shard")
        self.c = lax.axis_index("ctx")
        self.t = lax.axis_index("tensor")
        self.c_x = self.c + 1 - 2 * lax.rem(self.c, 2)
        self.c_y = lax.rem(self.c + 2, CTX)
        self.c_d = CTX - 1 - self.c
        self.x_dev = (self.s, self.c_x, self.t)
        self.y_dev = (self.s, self.c_y, self.t)
        self.right = (self.s, self.c, self.t + 1)
        self.left = (self.s, self.c, self.t - 1)
        self.used = 0
        self.local_used = 0
        self.sends = []
        self.locals = []

    def slots(self, count):
        first = self.used
        self.used += count
        assert self.used <= self.send_sems.shape[0]
        return first

    def plane_peer(self, step):
        index = lax.rem(self.s * CTX + self.c + step, self.shards * CTX)
        return (index // CTX, lax.rem(index, CTX), self.t)

    def core_peer(self, step):
        return (lax.rem(self.s + step, self.shards), self.c, self.t)

    def line_peer(self, step):
        return (self.s, self.c, lax.rem(self.t + step, LINE))

    def barrier(self, whole_line=False):
        sem = pltpu.get_barrier_semaphore()
        count = self.shards * CTX - 1
        for step in range(1, count + 1):
            pl.semaphore_signal(
                sem, inc=1, device_id=self.plane_peer(step), device_id_type=MESH
            )

        if whole_line:
            for step in range(1, LINE):
                pl.semaphore_signal(
                    sem, inc=1, device_id=self.line_peer(step), device_id_type=MESH
                )
            pl.semaphore_wait(sem, count + LINE - 1)
            return

        @pl.when(self.t > 0)
        def _():
            pl.semaphore_signal(sem, inc=1, device_id=self.left, device_id_type=MESH)

        @pl.when(self.t < LINE - 1)
        def _():
            pl.semaphore_signal(sem, inc=1, device_id=self.right, device_id_type=MESH)

        beside = (self.t + LINE - 1) // LINE + (2 * LINE - 2 - self.t) // LINE
        pl.semaphore_wait(sem, count + beside)

    def copy(self, src, dst, device, slot):
        return pltpu.make_async_remote_copy(
            src_ref=src,
            dst_ref=dst,
            send_sem=self.send_sems.at[slot],
            recv_sem=self.recv_sems.at[slot],
            device_id=device,
            device_id_type=MESH,
        )

    def send(self, src, dst, device, slot, cond=None):
        if cond is None:
            self.copy(src, dst, device, slot).start()
        else:

            @pl.when(cond)
            def _():
                self.copy(src, dst, device, slot).start()

        handle = (src, dst, device, slot, cond)
        self.sends.append(handle)
        return handle

    def sent(self, handle):
        self.sends = [other for other in self.sends if other is not handle]
        self.copy(*handle[:4]).wait_send()

    def recv(self, dst, slot):
        self.copy(dst, dst, self.x_dev, slot).wait_recv()

    def keep(self, src, dst):
        copy = pltpu.make_async_copy(src, dst, self.local_sems.at[self.local_used])
        self.local_used += 1
        assert self.local_used <= self.local_sems.shape[0]
        copy.start()
        return copy

    def keep_later(self, src, dst):
        self.locals.append(self.keep(src, dst))

    def finish(self):
        for src, dst, device, slot, cond in self.sends:
            if cond is None:
                self.copy(src, dst, device, slot).wait_send()
            else:

                @pl.when(cond)
                def _():
                    self.copy(src, dst, device, slot).wait_send()

        for copy in self.locals:
            copy.wait()


class PlaneGather:
    def __init__(self, links, src, full, stage=None):
        self.links, self.src, self.full, self.stage = links, src, full, stage
        self.rows = src.shape[0]
        self.first = links.slots(4 + 4 * (links.shards - 1))

    def block(self, s, c):
        start = pl.multiple_of((s * CTX + c) * self.rows, self.rows)
        return self.full.at[pl.ds(start, self.rows)]

    def half(self, s, c, which):
        size = self.rows // 2
        start = pl.multiple_of((s * CTX + c) * self.rows + which * size, size)
        return self.full.at[pl.ds(start, size)]

    def core_slot(self, step, part):
        return self.first + 4 + (step - 1) * 4 + part

    def core_send(self, src, c, part):
        links = self.links
        for step in range(1, links.shards):
            links.send(
                src,
                self.block(links.s, c),
                links.core_peer(step),
                self.core_slot(step, part),
            )

    def start(self):
        links = self.links
        own = self.block(links.s, links.c)
        links.send(self.src, own, links.x_dev, self.first)
        links.send(self.src, own, links.y_dev, self.first + 1)
        self.core_send(self.src, links.c, 0)
        self.local = links.keep(self.src, own if self.stage is None else self.stage)

    def settle(self):
        self.local.wait()
        self.local = self.links.keep(self.stage, self.block(self.links.s, self.links.c))

    def forward(self):
        links = self.links
        links.recv(self.block(links.s, links.c_x), self.first)
        links.recv(self.block(links.s, links.c_y), self.first + 1)
        from_x = self.half(links.s, links.c_x, 0)
        from_y = self.half(links.s, links.c_y, 1)
        links.send(from_x, from_x, links.y_dev, self.first + 2)
        links.send(from_y, from_y, links.x_dev, self.first + 3)
        self.core_send(self.block(links.s, links.c_x), links.c_x, 1)
        self.core_send(self.block(links.s, links.c_y), links.c_y, 2)

    def diagonal(self):
        links = self.links
        links.recv(self.half(links.s, links.c_d, 0), self.first + 2)
        links.recv(self.half(links.s, links.c_d, 1), self.first + 3)
        self.core_send(self.block(links.s, links.c_d), links.c_d, 3)

    def done(self):
        links = self.links
        for step in range(1, links.shards):
            other = lax.rem(links.s + links.shards - step, links.shards)
            for part, c in enumerate((links.c, links.c_x, links.c_y, links.c_d)):
                links.recv(self.block(other, c), self.core_slot(step, part))
        self.local.wait()


class LineGather:
    def __init__(self, links, own, full, tokens, pieces=1):
        self.links, self.own, self.full, self.tokens = links, own, full, tokens
        self.pieces, self.size = pieces, tokens // pieces
        self.first = links.slots(2 * (LINE - 1) * pieces)

    def block(self, owner, p):
        start = pl.multiple_of(place(owner) * self.tokens + p * self.size, self.size)
        return self.full.at[pl.ds(start, self.size)]

    def slot(self, side, k, p):
        return self.first + (side * (LINE - 1) + k - 1) * self.pieces + p

    def send(self, k, p=0):
        links = self.links
        t, u = links.t, LINE - 1 - links.t
        own = self.own.at[pl.ds(p * self.size, self.size)]
        right, left = self.block(t - k + 1, p), self.block(t + k - 1, p)
        links.send(
            own if k == 1 else right,
            right,
            links.right,
            self.slot(0, k, p),
            jnp.logical_and(t >= k - 1, t < LINE - 1),
        )
        links.send(
            own if k == 1 else left,
            left,
            links.left,
            self.slot(1, k, p),
            jnp.logical_and(u >= k - 1, u < LINE - 1),
        )

    def recv(self, k, p=0):
        links = self.links
        t, u = links.t, LINE - 1 - links.t

        @pl.when(t >= k)
        def _():
            links.recv(self.block(t - k, p), self.slot(0, k, p))

        @pl.when(u >= k)
        def _():
            links.recv(self.block(t + k, p), self.slot(1, k, p))


class LineScatter:
    def __init__(self, links, part, tokens, from_left, from_right, pieces=1):
        self.links, self.part, self.tokens = links, part, tokens
        self.from_left, self.from_right = from_left, from_right
        self.pieces, self.size = pieces, tokens // pieces
        self.first = links.slots(2 * (LINE - 1) * pieces)

    def slot(self, side, k, p):
        return self.first + (side * (LINE - 1) + k) * self.pieces + p

    def piece(self, ref, k, p):
        return ref.at[k, pl.ds(p * self.size, self.size)]

    def total(self, owner, k, p, arrived):
        @pl.loop(0, self.size // ROWS)
        def _(i):
            r = pl.multiple_of(p * self.size + i * ROWS, ROWS)
            q = pl.multiple_of(place(owner) * self.tokens + p * self.size + i * ROWS, ROWS)
            mine = self.part[pl.ds(q, ROWS), :].astype(f32)
            summed = mine + arrived[k, pl.ds(r, ROWS), :].astype(f32)
            arrived[k, pl.ds(r, ROWS), :] = summed.astype(arrived.dtype)

    def ends(self, k, p=0):
        links = self.links
        for side, behind, arrived, device in self.sides():
            owner = LINE - 1 - k if side == 0 else k
            piece, slot = self.piece(arrived, k, p), self.slot(side, k, p)

            @pl.when(behind == 0)
            def _():
                self.first_part(owner, k, p, arrived)

            links.send(piece, piece, device, slot, behind == 0)

    def sides(self):
        links = self.links
        return (
            (0, links.t, self.from_left, links.right),
            (1, LINE - 1 - links.t, self.from_right, links.left),
        )

    def stage(self, now, p=0):
        links = self.links
        for side, behind, arrived, device in self.sides():
            k = now - behind
            owner = LINE - 1 - k if side == 0 else k
            piece, slot = self.piece(arrived, k, p), self.slot(side, k, p)
            ready = jnp.logical_and(k >= 0, behind > 0)

            @pl.when(ready)
            def _():
                links.recv(piece, slot)
                self.total(owner, k, p, arrived)

            links.send(piece, piece, device, slot, ready)

    def first_part(self, owner, k, p, out):
        @pl.loop(0, self.size // ROWS)
        def _(i):
            r = pl.multiple_of(p * self.size + i * ROWS, ROWS)
            q = pl.multiple_of(place(owner) * self.tokens + p * self.size + i * ROWS, ROWS)
            out[k, pl.ds(r, ROWS), :] = self.part[pl.ds(q, ROWS), :].astype(out.dtype)

    def arrive(self, p=0):
        links = self.links
        t = links.t

        @pl.when(t > 0)
        def _():
            links.recv(
                self.piece(self.from_left, LINE - 1 - t, p), self.slot(0, LINE - 1 - t, p)
            )

        @pl.when(t < LINE - 1)
        def _():
            links.recv(self.piece(self.from_right, t, p), self.slot(1, t, p))

    def rows(self, r):
        t = self.links.t
        q = pl.multiple_of(place(t) * self.tokens + r, ROWS)
        k_l = jnp.minimum(LINE - 1 - t, LINE - 2)
        k_r = jnp.minimum(t, LINE - 2)
        zero = jnp.zeros((ROWS, self.part.shape[1]), f32)
        return (
            self.part[pl.ds(q, ROWS), :].astype(f32)
            + jnp.where(t > 0, self.from_left[k_l, pl.ds(r, ROWS), :].astype(f32), zero)
            + jnp.where(t < LINE - 1, self.from_right[k_r, pl.ds(r, ROWS), :].astype(f32), zero)
        )

    def owned(self, p, use):
        @pl.loop(0, self.size // ROWS)
        def _(i):
            r = pl.multiple_of(p * self.size + i * ROWS, ROWS)
            use(r, self.rows(r))


def line_ends(scatter, *hops):
    for k in hops:
        for p in range(scatter.pieces):
            scatter.ends(k, p)


def line_steps(scatter, now):
    for p in range(scatter.pieces):
        scatter.stage(now, p)


def line_finish(scatter, use, gather=None):
    for p in range(scatter.pieces):
        scatter.arrive(p)
        scatter.owned(p, use)
        if gather is not None:
            gather.send(1, p)


def line_spread(gather, k):
    for p in range(gather.pieces):
        gather.recv(k, p)
        if k < LINE - 1:
            gather.send(k + 1, p)


class PlaneScatter:
    def __init__(self, links, left, right, rows, core_in, x_in, y_in, x_last, y_last, out):
        self.links, self.left, self.right, self.rows = links, left, right, rows
        self.core_in, self.x_in, self.y_in = core_in, x_in, y_in
        self.x_last, self.y_last, self.out = x_last, y_last, out
        self.first = links.slots(links.shards - 1 + 6)
        self.tile = min(256, CTX * rows)

    def product(self, shard, i):
        start = pl.multiple_of(shard * (CTX * self.rows) + i * self.tile, self.tile)
        return tn_dot(self.left[:, pl.ds(start, self.tile)], self.right[...])

    @property
    def tiles(self):
        return CTX * self.rows // self.tile

    def other(self, step, stage, part=None):
        links = self.links
        target = lax.rem(links.s + step, links.shards)
        low, high = (0, self.tiles) if part is None else part

        @pl.loop(low, high)
        def _(i):
            r = pl.multiple_of(i * self.tile, self.tile)
            stage[pl.ds(r, self.tile), :] = self.product(target, i).astype(bf16)

        if high == self.tiles:
            return links.send(
                stage, self.core_in.at[step - 1], links.core_peer(step), self.first + step - 1
            )

    def own(self, part=None):
        links = self.links
        low, high = (0, self.tiles) if part is None else part
        if low == 0:
            for step in range(1, links.shards):
                links.recv(self.core_in.at[step - 1], self.first + step - 1)

        @pl.loop(low, high)
        def _(i):
            r = pl.multiple_of(i * self.tile, self.tile)
            summed = self.product(links.s, i)
            for step in range(1, links.shards):
                summed = summed + self.core_in[step - 1, pl.ds(r, self.tile), :].astype(f32)
            self.core_in[0, pl.ds(r, self.tile), :] = summed.astype(bf16)

    def half(self, c, which):
        size = self.rows // 2
        start = pl.multiple_of(c * self.rows + which * size, size)
        return self.core_in.at[0, pl.ds(start, size)]

    def exchange(self):
        links, first = self.links, self.first + self.links.shards - 1
        links.send(self.half(links.c_d, 0), self.x_in.at[1], links.x_dev, first)
        links.send(self.half(links.c_d, 1), self.y_in.at[1], links.y_dev, first + 1)
        links.send(self.half(links.c_x, 0), self.x_in.at[0], links.x_dev, first + 2)
        links.send(self.half(links.c_y, 1), self.y_in.at[0], links.y_dev, first + 3)

    def add(self, c, which, arrived):
        size = self.rows // 2

        @pl.loop(0, size // ROWS)
        def _(i):
            r = pl.multiple_of(i * ROWS, ROWS)
            q = pl.multiple_of(c * self.rows + which * size + i * ROWS, ROWS)
            mine = self.core_in[0, pl.ds(q, ROWS), :].astype(f32)
            summed = mine + arrived[1, pl.ds(r, ROWS), :].astype(f32)
            self.core_in[0, pl.ds(q, ROWS), :] = summed.astype(bf16)

    def fold(self):
        links, first = self.links, self.first + self.links.shards - 1
        links.recv(self.x_in.at[1], first)
        self.add(links.c_y, 0, self.x_in)
        links.send(self.half(links.c_y, 0), self.y_last, links.y_dev, first + 4)
        links.recv(self.y_in.at[1], first + 1)
        self.add(links.c_x, 1, self.y_in)
        links.send(self.half(links.c_x, 1), self.x_last, links.x_dev, first + 5)

    def total(self):
        links, first = self.links, self.first + self.links.shards - 1
        size = self.rows // 2
        links.recv(self.x_in.at[0], first + 2)
        links.recv(self.y_in.at[0], first + 3)
        links.recv(self.y_last, first + 4)
        links.recv(self.x_last, first + 5)
        for which, arrived, last in ((0, self.x_in, self.y_last), (1, self.y_in, self.x_last)):

            @pl.loop(0, size // ROWS)
            def _(i):
                r = pl.multiple_of(i * ROWS, ROWS)
                q = pl.multiple_of(links.c * self.rows + which * size + i * ROWS, ROWS)
                self.out[pl.ds(which * size + r, ROWS), :] = (
                    self.core_in[0, pl.ds(q, ROWS), :].astype(f32)
                    + arrived[0, pl.ds(r, ROWS), :].astype(f32)
                    + last[pl.ds(r, ROWS), :].astype(f32)
                )

    @staticmethod
    def scratch(shards, rows, columns):
        half = (rows // 2, columns)
        return [
            pltpu.VMEM((shards - 1, CTX * rows, columns), bf16),
            pltpu.VMEM((2,) + half, bf16),
            pltpu.VMEM((2,) + half, bf16),
            pltpu.VMEM(half, bf16),
            pltpu.VMEM(half, bf16),
            pltpu.VMEM((rows, columns), f32),
        ]


def any_spec():
    return pl.BlockSpec(memory_space=pl.ANY)


def vmem_spec():
    return pl.BlockSpec(memory_space=pltpu.VMEM)


def struct(shape, dtype):
    return jax.ShapeDtypeStruct(shape, dtype)


def forward_kernel(
    shards,
    x, og, wq, wkv, wo, wg, wu, wd, gain_a, gain_m, frequency, order,
    wq_o, wkv_o, wo_o, wg_o, wu_o, wd_o, n1_o, og_o, n2_o, mid_o, qaug_o, kaug_o, kv_o, att_o, x_o,
    lse, gains, cos, sin,
    x_all, n1_all, wq_all, wkv_all, wo_all, gains_all, qaug, kv_all, kaug, v_all, scores, weights,
    attn, part, from_left, from_right, mid, n2, og_stage, wg_stage, wu_stage, wd_stage, gpad,
    send_sems, recv_sems, local_sems,
):
    tokens, width = x.shape
    queries = tokens * LINE
    heads = qaug.shape[0]
    links = Links(shards, send_sems, recv_sems, local_sems)
    s, c, t = links.s, links.c, links.t

    gather_x = LineGather(links, x, x_all, tokens)
    gather_og = LineGather(links, og, og_o, tokens)
    gather_n2 = LineGather(links, n2, n2_o, tokens, PIECES)
    small = [PlaneGather(links, *pair) for pair in ((wq, wq_all), (wkv, wkv_all), (wo, wo_all))]
    large = [
        PlaneGather(links, *three)
        for three in ((wg, wg_o, wg_stage), (wu, wu_o, wu_stage), (wd, wd_o, wd_stage))
    ]
    scatter = LineScatter(links, part, tokens, from_left, from_right, PIECES)
    plane = shards * CTX
    gain_slot = links.slots(plane - 1)
    kv_slot = links.slots(3)

    me = s * CTX + c
    own = gain_a.shape[1]
    if own == width:
        gpad[0:1, :] = gain_a[...].astype(f32)
        gpad[1:2, :] = gain_m[...].astype(f32)
    else:
        gpad[...] = jnp.zeros_like(gpad)
        own_lanes = pl.ds(pl.multiple_of(me * own, own), own)
        gpad[0:1, own_lanes] = gain_a[...].astype(f32)
        gpad[1:2, own_lanes] = gain_m[...].astype(f32)
    links.barrier()
    for step in range(1, plane):
        links.send(gpad, gains_all.at[me], links.plane_peer(step), gain_slot + step - 1)
    own_gain = links.keep(gpad, gains_all.at[me])
    gather_x.send(1)
    own_rows = pl.ds(pl.multiple_of(place(t) * tokens, tokens), tokens)
    own_x = links.keep(x, x_all.at[own_rows])
    for gather in small:
        gather.start()

    per = queries // BLOCK
    lane = lax.broadcasted_iota(jnp.int32, (1, queries), 1)
    owner = jnp.zeros((1, queries), jnp.int32)
    for index in range(LINE):
        owner = jnp.where(lane // tokens == place(index), index, owner)
    slot = owner * tokens + lax.rem(lane, tokens)
    block_here = jnp.zeros((1, queries), jnp.int32)
    for index in range(per):
        block_here = jnp.where(slot // BLOCK == index, order[c * per + index], block_here)
    position = (block_here * BLOCK + lax.rem(slot, BLOCK)).astype(f32)
    angles = frequency[...] * position
    cos[...] = jnp.cos(angles)
    sin[...] = jnp.sin(angles)
    row = lax.broadcasted_iota(jnp.int32, (HD, queries), 0)
    bias = jnp.zeros((HD, queries), f32)
    for index in range(BLOCKS):
        barred = jnp.logical_and(row == index, order[index] > block_here)
        bias = jnp.where(barred, blocked, bias)
    bias = bias.astype(bf16)
    for h in range(heads):
        qaug[h, HD:, :] = bias

    own_gain.wait()
    for step in range(1, plane):
        other = lax.rem(me + plane - step, plane)
        links.recv(gains_all.at[other], gain_slot + step - 1)
    total = gains_all[0]
    for index in range(1, plane):
        total = total + gains_all[index]
    gains[...] = total
    own_x.wait()

    def norm_block(owner):
        @pl.loop(0, tokens // ROWS)
        def _(i):
            r = pl.multiple_of(place(owner) * tokens + i * ROWS, ROWS)
            v = x_all[pl.ds(r, ROWS), :].astype(f32)
            inverse = lax.rsqrt(jnp.mean(v * v, -1, keepdims=True) + epsilon)
            n1_all[pl.ds(r, ROWS), :] = (v * inverse * gains[0:1, :]).astype(bf16)

    own_og = links.keep(og, og_stage)
    norm_block(t)
    gather_x.recv(1)
    gather_x.send(2)
    for gather in small:
        gather.forward()
    large[0].start()
    norm_pair(gather_x, norm_block, 1)
    gather_x.recv(2)
    gather_x.send(3)
    gather_og.send(1)
    for gather in small:
        gather.diagonal()
    norm_pair(gather_x, norm_block, 2)
    own_og.wait()
    links.keep_later(og_stage, og_o.at[own_rows])
    gather_x.recv(3)
    norm_pair(gather_x, norm_block, 3)
    for gather in small:
        gather.done()

    kv_t = nn_dot(n1_all[...], wkv_all[...]).T
    half = HD // 2
    cosine, sine = cos[...], sin[...]
    k1, k2 = kv_t[0:half], kv_t[half:HD]
    kv_all[c, 0:half, :] = (k1 * cosine - k2 * sine).astype(bf16)
    kv_all[c, half:HD, :] = (k2 * cosine + k1 * sine).astype(bf16)
    kv_all[c, HD : 2 * HD, :] = kv_t[HD:].astype(bf16)
    for step in range(1, CTX):
        peer = lax.rem(c + step, CTX)
        links.send(kv_all.at[c], kv_all.at[c], (s, peer, t), kv_slot + step - 1)
    large[0].settle()
    large[0].forward()
    large[1].start()
    large[2].start()

    q_t = nn_dot(n1_all[...], wq_all[...]).T
    scale = HD ** (-0.5)
    for h in range(heads):
        v1, v2 = q_t[h * HD : h * HD + half], q_t[h * HD + half : (h + 1) * HD]
        qaug[h, 0:half, :] = ((v1 * cosine - v2 * sine).astype(bf16) * scale).astype(bf16)
        qaug[h, half:HD, :] = ((v2 * cosine + v1 * sine).astype(bf16) * scale).astype(bf16)
    links.keep_later(n1_all, n1_o)
    links.keep_later(x_all, x_o)
    links.keep_later(wq_all, wq_o)
    links.keep_later(wkv_all, wkv_o)
    links.keep_later(wo_all, wo_o)
    links.keep_later(qaug, qaug_o)
    for step in range(1, CTX):
        other = lax.rem(c + CTX - step, CTX)
        links.recv(kv_all.at[other], kv_slot + step - 1)
    for other in range(CTX):
        row = lax.broadcasted_iota(jnp.int32, (HD, queries), 0)
        lane = lax.broadcasted_iota(jnp.int32, (HD, queries), 1)
        mark = (row == other * (queries // BLOCK) + lax.rem(lane // tokens, 2)).astype(f32).astype(bf16)
        both = jnp.concatenate([kv_all[other, 0:HD, :], mark], 0)
        kaug[other * queries : (other + 1) * queries, :] = both.T
        v_all[:, other * queries : (other + 1) * queries] = kv_all[other, HD : 2 * HD, :]
    links.keep_later(kaug, kaug_o)
    links.keep_later(kv_all, kv_o)

    length = queries * CTX

    side = queries // 2

    def head(half, h):
        lanes = slice(half * side, (half + 1) * side)
        query = qaug[h, :, lanes]
        top = jnp.full((1, side), -jnp.inf, f32)
        for b in range(0, length, BLOCK):
            block_scores = nn_dot(kaug[b : b + BLOCK, :], query)
            scores[b : b + BLOCK, :] = block_scores
            top = jnp.maximum(top, jnp.max(block_scores, 0, keepdims=True))
        norm = jnp.zeros((1, side), f32)
        for b in range(0, length, BLOCK):
            exponent = jnp.exp(scores[b : b + BLOCK, :] - top)
            norm = norm + jnp.sum(exponent, 0, keepdims=True)
            weights[b : b + BLOCK, :] = exponent.astype(bf16)
        out = nn_dot(v_all[...], weights[...]) / norm
        attn[pl.ds(pl.multiple_of(h * HD, HD), HD), lanes] = out.astype(bf16)
        lse[pl.ds(h, 1), lanes] = top + jnp.log(norm)

    def project(half):
        rows = slice(half * side, (half + 1) * side)
        attn_rows = attn[:, rows].T
        for b in range(0, width, 512):
            part[rows, b : b + 512] = nt_dot(attn_rows, wo_all[b : b + 512, :])

    gather_og.recv(1)
    gather_og.send(2)
    pl.loop(0, heads)(functools.partial(head, 0))
    gather_og.recv(2)
    gather_og.send(3)
    project(0)
    line_ends(scatter, 0)
    large[1].settle()
    large[2].settle()
    pl.loop(0, heads)(functools.partial(head, 1))
    project(1)
    links.keep_later(attn, att_o)

    def finish_rows(r, summed):
        q = pl.multiple_of(place(t) * tokens + r, ROWS)
        middle = x_all[pl.ds(q, ROWS), :].astype(f32) + summed
        mid[pl.ds(r, ROWS), :] = middle
        inverse = lax.rsqrt(jnp.mean(middle * middle, -1, keepdims=True) + epsilon)
        n2[pl.ds(r, ROWS), :] = (middle * inverse * gains[1:2, :]).astype(bf16)

    line_ends(scatter, 1, 2)
    line_steps(scatter, 1)
    large[0].diagonal()
    line_steps(scatter, 2)
    line_finish(scatter, finish_rows, gather_n2)
    links.keep_later(n2, n2_o.at[own_rows])
    links.keep_later(mid, mid_o)
    large[1].forward()
    large[2].forward()
    line_spread(gather_n2, 1)
    line_spread(gather_n2, 2)
    large[1].diagonal()
    large[2].diagonal()
    gather_og.recv(3)
    line_spread(gather_n2, 3)
    for gather in large:
        gather.done()
    links.finish()


def norm_pair(gather, norm_block, k):
    t, u = gather.links.t, LINE - 1 - gather.links.t

    @pl.when(t >= k)
    def _():
        norm_block(t - k)

    @pl.when(u >= k)
    def _():
        norm_block(t + k)


def forward_call(shards, x, og, weights_in, gain_a, gain_m, frequency, order):
    wq, wkv, wo, wg, wu, wd = weights_in
    tokens, width = x.shape
    queries = tokens * LINE
    length = queries * CTX
    heads = wq.shape[1] // HD
    plane = shards * CTX
    full = [struct((width, w.shape[1]), bf16) for w in weights_in]
    outs = full + [
        struct((queries, width), bf16),
        struct((queries, width), bf16),
        struct((queries, width), bf16),
        struct((tokens, width), f32),
        struct((heads, 2 * HD, queries), bf16),
        struct((length, 2 * HD), bf16),
        struct((CTX, 2 * HD, queries), bf16),
        struct((heads * HD, queries), bf16),
        struct((queries, width), bf16),
        struct((heads, queries), f32),
        struct((2, width), f32),
        struct((HD // 2, queries), f32),
        struct((HD // 2, queries), f32),
    ]
    block = (LINE - 1, tokens, width)
    count = 12 * (1 + PIECES) + 6 * (4 + 4 * (shards - 1)) + plane - 1 + 3
    return pl.pallas_call(
        functools.partial(forward_kernel, shards),
        out_shape=outs,
        in_specs=[any_spec()] * 8
        + [vmem_spec()] * 3
        + [pl.BlockSpec(memory_space=pltpu.SMEM)],
        out_specs=[any_spec()] * 15 + [vmem_spec()] * 4,
        scratch_shapes=[
            pltpu.VMEM((queries, width), bf16),
            pltpu.VMEM((queries, width), bf16),
            pltpu.VMEM((width, wq.shape[1]), bf16),
            pltpu.VMEM((width, wkv.shape[1]), bf16),
            pltpu.VMEM((width, wo.shape[1]), bf16),
            pltpu.VMEM((plane, 2, width), f32),
            pltpu.VMEM((heads, 2 * HD, queries), bf16),
            pltpu.VMEM((CTX, 2 * HD, queries), bf16),
            pltpu.VMEM((length, 2 * HD), bf16),
            pltpu.VMEM((HD, length), bf16),
            pltpu.VMEM((length, queries // 2), f32),
            pltpu.VMEM((length, queries // 2), bf16),
            pltpu.VMEM((heads * HD, queries), bf16),
            pltpu.VMEM((queries, width), f32),
            pltpu.VMEM(block, bf16),
            pltpu.VMEM(block, bf16),
            pltpu.VMEM((tokens, width), f32),
            pltpu.VMEM((tokens, width), bf16),
            pltpu.VMEM((tokens, width), bf16),
            pltpu.VMEM(wg.shape, bf16),
            pltpu.VMEM(wu.shape, bf16),
            pltpu.VMEM(wd.shape, bf16),
            pltpu.VMEM((2, width), f32),
            pltpu.SemaphoreType.DMA((count,)),
            pltpu.SemaphoreType.DMA((count,)),
            pltpu.SemaphoreType.DMA((32,)),
        ],
        compiler_params=pltpu.CompilerParams(
            collective_id=0, has_side_effects=True, vmem_limit_bytes=60 * 2**20
        ),
        name="forward",
    )(x, og, wq, wkv, wo, wg, wu, wd, gain_a, gain_m, frequency, order)


def middle_kernel(
    shards, rows,
    n2_in, og_in, wg_in, wu_in, wd_in, mid_in, gains,
    dmid_o, dmid_all_o, gg_o, gd_o, branch_o, gu_part_o, gain_sum,
    n2, og, wg, wu, wd, mid, hidden, dgate, dup, part, branch,
    left, right, dmid, dsend, gain_rows, up_in,
    *rest,
):
    grads, (send_sems, recv_sems, local_sems) = rest[:-3], rest[-3:]
    tokens, width = mid.shape
    queries = n2.shape[0]
    columns = wg.shape[1]
    side = queries // 2
    links = Links(shards, send_sems, recv_sems, local_sems)
    t = links.t
    own_rows = pl.ds(pl.multiple_of(place(t) * tokens, tokens), tokens)

    sides = [slice(0, side), slice(side, queries)]
    full, rest_columns = columns // 256, columns % 256
    weights = ((wg_in, wg), (wu_in, wu), (wd_in, wd))

    def fetch(j, start, size, index):
        src, dst = weights[j]
        of = pl.ds(start, size)
        sem = local_sems.at[3 * index + j]
        return pltpu.make_async_copy(src.at[:, of], dst.at[:, of], sem)

    links.local_used = 3 * (full + 1)
    load_n2 = links.keep(n2_in.at[sides[0]], n2.at[sides[0]])
    for index in range(full):
        for j in range(3):
            fetch(j, index * 256, 256, index).start()
        if index == 0:
            load_og = links.keep(og_in.at[sides[0]], og.at[sides[0]])
    if rest_columns:
        for j in range(3):
            fetch(j, full * 256, rest_columns, full).start()
    load_n2b = links.keep(n2_in.at[sides[1]], n2.at[sides[1]])
    load_ogb = links.keep(og_in.at[sides[1]], og.at[sides[1]])
    load_mid = links.keep(mid_in, mid)
    scatter = LineScatter(links, part, tokens, left, right, PIECES)
    gather = LineGather(links, dsend, dmid_all_o, tokens, PIECES)
    down = PlaneScatter(links, og, hidden, rows, *grads[0:6])
    gate = PlaneScatter(links, n2, dgate, rows, *grads[6:12])
    up = PlaneScatter(links, n2, dup, rows, up_in, None, None, None, None, None)
    links.barrier()

    def feed_forward(half):
        at = sides[half]

        def tile(start, size, index):
            of = pl.ds(start, size)
            if half == 0:
                fetch(0, start, size, index).wait()
                fetch(1, start, size, index).wait()
            gate_act = nn_dot(n2[at, :], wg[:, of])
            up_act = nn_dot(n2[at, :], wu[:, of])
            if half == 0:
                fetch(2, start, size, index).wait()
            d_hidden = nn_dot(og[at, :], wd[:, of])
            sig = jax.nn.sigmoid(gate_act)
            silu = gate_act * sig
            hidden[at, of] = (silu * up_act).astype(bf16)
            d_gate = d_hidden * up_act * sig * (1.0 + gate_act * (1.0 - sig))
            dgate[at, of] = d_gate.astype(bf16)
            dup[at, of] = (d_hidden * silu).astype(bf16)

        @pl.loop(0, full)
        def _(index):
            tile(pl.multiple_of(index * 256, 256), 256, index)

        if rest_columns:
            tile(full * 256, rest_columns, full)

        @pl.loop(0, width // 512)
        def _(j):
            of = pl.ds(pl.multiple_of(j * 512, 512), 512)
            summed = nt_dot(dgate[at, :], wg[of, :]) + nt_dot(dup[at, :], wu[of, :])
            part[at, of] = summed.astype(bf16)

    piece = CTX * rows

    def others(grad, room):
        for step in range(1, shards):
            grad.other(step, room.at[pl.ds((step - 1) * piece, piece)])

    load_n2.wait()
    load_og.wait()
    feed_forward(0)
    line_ends(scatter, 0)
    load_n2b.wait()
    load_ogb.wait()
    feed_forward(1)
    line_ends(scatter, 1, 2)
    line_steps(scatter, 1)
    others(gate, wg)
    others(up, wu)
    gate.own()
    gate.exchange()
    line_steps(scatter, 2)

    @pl.loop(0, width // 512)
    def _(j):
        of = pl.ds(pl.multiple_of(j * 512, 512), 512)
        branch[:, of] = nt_dot(hidden[...], wd[of, :]).astype(bf16)

    links.keep_later(branch, branch_o)
    others(down, wd)
    load_mid.wait()
    gain_rows[...] = jnp.zeros_like(gain_rows)

    def finish_rows(r, d_normed):
        at = pl.ds(r, ROWS)
        q = pl.ds(pl.multiple_of(place(t) * tokens + r, ROWS), ROWS)
        middle = mid[at, :]
        inverse = lax.rsqrt(jnp.mean(middle * middle, -1, keepdims=True) + epsilon)
        unit = middle * inverse
        gain_rows[...] += d_normed * unit
        d_unit = d_normed * gains[1:2, :]
        back = inverse * (d_unit - unit * jnp.mean(d_unit * unit, -1, keepdims=True))
        d_middle = og[q, :].astype(f32) + back
        dmid[at, :] = d_middle
        dsend[at, :] = d_middle.astype(bf16)

    line_finish(scatter, finish_rows, gather)
    down.own()
    down.exchange()
    links.keep_later(dsend, dmid_all_o.at[own_rows])
    links.keep_later(dmid, dmid_o)
    line_spread(gather, 1)
    up.own()
    links.keep_later(up_in.at[0], gu_part_o)
    gain_sum[...] = jnp.sum(gain_rows[...], 0, keepdims=True)
    gate.fold()
    line_spread(gather, 2)
    down.fold()
    line_spread(gather, 3)
    gate.total()
    links.keep_later(gate.out, gg_o)
    down.total()
    links.keep_later(down.out, gd_o)
    links.finish()


def middle_call(shards, rows, n2, og, wg, wu, wd, mid, gains):
    queries, width = n2.shape
    tokens = mid.shape[0]
    columns = wg.shape[1]
    token = (tokens, width)
    wide = (queries, columns)
    block = (LINE - 1,) + token
    outs = [
        struct(token, f32),
        struct((queries, width), bf16),
        struct((rows, columns), f32),
        struct((rows, columns), f32),
        struct((queries, width), bf16),
        struct((CTX * rows, columns), bf16),
        struct((1, width), f32),
    ]
    count = 12 * PIECES + 3 * (shards - 1 + 6)
    return pl.pallas_call(
        functools.partial(middle_kernel, shards, rows),
        out_shape=outs,
        in_specs=[any_spec()] * 6 + [vmem_spec()],
        out_specs=[any_spec()] * 6 + [vmem_spec()],
        scratch_shapes=[
            pltpu.VMEM((queries, width), bf16),
            pltpu.VMEM((queries, width), bf16),
            pltpu.VMEM((width, columns), bf16),
            pltpu.VMEM((width, columns), bf16),
            pltpu.VMEM((width, columns), bf16),
            pltpu.VMEM(token, f32),
            pltpu.VMEM(wide, bf16),
            pltpu.VMEM(wide, bf16),
            pltpu.VMEM(wide, bf16),
            pltpu.VMEM((queries, width), bf16),
            pltpu.VMEM((queries, width), bf16),
            pltpu.VMEM(block, bf16),
            pltpu.VMEM(block, bf16),
            pltpu.VMEM(token, f32),
            pltpu.VMEM(token, bf16),
            pltpu.VMEM((ROWS, width), f32),
            pltpu.VMEM((shards - 1, CTX * rows, columns), bf16),
            *PlaneScatter.scratch(shards, rows, columns),
            *PlaneScatter.scratch(shards, rows, columns),
            pltpu.SemaphoreType.DMA((count,)),
            pltpu.SemaphoreType.DMA((count,)),
            pltpu.SemaphoreType.DMA((40,)),
        ],
        compiler_params=pltpu.CompilerParams(
            collective_id=1, has_side_effects=True, vmem_limit_bytes=63 * 2**20
        ),
        name="middle",
    )(n2, og, wg, wu, wd, mid, gains)


def backward_kernel(
    shards, rows,
    dmid_all_in, wo_in, wq_in, wkv_in, n1_in, qaug_in, kaug_in, kv_in, att_in, x_in, dmid_in,
    branch_in, gu_part_in, mid_in, lse, gains, gain_mlp, cos, sin,
    in_o, gq_o, gkv_o, go_o, gu_o, out_o, gain_o,
    dmid_all, wo, wq, wkv, n1, qaug, kaug, kv, att, x, dmid,
    d_out, attn_rows, v_rows, d_keys, d_values, d_query, d_query_rows, kv_send, kv_recv, d_kv, part,
    left, right, gain_rows, pair, plane_in, line_in, total, stage_o, stage_q, stage_kv,
    branch, left_b, right_b, mid, layer,
    *rest,
):
    grads, (send_sems, recv_sems, local_sems) = rest[:-3], rest[-3:]
    tokens, width = dmid.shape
    queries = n1.shape[0]
    heads = qaug.shape[0]
    length = kaug.shape[0]
    half = HD // 2
    plane = shards * CTX
    links = Links(shards, send_sems, recv_sems, local_sems)
    s, c, t = links.s, links.c, links.t

    scatter = LineScatter(links, part, tokens, left, right, PIECES)
    scatter_out = LineScatter(links, branch, tokens, left_b, right_b)
    g_o = PlaneScatter(links, dmid_all, attn_rows, rows, *grads[0:6])
    g_q = PlaneScatter(links, n1, d_query_rows, rows, *grads[6:12])
    g_kv = PlaneScatter(links, n1, d_kv, rows, *grads[12:18])
    g_u = PlaneScatter(links, None, None, rows, *grads[18:24])
    kv_slot = links.slots(CTX - 1)
    plane_slot = links.slots(plane - 1)
    line_slot = links.slots(LINE - 1)
    piece = CTX * rows
    loads = [
        links.keep(src, dst)
        for src, dst in (
            (branch_in, branch), (dmid_all_in, dmid_all), (wo_in, wo), (gu_part_in, g_u.core_in.at[0]),
            (att_in, att), (kv_in, kv), (qaug_in, qaug), (kaug_in, kaug), (n1_in, n1), (wq_in, wq),
            (wkv_in, wkv), (x_in, x), (dmid_in, dmid), (mid_in, mid),
        )
    ]

    def others(grad, stage):
        for step in range(1, shards):
            grad.other(step, stage.at[pl.ds((step - 1) * piece, piece)])

    links.barrier(whole_line=True)
    loads[0].wait()
    line_ends(scatter_out, 0)
    for load in loads[1:3]:
        load.wait()
    d_out[...] = nn_dot(dmid_all[...], wo[...]).astype(bf16).T
    loads[3].wait()
    g_u.exchange()
    for load in loads[4:8]:
        load.wait()
    attn_rows[...] = att[...].T
    for other in range(CTX):
        v_rows[other * queries : (other + 1) * queries, :] = kv[other, HD : 2 * HD, :].T
    d_keys[...] = jnp.zeros_like(d_keys)
    d_values[...] = jnp.zeros_like(d_values)

    def head(h):
        at = pl.ds(pl.multiple_of(h * HD, HD), HD)
        query = qaug[h]
        d_head = d_out[at, :]
        delta = jnp.sum(d_head.astype(f32) * att[at, :].astype(f32), 0, keepdims=True)
        log_sum = lse[pl.ds(h, 1), :]
        d_q = jnp.zeros((HD, queries), f32)
        for b in range(0, length, BLOCK):
            e = b + BLOCK
            probs = jnp.exp(nn_dot(kaug[b:e, :], query) - log_sum)
            d_probs = nn_dot(v_rows[b:e, :], d_head)
            d_scores = (probs * (d_probs - delta)).astype(bf16)
            d_values[b:e, :] += nt_dot(probs.astype(bf16), d_head)
            d_keys[b:e, :] += nt_dot(d_scores, query[0:HD])
            at_b = b % queries
            d_q = d_q + nn_dot(kv[b // queries, 0:HD, at_b : at_b + BLOCK], d_scores)
        d_query[at, :] = d_q * (HD ** (-0.5))

    pl.loop(0, heads // 2)(head)
    line_ends(scatter_out, 1, 2)
    scatter_out.stage(1)
    pl.loop(heads // 2, heads)(head)

    for other in range(CTX):
        block = slice(other * queries, (other + 1) * queries)
        both = jnp.concatenate([d_keys[block, :], d_values[block, :]], 1)
        kv_send[other] = both.astype(bf16)
    for step in range(1, CTX):
        peer = lax.rem(c + step, CTX)
        links.send(kv_send.at[peer], kv_recv.at[step - 1], (s, peer, t), kv_slot + step - 1)
    scatter_out.stage(2)
    for load in loads[8:]:
        load.wait()

    cosine, sine = cos[...], sin[...]
    for h in range(heads):
        at = h * HD
        d1, d2 = d_query[at : at + half, :], d_query[at + half : at + HD, :]
        d_query[at : at + half, :] = d1 * cosine + d2 * sine
        d_query[at + half : at + HD, :] = d2 * cosine - d1 * sine
    d_query_rows[...] = d_query[...].astype(bf16).T
    others(g_q, stage_q)
    others(g_o, stage_o)
    for step in range(1, CTX):
        links.recv(kv_recv.at[step - 1], kv_slot + step - 1)
    d_pair = kv_send[c].astype(f32)
    for step in range(1, CTX):
        d_pair = d_pair + kv_recv[step - 1].astype(f32)
    d_pair = d_pair.T
    d1, d2 = d_pair[0:half], d_pair[half:HD]
    turned = jnp.concatenate(
        [d1 * cosine + d2 * sine, d2 * cosine - d1 * sine, d_pair[HD:]], 0
    )
    d_kv[...] = turned.astype(bf16).T

    @pl.loop(0, width // 512)
    def _(j):
        at = pl.ds(pl.multiple_of(j * 512, 512), 512)
        summed = nt_dot(d_query_rows[...], wq[at, :]) + nt_dot(d_kv[...], wkv[at, :])
        part[:, at] = summed.astype(bf16)

    line_ends(scatter, 0, 1, 2)

    gain_rows[...] = jnp.zeros_like(gain_rows)

    @pl.loop(0, queries // ROWS)
    def _(i):
        r = pl.ds(pl.multiple_of(i * ROWS, ROWS), ROWS)
        v = x[r, :].astype(f32)
        inverse = lax.rsqrt(jnp.mean(v * v, -1, keepdims=True) + epsilon)
        gain_rows[...] += part[r, :].astype(f32) * (v * inverse)

    pair[0:1, :] = jnp.sum(gain_rows[...], 0, keepdims=True)
    pair[1:2, :] = gain_mlp[...]
    for step in range(1, plane):
        links.send(pair, plane_in.at[step - 1], links.plane_peer(step), plane_slot + step - 1)
    g_u.fold()
    g_o.own()
    g_o.exchange()
    line_steps(scatter, 1)
    summed = pair[...]
    for step in range(1, plane):
        links.recv(plane_in.at[step - 1], plane_slot + step - 1)
        summed = summed + plane_in[step - 1]
    total[...] = summed
    for step in range(1, LINE):
        links.send(total, line_in.at[step - 1], links.line_peer(step), line_slot + step - 1)
    others(g_kv, stage_kv)
    g_q.own()
    g_q.exchange()
    line_steps(scatter, 2)
    g_kv.own()
    g_kv.exchange()
    g_o.fold()
    scatter_out.arrive()

    def layer_rows(r, total_rows):
        layer[pl.ds(r, ROWS), :] = (mid[pl.ds(r, ROWS), :] + total_rows).astype(bf16)

    scatter_out.owned(0, layer_rows)
    links.keep_later(layer, out_o)
    g_q.fold()
    g_kv.fold()

    def finish_rows(r, d_normed):
        at = pl.ds(r, ROWS)
        q = pl.ds(pl.multiple_of(place(t) * tokens + r, ROWS), ROWS)
        v = x[q, :].astype(f32)
        inverse = lax.rsqrt(jnp.mean(v * v, -1, keepdims=True) + epsilon)
        unit = v * inverse
        d_unit = d_normed * gains[0:1, :]
        back = inverse * (d_unit - unit * jnp.mean(d_unit * unit, -1, keepdims=True))
        dmid[at, :] = dmid[at, :] + back

    line_finish(scatter, finish_rows)
    links.keep_later(dmid, in_o)
    g_u.total()
    links.keep_later(g_u.out, gu_o)
    g_o.total()
    links.keep_later(g_o.out, go_o)
    g_q.total()
    links.keep_later(g_q.out, gq_o)
    g_kv.total()
    links.keep_later(g_kv.out, gkv_o)
    for step in range(1, LINE):
        links.recv(line_in.at[step - 1], line_slot + step - 1)
        summed = summed + line_in[step - 1]
    gain_o[...] = summed
    links.finish()


def backward_call(
    shards, rows, dmid_all, wo, wq, wkv, n1, qaug, kaug, kv, att, x, dmid, branch, gu_part, mid,
    lse, gains, gain_mlp, cos, sin,
):
    tokens, width = dmid.shape
    queries = n1.shape[0]
    heads = qaug.shape[0]
    length = kaug.shape[0]
    inner = heads * HD
    columns = gu_part.shape[1]
    plane = shards * CTX
    piece = CTX * rows * (shards - 1)
    token = (tokens, width)
    block = (LINE - 1,) + token
    outs = [
        struct(token, f32),
        struct((rows, inner), f32),
        struct((rows, 2 * HD), f32),
        struct((rows, inner), f32),
        struct((rows, columns), f32),
        struct(token, bf16),
        struct((2, width), f32),
    ]
    count = 6 + 6 * PIECES + 4 * (shards - 1 + 6) + CTX - 1 + plane - 1 + LINE - 1
    return pl.pallas_call(
        functools.partial(backward_kernel, shards, rows),
        out_shape=outs,
        in_specs=[any_spec()] * 14 + [vmem_spec()] * 5,
        out_specs=[any_spec()] * 6 + [vmem_spec()],
        scratch_shapes=[
            pltpu.VMEM((queries, width), bf16),
            pltpu.VMEM((width, inner), bf16),
            pltpu.VMEM((width, inner), bf16),
            pltpu.VMEM((width, 2 * HD), bf16),
            pltpu.VMEM((queries, width), bf16),
            pltpu.VMEM(qaug.shape, bf16),
            pltpu.VMEM(kaug.shape, bf16),
            pltpu.VMEM(kv.shape, bf16),
            pltpu.VMEM((inner, queries), bf16),
            pltpu.VMEM((queries, width), bf16),
            pltpu.VMEM(token, f32),
            pltpu.VMEM((inner, queries), bf16),
            pltpu.VMEM((queries, inner), bf16),
            pltpu.VMEM((length, HD), bf16),
            pltpu.VMEM((length, HD), f32),
            pltpu.VMEM((length, HD), f32),
            pltpu.VMEM((inner, queries), f32),
            pltpu.VMEM((queries, inner), bf16),
            pltpu.VMEM((CTX, queries, 2 * HD), bf16),
            pltpu.VMEM((CTX - 1, queries, 2 * HD), bf16),
            pltpu.VMEM((queries, 2 * HD), bf16),
            pltpu.VMEM((queries, width), bf16),
            pltpu.VMEM(block, bf16),
            pltpu.VMEM(block, bf16),
            pltpu.VMEM((ROWS, width), f32),
            pltpu.VMEM((2, width), f32),
            pltpu.VMEM((plane - 1, 2, width), f32),
            pltpu.VMEM((LINE - 1, 2, width), f32),
            pltpu.VMEM((2, width), f32),
            pltpu.VMEM((piece, inner), bf16),
            pltpu.VMEM((piece, inner), bf16),
            pltpu.VMEM((piece, 2 * HD), bf16),
            pltpu.VMEM((queries, width), bf16),
            pltpu.VMEM(block, bf16),
            pltpu.VMEM(block, bf16),
            pltpu.VMEM(token, f32),
            pltpu.VMEM(token, bf16),
            *PlaneScatter.scratch(shards, rows, inner),
            *PlaneScatter.scratch(shards, rows, inner),
            *PlaneScatter.scratch(shards, rows, 2 * HD),
            *PlaneScatter.scratch(1 + 1, rows, columns),
            pltpu.SemaphoreType.DMA((count,)),
            pltpu.SemaphoreType.DMA((count,)),
            pltpu.SemaphoreType.DMA((32,)),
        ],
        compiler_params=pltpu.CompilerParams(
            collective_id=2, has_side_effects=True, vmem_limit_bytes=60 * 2**20
        ),
        name="backward",
    )(
        dmid_all, wo, wq, wkv, n1, qaug, kaug, kv, att, x, dmid, branch, gu_part, mid,
        lse, gains, gain_mlp, cos, sin,
    )


def finish_kernel(layer_in, *refs):
    count = len(refs) // 2
    layer_out = refs[count]
    layer_out[0] = layer_in[...]
    refs[count + 1][0] = refs[0][...]
    for src, dst in zip(refs[1:count], refs[count + 2 :]):
        dst[...] = src[...]


def finish_call(arrays, steps=4):
    rows = [array.shape[0] // steps for array in arrays]
    wide = [array.shape[1] for array in arrays]
    shapes = [struct((1,) * (i < 2) + array.shape, array.dtype) for i, array in enumerate(arrays)]
    return pl.pallas_call(
        finish_kernel,
        grid=(steps,),
        out_shape=shapes,
        in_specs=[pl.BlockSpec((r, n), lambda i: (i, 0)) for r, n in zip(rows, wide)],
        out_specs=[
            pl.BlockSpec((1, r, n), lambda i: (0, i, 0))
            if index < 2
            else pl.BlockSpec((r, n), lambda i: (i, 0))
            for index, (r, n) in enumerate(zip(rows, wide))
        ],
        compiler_params=pltpu.CompilerParams(vmem_limit_bytes=40 * 2**20),
        name="finish",
    )(*arrays)


def body(
    inputs, out_grad, block_order, gain_attn, w_query, w_keyval, w_output, gain_mlp, w_gate, w_up, w_down
):
    shards = lax.axis_size("shard")
    x, og = inputs[0], out_grad[0]
    tokens, width = x.shape
    s, c = lax.axis_index("shard"), lax.axis_index("ctx")
    frequency = np.float32(10000.0) ** (-np.arange(HD // 2, dtype=np.float32)[:, None] * 2.0 / HD)
    own = gain_attn.shape[0]
    start = (s * CTX + c) * own
    if own % 128 == 0:
        gain_a, gain_m = gain_attn[None], gain_mlp[None]
    else:
        place_gain = lambda gain: lax.dynamic_update_slice(
            jnp.zeros((1, width), f32), gain.astype(f32)[None], (0, start)
        )
        gain_a, gain_m = place_gain(gain_attn), place_gain(gain_mlp)
    (wq, wkv, wo, wg, wu, wd, n1, og_all, n2, mid, qaug, kaug, kv, att, x_all, lse, gains, cos, sin) = forward_call(
        shards, x, og, (w_query, w_keyval, w_output, w_gate, w_up, w_down), gain_a, gain_m,
        jnp.asarray(frequency, f32), block_order[0],
    )
    (dmid, dmid_all, grad_gate, grad_down, branch, gu_part, gm) = middle_call(
        shards, w_gate.shape[0], n2, og_all, wg, wu, wd, mid, gains
    )
    (input_grad, grad_query, grad_keyval, grad_output, grad_up, layer_out, both) = backward_call(
        shards, w_query.shape[0], dmid_all, wo, wq, wkv, n1, qaug, kaug, kv, att, x_all, dmid,
        branch, gu_part, mid, lse, gains, gm, cos, sin,
    )
    both = lax.dynamic_slice(both, (0, start), (2, gain_attn.shape[0]))
    (
        layer_out, input_grad, grad_query, grad_keyval, grad_output, grad_gate, grad_up, grad_down,
    ) = finish_call([
        layer_out, input_grad, grad_query, grad_keyval, grad_output, grad_gate, grad_up, grad_down,
    ])
    return (
        layer_out, input_grad, both[0], grad_query, grad_keyval, grad_output,
        both[1], grad_gate, grad_up, grad_down,
    )


def solution(mesh):
    plane = P(("shard", "ctx"), "tensor")
    gain = P(("shard", "ctx"))
    token = P("shard", ("ctx", "tensor"), None)
    return jax.shard_map(
        body,
        mesh=mesh,
        in_specs=(token, token, P("shard", None), gain, plane, plane, plane, gain, plane, plane, plane),
        out_specs=(token, token, gain, plane, plane, plane, gain, plane, plane, plane),
        check_vma=False,
    )
```

```python
import functools

import jax
import jax.numpy as jnp
import numpy as np
from jax import lax
from jax.experimental import pallas as pl
from jax.experimental.pallas import tpu as pltpu
from jax.sharding import PartitionSpec as P

HD = 64
BLOCK = 256
BLOCKS = 8
ROWS = 16
CTX = 4
LINE = 4
PIECES = 2

epsilon = 1e-05
blocked = -1e30

f32 = jnp.float32
bf16 = jnp.bfloat16
MESH = pl.DeviceIdType.MESH


def place(owner):
    return (owner + (owner + 1) // 2) % LINE if isinstance(owner, int) else lax.rem(
        owner + (owner + 1) // 2, LINE
    )


def nn_dot(left, right):
    return jnp.dot(left, right, preferred_element_type=f32)


def nt_dot(left, right):
    return lax.dot_general(left, right, (((1,), (1,)), ((), ())), preferred_element_type=f32)


def tn_dot(left, right):
    return lax.dot_general(left, right, (((0,), (0,)), ((), ())), preferred_element_type=f32)


class Links:
    def __init__(self, shards, send_sems, recv_sems, local_sems):
        self.shards = shards
        self.send_sems, self.recv_sems, self.local_sems = send_sems, recv_sems, local_sems
        self.s = lax.axis_index("shard")
        self.c = lax.axis_index("ctx")
        self.t = lax.axis_index("tensor")
        self.c_x = self.c + 1 - 2 * lax.rem(self.c, 2)
        self.c_y = lax.rem(self.c + 2, CTX)
        self.c_d = CTX - 1 - self.c
        self.x_dev = (self.s, self.c_x, self.t)
        self.y_dev = (self.s, self.c_y, self.t)
        self.right = (self.s, self.c, self.t + 1)
        self.left = (self.s, self.c, self.t - 1)
        self.used = 0
        self.local_used = 0
        self.sends = []
        self.locals = []

    def slots(self, count):
        first = self.used
        self.used += count
        assert self.used <= self.send_sems.shape[0]
        return first

    def plane_peer(self, step):
        index = lax.rem(self.s * CTX + self.c + step, self.shards * CTX)
        return (index // CTX, lax.rem(index, CTX), self.t)

    def core_peer(self, step):
        return (lax.rem(self.s + step, self.shards), self.c, self.t)

    def line_peer(self, step):
        return (self.s, self.c, lax.rem(self.t + step, LINE))

    def barrier(self, whole_line=False):
        sem = pltpu.get_barrier_semaphore()
        count = self.shards * CTX - 1
        for step in range(1, count + 1):
            pl.semaphore_signal(
                sem, inc=1, device_id=self.plane_peer(step), device_id_type=MESH
            )

        if whole_line:
            for step in range(1, LINE):
                pl.semaphore_signal(
                    sem, inc=1, device_id=self.line_peer(step), device_id_type=MESH
                )
            pl.semaphore_wait(sem, count + LINE - 1)
            return

        @pl.when(self.t > 0)
        def _():
            pl.semaphore_signal(sem, inc=1, device_id=self.left, device_id_type=MESH)

        @pl.when(self.t < LINE - 1)
        def _():
            pl.semaphore_signal(sem, inc=1, device_id=self.right, device_id_type=MESH)

        beside = (self.t + LINE - 1) // LINE + (2 * LINE - 2 - self.t) // LINE
        pl.semaphore_wait(sem, count + beside)

    def copy(self, src, dst, device, slot):
        return pltpu.make_async_remote_copy(
            src_ref=src,
            dst_ref=dst,
            send_sem=self.send_sems.at[slot],
            recv_sem=self.recv_sems.at[slot],
            device_id=device,
            device_id_type=MESH,
        )

    def send(self, src, dst, device, slot, cond=None):
        if cond is None:
            self.copy(src, dst, device, slot).start()
        else:

            @pl.when(cond)
            def _():
                self.copy(src, dst, device, slot).start()

        handle = (src, dst, device, slot, cond)
        self.sends.append(handle)
        return handle

    def sent(self, handle):
        self.sends = [other for other in self.sends if other is not handle]
        self.copy(*handle[:4]).wait_send()

    def recv(self, dst, slot):
        self.copy(dst, dst, self.x_dev, slot).wait_recv()

    def keep(self, src, dst):
        copy = pltpu.make_async_copy(src, dst, self.local_sems.at[self.local_used])
        self.local_used += 1
        assert self.local_used <= self.local_sems.shape[0]
        copy.start()
        return copy

    def keep_later(self, src, dst):
        self.locals.append(self.keep(src, dst))

    def finish(self):
        for src, dst, device, slot, cond in self.sends:
            if cond is None:
                self.copy(src, dst, device, slot).wait_send()
            else:

                @pl.when(cond)
                def _():
                    self.copy(src, dst, device, slot).wait_send()

        for copy in self.locals:
            copy.wait()


class PlaneGather:
    def __init__(self, links, src, full, stage=None):
        self.links, self.src, self.full, self.stage = links, src, full, stage
        self.rows = src.shape[0]
        self.first = links.slots(4 + 4 * (links.shards - 1))

    def block(self, s, c):
        start = pl.multiple_of((s * CTX + c) * self.rows, self.rows)
        return self.full.at[pl.ds(start, self.rows)]

    def half(self, s, c, which):
        size = self.rows // 2
        start = pl.multiple_of((s * CTX + c) * self.rows + which * size, size)
        return self.full.at[pl.ds(start, size)]

    def core_slot(self, step, part):
        return self.first + 4 + (step - 1) * 4 + part

    def core_send(self, src, c, part):
        links = self.links
        for step in range(1, links.shards):
            links.send(
                src,
                self.block(links.s, c),
                links.core_peer(step),
                self.core_slot(step, part),
            )

    def start(self):
        links = self.links
        own = self.block(links.s, links.c)
        links.send(self.src, own, links.x_dev, self.first)
        links.send(self.src, own, links.y_dev, self.first + 1)
        self.core_send(self.src, links.c, 0)
        self.local = links.keep(self.src, own if self.stage is None else self.stage)

    def settle(self):
        self.local.wait()
        self.local = self.links.keep(self.stage, self.block(self.links.s, self.links.c))

    def forward(self):
        links = self.links
        links.recv(self.block(links.s, links.c_x), self.first)
        links.recv(self.block(links.s, links.c_y), self.first + 1)
        from_x = self.half(links.s, links.c_x, 0)
        from_y = self.half(links.s, links.c_y, 1)
        links.send(from_x, from_x, links.y_dev, self.first + 2)
        links.send(from_y, from_y, links.x_dev, self.first + 3)
        self.core_send(self.block(links.s, links.c_x), links.c_x, 1)
        self.core_send(self.block(links.s, links.c_y), links.c_y, 2)

    def diagonal(self):
        links = self.links
        links.recv(self.half(links.s, links.c_d, 0), self.first + 2)
        links.recv(self.half(links.s, links.c_d, 1), self.first + 3)
        self.core_send(self.block(links.s, links.c_d), links.c_d, 3)

    def done(self):
        links = self.links
        for step in range(1, links.shards):
            other = lax.rem(links.s + links.shards - step, links.shards)
            for part, c in enumerate((links.c, links.c_x, links.c_y, links.c_d)):
                links.recv(self.block(other, c), self.core_slot(step, part))
        self.local.wait()


class LineGather:
    def __init__(self, links, own, full, tokens, pieces=1):
        self.links, self.own, self.full, self.tokens = links, own, full, tokens
        self.pieces, self.size = pieces, tokens // pieces
        self.first = links.slots(2 * (LINE - 1) * pieces)

    def block(self, owner, p):
        start = pl.multiple_of(place(owner) * self.tokens + p * self.size, self.size)
        return self.full.at[pl.ds(start, self.size)]

    def slot(self, side, k, p):
        return self.first + (side * (LINE - 1) + k - 1) * self.pieces + p

    def send(self, k, p=0):
        links = self.links
        t, u = links.t, LINE - 1 - links.t
        own = self.own.at[pl.ds(p * self.size, self.size)]
        right, left = self.block(t - k + 1, p), self.block(t + k - 1, p)
        links.send(
            own if k == 1 else right,
            right,
            links.right,
            self.slot(0, k, p),
            jnp.logical_and(t >= k - 1, t < LINE - 1),
        )
        links.send(
            own if k == 1 else left,
            left,
            links.left,
            self.slot(1, k, p),
            jnp.logical_and(u >= k - 1, u < LINE - 1),
        )

    def recv(self, k, p=0):
        links = self.links
        t, u = links.t, LINE - 1 - links.t

        @pl.when(t >= k)
        def _():
            links.recv(self.block(t - k, p), self.slot(0, k, p))

        @pl.when(u >= k)
        def _():
            links.recv(self.block(t + k, p), self.slot(1, k, p))


class LineScatter:
    def __init__(self, links, part, tokens, from_left, from_right, pieces=1):
        self.links, self.part, self.tokens = links, part, tokens
        self.from_left, self.from_right = from_left, from_right
        self.pieces, self.size = pieces, tokens // pieces
        self.first = links.slots(2 * (LINE - 1) * pieces)

    def slot(self, side, k, p):
        return self.first + (side * (LINE - 1) + k) * self.pieces + p

    def piece(self, ref, k, p):
        return ref.at[k, pl.ds(p * self.size, self.size)]

    def total(self, owner, k, p, arrived):
        @pl.loop(0, self.size // ROWS)
        def _(i):
            r = pl.multiple_of(p * self.size + i * ROWS, ROWS)
            q = pl.multiple_of(place(owner) * self.tokens + p * self.size + i * ROWS, ROWS)
            mine = self.part[pl.ds(q, ROWS), :].astype(f32)
            summed = mine + arrived[k, pl.ds(r, ROWS), :].astype(f32)
            arrived[k, pl.ds(r, ROWS), :] = summed.astype(arrived.dtype)

    def ends(self, k, p=0):
        links = self.links
        for side, behind, arrived, device in self.sides():
            owner = LINE - 1 - k if side == 0 else k
            piece, slot = self.piece(arrived, k, p), self.slot(side, k, p)

            @pl.when(behind == 0)
            def _():
                self.first_part(owner, k, p, arrived)

            links.send(piece, piece, device, slot, behind == 0)

    def sides(self):
        links = self.links
        return (
            (0, links.t, self.from_left, links.right),
            (1, LINE - 1 - links.t, self.from_right, links.left),
        )

    def stage(self, now, p=0):
        links = self.links
        for side, behind, arrived, device in self.sides():
            k = now - behind
            owner = LINE - 1 - k if side == 0 else k
            piece, slot = self.piece(arrived, k, p), self.slot(side, k, p)
            ready = jnp.logical_and(k >= 0, behind > 0)

            @pl.when(ready)
            def _():
                links.recv(piece, slot)
                self.total(owner, k, p, arrived)

            links.send(piece, piece, device, slot, ready)

    def first_part(self, owner, k, p, out):
        @pl.loop(0, self.size // ROWS)
        def _(i):
            r = pl.multiple_of(p * self.size + i * ROWS, ROWS)
            q = pl.multiple_of(place(owner) * self.tokens + p * self.size + i * ROWS, ROWS)
            out[k, pl.ds(r, ROWS), :] = self.part[pl.ds(q, ROWS), :].astype(out.dtype)

    def arrive(self, p=0):
        links = self.links
        t = links.t

        @pl.when(t > 0)
        def _():
            links.recv(
                self.piece(self.from_left, LINE - 1 - t, p), self.slot(0, LINE - 1 - t, p)
            )

        @pl.when(t < LINE - 1)
        def _():
            links.recv(self.piece(self.from_right, t, p), self.slot(1, t, p))

    def rows(self, r):
        t = self.links.t
        q = pl.multiple_of(place(t) * self.tokens + r, ROWS)
        k_l = jnp.minimum(LINE - 1 - t, LINE - 2)
        k_r = jnp.minimum(t, LINE - 2)
        zero = jnp.zeros((ROWS, self.part.shape[1]), f32)
        return (
            self.part[pl.ds(q, ROWS), :].astype(f32)
            + jnp.where(t > 0, self.from_left[k_l, pl.ds(r, ROWS), :].astype(f32), zero)
            + jnp.where(t < LINE - 1, self.from_right[k_r, pl.ds(r, ROWS), :].astype(f32), zero)
        )

    def owned(self, p, use):
        @pl.loop(0, self.size // ROWS)
        def _(i):
            r = pl.multiple_of(p * self.size + i * ROWS, ROWS)
            use(r, self.rows(r))


def line_ends(scatter, *hops):
    for k in hops:
        for p in range(scatter.pieces):
            scatter.ends(k, p)


def line_steps(scatter, now):
    for p in range(scatter.pieces):
        scatter.stage(now, p)


def line_finish(scatter, use, gather=None):
    for p in range(scatter.pieces):
        scatter.arrive(p)
        scatter.owned(p, use)
        if gather is not None:
            gather.send(1, p)


def line_spread(gather, k):
    for p in range(gather.pieces):
        gather.recv(k, p)
        if k < LINE - 1:
            gather.send(k + 1, p)


class PlaneScatter:
    def __init__(self, links, left, right, rows, core_in, x_in, y_in, x_last, y_last, out):
        self.links, self.left, self.right, self.rows = links, left, right, rows
        self.core_in, self.x_in, self.y_in = core_in, x_in, y_in
        self.x_last, self.y_last, self.out = x_last, y_last, out
        self.first = links.slots(links.shards - 1 + 6)
        self.tile = min(256, CTX * rows)

    def product(self, shard, i):
        start = pl.multiple_of(shard * (CTX * self.rows) + i * self.tile, self.tile)
        return tn_dot(self.left[:, pl.ds(start, self.tile)], self.right[...])

    @property
    def tiles(self):
        return CTX * self.rows // self.tile

    def other(self, step, stage, part=None):
        links = self.links
        target = lax.rem(links.s + step, links.shards)
        low, high = (0, self.tiles) if part is None else part

        @pl.loop(low, high)
        def _(i):
            r = pl.multiple_of(i * self.tile, self.tile)
            stage[pl.ds(r, self.tile), :] = self.product(target, i).astype(bf16)

        if high == self.tiles:
            return links.send(
                stage, self.core_in.at[step - 1], links.core_peer(step), self.first + step - 1
            )

    def own(self, part=None):
        links = self.links
        low, high = (0, self.tiles) if part is None else part
        if low == 0:
            for step in range(1, links.shards):
                links.recv(self.core_in.at[step - 1], self.first + step - 1)

        @pl.loop(low, high)
        def _(i):
            r = pl.multiple_of(i * self.tile, self.tile)
            summed = self.product(links.s, i)
            for step in range(1, links.shards):
                summed = summed + self.core_in[step - 1, pl.ds(r, self.tile), :].astype(f32)
            self.core_in[0, pl.ds(r, self.tile), :] = summed.astype(bf16)

    def half(self, c, which):
        size = self.rows // 2
        start = pl.multiple_of(c * self.rows + which * size, size)
        return self.core_in.at[0, pl.ds(start, size)]

    def exchange(self):
        links, first = self.links, self.first + self.links.shards - 1
        links.send(self.half(links.c_d, 0), self.x_in.at[1], links.x_dev, first)
        links.send(self.half(links.c_d, 1), self.y_in.at[1], links.y_dev, first + 1)
        links.send(self.half(links.c_x, 0), self.x_in.at[0], links.x_dev, first + 2)
        links.send(self.half(links.c_y, 1), self.y_in.at[0], links.y_dev, first + 3)

    def add(self, c, which, arrived):
        size = self.rows // 2

        @pl.loop(0, size // ROWS)
        def _(i):
            r = pl.multiple_of(i * ROWS, ROWS)
            q = pl.multiple_of(c * self.rows + which * size + i * ROWS, ROWS)
            mine = self.core_in[0, pl.ds(q, ROWS), :].astype(f32)
            summed = mine + arrived[1, pl.ds(r, ROWS), :].astype(f32)
            self.core_in[0, pl.ds(q, ROWS), :] = summed.astype(bf16)

    def arrived(self):
        links, first = self.links, self.first + self.links.shards - 1
        for ref, offset in ((self.x_in, 0), (self.y_in, 1)):
            for part in range(2):
                links.recv(ref.at[1 - part], first + offset + 2 * part)

    def fold(self, here=False):
        links, first = self.links, self.first + self.links.shards - 1
        if not here:
            links.recv(self.x_in.at[1], first)
        self.add(links.c_y, 0, self.x_in)
        links.send(self.half(links.c_y, 0), self.y_last, links.y_dev, first + 4)
        if not here:
            links.recv(self.y_in.at[1], first + 1)
        self.add(links.c_x, 1, self.y_in)
        links.send(self.half(links.c_x, 1), self.x_last, links.x_dev, first + 5)

    def total(self, here=False):
        links, first = self.links, self.first + self.links.shards - 1
        size = self.rows // 2
        if not here:
            links.recv(self.x_in.at[0], first + 2)
            links.recv(self.y_in.at[0], first + 3)
        links.recv(self.y_last, first + 4)
        links.recv(self.x_last, first + 5)
        for which, arrived, last in ((0, self.x_in, self.y_last), (1, self.y_in, self.x_last)):

            @pl.loop(0, size // ROWS)
            def _(i):
                r = pl.multiple_of(i * ROWS, ROWS)
                q = pl.multiple_of(links.c * self.rows + which * size + i * ROWS, ROWS)
                self.out[pl.ds(which * size + r, ROWS), :] = (
                    self.core_in[0, pl.ds(q, ROWS), :].astype(f32)
                    + arrived[0, pl.ds(r, ROWS), :].astype(f32)
                    + last[pl.ds(r, ROWS), :].astype(f32)
                )

    @staticmethod
    def scratch(shards, rows, columns):
        half = (rows // 2, columns)
        return [
            pltpu.VMEM((shards - 1, CTX * rows, columns), bf16),
            pltpu.VMEM((2,) + half, bf16),
            pltpu.VMEM((2,) + half, bf16),
            pltpu.VMEM(half, bf16),
            pltpu.VMEM(half, bf16),
            pltpu.VMEM((rows, columns), f32),
        ]


def any_spec():
    return pl.BlockSpec(memory_space=pl.ANY)


def vmem_spec():
    return pl.BlockSpec(memory_space=pltpu.VMEM)


def struct(shape, dtype):
    return jax.ShapeDtypeStruct(shape, dtype)


def forward_kernel(
    shards,
    x, og, wq, wkv, wo, wg, wu, wd, gain_in, frequency, order,
    wq_o, wkv_o, wo_o, wg_o, wu_o, wd_o, n1_o, og_o, n2_o, mid_o, qaug_o, kaug_o, kv_o, att_o, x_o,
    lse, gains, cos, sin,
    x_all, n1_all, wq_all, wkv_all, wo_all, gains_all, qaug, kv_all, kaug, v_all, scores, weights,
    attn, part, from_left, from_right, mid, n2, og_stage, wg_stage, wu_stage, wd_stage, gpad,
    send_sems, recv_sems, local_sems,
):
    tokens, width = x.shape
    queries = tokens * LINE
    heads = qaug.shape[0]
    links = Links(shards, send_sems, recv_sems, local_sems)
    s, c, t = links.s, links.c, links.t

    gather_x = LineGather(links, x, x_all, tokens, PIECES)
    gather_og = LineGather(links, og, og_o, tokens)
    gather_n2 = LineGather(links, n2, n2_o, tokens, PIECES)
    small = [PlaneGather(links, *pair) for pair in ((wq, wq_all), (wkv, wkv_all), (wo, wo_all))]
    large = [
        PlaneGather(links, *three)
        for three in ((wg, wg_o, wg_stage), (wu, wu_o, wu_stage), (wd, wd_o, wd_stage))
    ]
    scatter = LineScatter(links, part, tokens, from_left, from_right, PIECES)
    plane = shards * CTX
    gain_slot = links.slots(plane - 1)
    kv_slot = links.slots((CTX - 1) * (2 * LINE - 1))

    me = s * CTX + c
    own_gains = gain_in.shape[1]
    if own_gains == width:
        gpad[...] = gain_in[...]
    else:
        gpad[...] = jnp.zeros_like(gpad)
        gpad[:, pl.ds(pl.multiple_of(me * own_gains, own_gains), own_gains)] = gain_in[...]
    links.barrier()
    for step in range(1, plane):
        links.send(gpad, gains_all.at[me], links.plane_peer(step), gain_slot + step - 1)
    own_gain = links.keep(gpad, gains_all.at[me])
    for p in range(PIECES):
        gather_x.send(1, p)
    own_rows = pl.ds(pl.multiple_of(place(t) * tokens, tokens), tokens)
    own_x = links.keep(x, x_all.at[own_rows])
    for gather in small:
        gather.start()

    per = queries // BLOCK
    lane = lax.broadcasted_iota(jnp.int32, (1, queries), 1)
    owner = jnp.zeros((1, queries), jnp.int32)
    for index in range(LINE):
        owner = jnp.where(lane // tokens == place(index), index, owner)
    slot = owner * tokens + lax.rem(lane, tokens)
    block_here = jnp.zeros((1, queries), jnp.int32)
    for index in range(per):
        block_here = jnp.where(slot // BLOCK == index, order[c * per + index], block_here)
    position = (block_here * BLOCK + lax.rem(slot, BLOCK)).astype(f32)
    angles = frequency[...] * position
    cos[...] = jnp.cos(angles)
    sin[...] = jnp.sin(angles)
    row = lax.broadcasted_iota(jnp.int32, (HD, queries), 0)
    bias = jnp.zeros((HD, queries), f32)
    for index in range(BLOCKS):
        barred = jnp.logical_and(row == index, order[index] > block_here)
        bias = jnp.where(barred, blocked, bias)
    bias = bias.astype(bf16)
    for h in range(heads):
        qaug[h, HD:, :] = bias

    own_gain.wait()
    for step in range(1, plane):
        other = lax.rem(me + plane - step, plane)
        links.recv(gains_all.at[other], gain_slot + step - 1)
    total = gains_all[0]
    for index in range(1, plane):
        total = total + gains_all[index]
    gains[...] = total
    own_x.wait()

    def norm_block(owner):
        @pl.loop(0, tokens // ROWS)
        def _(i):
            r = pl.multiple_of(place(owner) * tokens + i * ROWS, ROWS)
            v = x_all[pl.ds(r, ROWS), :].astype(f32)
            inverse = lax.rsqrt(jnp.mean(v * v, -1, keepdims=True) + epsilon)
            n1_all[pl.ds(r, ROWS), :] = (v * inverse * gains[0:1, :]).astype(bf16)

    own_og = links.keep(og, og_stage)
    norm_block(t)
    line_spread(gather_x, 1)
    for gather in small:
        gather.forward()
    norm_pair(gather_x, norm_block, 1)
    line_spread(gather_x, 2)
    gather_og.send(1)
    for gather in small:
        gather.diagonal()
    norm_pair(gather_x, norm_block, 2)
    own_og.wait()
    links.keep_later(og_stage, og_o.at[own_rows])
    for gather in small:
        gather.done()

    half = HD // 2
    scale = HD ** (-0.5)

    def lanes_of(owner):
        return pl.ds(pl.multiple_of(place(owner) * tokens, tokens), tokens)

    def turn(v1, v2, cosine, sine):
        return (v1 * cosine - v2 * sine).astype(bf16), (v2 * cosine + v1 * sine).astype(bf16)

    def project_block(owner):
        at = lanes_of(owner)
        cosine, sine = cos[:, at], sin[:, at]
        kv_t = nn_dot(n1_all[at, :], wkv_all[...]).T
        k1, k2 = turn(kv_t[0:half], kv_t[half:HD], cosine, sine)
        kv_all[c, 0:half, at] = k1
        kv_all[c, half:HD, at] = k2
        kv_all[c, HD : 2 * HD, at] = kv_t[HD:].astype(bf16)
        q_t = nn_dot(n1_all[at, :], wq_all[...]).T
        for h in range(heads):
            b = h * HD
            q1, q2 = turn(q_t[b : b + half], q_t[b + half : b + HD], cosine, sine)
            qaug[h, 0:half, at] = (q1 * scale).astype(bf16)
            qaug[h, half:HD, at] = (q2 * scale).astype(bf16)

    u = LINE - 1 - t
    arrivals = [(t, None)]
    for k in range(1, LINE):
        arrivals += [(t - k, t >= k), (t + k, u >= k)]

    def send_block(index):
        owner, cond = arrivals[index]
        for step in range(1, CTX):
            peer = lax.rem(c + step, CTX)
            ref = kv_all.at[c, :, lanes_of(owner)]
            links.send(ref, ref, (s, peer, t), kv_slot + index * (CTX - 1) + step - 1, cond)

    def recv_block(index):
        owner, cond = arrivals[index]

        def wait():
            for step in range(1, CTX):
                other = lax.rem(c + CTX - step, CTX)
                slot = kv_slot + index * (CTX - 1) + step - 1
                links.recv(kv_all.at[other, :, lanes_of(owner)], slot)

        if cond is None:
            wait()
        else:
            pl.when(cond)(wait)

    project_block(t)
    send_block(0)
    for k in range(1, LINE):
        if k == LINE - 1:
            line_spread(gather_x, k)
            norm_pair(gather_x, norm_block, k)
        norm_pair(gather_x, project_block, k)
        send_block(2 * k - 1)
        send_block(2 * k)
    for gather in large:
        gather.start()
    links.keep_later(n1_all, n1_o)
    links.keep_later(x_all, x_o)
    links.keep_later(wq_all, wq_o)
    links.keep_later(wkv_all, wkv_o)
    links.keep_later(wo_all, wo_o)
    links.keep_later(qaug, qaug_o)
    for index in range(len(arrivals)):
        recv_block(index)
    for other in range(CTX):
        row = lax.broadcasted_iota(jnp.int32, (HD, queries), 0)
        lane = lax.broadcasted_iota(jnp.int32, (HD, queries), 1)
        mark = (row == other * (queries // BLOCK) + lax.rem(lane // tokens, 2)).astype(f32).astype(bf16)
        both = jnp.concatenate([kv_all[other, 0:HD, :], mark], 0)
        kaug[other * queries : (other + 1) * queries, :] = both.T
        v_all[:, other * queries : (other + 1) * queries] = kv_all[other, HD : 2 * HD, :]
    links.keep_later(kaug, kaug_o)
    links.keep_later(kv_all, kv_o)

    length = queries * CTX

    far = pl.multiple_of(jnp.where(t < LINE // 2, tokens, 0), tokens)
    near = pl.multiple_of(jnp.where(t < LINE // 2, 0, tokens), tokens)

    def head(start, size, h):
        lanes = pl.ds(start, size)
        query = qaug[h, :, lanes]
        top = jnp.full((1, size), -jnp.inf, f32)
        for b in range(0, length, BLOCK):
            block_scores = nn_dot(kaug[b : b + BLOCK, :], query)
            scores[b : b + BLOCK, 0:size] = block_scores
            top = jnp.maximum(top, jnp.max(block_scores, 0, keepdims=True))
        norm = jnp.zeros((1, size), f32)
        for b in range(0, length, BLOCK):
            exponent = jnp.exp(scores[b : b + BLOCK, 0:size] - top)
            norm = norm + jnp.sum(exponent, 0, keepdims=True)
            weights[b : b + BLOCK, 0:size] = exponent.astype(bf16)
        out = nn_dot(v_all[...], weights[:, 0:size]) / norm
        attn[pl.ds(pl.multiple_of(h * HD, HD), HD), lanes] = out.astype(bf16)
        lse[h, :, lanes] = top + jnp.log(norm)

    def attend(start, size):
        pl.loop(0, heads)(functools.partial(head, start, size))
        rows = pl.ds(start, size)
        attn_rows = attn[:, rows].T
        for b in range(0, width, 512):
            part[rows, b : b + 512] = nt_dot(attn_rows, wo_all[b : b + 512, :])

    attend(far, tokens)
    line_ends(scatter, 0)
    gather_og.recv(1)
    gather_og.send(2)
    for gather in large:
        gather.settle()
    attend(2 * tokens, 2 * tokens)
    line_ends(scatter, 1, 2)
    gather_og.recv(2)
    gather_og.send(3)
    line_steps(scatter, 1)
    attend(near, tokens)
    links.keep_later(attn, att_o)

    def finish_rows(r, summed):
        q = pl.multiple_of(place(t) * tokens + r, ROWS)
        middle = x_all[pl.ds(q, ROWS), :].astype(f32) + summed
        mid[pl.ds(r, ROWS), :] = middle
        inverse = lax.rsqrt(jnp.mean(middle * middle, -1, keepdims=True) + epsilon)
        n2[pl.ds(r, ROWS), :] = (middle * inverse * gains[1:2, :]).astype(bf16)

    large[0].forward()
    line_steps(scatter, 2)
    large[1].forward()
    line_finish(scatter, finish_rows, gather_n2)
    large[2].forward()
    links.keep_later(n2, n2_o.at[own_rows])
    links.keep_later(mid, mid_o)
    line_spread(gather_n2, 1)
    large[0].diagonal()
    large[1].diagonal()
    line_spread(gather_n2, 2)
    large[2].diagonal()
    gather_og.recv(3)
    line_spread(gather_n2, 3)
    for gather in large:
        gather.done()
    links.finish()


def norm_pair(gather, norm_block, k):
    t, u = gather.links.t, LINE - 1 - gather.links.t

    @pl.when(t >= k)
    def _():
        norm_block(t - k)

    @pl.when(u >= k)
    def _():
        norm_block(t + k)


def forward_call(shards, x, og, weights_in, gain_in, frequency, order):
    wq, wkv, wo, wg, wu, wd = weights_in
    tokens, width = x.shape
    queries = tokens * LINE
    length = queries * CTX
    heads = wq.shape[1] // HD
    plane = shards * CTX
    full = [struct((width, w.shape[1]), bf16) for w in weights_in]
    outs = full + [
        struct((queries, width), bf16),
        struct((queries, width), bf16),
        struct((queries, width), bf16),
        struct((tokens, width), f32),
        struct((heads, 2 * HD, queries), bf16),
        struct((length, 2 * HD), bf16),
        struct((CTX, 2 * HD, queries), bf16),
        struct((heads * HD, queries), bf16),
        struct((queries, width), bf16),
        struct((heads, 1, queries), f32),
        struct((2, width), f32),
        struct((HD // 2, queries), f32),
        struct((HD // 2, queries), f32),
    ]
    block = (LINE - 1, tokens, width)
    count = 6 + 18 * PIECES + 6 * (4 + 4 * (shards - 1)) + plane - 1 + 21
    return pl.pallas_call(
        functools.partial(forward_kernel, shards),
        out_shape=outs,
        in_specs=[any_spec()] * 8
        + [vmem_spec()] * 2
        + [pl.BlockSpec(memory_space=pltpu.SMEM)],
        out_specs=[any_spec()] * 15 + [vmem_spec()] * 4,
        scratch_shapes=[
            pltpu.VMEM((queries, width), bf16),
            pltpu.VMEM((queries, width), bf16),
            pltpu.VMEM((width, wq.shape[1]), bf16),
            pltpu.VMEM((width, wkv.shape[1]), bf16),
            pltpu.VMEM((width, wo.shape[1]), bf16),
            pltpu.VMEM((plane, 2, width), f32),
            pltpu.VMEM((heads, 2 * HD, queries), bf16),
            pltpu.VMEM((CTX, 2 * HD, queries), bf16),
            pltpu.VMEM((length, 2 * HD), bf16),
            pltpu.VMEM((HD, length), bf16),
            pltpu.VMEM((length, queries // 2), f32),
            pltpu.VMEM((length, queries // 2), bf16),
            pltpu.VMEM((heads * HD, queries), bf16),
            pltpu.VMEM((queries, width), f32),
            pltpu.VMEM(block, bf16),
            pltpu.VMEM(block, bf16),
            pltpu.VMEM((tokens, width), f32),
            pltpu.VMEM((tokens, width), bf16),
            pltpu.VMEM((tokens, width), bf16),
            pltpu.VMEM(wg.shape, bf16),
            pltpu.VMEM(wu.shape, bf16),
            pltpu.VMEM(wd.shape, bf16),
            pltpu.VMEM((2, width), f32),
            pltpu.SemaphoreType.DMA((count,)),
            pltpu.SemaphoreType.DMA((count,)),
            pltpu.SemaphoreType.DMA((32,)),
        ],
        compiler_params=pltpu.CompilerParams(
            collective_id=0, has_side_effects=True, vmem_limit_bytes=60 * 2**20
        ),
        name="forward",
    )(x, og, wq, wkv, wo, wg, wu, wd, gain_in, frequency, order)


def middle_kernel(
    shards, rows,
    n2_in, og_in, wg_in, wu_in, wd_in, mid_in, gains,
    dmid_o, dmid_all_o, gg_o, gd_part_o, gd_x_o, gd_y_o, branch_o, gu_part_o, gain_sum,
    n2, og, wg, wu, wd, mid, hidden, dgate, dup, part, branch,
    left, right, dmid, dsend, gain_rows, up_in,
    *rest,
):
    grads, (send_sems, recv_sems, local_sems) = rest[:-3], rest[-3:]
    tokens, width = mid.shape
    queries = n2.shape[0]
    columns = wg.shape[1]
    links = Links(shards, send_sems, recv_sems, local_sems)
    t = links.t
    own_rows = pl.ds(pl.multiple_of(place(t) * tokens, tokens), tokens)

    far = pl.multiple_of(jnp.where(t < LINE // 2, tokens, 0), tokens)
    near = pl.multiple_of(jnp.where(t < LINE // 2, 0, tokens), tokens)
    sides = [pl.ds(far, tokens), pl.ds(2 * tokens, 2 * tokens), pl.ds(near, tokens)]
    full, rest_columns = columns // 256, columns % 256
    weights = ((wg_in, wg), (wu_in, wu), (wd_in, wd))

    def fetch(j, start, size, index):
        src, dst = weights[j]
        of = pl.ds(start, size)
        sem = local_sems.at[3 * index + j]
        return pltpu.make_async_copy(src.at[:, of], dst.at[:, of], sem)

    links.local_used = 3 * (full + 1)
    load_n2 = [links.keep(n2_in.at[sides[0]], n2.at[sides[0]])]
    for index in range(full):
        for j in range(3):
            fetch(j, index * 256, 256, index).start()
        if index == 0:
            load_og = [links.keep(og_in.at[sides[0]], og.at[sides[0]])]
    if rest_columns:
        for j in range(3):
            fetch(j, full * 256, rest_columns, full).start()
    load_n2 += [links.keep(n2_in.at[at], n2.at[at]) for at in sides[1:]]
    load_og += [links.keep(og_in.at[at], og.at[at]) for at in sides[1:]]
    load_mid = links.keep(mid_in, mid)
    scatter = LineScatter(links, part, tokens, left, right, PIECES)
    gather = LineGather(links, dsend, dmid_all_o, tokens, PIECES)
    down = PlaneScatter(links, og, hidden, rows, *grads[0:6])
    gate = PlaneScatter(links, n2, dgate, rows, *grads[6:12])
    up = PlaneScatter(links, n2, dup, rows, up_in, None, None, None, None, None)
    links.barrier()

    def feed_forward(half):
        at = sides[half]
        load_n2[half].wait()
        load_og[half].wait()

        def tile(start, size, index):
            of = pl.ds(start, size)
            if half == 0:
                fetch(0, start, size, index).wait()
                fetch(1, start, size, index).wait()
            gate_act = nn_dot(n2[at, :], wg[:, of])
            up_act = nn_dot(n2[at, :], wu[:, of])
            if half == 0:
                fetch(2, start, size, index).wait()
            d_hidden = nn_dot(og[at, :], wd[:, of])
            sig = jax.nn.sigmoid(gate_act)
            silu = gate_act * sig
            hidden[at, of] = (silu * up_act).astype(bf16)
            d_gate = d_hidden * up_act * sig * (1.0 + gate_act * (1.0 - sig))
            dgate[at, of] = d_gate.astype(bf16)
            dup[at, of] = (d_hidden * silu).astype(bf16)

        @pl.loop(0, full)
        def _(index):
            tile(pl.multiple_of(index * 256, 256), 256, index)

        if rest_columns:
            tile(full * 256, rest_columns, full)

        @pl.loop(0, width // 512)
        def _(j):
            of = pl.ds(pl.multiple_of(j * 512, 512), 512)
            summed = nt_dot(dgate[at, :], wg[of, :]) + nt_dot(dup[at, :], wu[of, :])
            part[at, of] = summed.astype(bf16)

    piece = CTX * rows

    def others(grad, room):
        for step in range(1, shards):
            grad.other(step, room.at[pl.ds((step - 1) * piece, piece)])

    feed_forward(0)
    line_ends(scatter, 0)
    feed_forward(1)
    line_ends(scatter, 1, 2)
    line_steps(scatter, 1)
    feed_forward(2)
    others(gate, wg)
    line_steps(scatter, 2)

    @pl.loop(0, width // 512)
    def _(j):
        of = pl.ds(pl.multiple_of(j * 512, 512), 512)
        branch[:, of] = nt_dot(hidden[...], wd[of, :]).astype(bf16)

    links.keep_later(branch, branch_o)
    gate.own()
    gate.exchange()
    others(down, wd)
    load_mid.wait()
    gain_rows[...] = jnp.zeros_like(gain_rows)

    def finish_rows(r, d_normed):
        at = pl.ds(r, ROWS)
        q = pl.ds(pl.multiple_of(place(t) * tokens + r, ROWS), ROWS)
        middle = mid[at, :]
        inverse = lax.rsqrt(jnp.mean(middle * middle, -1, keepdims=True) + epsilon)
        unit = middle * inverse
        gain_rows[...] += d_normed * unit
        d_unit = d_normed * gains[1:2, :]
        back = inverse * (d_unit - unit * jnp.mean(d_unit * unit, -1, keepdims=True))
        d_middle = og[q, :].astype(f32) + back
        dmid[at, :] = d_middle
        dsend[at, :] = d_middle.astype(bf16)

    line_finish(scatter, finish_rows, gather)
    gate.fold()
    down.own()
    down.exchange()
    links.keep_later(dsend, dmid_all_o.at[own_rows])
    links.keep_later(dmid, dmid_o)
    links.keep_later(down.core_in.at[0], gd_part_o)
    line_spread(gather, 1)
    others(up, wu)
    gain_sum[...] = jnp.sum(gain_rows[...], 0, keepdims=True)
    line_spread(gather, 2)
    up.own()
    links.keep_later(up_in.at[0], gu_part_o)
    gate.total()
    links.keep_later(gate.out, gg_o)
    line_spread(gather, 3)
    down.arrived()
    links.keep_later(down.x_in, gd_x_o)
    links.keep_later(down.y_in, gd_y_o)
    links.finish()


def middle_call(shards, rows, n2, og, wg, wu, wd, mid, gains):
    queries, width = n2.shape
    tokens = mid.shape[0]
    columns = wg.shape[1]
    token = (tokens, width)
    wide = (queries, columns)
    block = (LINE - 1,) + token
    outs = [
        struct(token, f32),
        struct((queries, width), bf16),
        struct((rows, columns), f32),
        struct((CTX * rows, columns), bf16),
        struct((2, rows // 2, columns), bf16),
        struct((2, rows // 2, columns), bf16),
        struct((queries, width), bf16),
        struct((CTX * rows, columns), bf16),
        struct((1, width), f32),
    ]
    count = 12 * PIECES + 3 * (shards - 1 + 6)
    return pl.pallas_call(
        functools.partial(middle_kernel, shards, rows),
        out_shape=outs,
        in_specs=[any_spec()] * 6 + [vmem_spec()],
        out_specs=[any_spec()] * 8 + [vmem_spec()],
        scratch_shapes=[
            pltpu.VMEM((queries, width), bf16),
            pltpu.VMEM((queries, width), bf16),
            pltpu.VMEM((width, columns), bf16),
            pltpu.VMEM((width, columns), bf16),
            pltpu.VMEM((width, columns), bf16),
            pltpu.VMEM(token, f32),
            pltpu.VMEM(wide, bf16),
            pltpu.VMEM(wide, bf16),
            pltpu.VMEM(wide, bf16),
            pltpu.VMEM((queries, width), bf16),
            pltpu.VMEM((queries, width), bf16),
            pltpu.VMEM(block, bf16),
            pltpu.VMEM(block, bf16),
            pltpu.VMEM(token, f32),
            pltpu.VMEM(token, bf16),
            pltpu.VMEM((ROWS, width), f32),
            pltpu.VMEM((shards - 1, CTX * rows, columns), bf16),
            *PlaneScatter.scratch(shards, rows, columns),
            *PlaneScatter.scratch(shards, rows, columns),
            pltpu.SemaphoreType.DMA((count,)),
            pltpu.SemaphoreType.DMA((count,)),
            pltpu.SemaphoreType.DMA((40,)),
        ],
        compiler_params=pltpu.CompilerParams(
            collective_id=1, has_side_effects=True, vmem_limit_bytes=63 * 2**20
        ),
        name="middle",
    )(n2, og, wg, wu, wd, mid, gains)


def backward_kernel(
    shards, rows,
    dmid_all_in, wo_in, wq_in, wkv_in, n1_in, qaug_in, kaug_in, kv_in, att_in, x_in, dmid_in,
    branch_in, gu_part_in, gd_part_in, gd_x_in, gd_y_in, mid_in, lse, gains, gain_mlp, cos, sin,
    in_o, gq_o, gkv_o, go_o, gu_o, gd_o, out_o, gain_o,
    dmid_all, wo, wq, wkv, n1, qaug, kaug, kv, att, x, dmid,
    d_out, attn_rows, v_rows, d_keys, d_values, d_query, d_query_rows, kv_send, kv_recv, d_kv, part,
    left, right, gain_rows, pair, plane_in, line_in, total, stage_o, stage_q, stage_kv,
    branch, left_b, right_b, mid, layer, gain_sum, part_query,
    *rest,
):
    grads, (send_sems, recv_sems, local_sems) = rest[:-3], rest[-3:]
    tokens, width = dmid.shape
    queries = n1.shape[0]
    heads = qaug.shape[0]
    length = kaug.shape[0]
    half = HD // 2
    plane = shards * CTX
    links = Links(shards, send_sems, recv_sems, local_sems)
    s, c, t = links.s, links.c, links.t

    scatter = LineScatter(links, part, tokens, left, right, PIECES)
    scatter_out = LineScatter(links, branch, tokens, left_b, right_b)
    g_o = PlaneScatter(links, dmid_all, attn_rows, rows, *grads[0:6])
    g_q = PlaneScatter(links, n1, d_query_rows, rows, *grads[6:12])
    g_kv = PlaneScatter(links, n1, d_kv, rows, *grads[12:18])
    g_u = PlaneScatter(links, None, None, rows, *grads[18:24])
    g_d = PlaneScatter(links, None, None, rows, *grads[24:30])
    kv_slot = links.slots(CTX - 1)
    plane_slot = links.slots(plane - 1)
    line_slot = links.slots(LINE - 1)
    piece = CTX * rows
    loads = [
        links.keep(src, dst)
        for src, dst in (
            (branch_in, branch), (dmid_all_in, dmid_all), (wo_in, wo), (gu_part_in, g_u.core_in.at[0]),
            (att_in, att), (kv_in, kv), (qaug_in, qaug), (kaug_in, kaug),
            (gd_part_in, g_d.core_in.at[0]), (gd_x_in, g_d.x_in), (gd_y_in, g_d.y_in), (n1_in, n1),
            (wq_in, wq), (wkv_in, wkv), (x_in, x), (dmid_in, dmid), (mid_in, mid),
        )
    ]

    def others(grad, stage):
        for step in range(1, shards):
            grad.other(step, stage.at[pl.ds((step - 1) * piece, piece)])

    links.barrier(whole_line=True)
    loads[0].wait()
    line_ends(scatter_out, 0)
    for load in loads[1:3]:
        load.wait()
    d_out[...] = nn_dot(dmid_all[...], wo[...]).astype(bf16).T
    loads[3].wait()
    g_u.exchange()
    for load in loads[4:8]:
        load.wait()
    attn_rows[...] = att[...].T
    for other in range(CTX):
        v_rows[other * queries : (other + 1) * queries, :] = kv[other, HD : 2 * HD, :].T
    d_keys[...] = jnp.zeros_like(d_keys)
    d_values[...] = jnp.zeros_like(d_values)
    for load in loads[8:11]:
        load.wait()
    g_d.fold(here=True)

    def head(h):
        at = pl.ds(pl.multiple_of(h * HD, HD), HD)
        query = qaug[h]
        d_head = d_out[at, :]
        delta = jnp.sum(d_head.astype(f32) * att[at, :].astype(f32), 0, keepdims=True)
        log_sum = lse[h]
        d_q = jnp.zeros((HD, queries), f32)
        for b in range(0, length, BLOCK):
            e = b + BLOCK
            probs = jnp.exp(nn_dot(kaug[b:e, :], query) - log_sum)
            d_probs = nn_dot(v_rows[b:e, :], d_head)
            d_scores = (probs * (d_probs - delta)).astype(bf16)
            d_values[b:e, :] += nt_dot(probs.astype(bf16), d_head)
            d_keys[b:e, :] += nt_dot(d_scores, query[0:HD])
            at_b = b % queries
            d_q = d_q + nn_dot(kv[b // queries, 0:HD, at_b : at_b + BLOCK], d_scores)
        d_query[at, :] = d_q * (HD ** (-0.5))

    pl.loop(0, heads // 2)(head)
    line_ends(scatter_out, 1, 2)
    scatter_out.stage(1)
    pl.loop(heads // 2, heads)(head)

    for other in range(CTX):
        block = slice(other * queries, (other + 1) * queries)
        both = jnp.concatenate([d_keys[block, :], d_values[block, :]], 1)
        kv_send[other] = both.astype(bf16)
    for step in range(1, CTX):
        peer = lax.rem(c + step, CTX)
        links.send(kv_send.at[peer], kv_recv.at[step - 1], (s, peer, t), kv_slot + step - 1)
    scatter_out.stage(2)
    for load in loads[11:]:
        load.wait()

    cosine, sine = cos[...], sin[...]
    for h in range(heads):
        at = h * HD
        d1, d2 = d_query[at : at + half, :], d_query[at + half : at + HD, :]
        d_query[at : at + half, :] = d1 * cosine + d2 * sine
        d_query[at + half : at + HD, :] = d2 * cosine - d1 * sine
    d_query_rows[...] = d_query[...].astype(bf16).T
    for b in range(0, width, 512):
        part_query[:, b : b + 512] = nt_dot(d_query_rows[...], wq[b : b + 512, :])
    others(g_q, stage_q)
    others(g_o, stage_o)
    for step in range(1, CTX):
        links.recv(kv_recv.at[step - 1], kv_slot + step - 1)
    d_pair = kv_send[c].astype(f32)
    for step in range(1, CTX):
        d_pair = d_pair + kv_recv[step - 1].astype(f32)
    d_pair = d_pair.T
    d1, d2 = d_pair[0:half], d_pair[half:HD]
    turned = jnp.concatenate(
        [d1 * cosine + d2 * sine, d2 * cosine - d1 * sine, d_pair[HD:]], 0
    )
    d_kv[...] = turned.astype(bf16).T

    for b in range(0, width, 512):
        summed = part_query[:, b : b + 512] + nt_dot(d_kv[...], wkv[b : b + 512, :])
        part[:, b : b + 512] = summed.astype(bf16)

    line_ends(scatter, 0, 1)

    gain_rows[...] = jnp.zeros_like(gain_rows)

    @pl.loop(0, queries // ROWS)
    def _(i):
        r = pl.ds(pl.multiple_of(i * ROWS, ROWS), ROWS)
        v = x[r, :].astype(f32)
        inverse = lax.rsqrt(jnp.mean(v * v, -1, keepdims=True) + epsilon)
        gain_rows[...] += part[r, :].astype(f32) * (v * inverse)

    pair[0:1, :] = jnp.sum(gain_rows[...], 0, keepdims=True)
    pair[1:2, :] = gain_mlp[...]
    for step in range(1, plane):
        links.send(pair, plane_in.at[step - 1], links.plane_peer(step), plane_slot + step - 1)
    g_u.fold()
    line_steps(scatter, 1)
    g_o.own()
    g_o.exchange()
    summed = pair[...]
    for step in range(1, plane):
        links.recv(plane_in.at[step - 1], plane_slot + step - 1)
        summed = summed + plane_in[step - 1]
    total[...] = summed
    for step in range(1, LINE):
        links.send(total, line_in.at[step - 1], links.line_peer(step), line_slot + step - 1)
    line_ends(scatter, 2)
    others(g_kv, stage_kv)
    g_q.own()
    g_q.exchange()
    line_steps(scatter, 2)
    g_kv.own()
    g_kv.exchange()
    g_o.fold()
    scatter_out.arrive()

    def layer_rows(r, total_rows):
        layer[pl.ds(r, ROWS), :] = (mid[pl.ds(r, ROWS), :] + total_rows).astype(bf16)

    scatter_out.owned(0, layer_rows)
    links.keep_later(layer, out_o)
    g_q.fold()
    g_kv.fold()
    g_u.total()
    links.keep_later(g_u.out, gu_o)
    g_o.total()
    links.keep_later(g_o.out, go_o)
    g_d.total(here=True)
    links.keep_later(g_d.out, gd_o)

    def finish_rows(r, d_normed):
        at = pl.ds(r, ROWS)
        q = pl.ds(pl.multiple_of(place(t) * tokens + r, ROWS), ROWS)
        v = x[q, :].astype(f32)
        inverse = lax.rsqrt(jnp.mean(v * v, -1, keepdims=True) + epsilon)
        unit = v * inverse
        d_unit = d_normed * gains[0:1, :]
        back = inverse * (d_unit - unit * jnp.mean(d_unit * unit, -1, keepdims=True))
        dmid[at, :] = dmid[at, :] + back

    line_finish(scatter, finish_rows)
    links.keep_later(dmid, in_o)
    g_q.total()
    links.keep_later(g_q.out, gq_o)
    g_kv.total()
    links.keep_later(g_kv.out, gkv_o)
    for step in range(1, LINE):
        links.recv(line_in.at[step - 1], line_slot + step - 1)
        summed = summed + line_in[step - 1]
    own_gains = gain_o.shape[1]
    if own_gains == width:
        gain_o[...] = summed
    else:
        gain_sum[...] = summed
        me = s * CTX + c
        gain_o[...] = gain_sum[:, pl.ds(pl.multiple_of(me * own_gains, own_gains), own_gains)]
    links.finish()


def backward_call(
    shards, rows, dmid_all, wo, wq, wkv, n1, qaug, kaug, kv, att, x, dmid, branch, gu_part,
    gd_part, gd_x, gd_y, mid, lse, gains, gain_mlp, cos, sin,
):
    tokens, width = dmid.shape
    queries = n1.shape[0]
    heads = qaug.shape[0]
    length = kaug.shape[0]
    inner = heads * HD
    columns = gu_part.shape[1]
    plane = shards * CTX
    own_gains = width // plane if width // plane % 128 == 0 else width
    piece = CTX * rows * (shards - 1)
    token = (tokens, width)
    block = (LINE - 1,) + token
    outs = [
        struct(token, f32),
        struct((rows, inner), f32),
        struct((rows, 2 * HD), f32),
        struct((rows, inner), f32),
        struct((rows, columns), f32),
        struct((rows, columns), f32),
        struct(token, bf16),
        struct((2, own_gains), f32),
    ]
    count = 6 + 6 * PIECES + 5 * (shards - 1 + 6) + CTX - 1 + plane - 1 + LINE - 1
    return pl.pallas_call(
        functools.partial(backward_kernel, shards, rows),
        out_shape=outs,
        in_specs=[any_spec()] * 17 + [vmem_spec()] * 5,
        out_specs=[any_spec()] * 7 + [vmem_spec()],
        scratch_shapes=[
            pltpu.VMEM((queries, width), bf16),
            pltpu.VMEM((width, inner), bf16),
            pltpu.VMEM((width, inner), bf16),
            pltpu.VMEM((width, 2 * HD), bf16),
            pltpu.VMEM((queries, width), bf16),
            pltpu.VMEM(qaug.shape, bf16),
            pltpu.VMEM(kaug.shape, bf16),
            pltpu.VMEM(kv.shape, bf16),
            pltpu.VMEM((inner, queries), bf16),
            pltpu.VMEM((queries, width), bf16),
            pltpu.VMEM(token, f32),
            pltpu.VMEM((inner, queries), bf16),
            pltpu.VMEM((queries, inner), bf16),
            pltpu.VMEM((length, HD), bf16),
            pltpu.VMEM((length, HD), f32),
            pltpu.VMEM((length, HD), f32),
            pltpu.VMEM((inner, queries), f32),
            pltpu.VMEM((queries, inner), bf16),
            pltpu.VMEM((CTX, queries, 2 * HD), bf16),
            pltpu.VMEM((CTX - 1, queries, 2 * HD), bf16),
            pltpu.VMEM((queries, 2 * HD), bf16),
            pltpu.VMEM((queries, width), bf16),
            pltpu.VMEM(block, bf16),
            pltpu.VMEM(block, bf16),
            pltpu.VMEM((ROWS, width), f32),
            pltpu.VMEM((2, width), f32),
            pltpu.VMEM((plane - 1, 2, width), f32),
            pltpu.VMEM((LINE - 1, 2, width), f32),
            pltpu.VMEM((2, width), f32),
            pltpu.VMEM((piece, inner), bf16),
            pltpu.VMEM((piece, inner), bf16),
            pltpu.VMEM((piece, 2 * HD), bf16),
            pltpu.VMEM((queries, width), bf16),
            pltpu.VMEM(block, bf16),
            pltpu.VMEM(block, bf16),
            pltpu.VMEM(token, f32),
            pltpu.VMEM(token, bf16),
            pltpu.VMEM((2, width), f32),
            pltpu.VMEM((queries, width), f32),
            *PlaneScatter.scratch(shards, rows, inner),
            *PlaneScatter.scratch(shards, rows, inner),
            *PlaneScatter.scratch(shards, rows, 2 * HD),
            *PlaneScatter.scratch(1 + 1, rows, columns),
            *PlaneScatter.scratch(1 + 1, rows, columns),
            pltpu.SemaphoreType.DMA((count,)),
            pltpu.SemaphoreType.DMA((count,)),
            pltpu.SemaphoreType.DMA((32,)),
        ],
        compiler_params=pltpu.CompilerParams(
            collective_id=2, has_side_effects=True, vmem_limit_bytes=60 * 2**20
        ),
        name="backward",
    )(
        dmid_all, wo, wq, wkv, n1, qaug, kaug, kv, att, x, dmid, branch, gu_part,
        gd_part, gd_x, gd_y, mid, lse, gains, gain_mlp, cos, sin,
    )


def finish_kernel(gains, layer_in, *refs):
    count = (len(refs) - 2) // 2
    layer_out = refs[count]
    layer_out[0] = layer_in[...]
    refs[count + 1][0] = refs[0][...]
    for src, dst in zip(refs[1:count], refs[count + 2 : -2]):
        dst[...] = src[...]
    for row, dst in enumerate(refs[-2:]):
        dst[...] = gains[row : row + 1, :]


def finish_call(arrays, gains, steps=4):
    rows = [array.shape[0] // steps for array in arrays]
    wide = [array.shape[1] for array in arrays]
    own = gains.shape[1]
    shapes = [struct((1,) * (i < 2) + array.shape, array.dtype) for i, array in enumerate(arrays)]
    return pl.pallas_call(
        finish_kernel,
        grid=(steps,),
        out_shape=shapes + [struct((1, own), f32)] * 2,
        in_specs=[pl.BlockSpec((2, own), lambda i: (0, 0))]
        + [pl.BlockSpec((r, n), lambda i: (i, 0)) for r, n in zip(rows, wide)],
        out_specs=[
            pl.BlockSpec((1, r, n), lambda i: (0, i, 0))
            if index < 2
            else pl.BlockSpec((r, n), lambda i: (i, 0))
            for index, (r, n) in enumerate(zip(rows, wide))
        ]
        + [pl.BlockSpec((1, own), lambda i: (0, 0))] * 2,
        compiler_params=pltpu.CompilerParams(vmem_limit_bytes=60 * 2**20),
        name="finish",
    )(gains, *arrays)


def body(
    inputs, out_grad, block_order, gain_attn, w_query, w_keyval, w_output, gain_mlp, w_gate, w_up, w_down
):
    shards = lax.axis_size("shard")
    x, og = inputs[0], out_grad[0]
    tokens, width = x.shape
    s, c = lax.axis_index("shard"), lax.axis_index("ctx")
    frequency = np.float32(10000.0) ** (-np.arange(HD // 2, dtype=np.float32)[:, None] * 2.0 / HD)
    own = gain_attn.shape[0]
    start = (s * CTX + c) * own
    row = lax.broadcasted_iota(jnp.int32, (2, own), 0)
    gain_in = jnp.where(row == 0, gain_attn.astype(f32), gain_mlp.astype(f32))
    aligned = own % 128 == 0
    if not aligned:
        gain_in = lax.dynamic_update_slice(jnp.zeros((2, width), f32), gain_in, (0, start))
    (wq, wkv, wo, wg, wu, wd, n1, og_all, n2, mid, qaug, kaug, kv, att, x_all, lse, gains, cos, sin) = forward_call(
        shards, x, og, (w_query, w_keyval, w_output, w_gate, w_up, w_down), gain_in,
        jnp.asarray(frequency, f32), block_order[0],
    )
    (dmid, dmid_all, grad_gate, gd_part, gd_x, gd_y, branch, gu_part, gm) = middle_call(
        shards, w_gate.shape[0], n2, og_all, wg, wu, wd, mid, gains
    )
    (input_grad, grad_query, grad_keyval, grad_output, grad_up, grad_down, layer_out, both) = backward_call(
        shards, w_query.shape[0], dmid_all, wo, wq, wkv, n1, qaug, kaug, kv, att, x_all, dmid,
        branch, gu_part, gd_part, gd_x, gd_y, mid, lse, gains, gm, cos, sin,
    )
    if not aligned:
        both = lax.dynamic_slice(both, (0, start), (2, own))
    (
        layer_out, input_grad, grad_query, grad_keyval, grad_output, grad_gate, grad_up, grad_down,
        *gain_grads,
    ) = finish_call([
        layer_out, input_grad, grad_query, grad_keyval, grad_output, grad_gate, grad_up, grad_down,
    ], both)
    return (
        layer_out, input_grad, gain_grads[0][0], grad_query, grad_keyval, grad_output,
        gain_grads[1][0], grad_gate, grad_up, grad_down,
    )


def solution(mesh):
    plane = P(("shard", "ctx"), "tensor")
    gain = P(("shard", "ctx"))
    token = P("shard", ("ctx", "tensor"), None)
    return jax.shard_map(
        body,
        mesh=mesh,
        in_specs=(token, token, P("shard", None), gain, plane, plane, plane, gain, plane, plane, plane),
        out_specs=(token, token, gain, plane, plane, plane, gain, plane, plane, plane),
        check_vma=False,
    )
```

```python
import functools

import jax
import jax.numpy as jnp
import numpy as np
from jax import lax
from jax.experimental import pallas as pl
from jax.experimental.pallas import tpu as pltpu
from jax.sharding import PartitionSpec as P

HD = 64
BLOCK = 256
BLOCKS = 8
ROWS = 16
CTX = 4
LINE = 4
PIECES = 2

epsilon = 1e-05
blocked = -1e30

f32 = jnp.float32
bf16 = jnp.bfloat16
MESH = pl.DeviceIdType.MESH


def place(owner):
    return (owner + (owner + 1) // 2) % LINE if isinstance(owner, int) else lax.rem(
        owner + (owner + 1) // 2, LINE
    )


def nn_dot(left, right):
    return jnp.dot(left, right, preferred_element_type=f32)


def nt_dot(left, right):
    return lax.dot_general(left, right, (((1,), (1,)), ((), ())), preferred_element_type=f32)


def tn_dot(left, right):
    return lax.dot_general(left, right, (((0,), (0,)), ((), ())), preferred_element_type=f32)


class Links:
    def __init__(self, shards, send_sems, recv_sems, local_sems):
        self.shards = shards
        self.send_sems, self.recv_sems, self.local_sems = send_sems, recv_sems, local_sems
        self.s = lax.axis_index("shard")
        self.c = lax.axis_index("ctx")
        self.t = lax.axis_index("tensor")
        self.c_x = self.c + 1 - 2 * lax.rem(self.c, 2)
        self.c_y = lax.rem(self.c + 2, CTX)
        self.c_d = CTX - 1 - self.c
        self.x_dev = (self.s, self.c_x, self.t)
        self.y_dev = (self.s, self.c_y, self.t)
        self.right = (self.s, self.c, self.t + 1)
        self.left = (self.s, self.c, self.t - 1)
        self.used = 0
        self.local_used = 0
        self.sends = []
        self.locals = []

    def slots(self, count):
        first = self.used
        self.used += count
        assert self.used <= self.send_sems.shape[0]
        return first

    def plane_peer(self, step):
        index = lax.rem(self.s * CTX + self.c + step, self.shards * CTX)
        return (index // CTX, lax.rem(index, CTX), self.t)

    def core_peer(self, step):
        return (lax.rem(self.s + step, self.shards), self.c, self.t)

    def line_peer(self, step):
        return (self.s, self.c, lax.rem(self.t + step, LINE))

    def barrier(self, whole_line=False):
        sem = pltpu.get_barrier_semaphore()
        count = self.shards * CTX - 1
        for step in range(1, count + 1):
            pl.semaphore_signal(
                sem, inc=1, device_id=self.plane_peer(step), device_id_type=MESH
            )

        if whole_line:
            for step in range(1, LINE):
                pl.semaphore_signal(
                    sem, inc=1, device_id=self.line_peer(step), device_id_type=MESH
                )
            pl.semaphore_wait(sem, count + LINE - 1)
            return

        @pl.when(self.t > 0)
        def _():
            pl.semaphore_signal(sem, inc=1, device_id=self.left, device_id_type=MESH)

        @pl.when(self.t < LINE - 1)
        def _():
            pl.semaphore_signal(sem, inc=1, device_id=self.right, device_id_type=MESH)

        beside = (self.t + LINE - 1) // LINE + (2 * LINE - 2 - self.t) // LINE
        pl.semaphore_wait(sem, count + beside)

    def copy(self, src, dst, device, slot):
        return pltpu.make_async_remote_copy(
            src_ref=src,
            dst_ref=dst,
            send_sem=self.send_sems.at[slot],
            recv_sem=self.recv_sems.at[slot],
            device_id=device,
            device_id_type=MESH,
        )

    def send(self, src, dst, device, slot, cond=None):
        if cond is None:
            self.copy(src, dst, device, slot).start()
        else:

            @pl.when(cond)
            def _():
                self.copy(src, dst, device, slot).start()

        handle = (src, dst, device, slot, cond)
        self.sends.append(handle)
        return handle

    def sent(self, handle):
        self.sends = [other for other in self.sends if other is not handle]
        self.copy(*handle[:4]).wait_send()

    def recv(self, dst, slot):
        self.copy(dst, dst, self.x_dev, slot).wait_recv()

    def keep(self, src, dst):
        copy = pltpu.make_async_copy(src, dst, self.local_sems.at[self.local_used])
        self.local_used += 1
        assert self.local_used <= self.local_sems.shape[0]
        copy.start()
        return copy

    def keep_later(self, src, dst):
        self.locals.append(self.keep(src, dst))

    def finish(self):
        for src, dst, device, slot, cond in self.sends:
            if cond is None:
                self.copy(src, dst, device, slot).wait_send()
            else:

                @pl.when(cond)
                def _():
                    self.copy(src, dst, device, slot).wait_send()

        for copy in self.locals:
            copy.wait()


class PlaneGather:
    def __init__(self, links, src, full, stage=None):
        self.links, self.src, self.full, self.stage = links, src, full, stage
        self.rows = src.shape[0]
        self.first = links.slots(4 + 4 * (links.shards - 1))

    def block(self, s, c):
        start = pl.multiple_of((s * CTX + c) * self.rows, self.rows)
        return self.full.at[pl.ds(start, self.rows)]

    def half(self, s, c, which):
        size = self.rows // 2
        start = pl.multiple_of((s * CTX + c) * self.rows + which * size, size)
        return self.full.at[pl.ds(start, size)]

    def core_slot(self, step, part):
        return self.first + 4 + (step - 1) * 4 + part

    def core_send(self, src, c, part):
        links = self.links
        for step in range(1, links.shards):
            links.send(
                src,
                self.block(links.s, c),
                links.core_peer(step),
                self.core_slot(step, part),
            )

    def start(self):
        links = self.links
        own = self.block(links.s, links.c)
        links.send(self.src, own, links.x_dev, self.first)
        links.send(self.src, own, links.y_dev, self.first + 1)
        self.core_send(self.src, links.c, 0)
        self.local = links.keep(self.src, own if self.stage is None else self.stage)

    def settle(self):
        self.local.wait()
        self.local = self.links.keep(self.stage, self.block(self.links.s, self.links.c))

    def forward(self):
        links = self.links
        links.recv(self.block(links.s, links.c_x), self.first)
        links.recv(self.block(links.s, links.c_y), self.first + 1)
        from_x = self.half(links.s, links.c_x, 0)
        from_y = self.half(links.s, links.c_y, 1)
        links.send(from_x, from_x, links.y_dev, self.first + 2)
        links.send(from_y, from_y, links.x_dev, self.first + 3)
        self.core_send(self.block(links.s, links.c_x), links.c_x, 1)
        self.core_send(self.block(links.s, links.c_y), links.c_y, 2)

    def diagonal(self):
        links = self.links
        links.recv(self.half(links.s, links.c_d, 0), self.first + 2)
        links.recv(self.half(links.s, links.c_d, 1), self.first + 3)
        self.core_send(self.block(links.s, links.c_d), links.c_d, 3)

    def done(self):
        links = self.links
        for step in range(1, links.shards):
            other = lax.rem(links.s + links.shards - step, links.shards)
            for part, c in enumerate((links.c, links.c_x, links.c_y, links.c_d)):
                links.recv(self.block(other, c), self.core_slot(step, part))
        self.local.wait()


class LineGather:
    def __init__(self, links, own, full, tokens, pieces=1):
        self.links, self.own, self.full, self.tokens = links, own, full, tokens
        self.pieces, self.size = pieces, tokens // pieces
        self.first = links.slots(2 * (LINE - 1) * pieces)

    def block(self, owner, p):
        start = pl.multiple_of(place(owner) * self.tokens + p * self.size, self.size)
        return self.full.at[pl.ds(start, self.size)]

    def slot(self, side, k, p):
        return self.first + (side * (LINE - 1) + k - 1) * self.pieces + p

    def send(self, k, p=0):
        links = self.links
        t, u = links.t, LINE - 1 - links.t
        own = self.own.at[pl.ds(p * self.size, self.size)]
        right, left = self.block(t - k + 1, p), self.block(t + k - 1, p)
        links.send(
            own if k == 1 else right,
            right,
            links.right,
            self.slot(0, k, p),
            jnp.logical_and(t >= k - 1, t < LINE - 1),
        )
        links.send(
            own if k == 1 else left,
            left,
            links.left,
            self.slot(1, k, p),
            jnp.logical_and(u >= k - 1, u < LINE - 1),
        )

    def recv(self, k, p=0):
        links = self.links
        t, u = links.t, LINE - 1 - links.t

        @pl.when(t >= k)
        def _():
            links.recv(self.block(t - k, p), self.slot(0, k, p))

        @pl.when(u >= k)
        def _():
            links.recv(self.block(t + k, p), self.slot(1, k, p))


class LineScatter:
    def __init__(self, links, part, tokens, from_left, from_right, pieces=1):
        self.links, self.part, self.tokens = links, part, tokens
        self.from_left, self.from_right = from_left, from_right
        self.pieces, self.size = pieces, tokens // pieces
        self.first = links.slots(2 * (LINE - 1) * pieces)

    def slot(self, side, k, p):
        return self.first + (side * (LINE - 1) + k) * self.pieces + p

    def piece(self, ref, k, p):
        return ref.at[k, pl.ds(p * self.size, self.size)]

    def total(self, owner, k, p, arrived):
        @pl.loop(0, self.size // ROWS)
        def _(i):
            r = pl.multiple_of(p * self.size + i * ROWS, ROWS)
            q = pl.multiple_of(place(owner) * self.tokens + p * self.size + i * ROWS, ROWS)
            mine = self.part[pl.ds(q, ROWS), :].astype(f32)
            summed = mine + arrived[k, pl.ds(r, ROWS), :].astype(f32)
            arrived[k, pl.ds(r, ROWS), :] = summed.astype(arrived.dtype)

    def ends(self, k, p=0):
        links = self.links
        for side, behind, arrived, device in self.sides():
            owner = LINE - 1 - k if side == 0 else k
            piece, slot = self.piece(arrived, k, p), self.slot(side, k, p)

            @pl.when(behind == 0)
            def _():
                self.first_part(owner, k, p, arrived)

            links.send(piece, piece, device, slot, behind == 0)

    def sides(self):
        links = self.links
        return (
            (0, links.t, self.from_left, links.right),
            (1, LINE - 1 - links.t, self.from_right, links.left),
        )

    def stage(self, now, p=0):
        links = self.links
        for side, behind, arrived, device in self.sides():
            k = now - behind
            owner = LINE - 1 - k if side == 0 else k
            piece, slot = self.piece(arrived, k, p), self.slot(side, k, p)
            ready = jnp.logical_and(k >= 0, behind > 0)

            @pl.when(ready)
            def _():
                links.recv(piece, slot)
                self.total(owner, k, p, arrived)

            links.send(piece, piece, device, slot, ready)

    def first_part(self, owner, k, p, out):
        @pl.loop(0, self.size // ROWS)
        def _(i):
            r = pl.multiple_of(p * self.size + i * ROWS, ROWS)
            q = pl.multiple_of(place(owner) * self.tokens + p * self.size + i * ROWS, ROWS)
            out[k, pl.ds(r, ROWS), :] = self.part[pl.ds(q, ROWS), :].astype(out.dtype)

    def arrive(self, p=0):
        links = self.links
        t = links.t

        @pl.when(t > 0)
        def _():
            links.recv(
                self.piece(self.from_left, LINE - 1 - t, p), self.slot(0, LINE - 1 - t, p)
            )

        @pl.when(t < LINE - 1)
        def _():
            links.recv(self.piece(self.from_right, t, p), self.slot(1, t, p))

    def rows(self, r):
        t = self.links.t
        q = pl.multiple_of(place(t) * self.tokens + r, ROWS)
        k_l = jnp.minimum(LINE - 1 - t, LINE - 2)
        k_r = jnp.minimum(t, LINE - 2)
        zero = jnp.zeros((ROWS, self.part.shape[1]), f32)
        return (
            self.part[pl.ds(q, ROWS), :].astype(f32)
            + jnp.where(t > 0, self.from_left[k_l, pl.ds(r, ROWS), :].astype(f32), zero)
            + jnp.where(t < LINE - 1, self.from_right[k_r, pl.ds(r, ROWS), :].astype(f32), zero)
        )

    def owned(self, p, use):
        @pl.loop(0, self.size // ROWS)
        def _(i):
            r = pl.multiple_of(p * self.size + i * ROWS, ROWS)
            use(r, self.rows(r))


def line_ends(scatter, *hops):
    for k in hops:
        for p in range(scatter.pieces):
            scatter.ends(k, p)


def line_steps(scatter, now):
    for p in range(scatter.pieces):
        scatter.stage(now, p)


def line_finish(scatter, use, gather=None):
    for p in range(scatter.pieces):
        scatter.arrive(p)
        scatter.owned(p, use)
        if gather is not None:
            gather.send(1, p)


def line_spread(gather, k):
    for p in range(gather.pieces):
        gather.recv(k, p)
        if k < LINE - 1:
            gather.send(k + 1, p)


class PlaneScatter:
    def __init__(self, links, left, right, rows, core_in, x_in, y_in, x_last, y_last, out):
        self.links, self.left, self.right, self.rows = links, left, right, rows
        self.core_in, self.x_in, self.y_in = core_in, x_in, y_in
        self.x_last, self.y_last, self.out = x_last, y_last, out
        self.first = links.slots(links.shards - 1 + 6)
        self.tile = min(256, CTX * rows)

    def product(self, shard, i):
        start = pl.multiple_of(shard * (CTX * self.rows) + i * self.tile, self.tile)
        return tn_dot(self.left[:, pl.ds(start, self.tile)], self.right[...])

    @property
    def tiles(self):
        return CTX * self.rows // self.tile

    def other(self, step, stage, part=None):
        links = self.links
        target = lax.rem(links.s + step, links.shards)
        low, high = (0, self.tiles) if part is None else part

        @pl.loop(low, high)
        def _(i):
            r = pl.multiple_of(i * self.tile, self.tile)
            stage[pl.ds(r, self.tile), :] = self.product(target, i).astype(bf16)

        if high == self.tiles:
            return links.send(
                stage, self.core_in.at[step - 1], links.core_peer(step), self.first + step - 1
            )

    def own(self, part=None):
        links = self.links
        low, high = (0, self.tiles) if part is None else part
        if low == 0:
            for step in range(1, links.shards):
                links.recv(self.core_in.at[step - 1], self.first + step - 1)

        @pl.loop(low, high)
        def _(i):
            r = pl.multiple_of(i * self.tile, self.tile)
            summed = self.product(links.s, i)
            for step in range(1, links.shards):
                summed = summed + self.core_in[step - 1, pl.ds(r, self.tile), :].astype(f32)
            self.core_in[0, pl.ds(r, self.tile), :] = summed.astype(bf16)

    def half(self, c, which):
        size = self.rows // 2
        start = pl.multiple_of(c * self.rows + which * size, size)
        return self.core_in.at[0, pl.ds(start, size)]

    def exchange(self):
        links, first = self.links, self.first + self.links.shards - 1
        links.send(self.half(links.c_d, 0), self.x_in.at[1], links.x_dev, first)
        links.send(self.half(links.c_d, 1), self.y_in.at[1], links.y_dev, first + 1)
        links.send(self.half(links.c_x, 0), self.x_in.at[0], links.x_dev, first + 2)
        links.send(self.half(links.c_y, 1), self.y_in.at[0], links.y_dev, first + 3)

    def add(self, c, which, arrived):
        size = self.rows // 2

        @pl.loop(0, size // ROWS)
        def _(i):
            r = pl.multiple_of(i * ROWS, ROWS)
            q = pl.multiple_of(c * self.rows + which * size + i * ROWS, ROWS)
            mine = self.core_in[0, pl.ds(q, ROWS), :].astype(f32)
            summed = mine + arrived[1, pl.ds(r, ROWS), :].astype(f32)
            self.core_in[0, pl.ds(q, ROWS), :] = summed.astype(bf16)

    def arrived(self):
        links, first = self.links, self.first + self.links.shards - 1
        for ref, offset in ((self.x_in, 0), (self.y_in, 1)):
            for part in range(2):
                links.recv(ref.at[1 - part], first + offset + 2 * part)

    def fold(self, here=False):
        links, first = self.links, self.first + self.links.shards - 1
        if not here:
            links.recv(self.x_in.at[1], first)
        self.add(links.c_y, 0, self.x_in)
        links.send(self.half(links.c_y, 0), self.y_last, links.y_dev, first + 4)
        if not here:
            links.recv(self.y_in.at[1], first + 1)
        self.add(links.c_x, 1, self.y_in)
        links.send(self.half(links.c_x, 1), self.x_last, links.x_dev, first + 5)

    def total(self, here=False):
        links, first = self.links, self.first + self.links.shards - 1
        size = self.rows // 2
        if not here:
            links.recv(self.x_in.at[0], first + 2)
            links.recv(self.y_in.at[0], first + 3)
        links.recv(self.y_last, first + 4)
        links.recv(self.x_last, first + 5)
        for which, arrived, last in ((0, self.x_in, self.y_last), (1, self.y_in, self.x_last)):

            @pl.loop(0, size // ROWS)
            def _(i):
                r = pl.multiple_of(i * ROWS, ROWS)
                q = pl.multiple_of(links.c * self.rows + which * size + i * ROWS, ROWS)
                self.out[pl.ds(which * size + r, ROWS), :] = (
                    self.core_in[0, pl.ds(q, ROWS), :].astype(f32)
                    + arrived[0, pl.ds(r, ROWS), :].astype(f32)
                    + last[pl.ds(r, ROWS), :].astype(f32)
                )

    @staticmethod
    def scratch(shards, rows, columns):
        half = (rows // 2, columns)
        return [
            pltpu.VMEM((shards - 1, CTX * rows, columns), bf16),
            pltpu.VMEM((2,) + half, bf16),
            pltpu.VMEM((2,) + half, bf16),
            pltpu.VMEM(half, bf16),
            pltpu.VMEM(half, bf16),
            pltpu.VMEM((rows, columns), f32),
        ]


def any_spec():
    return pl.BlockSpec(memory_space=pl.ANY)


def vmem_spec():
    return pl.BlockSpec(memory_space=pltpu.VMEM)


def struct(shape, dtype):
    return jax.ShapeDtypeStruct(shape, dtype)


def forward_kernel(
    shards,
    x, og, wq, wkv, wo, wg, wu, wd, gain_in, frequency, order,
    wq_o, wkv_o, wo_o, wg_o, wu_o, wd_o, n1_o, og_o, n2_o, mid_o, qaug_o, kaug_o, kv_o, att_o, x_o,
    lse, gains, cos, sin,
    x_all, n1_all, wq_all, wkv_all, wo_all, gains_all, qaug, kv_all, kaug, v_all, scores, weights,
    attn, part, from_left, from_right, mid, n2, og_stage, wg_stage, wu_stage, wd_stage, gpad,
    send_sems, recv_sems, local_sems,
):
    tokens, width = x.shape
    queries = tokens * LINE
    heads = qaug.shape[0]
    links = Links(shards, send_sems, recv_sems, local_sems)
    s, c, t = links.s, links.c, links.t

    gather_x = LineGather(links, x, x_all, tokens, PIECES)
    gather_og = LineGather(links, og, og_o, tokens)
    gather_n2 = LineGather(links, n2, n2_o, tokens, PIECES)
    small = [PlaneGather(links, *pair) for pair in ((wq, wq_all), (wkv, wkv_all), (wo, wo_all))]
    large = [
        PlaneGather(links, *three)
        for three in ((wg, wg_o, wg_stage), (wu, wu_o, wu_stage), (wd, wd_o, wd_stage))
    ]
    scatter = LineScatter(links, part, tokens, from_left, from_right, PIECES)
    plane = shards * CTX
    gain_slot = links.slots(plane - 1)
    kv_slot = links.slots((CTX - 1) * (2 * LINE - 1))

    me = s * CTX + c
    own_gains = gain_in.shape[1]
    if own_gains == width:
        gpad[...] = gain_in[...].astype(f32)
    else:
        gpad[...] = jnp.zeros_like(gpad)
        gpad[:, pl.ds(pl.multiple_of(me * own_gains, own_gains), own_gains)] = gain_in[
            ...
        ].astype(f32)
    links.barrier()
    for step in range(1, plane):
        links.send(gpad, gains_all.at[me], links.plane_peer(step), gain_slot + step - 1)
    own_gain = links.keep(gpad, gains_all.at[me])
    for p in range(PIECES):
        gather_x.send(1, p)
    own_rows = pl.ds(pl.multiple_of(place(t) * tokens, tokens), tokens)
    own_x = links.keep(x, x_all.at[own_rows])
    for gather in small:
        gather.start()

    per = queries // BLOCK
    lane = lax.broadcasted_iota(jnp.int32, (1, queries), 1)
    owner = jnp.zeros((1, queries), jnp.int32)
    for index in range(LINE):
        owner = jnp.where(lane // tokens == place(index), index, owner)
    slot = owner * tokens + lax.rem(lane, tokens)
    block_here = jnp.zeros((1, queries), jnp.int32)
    for index in range(per):
        block_here = jnp.where(slot // BLOCK == index, order[c * per + index], block_here)
    position = (block_here * BLOCK + lax.rem(slot, BLOCK)).astype(f32)
    angles = frequency[...] * position
    cos[...] = jnp.cos(angles)
    sin[...] = jnp.sin(angles)
    row = lax.broadcasted_iota(jnp.int32, (HD, queries), 0)
    bias = jnp.zeros((HD, queries), f32)
    for index in range(BLOCKS):
        barred = jnp.logical_and(row == index, order[index] > block_here)
        bias = jnp.where(barred, blocked, bias)
    bias = bias.astype(bf16)
    for h in range(heads):
        qaug[h, HD:, :] = bias

    own_gain.wait()
    for step in range(1, plane):
        other = lax.rem(me + plane - step, plane)
        links.recv(gains_all.at[other], gain_slot + step - 1)
    total = gains_all[0]
    for index in range(1, plane):
        total = total + gains_all[index]
    gains[...] = total
    own_x.wait()

    def norm_block(owner):
        @pl.loop(0, tokens // ROWS)
        def _(i):
            r = pl.multiple_of(place(owner) * tokens + i * ROWS, ROWS)
            v = x_all[pl.ds(r, ROWS), :].astype(f32)
            inverse = lax.rsqrt(jnp.mean(v * v, -1, keepdims=True) + epsilon)
            n1_all[pl.ds(r, ROWS), :] = (v * inverse * gains[0:1, :]).astype(bf16)

    own_og = links.keep(og, og_stage)
    norm_block(t)
    line_spread(gather_x, 1)
    for gather in small:
        gather.forward()
    norm_pair(gather_x, norm_block, 1)
    line_spread(gather_x, 2)
    gather_og.send(1)
    for gather in small:
        gather.diagonal()
    norm_pair(gather_x, norm_block, 2)
    own_og.wait()
    links.keep_later(og_stage, og_o.at[own_rows])
    for gather in small:
        gather.done()

    half = HD // 2
    scale = HD ** (-0.5)

    def lanes_of(owner):
        return pl.ds(pl.multiple_of(place(owner) * tokens, tokens), tokens)

    def turn(v1, v2, cosine, sine):
        return (v1 * cosine - v2 * sine).astype(bf16), (v2 * cosine + v1 * sine).astype(bf16)

    def project_block(owner):
        at = lanes_of(owner)
        cosine, sine = cos[:, at], sin[:, at]
        kv_t = nn_dot(n1_all[at, :], wkv_all[...]).T
        k1, k2 = turn(kv_t[0:half], kv_t[half:HD], cosine, sine)
        kv_all[c, 0:half, at] = k1
        kv_all[c, half:HD, at] = k2
        kv_all[c, HD : 2 * HD, at] = kv_t[HD:].astype(bf16)
        q_t = nn_dot(n1_all[at, :], wq_all[...]).T
        for h in range(heads):
            b = h * HD
            q1, q2 = turn(q_t[b : b + half], q_t[b + half : b + HD], cosine, sine)
            qaug[h, 0:half, at] = (q1 * scale).astype(bf16)
            qaug[h, half:HD, at] = (q2 * scale).astype(bf16)

    u = LINE - 1 - t
    arrivals = [(t, None)]
    for k in range(1, LINE):
        arrivals += [(t - k, t >= k), (t + k, u >= k)]

    def send_block(index):
        owner, cond = arrivals[index]
        for step in range(1, CTX):
            peer = lax.rem(c + step, CTX)
            ref = kv_all.at[c, :, lanes_of(owner)]
            links.send(ref, ref, (s, peer, t), kv_slot + index * (CTX - 1) + step - 1, cond)

    def recv_block(index):
        owner, cond = arrivals[index]

        def wait():
            for step in range(1, CTX):
                other = lax.rem(c + CTX - step, CTX)
                slot = kv_slot + index * (CTX - 1) + step - 1
                links.recv(kv_all.at[other, :, lanes_of(owner)], slot)

        if cond is None:
            wait()
        else:
            pl.when(cond)(wait)

    project_block(t)
    send_block(0)
    for k in range(1, LINE):
        if k == LINE - 1:
            line_spread(gather_x, k)
            norm_pair(gather_x, norm_block, k)
        norm_pair(gather_x, project_block, k)
        send_block(2 * k - 1)
        send_block(2 * k)
    for gather in large:
        gather.start()
    links.keep_later(n1_all, n1_o)
    links.keep_later(x_all, x_o)
    links.keep_later(wq_all, wq_o)
    links.keep_later(wkv_all, wkv_o)
    links.keep_later(wo_all, wo_o)
    links.keep_later(qaug, qaug_o)
    for index in range(len(arrivals)):
        recv_block(index)
    for other in range(CTX):
        row = lax.broadcasted_iota(jnp.int32, (HD, queries), 0)
        lane = lax.broadcasted_iota(jnp.int32, (HD, queries), 1)
        mark = (row == other * (queries // BLOCK) + lax.rem(lane // tokens, 2)).astype(f32).astype(bf16)
        both = jnp.concatenate([kv_all[other, 0:HD, :], mark], 0)
        kaug[other * queries : (other + 1) * queries, :] = both.T
        v_all[:, other * queries : (other + 1) * queries] = kv_all[other, HD : 2 * HD, :]
    links.keep_later(kaug, kaug_o)
    links.keep_later(kv_all, kv_o)

    length = queries * CTX

    far = pl.multiple_of(jnp.where(t < LINE // 2, tokens, 0), tokens)
    near = pl.multiple_of(jnp.where(t < LINE // 2, 0, tokens), tokens)

    def head(start, size, h):
        lanes = pl.ds(start, size)
        query = qaug[h, :, lanes]
        top = jnp.full((1, size), -jnp.inf, f32)
        for b in range(0, length, BLOCK):
            block_scores = nn_dot(kaug[b : b + BLOCK, :], query)
            scores[b : b + BLOCK, 0:size] = block_scores
            top = jnp.maximum(top, jnp.max(block_scores, 0, keepdims=True))
        norm = jnp.zeros((1, size), f32)
        for b in range(0, length, BLOCK):
            exponent = jnp.exp(scores[b : b + BLOCK, 0:size] - top)
            norm = norm + jnp.sum(exponent, 0, keepdims=True)
            weights[b : b + BLOCK, 0:size] = exponent.astype(bf16)
        out = nn_dot(v_all[...], weights[:, 0:size]) / norm
        attn[pl.ds(pl.multiple_of(h * HD, HD), HD), lanes] = out.astype(bf16)
        lse[h, :, lanes] = top + jnp.log(norm)

    def attend(start, size):
        pl.loop(0, heads)(functools.partial(head, start, size))
        rows = pl.ds(start, size)
        attn_rows = attn[:, rows].T
        for b in range(0, width, 512):
            part[rows, b : b + 512] = nt_dot(attn_rows, wo_all[b : b + 512, :])

    attend(far, tokens)
    line_ends(scatter, 0)
    gather_og.recv(1)
    gather_og.send(2)
    for gather in large:
        gather.settle()
    attend(2 * tokens, 2 * tokens)
    line_ends(scatter, 1, 2)
    gather_og.recv(2)
    gather_og.send(3)
    line_steps(scatter, 1)
    attend(near, tokens)
    links.keep_later(attn, att_o)

    def finish_rows(r, summed):
        q = pl.multiple_of(place(t) * tokens + r, ROWS)
        middle = x_all[pl.ds(q, ROWS), :].astype(f32) + summed
        mid[pl.ds(r, ROWS), :] = middle
        inverse = lax.rsqrt(jnp.mean(middle * middle, -1, keepdims=True) + epsilon)
        n2[pl.ds(r, ROWS), :] = (middle * inverse * gains[1:2, :]).astype(bf16)

    large[0].forward()
    line_steps(scatter, 2)
    large[1].forward()
    line_finish(scatter, finish_rows, gather_n2)
    large[2].forward()
    links.keep_later(n2, n2_o.at[own_rows])
    links.keep_later(mid, mid_o)
    line_spread(gather_n2, 1)
    large[0].diagonal()
    large[1].diagonal()
    line_spread(gather_n2, 2)
    large[2].diagonal()
    gather_og.recv(3)
    line_spread(gather_n2, 3)
    for gather in large:
        gather.done()
    links.finish()


def norm_pair(gather, norm_block, k):
    t, u = gather.links.t, LINE - 1 - gather.links.t

    @pl.when(t >= k)
    def _():
        norm_block(t - k)

    @pl.when(u >= k)
    def _():
        norm_block(t + k)


def forward_call(shards, x, og, weights_in, gain_in, frequency, order):
    wq, wkv, wo, wg, wu, wd = weights_in
    tokens, width = x.shape
    queries = tokens * LINE
    length = queries * CTX
    heads = wq.shape[1] // HD
    plane = shards * CTX
    full = [struct((width, w.shape[1]), bf16) for w in weights_in]
    outs = full + [
        struct((queries, width), bf16),
        struct((queries, width), bf16),
        struct((queries, width), bf16),
        struct((tokens, width), f32),
        struct((heads, 2 * HD, queries), bf16),
        struct((length, 2 * HD), bf16),
        struct((CTX, 2 * HD, queries), bf16),
        struct((heads * HD, queries), bf16),
        struct((queries, width), bf16),
        struct((heads, 1, queries), f32),
        struct((2, width), f32),
        struct((HD // 2, queries), f32),
        struct((HD // 2, queries), f32),
    ]
    block = (LINE - 1, tokens, width)
    count = 6 + 18 * PIECES + 6 * (4 + 4 * (shards - 1)) + plane - 1 + 21
    return pl.pallas_call(
        functools.partial(forward_kernel, shards),
        out_shape=outs,
        in_specs=[any_spec()] * 8
        + [vmem_spec()] * 2
        + [pl.BlockSpec(memory_space=pltpu.SMEM)],
        out_specs=[any_spec()] * 15 + [vmem_spec()] * 4,
        scratch_shapes=[
            pltpu.VMEM((queries, width), bf16),
            pltpu.VMEM((queries, width), bf16),
            pltpu.VMEM((width, wq.shape[1]), bf16),
            pltpu.VMEM((width, wkv.shape[1]), bf16),
            pltpu.VMEM((width, wo.shape[1]), bf16),
            pltpu.VMEM((plane, 2, width), f32),
            pltpu.VMEM((heads, 2 * HD, queries), bf16),
            pltpu.VMEM((CTX, 2 * HD, queries), bf16),
            pltpu.VMEM((length, 2 * HD), bf16),
            pltpu.VMEM((HD, length), bf16),
            pltpu.VMEM((length, queries // 2), f32),
            pltpu.VMEM((length, queries // 2), bf16),
            pltpu.VMEM((heads * HD, queries), bf16),
            pltpu.VMEM((queries, width), f32),
            pltpu.VMEM(block, bf16),
            pltpu.VMEM(block, bf16),
            pltpu.VMEM((tokens, width), f32),
            pltpu.VMEM((tokens, width), bf16),
            pltpu.VMEM((tokens, width), bf16),
            pltpu.VMEM(wg.shape, bf16),
            pltpu.VMEM(wu.shape, bf16),
            pltpu.VMEM(wd.shape, bf16),
            pltpu.VMEM((2, width), f32),
            pltpu.SemaphoreType.DMA((count,)),
            pltpu.SemaphoreType.DMA((count,)),
            pltpu.SemaphoreType.DMA((32,)),
        ],
        compiler_params=pltpu.CompilerParams(
            collective_id=0, has_side_effects=True, vmem_limit_bytes=60 * 2**20
        ),
        name="forward",
    )(x, og, wq, wkv, wo, wg, wu, wd, gain_in, frequency, order)


def middle_kernel(
    shards, rows,
    n2_in, og_in, wg_in, wu_in, wd_in, mid_in, gains,
    dmid_o, dmid_all_o, gg_o, gd_part_o, gd_x_o, gd_y_o, branch_o, gu_part_o, gain_sum,
    n2, og, wg, wu, wd, mid, hidden, dgate, dup, part, branch,
    left, right, dmid, dsend, gain_rows, up_in,
    *rest,
):
    grads, (send_sems, recv_sems, local_sems) = rest[:-3], rest[-3:]
    tokens, width = mid.shape
    queries = n2.shape[0]
    columns = wg.shape[1]
    links = Links(shards, send_sems, recv_sems, local_sems)
    t = links.t
    own_rows = pl.ds(pl.multiple_of(place(t) * tokens, tokens), tokens)

    far = pl.multiple_of(jnp.where(t < LINE // 2, tokens, 0), tokens)
    near = pl.multiple_of(jnp.where(t < LINE // 2, 0, tokens), tokens)
    sides = [pl.ds(far, tokens), pl.ds(2 * tokens, 2 * tokens), pl.ds(near, tokens)]
    full, rest_columns = columns // 256, columns % 256
    weights = ((wg_in, wg), (wu_in, wu), (wd_in, wd))

    def fetch(j, start, size, index):
        src, dst = weights[j]
        of = pl.ds(start, size)
        sem = local_sems.at[3 * index + j]
        return pltpu.make_async_copy(src.at[:, of], dst.at[:, of], sem)

    links.local_used = 3 * (full + 1)
    load_n2 = [links.keep(n2_in.at[sides[0]], n2.at[sides[0]])]
    for index in range(full):
        for j in range(3):
            fetch(j, index * 256, 256, index).start()
        if index == 0:
            load_og = [links.keep(og_in.at[sides[0]], og.at[sides[0]])]
    if rest_columns:
        for j in range(3):
            fetch(j, full * 256, rest_columns, full).start()
    load_n2 += [links.keep(n2_in.at[at], n2.at[at]) for at in sides[1:]]
    load_og += [links.keep(og_in.at[at], og.at[at]) for at in sides[1:]]
    load_mid = links.keep(mid_in, mid)
    scatter = LineScatter(links, part, tokens, left, right, PIECES)
    gather = LineGather(links, dsend, dmid_all_o, tokens, PIECES)
    down = PlaneScatter(links, og, hidden, rows, *grads[0:6])
    gate = PlaneScatter(links, n2, dgate, rows, *grads[6:12])
    up = PlaneScatter(links, n2, dup, rows, up_in, None, None, None, None, None)
    links.barrier()

    def feed_forward(half):
        at = sides[half]
        load_n2[half].wait()
        load_og[half].wait()

        def tile(start, size, index):
            of = pl.ds(start, size)
            if half == 0:
                fetch(0, start, size, index).wait()
                fetch(1, start, size, index).wait()
            gate_act = nn_dot(n2[at, :], wg[:, of])
            up_act = nn_dot(n2[at, :], wu[:, of])
            if half == 0:
                fetch(2, start, size, index).wait()
            d_hidden = nn_dot(og[at, :], wd[:, of])
            sig = jax.nn.sigmoid(gate_act)
            silu = gate_act * sig
            hidden[at, of] = (silu * up_act).astype(bf16)
            d_gate = d_hidden * up_act * sig * (1.0 + gate_act * (1.0 - sig))
            dgate[at, of] = d_gate.astype(bf16)
            dup[at, of] = (d_hidden * silu).astype(bf16)

        @pl.loop(0, full)
        def _(index):
            tile(pl.multiple_of(index * 256, 256), 256, index)

        if rest_columns:
            tile(full * 256, rest_columns, full)

        @pl.loop(0, width // 512)
        def _(j):
            of = pl.ds(pl.multiple_of(j * 512, 512), 512)
            summed = nt_dot(dgate[at, :], wg[of, :]) + nt_dot(dup[at, :], wu[of, :])
            part[at, of] = summed.astype(bf16)

    piece = CTX * rows

    def others(grad, room):
        for step in range(1, shards):
            grad.other(step, room.at[pl.ds((step - 1) * piece, piece)])

    feed_forward(0)
    line_ends(scatter, 0)
    feed_forward(1)
    line_ends(scatter, 1, 2)
    line_steps(scatter, 1)
    feed_forward(2)
    others(gate, wg)
    line_steps(scatter, 2)

    @pl.loop(0, width // 512)
    def _(j):
        of = pl.ds(pl.multiple_of(j * 512, 512), 512)
        branch[:, of] = nt_dot(hidden[...], wd[of, :]).astype(bf16)

    links.keep_later(branch, branch_o)
    gate.own()
    gate.exchange()
    others(down, wd)
    load_mid.wait()
    gain_rows[...] = jnp.zeros_like(gain_rows)

    def finish_rows(r, d_normed):
        at = pl.ds(r, ROWS)
        q = pl.ds(pl.multiple_of(place(t) * tokens + r, ROWS), ROWS)
        middle = mid[at, :]
        inverse = lax.rsqrt(jnp.mean(middle * middle, -1, keepdims=True) + epsilon)
        unit = middle * inverse
        gain_rows[...] += d_normed * unit
        d_unit = d_normed * gains[1:2, :]
        back = inverse * (d_unit - unit * jnp.mean(d_unit * unit, -1, keepdims=True))
        d_middle = og[q, :].astype(f32) + back
        dmid[at, :] = d_middle
        dsend[at, :] = d_middle.astype(bf16)

    line_finish(scatter, finish_rows, gather)
    gate.fold()
    down.own()
    down.exchange()
    links.keep_later(dsend, dmid_all_o.at[own_rows])
    links.keep_later(dmid, dmid_o)
    links.keep_later(down.core_in.at[0], gd_part_o)
    line_spread(gather, 1)
    others(up, wu)
    gain_sum[...] = jnp.sum(gain_rows[...], 0, keepdims=True)
    line_spread(gather, 2)
    up.own()
    links.keep_later(up_in.at[0], gu_part_o)
    gate.total()
    links.keep_later(gate.out, gg_o)
    line_spread(gather, 3)
    down.arrived()
    links.keep_later(down.x_in, gd_x_o)
    links.keep_later(down.y_in, gd_y_o)
    links.finish()


def middle_call(shards, rows, n2, og, wg, wu, wd, mid, gains):
    queries, width = n2.shape
    tokens = mid.shape[0]
    columns = wg.shape[1]
    token = (tokens, width)
    wide = (queries, columns)
    block = (LINE - 1,) + token
    outs = [
        struct(token, f32),
        struct((queries, width), bf16),
        struct((rows, columns), f32),
        struct((CTX * rows, columns), bf16),
        struct((2, rows // 2, columns), bf16),
        struct((2, rows // 2, columns), bf16),
        struct((queries, width), bf16),
        struct((CTX * rows, columns), bf16),
        struct((1, width), f32),
    ]
    count = 12 * PIECES + 3 * (shards - 1 + 6)
    return pl.pallas_call(
        functools.partial(middle_kernel, shards, rows),
        out_shape=outs,
        in_specs=[any_spec()] * 6 + [vmem_spec()],
        out_specs=[any_spec()] * 8 + [vmem_spec()],
        scratch_shapes=[
            pltpu.VMEM((queries, width), bf16),
            pltpu.VMEM((queries, width), bf16),
            pltpu.VMEM((width, columns), bf16),
            pltpu.VMEM((width, columns), bf16),
            pltpu.VMEM((width, columns), bf16),
            pltpu.VMEM(token, f32),
            pltpu.VMEM(wide, bf16),
            pltpu.VMEM(wide, bf16),
            pltpu.VMEM(wide, bf16),
            pltpu.VMEM((queries, width), bf16),
            pltpu.VMEM((queries, width), bf16),
            pltpu.VMEM(block, bf16),
            pltpu.VMEM(block, bf16),
            pltpu.VMEM(token, f32),
            pltpu.VMEM(token, bf16),
            pltpu.VMEM((ROWS, width), f32),
            pltpu.VMEM((shards - 1, CTX * rows, columns), bf16),
            *PlaneScatter.scratch(shards, rows, columns),
            *PlaneScatter.scratch(shards, rows, columns),
            pltpu.SemaphoreType.DMA((count,)),
            pltpu.SemaphoreType.DMA((count,)),
            pltpu.SemaphoreType.DMA((40,)),
        ],
        compiler_params=pltpu.CompilerParams(
            collective_id=1, has_side_effects=True, vmem_limit_bytes=63 * 2**20
        ),
        name="middle",
    )(n2, og, wg, wu, wd, mid, gains)


def backward_kernel(
    shards, rows,
    dmid_all_in, wo_in, wq_in, wkv_in, n1_in, qaug_in, kaug_in, kv_in, att_in, x_in, dmid_in,
    branch_in, gu_part_in, gd_part_in, gd_x_in, gd_y_in, mid_in, lse, gains, gain_mlp, cos, sin,
    in_o, gq_o, gkv_o, go_o, gu_o, gd_o, out_o, gain_o,
    dmid_all, wo, wq, wkv, n1, qaug, kaug, kv, att, x, dmid,
    d_out, attn_rows, v_rows, d_keys, d_values, d_query, d_query_rows, kv_send, kv_recv, d_kv, part,
    left, right, gain_rows, pair, plane_in, line_in, total, stage_o, stage_q, stage_kv,
    branch, left_b, right_b, mid, layer, gain_sum, part_query,
    *rest,
):
    grads, (send_sems, recv_sems, local_sems) = rest[:-3], rest[-3:]
    tokens, width = dmid.shape
    queries = n1.shape[0]
    heads = qaug.shape[0]
    length = kaug.shape[0]
    half = HD // 2
    plane = shards * CTX
    links = Links(shards, send_sems, recv_sems, local_sems)
    s, c, t = links.s, links.c, links.t

    scatter = LineScatter(links, part, tokens, left, right, PIECES)
    scatter_out = LineScatter(links, branch, tokens, left_b, right_b)
    g_o = PlaneScatter(links, dmid_all, attn_rows, rows, *grads[0:6])
    g_q = PlaneScatter(links, n1, d_query_rows, rows, *grads[6:12])
    g_kv = PlaneScatter(links, n1, d_kv, rows, *grads[12:18])
    g_u = PlaneScatter(links, None, None, rows, *grads[18:24])
    g_d = PlaneScatter(links, None, None, rows, *grads[24:30])
    kv_slot = links.slots(CTX - 1)
    plane_slot = links.slots(plane - 1)
    line_slot = links.slots(LINE - 1)
    piece = CTX * rows
    loads = [
        links.keep(src, dst)
        for src, dst in (
            (branch_in, branch), (dmid_all_in, dmid_all), (wo_in, wo), (gu_part_in, g_u.core_in.at[0]),
            (att_in, att), (kv_in, kv), (qaug_in, qaug), (kaug_in, kaug),
            (gd_part_in, g_d.core_in.at[0]), (gd_x_in, g_d.x_in), (gd_y_in, g_d.y_in), (n1_in, n1),
            (wq_in, wq), (wkv_in, wkv), (x_in, x), (dmid_in, dmid), (mid_in, mid),
        )
    ]

    def others(grad, stage):
        for step in range(1, shards):
            grad.other(step, stage.at[pl.ds((step - 1) * piece, piece)])

    links.barrier(whole_line=True)
    loads[0].wait()
    line_ends(scatter_out, 0)
    for load in loads[1:3]:
        load.wait()
    d_out[...] = nn_dot(dmid_all[...], wo[...]).astype(bf16).T
    loads[3].wait()
    g_u.exchange()
    for load in loads[4:8]:
        load.wait()
    for other in range(CTX):
        v_rows[other * queries : (other + 1) * queries, :] = kv[other, HD : 2 * HD, :].T
    d_keys[...] = jnp.zeros_like(d_keys)
    d_values[...] = jnp.zeros_like(d_values)

    def head(h):
        at = pl.ds(pl.multiple_of(h * HD, HD), HD)
        query = qaug[h]
        d_head = d_out[at, :]
        delta = jnp.sum(d_head.astype(f32) * att[at, :].astype(f32), 0, keepdims=True)
        log_sum = lse[h]
        d_q = jnp.zeros((HD, queries), f32)
        for b in range(0, length, BLOCK):
            e = b + BLOCK
            probs = jnp.exp(nn_dot(kaug[b:e, :], query) - log_sum)
            d_probs = nn_dot(v_rows[b:e, :], d_head)
            d_scores = (probs * (d_probs - delta)).astype(bf16)
            d_values[b:e, :] += nt_dot(probs.astype(bf16), d_head)
            d_keys[b:e, :] += nt_dot(d_scores, query[0:HD])
            at_b = b % queries
            d_q = d_q + nn_dot(kv[b // queries, 0:HD, at_b : at_b + BLOCK], d_scores)
        d_query[at, :] = d_q * (HD ** (-0.5))

    pl.loop(0, heads // 2)(head)
    line_ends(scatter_out, 1, 2)
    scatter_out.stage(1)
    for load in loads[8:11]:
        load.wait()
    g_d.fold(here=True)
    pl.loop(heads // 2, heads)(head)

    for other in range(CTX):
        block = slice(other * queries, (other + 1) * queries)
        both = jnp.concatenate([d_keys[block, :], d_values[block, :]], 1)
        kv_send[other] = both.astype(bf16)
    for step in range(1, CTX):
        peer = lax.rem(c + step, CTX)
        links.send(kv_send.at[peer], kv_recv.at[step - 1], (s, peer, t), kv_slot + step - 1)
    scatter_out.stage(2)
    for load in loads[11:]:
        load.wait()

    cosine, sine = cos[...], sin[...]
    for h in range(heads):
        at = h * HD
        d1, d2 = d_query[at : at + half, :], d_query[at + half : at + HD, :]
        d_query[at : at + half, :] = d1 * cosine + d2 * sine
        d_query[at + half : at + HD, :] = d2 * cosine - d1 * sine
    d_query_rows[...] = d_query[...].astype(bf16).T
    for b in range(0, width, 512):
        part_query[:, b : b + 512] = nt_dot(d_query_rows[...], wq[b : b + 512, :])
    others(g_q, stage_q)
    attn_rows[...] = att[...].T
    others(g_o, stage_o)
    for step in range(1, CTX):
        links.recv(kv_recv.at[step - 1], kv_slot + step - 1)
    d_pair = kv_send[c].astype(f32)
    for step in range(1, CTX):
        d_pair = d_pair + kv_recv[step - 1].astype(f32)
    d_pair = d_pair.T
    d1, d2 = d_pair[0:half], d_pair[half:HD]
    turned = jnp.concatenate(
        [d1 * cosine + d2 * sine, d2 * cosine - d1 * sine, d_pair[HD:]], 0
    )
    d_kv[...] = turned.astype(bf16).T

    for b in range(0, width, 512):
        summed = part_query[:, b : b + 512] + nt_dot(d_kv[...], wkv[b : b + 512, :])
        part[:, b : b + 512] = summed.astype(bf16)

    line_ends(scatter, 0, 1)

    gain_rows[...] = jnp.zeros_like(gain_rows)

    @pl.loop(0, queries // ROWS)
    def _(i):
        r = pl.ds(pl.multiple_of(i * ROWS, ROWS), ROWS)
        v = x[r, :].astype(f32)
        inverse = lax.rsqrt(jnp.mean(v * v, -1, keepdims=True) + epsilon)
        gain_rows[...] += part[r, :].astype(f32) * (v * inverse)

    pair[0:1, :] = jnp.sum(gain_rows[...], 0, keepdims=True)
    pair[1:2, :] = gain_mlp[...]
    for step in range(1, plane):
        links.send(pair, plane_in.at[step - 1], links.plane_peer(step), plane_slot + step - 1)
    g_u.fold()
    line_steps(scatter, 1)
    g_o.own()
    g_o.exchange()
    summed = pair[...]
    for step in range(1, plane):
        links.recv(plane_in.at[step - 1], plane_slot + step - 1)
        summed = summed + plane_in[step - 1]
    total[...] = summed
    for step in range(1, LINE):
        links.send(total, line_in.at[step - 1], links.line_peer(step), line_slot + step - 1)
    line_ends(scatter, 2)
    others(g_kv, stage_kv)
    g_q.own()
    g_q.exchange()
    line_steps(scatter, 2)
    g_kv.own()
    g_kv.exchange()
    g_o.fold()
    scatter_out.arrive()

    def layer_rows(r, total_rows):
        layer[pl.ds(r, ROWS), :] = (mid[pl.ds(r, ROWS), :] + total_rows).astype(bf16)

    scatter_out.owned(0, layer_rows)
    links.keep_later(layer, out_o)
    g_q.fold()
    g_kv.fold()
    g_u.total()
    links.keep_later(g_u.out, gu_o)
    g_o.total()
    links.keep_later(g_o.out, go_o)
    g_d.total(here=True)
    links.keep_later(g_d.out, gd_o)

    def finish_rows(r, d_normed):
        at = pl.ds(r, ROWS)
        q = pl.ds(pl.multiple_of(place(t) * tokens + r, ROWS), ROWS)
        v = x[q, :].astype(f32)
        inverse = lax.rsqrt(jnp.mean(v * v, -1, keepdims=True) + epsilon)
        unit = v * inverse
        d_unit = d_normed * gains[0:1, :]
        back = inverse * (d_unit - unit * jnp.mean(d_unit * unit, -1, keepdims=True))
        dmid[at, :] = dmid[at, :] + back

    scatter.arrive(0)
    scatter.owned(0, finish_rows)
    g_q.total()
    links.keep_later(g_q.out, gq_o)
    g_kv.total()
    links.keep_later(g_kv.out, gkv_o)
    for p in range(1, PIECES):
        scatter.arrive(p)
        scatter.owned(p, finish_rows)
    links.keep_later(dmid, in_o)
    for step in range(1, LINE):
        links.recv(line_in.at[step - 1], line_slot + step - 1)
        summed = summed + line_in[step - 1]
    own_gains = gain_o.shape[1]
    if own_gains == width:
        gain_o[...] = summed
    else:
        gain_sum[...] = summed
        me = s * CTX + c
        gain_o[...] = gain_sum[:, pl.ds(pl.multiple_of(me * own_gains, own_gains), own_gains)]
    links.finish()


def backward_call(
    shards, rows, dmid_all, wo, wq, wkv, n1, qaug, kaug, kv, att, x, dmid, branch, gu_part,
    gd_part, gd_x, gd_y, mid, lse, gains, gain_mlp, cos, sin,
):
    tokens, width = dmid.shape
    queries = n1.shape[0]
    heads = qaug.shape[0]
    length = kaug.shape[0]
    inner = heads * HD
    columns = gu_part.shape[1]
    plane = shards * CTX
    own_gains = width // plane if width // plane % 128 == 0 else width
    piece = CTX * rows * (shards - 1)
    token = (tokens, width)
    block = (LINE - 1,) + token
    outs = [
        struct(token, f32),
        struct((rows, inner), f32),
        struct((rows, 2 * HD), f32),
        struct((rows, inner), f32),
        struct((rows, columns), f32),
        struct((rows, columns), f32),
        struct(token, bf16),
        struct((2, own_gains), f32),
    ]
    count = 6 + 6 * PIECES + 5 * (shards - 1 + 6) + CTX - 1 + plane - 1 + LINE - 1
    return pl.pallas_call(
        functools.partial(backward_kernel, shards, rows),
        out_shape=outs,
        in_specs=[any_spec()] * 17 + [vmem_spec()] * 5,
        out_specs=[any_spec()] * 7 + [vmem_spec()],
        scratch_shapes=[
            pltpu.VMEM((queries, width), bf16),
            pltpu.VMEM((width, inner), bf16),
            pltpu.VMEM((width, inner), bf16),
            pltpu.VMEM((width, 2 * HD), bf16),
            pltpu.VMEM((queries, width), bf16),
            pltpu.VMEM(qaug.shape, bf16),
            pltpu.VMEM(kaug.shape, bf16),
            pltpu.VMEM(kv.shape, bf16),
            pltpu.VMEM((inner, queries), bf16),
            pltpu.VMEM((queries, width), bf16),
            pltpu.VMEM(token, f32),
            pltpu.VMEM((inner, queries), bf16),
            pltpu.VMEM((queries, inner), bf16),
            pltpu.VMEM((length, HD), bf16),
            pltpu.VMEM((length, HD), f32),
            pltpu.VMEM((length, HD), f32),
            pltpu.VMEM((inner, queries), f32),
            pltpu.VMEM((queries, inner), bf16),
            pltpu.VMEM((CTX, queries, 2 * HD), bf16),
            pltpu.VMEM((CTX - 1, queries, 2 * HD), bf16),
            pltpu.VMEM((queries, 2 * HD), bf16),
            pltpu.VMEM((queries, width), bf16),
            pltpu.VMEM(block, bf16),
            pltpu.VMEM(block, bf16),
            pltpu.VMEM((ROWS, width), f32),
            pltpu.VMEM((2, width), f32),
            pltpu.VMEM((plane - 1, 2, width), f32),
            pltpu.VMEM((LINE - 1, 2, width), f32),
            pltpu.VMEM((2, width), f32),
            pltpu.VMEM((piece, inner), bf16),
            pltpu.VMEM((piece, inner), bf16),
            pltpu.VMEM((piece, 2 * HD), bf16),
            pltpu.VMEM((queries, width), bf16),
            pltpu.VMEM(block, bf16),
            pltpu.VMEM(block, bf16),
            pltpu.VMEM(token, f32),
            pltpu.VMEM(token, bf16),
            pltpu.VMEM((2, width), f32),
            pltpu.VMEM((queries, width), f32),
            *PlaneScatter.scratch(shards, rows, inner),
            *PlaneScatter.scratch(shards, rows, inner),
            *PlaneScatter.scratch(shards, rows, 2 * HD),
            *PlaneScatter.scratch(1 + 1, rows, columns),
            *PlaneScatter.scratch(1 + 1, rows, columns),
            pltpu.SemaphoreType.DMA((count,)),
            pltpu.SemaphoreType.DMA((count,)),
            pltpu.SemaphoreType.DMA((32,)),
        ],
        compiler_params=pltpu.CompilerParams(
            collective_id=2, has_side_effects=True, vmem_limit_bytes=60 * 2**20
        ),
        name="backward",
    )(
        dmid_all, wo, wq, wkv, n1, qaug, kaug, kv, att, x, dmid, branch, gu_part,
        gd_part, gd_x, gd_y, mid, lse, gains, gain_mlp, cos, sin,
    )


def finish_kernel(gains, layer_in, *refs):
    count = (len(refs) - 2) // 2
    layer_out = refs[count]
    layer_out[0] = layer_in[...]
    refs[count + 1][0] = refs[0][...]
    for src, dst in zip(refs[1:count], refs[count + 2 : -2]):
        dst[...] = src[...]
    for row, dst in enumerate(refs[-2:]):
        dst[...] = gains[row : row + 1, :]


def finish_call(arrays, gains, steps=8):
    rows = [array.shape[0] // steps for array in arrays]
    wide = [array.shape[1] for array in arrays]
    own = gains.shape[1]
    shapes = [struct((1,) * (i < 2) + array.shape, array.dtype) for i, array in enumerate(arrays)]
    return pl.pallas_call(
        finish_kernel,
        grid=(steps,),
        out_shape=shapes + [struct((1, own), f32)] * 2,
        in_specs=[pl.BlockSpec((2, own), lambda i: (0, 0))]
        + [pl.BlockSpec((r, n), lambda i: (i, 0)) for r, n in zip(rows, wide)],
        out_specs=[
            pl.BlockSpec((1, r, n), lambda i: (0, i, 0))
            if index < 2
            else pl.BlockSpec((r, n), lambda i: (i, 0))
            for index, (r, n) in enumerate(zip(rows, wide))
        ]
        + [pl.BlockSpec((1, own), lambda i: (0, 0))] * 2,
        compiler_params=pltpu.CompilerParams(vmem_limit_bytes=60 * 2**20),
        name="finish",
    )(gains, *arrays)


def body(
    inputs, out_grad, block_order, gain_attn, w_query, w_keyval, w_output, gain_mlp, w_gate, w_up, w_down
):
    shards = lax.axis_size("shard")
    x, og = inputs[0], out_grad[0]
    tokens, width = x.shape
    s, c = lax.axis_index("shard"), lax.axis_index("ctx")
    frequency = np.float32(10000.0) ** (-np.arange(HD // 2, dtype=np.float32)[:, None] * 2.0 / HD)
    own = gain_attn.shape[0]
    start = (s * CTX + c) * own
    row = lax.broadcasted_iota(jnp.int32, (2, own), 0)
    gain_in = jnp.where(row == 0, gain_attn, gain_mlp)
    aligned = own % 128 == 0
    if not aligned:
        gain_in = lax.dynamic_update_slice(jnp.zeros((2, width), bf16), gain_in, (0, start))
    (wq, wkv, wo, wg, wu, wd, n1, og_all, n2, mid, qaug, kaug, kv, att, x_all, lse, gains, cos, sin) = forward_call(
        shards, x, og, (w_query, w_keyval, w_output, w_gate, w_up, w_down), gain_in,
        jnp.asarray(frequency, f32), block_order[0],
    )
    (dmid, dmid_all, grad_gate, gd_part, gd_x, gd_y, branch, gu_part, gm) = middle_call(
        shards, w_gate.shape[0], n2, og_all, wg, wu, wd, mid, gains
    )
    (input_grad, grad_query, grad_keyval, grad_output, grad_up, grad_down, layer_out, both) = backward_call(
        shards, w_query.shape[0], dmid_all, wo, wq, wkv, n1, qaug, kaug, kv, att, x_all, dmid,
        branch, gu_part, gd_part, gd_x, gd_y, mid, lse, gains, gm, cos, sin,
    )
    if not aligned:
        both = lax.dynamic_slice(both, (0, start), (2, own))
    (
        layer_out, input_grad, grad_query, grad_keyval, grad_output, grad_gate, grad_up, grad_down,
        *gain_grads,
    ) = finish_call([
        layer_out, input_grad, grad_query, grad_keyval, grad_output, grad_gate, grad_up, grad_down,
    ], both)
    return (
        layer_out, input_grad, gain_grads[0][0], grad_query, grad_keyval, grad_output,
        gain_grads[1][0], grad_gate, grad_up, grad_down,
    )


def solution(mesh):
    plane = P(("shard", "ctx"), "tensor")
    gain = P(("shard", "ctx"))
    token = P("shard", ("ctx", "tensor"), None)
    return jax.shard_map(
        body,
        mesh=mesh,
        in_specs=(token, token, P("shard", None), gain, plane, plane, plane, gain, plane, plane, plane),
        out_specs=(token, token, gain, plane, plane, plane, gain, plane, plane, plane),
        check_vma=False,
    )
```

```python
import functools

import jax
import jax.numpy as jnp
import numpy as np
from jax import lax
from jax.experimental import pallas as pl
from jax.experimental.pallas import tpu as pltpu
from jax.sharding import PartitionSpec as P

HD = 64
BLOCK = 256
BLOCKS = 8
ROWS = 16
CTX = 4
LINE = 4
PIECES = 2

epsilon = 1e-05
blocked = -1e30

f32 = jnp.float32
bf16 = jnp.bfloat16
MESH = pl.DeviceIdType.MESH


def place(owner):
    return (owner + (owner + 1) // 2) % LINE if isinstance(owner, int) else lax.rem(
        owner + (owner + 1) // 2, LINE
    )


def nn_dot(left, right):
    return jnp.dot(left, right, preferred_element_type=f32)


def nt_dot(left, right):
    return lax.dot_general(left, right, (((1,), (1,)), ((), ())), preferred_element_type=f32)


def tn_dot(left, right):
    return lax.dot_general(left, right, (((0,), (0,)), ((), ())), preferred_element_type=f32)


class Links:
    def __init__(self, shards, send_sems, recv_sems, local_sems):
        self.shards = shards
        self.send_sems, self.recv_sems, self.local_sems = send_sems, recv_sems, local_sems
        self.s = lax.axis_index("shard")
        self.c = lax.axis_index("ctx")
        self.t = lax.axis_index("tensor")
        self.c_x = self.c + 1 - 2 * lax.rem(self.c, 2)
        self.c_y = lax.rem(self.c + 2, CTX)
        self.c_d = CTX - 1 - self.c
        self.x_dev = (self.s, self.c_x, self.t)
        self.y_dev = (self.s, self.c_y, self.t)
        self.right = (self.s, self.c, self.t + 1)
        self.left = (self.s, self.c, self.t - 1)
        self.used = 0
        self.local_used = 0
        self.sends = []
        self.locals = []

    def slots(self, count):
        first = self.used
        self.used += count
        assert self.used <= self.send_sems.shape[0]
        return first

    def plane_peer(self, step):
        index = lax.rem(self.s * CTX + self.c + step, self.shards * CTX)
        return (index // CTX, lax.rem(index, CTX), self.t)

    def core_peer(self, step):
        return (lax.rem(self.s + step, self.shards), self.c, self.t)

    def line_peer(self, step):
        return (self.s, self.c, lax.rem(self.t + step, LINE))

    def greet(self, whole_line=False):
        sem = pltpu.get_barrier_semaphore()
        count = self.shards * CTX - 1
        for step in range(1, count + 1):
            pl.semaphore_signal(
                sem, inc=1, device_id=self.plane_peer(step), device_id_type=MESH
            )
        if whole_line:
            for step in range(1, LINE):
                pl.semaphore_signal(
                    sem, inc=1, device_id=self.line_peer(step), device_id_type=MESH
                )
            self.partners = count + LINE - 1
            return

        @pl.when(self.t > 0)
        def _():
            pl.semaphore_signal(sem, inc=1, device_id=self.left, device_id_type=MESH)

        @pl.when(self.t < LINE - 1)
        def _():
            pl.semaphore_signal(sem, inc=1, device_id=self.right, device_id_type=MESH)

        beside = (self.t + LINE - 1) // LINE + (2 * LINE - 2 - self.t) // LINE
        self.partners = count + beside

    def met(self):
        pl.semaphore_wait(pltpu.get_barrier_semaphore(), self.partners)

    def copy(self, src, dst, device, slot):
        return pltpu.make_async_remote_copy(
            src_ref=src,
            dst_ref=dst,
            send_sem=self.send_sems.at[slot],
            recv_sem=self.recv_sems.at[slot],
            device_id=device,
            device_id_type=MESH,
        )

    def send(self, src, dst, device, slot, cond=None):
        if cond is None:
            self.copy(src, dst, device, slot).start()
        else:

            @pl.when(cond)
            def _():
                self.copy(src, dst, device, slot).start()

        handle = (src, dst, device, slot, cond)
        self.sends.append(handle)
        return handle

    def sent(self, handle):
        self.sends = [other for other in self.sends if other is not handle]
        self.copy(*handle[:4]).wait_send()

    def recv(self, dst, slot):
        self.copy(dst, dst, self.x_dev, slot).wait_recv()

    def keep(self, src, dst):
        copy = pltpu.make_async_copy(src, dst, self.local_sems.at[self.local_used])
        self.local_used += 1
        assert self.local_used <= self.local_sems.shape[0]
        copy.start()
        return copy

    def keep_later(self, src, dst):
        self.locals.append(self.keep(src, dst))

    def finish(self):
        for src, dst, device, slot, cond in self.sends:
            if cond is None:
                self.copy(src, dst, device, slot).wait_send()
            else:

                @pl.when(cond)
                def _():
                    self.copy(src, dst, device, slot).wait_send()

        for copy in self.locals:
            copy.wait()


class PlaneGather:
    def __init__(self, links, src, full, stage=None):
        self.links, self.src, self.full, self.stage = links, src, full, stage
        self.rows = src.shape[0]
        self.first = links.slots(4 + 4 * (links.shards - 1))

    def block(self, s, c):
        start = pl.multiple_of((s * CTX + c) * self.rows, self.rows)
        return self.full.at[pl.ds(start, self.rows)]

    def half(self, s, c, which):
        size = self.rows // 2
        start = pl.multiple_of((s * CTX + c) * self.rows + which * size, size)
        return self.full.at[pl.ds(start, size)]

    def core_slot(self, step, part):
        return self.first + 4 + (step - 1) * 4 + part

    def core_send(self, src, c, part):
        links = self.links
        for step in range(1, links.shards):
            links.send(
                src,
                self.block(links.s, c),
                links.core_peer(step),
                self.core_slot(step, part),
            )

    def start(self):
        links = self.links
        own = self.block(links.s, links.c)
        links.send(self.src, own, links.x_dev, self.first)
        links.send(self.src, own, links.y_dev, self.first + 1)
        self.core_send(self.src, links.c, 0)
        self.local = links.keep(self.src, own if self.stage is None else self.stage)

    def settle(self):
        self.local.wait()
        self.local = self.links.keep(self.stage, self.block(self.links.s, self.links.c))

    def forward(self):
        links = self.links
        links.recv(self.block(links.s, links.c_x), self.first)
        links.recv(self.block(links.s, links.c_y), self.first + 1)
        from_x = self.half(links.s, links.c_x, 0)
        from_y = self.half(links.s, links.c_y, 1)
        links.send(from_x, from_x, links.y_dev, self.first + 2)
        links.send(from_y, from_y, links.x_dev, self.first + 3)
        self.core_send(self.block(links.s, links.c_x), links.c_x, 1)
        self.core_send(self.block(links.s, links.c_y), links.c_y, 2)

    def diagonal(self):
        links = self.links
        links.recv(self.half(links.s, links.c_d, 0), self.first + 2)
        links.recv(self.half(links.s, links.c_d, 1), self.first + 3)
        self.core_send(self.block(links.s, links.c_d), links.c_d, 3)

    def done(self):
        links = self.links
        for step in range(1, links.shards):
            other = lax.rem(links.s + links.shards - step, links.shards)
            for part, c in enumerate((links.c, links.c_x, links.c_y, links.c_d)):
                links.recv(self.block(other, c), self.core_slot(step, part))
        self.local.wait()


class LineGather:
    def __init__(self, links, own, full, tokens, pieces=1):
        self.links, self.own, self.full, self.tokens = links, own, full, tokens
        self.pieces, self.size = pieces, tokens // pieces
        self.first = links.slots(2 * (LINE - 1) * pieces)

    def block(self, owner, p):
        start = pl.multiple_of(place(owner) * self.tokens + p * self.size, self.size)
        return self.full.at[pl.ds(start, self.size)]

    def slot(self, side, k, p):
        return self.first + (side * (LINE - 1) + k - 1) * self.pieces + p

    def send(self, k, p=0):
        links = self.links
        t, u = links.t, LINE - 1 - links.t
        own = self.own.at[pl.ds(p * self.size, self.size)]
        right, left = self.block(t - k + 1, p), self.block(t + k - 1, p)
        links.send(
            own if k == 1 else right,
            right,
            links.right,
            self.slot(0, k, p),
            jnp.logical_and(t >= k - 1, t < LINE - 1),
        )
        links.send(
            own if k == 1 else left,
            left,
            links.left,
            self.slot(1, k, p),
            jnp.logical_and(u >= k - 1, u < LINE - 1),
        )

    def recv(self, k, p=0):
        links = self.links
        t, u = links.t, LINE - 1 - links.t

        @pl.when(t >= k)
        def _():
            links.recv(self.block(t - k, p), self.slot(0, k, p))

        @pl.when(u >= k)
        def _():
            links.recv(self.block(t + k, p), self.slot(1, k, p))


class LineScatter:
    def __init__(self, links, part, tokens, from_left, from_right, pieces=1):
        self.links, self.part, self.tokens = links, part, tokens
        self.from_left, self.from_right = from_left, from_right
        self.pieces, self.size = pieces, tokens // pieces
        self.first = links.slots(2 * (LINE - 1) * pieces)

    def slot(self, side, k, p):
        return self.first + (side * (LINE - 1) + k) * self.pieces + p

    def piece(self, ref, k, p):
        return ref.at[k, pl.ds(p * self.size, self.size)]

    def total(self, owner, k, p, arrived):
        @pl.loop(0, self.size // ROWS)
        def _(i):
            r = pl.multiple_of(p * self.size + i * ROWS, ROWS)
            q = pl.multiple_of(place(owner) * self.tokens + p * self.size + i * ROWS, ROWS)
            mine = self.part[pl.ds(q, ROWS), :].astype(f32)
            summed = mine + arrived[k, pl.ds(r, ROWS), :].astype(f32)
            arrived[k, pl.ds(r, ROWS), :] = summed.astype(arrived.dtype)

    def ends(self, k, p=0):
        links = self.links
        for side, behind, arrived, device in self.sides():
            owner = LINE - 1 - k if side == 0 else k
            piece, slot = self.piece(arrived, k, p), self.slot(side, k, p)

            @pl.when(behind == 0)
            def _():
                self.first_part(owner, k, p, arrived)

            links.send(piece, piece, device, slot, behind == 0)

    def sides(self):
        links = self.links
        return (
            (0, links.t, self.from_left, links.right),
            (1, LINE - 1 - links.t, self.from_right, links.left),
        )

    def stage(self, now, p=0):
        links = self.links
        for side, behind, arrived, device in self.sides():
            k = now - behind
            owner = LINE - 1 - k if side == 0 else k
            piece, slot = self.piece(arrived, k, p), self.slot(side, k, p)
            ready = jnp.logical_and(k >= 0, behind > 0)

            @pl.when(ready)
            def _():
                links.recv(piece, slot)
                self.total(owner, k, p, arrived)

            links.send(piece, piece, device, slot, ready)

    def first_part(self, owner, k, p, out):
        @pl.loop(0, self.size // ROWS)
        def _(i):
            r = pl.multiple_of(p * self.size + i * ROWS, ROWS)
            q = pl.multiple_of(place(owner) * self.tokens + p * self.size + i * ROWS, ROWS)
            out[k, pl.ds(r, ROWS), :] = self.part[pl.ds(q, ROWS), :].astype(out.dtype)

    def arrive(self, p=0):
        links = self.links
        t = links.t

        @pl.when(t > 0)
        def _():
            links.recv(
                self.piece(self.from_left, LINE - 1 - t, p), self.slot(0, LINE - 1 - t, p)
            )

        @pl.when(t < LINE - 1)
        def _():
            links.recv(self.piece(self.from_right, t, p), self.slot(1, t, p))

    def rows(self, r):
        t = self.links.t
        q = pl.multiple_of(place(t) * self.tokens + r, ROWS)
        k_l = jnp.minimum(LINE - 1 - t, LINE - 2)
        k_r = jnp.minimum(t, LINE - 2)
        zero = jnp.zeros((ROWS, self.part.shape[1]), f32)
        return (
            self.part[pl.ds(q, ROWS), :].astype(f32)
            + jnp.where(t > 0, self.from_left[k_l, pl.ds(r, ROWS), :].astype(f32), zero)
            + jnp.where(t < LINE - 1, self.from_right[k_r, pl.ds(r, ROWS), :].astype(f32), zero)
        )

    def owned(self, p, use):
        @pl.loop(0, self.size // ROWS)
        def _(i):
            r = pl.multiple_of(p * self.size + i * ROWS, ROWS)
            use(r, self.rows(r))


def line_ends(scatter, *hops):
    for k in hops:
        for p in range(scatter.pieces):
            scatter.ends(k, p)


def line_steps(scatter, now):
    for p in range(scatter.pieces):
        scatter.stage(now, p)


def line_finish(scatter, use, gather=None):
    for p in range(scatter.pieces):
        scatter.arrive(p)
        scatter.owned(p, use)
        if gather is not None:
            gather.send(1, p)


def line_spread(gather, k):
    for p in range(gather.pieces):
        gather.recv(k, p)
        if k < LINE - 1:
            gather.send(k + 1, p)


class PlaneScatter:
    def __init__(self, links, left, right, rows, core_in, x_in, y_in, x_last, y_last, out):
        self.links, self.left, self.right, self.rows = links, left, right, rows
        self.core_in, self.x_in, self.y_in = core_in, x_in, y_in
        self.x_last, self.y_last, self.out = x_last, y_last, out
        self.first = links.slots(links.shards - 1 + 6)
        self.tile = min(256, CTX * rows)

    def product(self, shard, i):
        start = pl.multiple_of(shard * (CTX * self.rows) + i * self.tile, self.tile)
        return tn_dot(self.left[:, pl.ds(start, self.tile)], self.right[...])

    @property
    def tiles(self):
        return CTX * self.rows // self.tile

    def other(self, step, stage, part=None):
        links = self.links
        target = lax.rem(links.s + step, links.shards)
        low, high = (0, self.tiles) if part is None else part

        @pl.loop(low, high)
        def _(i):
            r = pl.multiple_of(i * self.tile, self.tile)
            stage[pl.ds(r, self.tile), :] = self.product(target, i).astype(bf16)

        if high == self.tiles:
            return links.send(
                stage, self.core_in.at[step - 1], links.core_peer(step), self.first + step - 1
            )

    def own(self, part=None):
        links = self.links
        low, high = (0, self.tiles) if part is None else part
        if low == 0:
            for step in range(1, links.shards):
                links.recv(self.core_in.at[step - 1], self.first + step - 1)

        @pl.loop(low, high)
        def _(i):
            r = pl.multiple_of(i * self.tile, self.tile)
            summed = self.product(links.s, i)
            for step in range(1, links.shards):
                summed = summed + self.core_in[step - 1, pl.ds(r, self.tile), :].astype(f32)
            self.core_in[0, pl.ds(r, self.tile), :] = summed.astype(bf16)

    def half(self, c, which):
        size = self.rows // 2
        start = pl.multiple_of(c * self.rows + which * size, size)
        return self.core_in.at[0, pl.ds(start, size)]

    def exchange(self):
        links, first = self.links, self.first + self.links.shards - 1
        links.send(self.half(links.c_d, 0), self.x_in.at[1], links.x_dev, first)
        links.send(self.half(links.c_d, 1), self.y_in.at[1], links.y_dev, first + 1)
        links.send(self.half(links.c_x, 0), self.x_in.at[0], links.x_dev, first + 2)
        links.send(self.half(links.c_y, 1), self.y_in.at[0], links.y_dev, first + 3)

    def add(self, c, which, arrived):
        size = self.rows // 2

        @pl.loop(0, size // ROWS)
        def _(i):
            r = pl.multiple_of(i * ROWS, ROWS)
            q = pl.multiple_of(c * self.rows + which * size + i * ROWS, ROWS)
            mine = self.core_in[0, pl.ds(q, ROWS), :].astype(f32)
            summed = mine + arrived[1, pl.ds(r, ROWS), :].astype(f32)
            self.core_in[0, pl.ds(q, ROWS), :] = summed.astype(bf16)

    def arrived(self):
        links, first = self.links, self.first + self.links.shards - 1
        for ref, offset in ((self.x_in, 0), (self.y_in, 1)):
            for part in range(2):
                links.recv(ref.at[1 - part], first + offset + 2 * part)

    def fold(self, here=False):
        links, first = self.links, self.first + self.links.shards - 1
        if not here:
            links.recv(self.x_in.at[1], first)
        self.add(links.c_y, 0, self.x_in)
        links.send(self.half(links.c_y, 0), self.y_last, links.y_dev, first + 4)
        if not here:
            links.recv(self.y_in.at[1], first + 1)
        self.add(links.c_x, 1, self.y_in)
        links.send(self.half(links.c_x, 1), self.x_last, links.x_dev, first + 5)

    def total(self, here=False):
        links, first = self.links, self.first + self.links.shards - 1
        size = self.rows // 2
        if not here:
            links.recv(self.x_in.at[0], first + 2)
            links.recv(self.y_in.at[0], first + 3)
        links.recv(self.y_last, first + 4)
        links.recv(self.x_last, first + 5)
        for which, arrived, last in ((0, self.x_in, self.y_last), (1, self.y_in, self.x_last)):

            @pl.loop(0, size // ROWS)
            def _(i):
                r = pl.multiple_of(i * ROWS, ROWS)
                q = pl.multiple_of(links.c * self.rows + which * size + i * ROWS, ROWS)
                self.out[pl.ds(which * size + r, ROWS), :] = (
                    self.core_in[0, pl.ds(q, ROWS), :].astype(f32)
                    + arrived[0, pl.ds(r, ROWS), :].astype(f32)
                    + last[pl.ds(r, ROWS), :].astype(f32)
                )

    @staticmethod
    def scratch(shards, rows, columns):
        half = (rows // 2, columns)
        return [
            pltpu.VMEM((shards - 1, CTX * rows, columns), bf16),
            pltpu.VMEM((2,) + half, bf16),
            pltpu.VMEM((2,) + half, bf16),
            pltpu.VMEM(half, bf16),
            pltpu.VMEM(half, bf16),
            pltpu.VMEM((rows, columns), f32),
        ]


def any_spec():
    return pl.BlockSpec(memory_space=pl.ANY)


def vmem_spec():
    return pl.BlockSpec(memory_space=pltpu.VMEM)


def struct(shape, dtype):
    return jax.ShapeDtypeStruct(shape, dtype)


def forward_kernel(
    shards,
    x, og, wq, wkv, wo, wg, wu, wd, gain_in, frequency, order,
    wq_o, wkv_o, wo_o, wg_o, wu_o, wd_o, n1_o, og_o, n2_o, mid_o, qaug_o, kaug_o, kv_o, att_o, x_o,
    lse, gains, cos, sin,
    x_all, n1_all, wq_all, wkv_all, wo_all, gains_all, qaug, kv_all, kaug, v_all, scores, weights,
    attn, part, from_left, from_right, mid, n2, og_stage, wg_stage, wu_stage, wd_stage, gpad,
    send_sems, recv_sems, local_sems,
):
    tokens, width = x.shape
    queries = tokens * LINE
    heads = qaug.shape[0]
    links = Links(shards, send_sems, recv_sems, local_sems)
    s, c, t = links.s, links.c, links.t

    gather_x = LineGather(links, x, x_all, tokens, PIECES)
    gather_og = LineGather(links, og, og_o, tokens)
    gather_n2 = LineGather(links, n2, n2_o, tokens, PIECES)
    small = [PlaneGather(links, *pair) for pair in ((wq, wq_all), (wkv, wkv_all), (wo, wo_all))]
    large = [
        PlaneGather(links, *three)
        for three in ((wg, wg_o, wg_stage), (wu, wu_o, wu_stage), (wd, wd_o, wd_stage))
    ]
    scatter = LineScatter(links, part, tokens, from_left, from_right, PIECES)
    plane = shards * CTX
    gain_slot = links.slots(plane - 1)
    kv_slot = links.slots((CTX - 1) * (2 * LINE - 1))

    links.greet()
    me = s * CTX + c
    own_gains = gain_in.shape[1]
    if own_gains == width:
        gpad[...] = gain_in[...].astype(f32)
    else:
        gpad[...] = jnp.zeros_like(gpad)
        gpad[:, pl.ds(pl.multiple_of(me * own_gains, own_gains), own_gains)] = gain_in[
            ...
        ].astype(f32)
    links.met()
    for step in range(1, plane):
        links.send(gpad, gains_all.at[me], links.plane_peer(step), gain_slot + step - 1)
    own_gain = links.keep(gpad, gains_all.at[me])
    for p in range(PIECES):
        gather_x.send(1, p)
    own_rows = pl.ds(pl.multiple_of(place(t) * tokens, tokens), tokens)
    own_x = links.keep(x, x_all.at[own_rows])
    for gather in small:
        gather.start()

    per = queries // BLOCK
    lane = lax.broadcasted_iota(jnp.int32, (1, queries), 1)
    owner = jnp.zeros((1, queries), jnp.int32)
    for index in range(LINE):
        owner = jnp.where(lane // tokens == place(index), index, owner)
    slot = owner * tokens + lax.rem(lane, tokens)
    block_here = jnp.zeros((1, queries), jnp.int32)
    for index in range(per):
        block_here = jnp.where(slot // BLOCK == index, order[c * per + index], block_here)
    position = (block_here * BLOCK + lax.rem(slot, BLOCK)).astype(f32)
    angles = frequency[...] * position
    cos[...] = jnp.cos(angles)
    sin[...] = jnp.sin(angles)
    row = lax.broadcasted_iota(jnp.int32, (HD, queries), 0)
    bias = jnp.zeros((HD, queries), f32)
    for index in range(BLOCKS):
        barred = jnp.logical_and(row == index, order[index] > block_here)
        bias = jnp.where(barred, blocked, bias)
    bias = bias.astype(bf16)
    for h in range(heads):
        qaug[h, HD:, :] = bias

    own_gain.wait()
    for step in range(1, plane):
        other = lax.rem(me + plane - step, plane)
        links.recv(gains_all.at[other], gain_slot + step - 1)
    total = gains_all[0]
    for index in range(1, plane):
        total = total + gains_all[index]
    gains[...] = total
    own_x.wait()

    def norm_block(owner):
        @pl.loop(0, tokens // ROWS)
        def _(i):
            r = pl.multiple_of(place(owner) * tokens + i * ROWS, ROWS)
            v = x_all[pl.ds(r, ROWS), :].astype(f32)
            inverse = lax.rsqrt(jnp.mean(v * v, -1, keepdims=True) + epsilon)
            n1_all[pl.ds(r, ROWS), :] = (v * inverse * gains[0:1, :]).astype(bf16)

    own_og = links.keep(og, og_stage)
    norm_block(t)
    line_spread(gather_x, 1)
    for gather in small:
        gather.forward()
    norm_pair(gather_x, norm_block, 1)
    line_spread(gather_x, 2)
    gather_og.send(1)
    for gather in small:
        gather.diagonal()
    norm_pair(gather_x, norm_block, 2)
    own_og.wait()
    links.keep_later(og_stage, og_o.at[own_rows])
    for gather in small:
        gather.done()

    half = HD // 2
    scale = HD ** (-0.5)

    def lanes_of(owner):
        return pl.ds(pl.multiple_of(place(owner) * tokens, tokens), tokens)

    def turn(v1, v2, cosine, sine):
        return (v1 * cosine - v2 * sine).astype(bf16), (v2 * cosine + v1 * sine).astype(bf16)

    def project_block(owner):
        at = lanes_of(owner)
        cosine, sine = cos[:, at], sin[:, at]
        kv_t = nn_dot(n1_all[at, :], wkv_all[...]).T
        k1, k2 = turn(kv_t[0:half], kv_t[half:HD], cosine, sine)
        kv_all[c, 0:half, at] = k1
        kv_all[c, half:HD, at] = k2
        kv_all[c, HD : 2 * HD, at] = kv_t[HD:].astype(bf16)
        q_t = nn_dot(n1_all[at, :], wq_all[...]).T
        for h in range(heads):
            b = h * HD
            q1, q2 = turn(q_t[b : b + half], q_t[b + half : b + HD], cosine, sine)
            qaug[h, 0:half, at] = (q1 * scale).astype(bf16)
            qaug[h, half:HD, at] = (q2 * scale).astype(bf16)

    u = LINE - 1 - t
    arrivals = [(t, None)]
    for k in range(1, LINE):
        arrivals += [(t - k, t >= k), (t + k, u >= k)]

    def send_block(index):
        owner, cond = arrivals[index]
        for step in range(1, CTX):
            peer = lax.rem(c + step, CTX)
            ref = kv_all.at[c, :, lanes_of(owner)]
            links.send(ref, ref, (s, peer, t), kv_slot + index * (CTX - 1) + step - 1, cond)

    def recv_block(index):
        owner, cond = arrivals[index]

        def wait():
            for step in range(1, CTX):
                other = lax.rem(c + CTX - step, CTX)
                slot = kv_slot + index * (CTX - 1) + step - 1
                links.recv(kv_all.at[other, :, lanes_of(owner)], slot)

        if cond is None:
            wait()
        else:
            pl.when(cond)(wait)

    project_block(t)
    send_block(0)
    for k in range(1, LINE):
        if k == LINE - 1:
            line_spread(gather_x, k)
            norm_pair(gather_x, norm_block, k)
        norm_pair(gather_x, project_block, k)
        send_block(2 * k - 1)
        send_block(2 * k)
    for gather in large:
        gather.start()
    links.keep_later(n1_all, n1_o)
    links.keep_later(x_all, x_o)
    links.keep_later(wq_all, wq_o)
    links.keep_later(wkv_all, wkv_o)
    links.keep_later(wo_all, wo_o)
    links.keep_later(qaug, qaug_o)
    for index in range(len(arrivals)):
        recv_block(index)
    for other in range(CTX):
        row = lax.broadcasted_iota(jnp.int32, (HD, queries), 0)
        lane = lax.broadcasted_iota(jnp.int32, (HD, queries), 1)
        mark = (row == other * (queries // BLOCK) + lax.rem(lane // tokens, 2)).astype(f32).astype(bf16)
        both = jnp.concatenate([kv_all[other, 0:HD, :], mark], 0)
        kaug[other * queries : (other + 1) * queries, :] = both.T
        v_all[:, other * queries : (other + 1) * queries] = kv_all[other, HD : 2 * HD, :]
    links.keep_later(kaug, kaug_o)
    links.keep_later(kv_all, kv_o)

    length = queries * CTX

    far = pl.multiple_of(jnp.where(t < LINE // 2, tokens, 0), tokens)
    near = pl.multiple_of(jnp.where(t < LINE // 2, 0, tokens), tokens)

    def soften(query):
        size = query.shape[1]
        top = jnp.full((1, size), -jnp.inf, f32)
        for b in range(0, length, BLOCK):
            block_scores = nn_dot(kaug[b : b + BLOCK, :], query)
            scores[b : b + BLOCK, :] = block_scores
            top = jnp.maximum(top, jnp.max(block_scores, 0, keepdims=True))
        norm = jnp.zeros((1, size), f32)
        for b in range(0, length, BLOCK):
            exponent = jnp.exp(scores[b : b + BLOCK, :] - top)
            norm = norm + jnp.sum(exponent, 0, keepdims=True)
            weights[b : b + BLOCK, :] = exponent.astype(bf16)
        out = nn_dot(v_all[...], weights[...]) / norm
        return out.astype(bf16), top + jnp.log(norm)

    def put(h, lanes, out, log_sum):
        attn[pl.ds(pl.multiple_of(h * HD, HD), HD), lanes] = out
        lse[h, :, lanes] = log_sum

    def head(lanes, h):
        put(h, lanes, *soften(qaug[h, :, lanes]))

    def head_pair(lanes, g):
        h = 2 * g
        both = jnp.concatenate([qaug[h, :, lanes], qaug[h + 1, :, lanes]], 1)
        out, log_sum = soften(both)
        put(h, lanes, out[:, 0:tokens], log_sum[:, 0:tokens])
        put(h + 1, lanes, out[:, tokens:], log_sum[:, tokens:])

    def attend(start, size):
        if size == tokens:
            pl.loop(0, heads // 2)(functools.partial(head_pair, pl.ds(start, size)))
        else:
            pl.loop(0, heads)(functools.partial(head, pl.ds(start, size)))
        rows = pl.ds(start, size)
        attn_rows = attn[:, rows].T
        for b in range(0, width, 512):
            part[rows, b : b + 512] = nt_dot(attn_rows, wo_all[b : b + 512, :])

    attend(far, tokens)
    line_ends(scatter, 0)
    gather_og.recv(1)
    gather_og.send(2)
    for gather in large:
        gather.settle()
    attend(2 * tokens, 2 * tokens)
    line_ends(scatter, 1, 2)
    gather_og.recv(2)
    gather_og.send(3)
    line_steps(scatter, 1)
    attend(near, tokens)
    links.keep_later(attn, att_o)

    def finish_rows(r, summed):
        q = pl.multiple_of(place(t) * tokens + r, ROWS)
        middle = x_all[pl.ds(q, ROWS), :].astype(f32) + summed
        mid[pl.ds(r, ROWS), :] = middle
        inverse = lax.rsqrt(jnp.mean(middle * middle, -1, keepdims=True) + epsilon)
        n2[pl.ds(r, ROWS), :] = (middle * inverse * gains[1:2, :]).astype(bf16)

    large[0].forward()
    line_steps(scatter, 2)
    large[1].forward()
    line_finish(scatter, finish_rows, gather_n2)
    large[2].forward()
    links.keep_later(n2, n2_o.at[own_rows])
    links.keep_later(mid, mid_o)
    line_spread(gather_n2, 1)
    large[0].diagonal()
    large[1].diagonal()
    line_spread(gather_n2, 2)
    large[2].diagonal()
    gather_og.recv(3)
    line_spread(gather_n2, 3)
    for gather in large:
        gather.done()
    links.finish()


def norm_pair(gather, norm_block, k):
    t, u = gather.links.t, LINE - 1 - gather.links.t

    @pl.when(t >= k)
    def _():
        norm_block(t - k)

    @pl.when(u >= k)
    def _():
        norm_block(t + k)


def forward_call(shards, x, og, weights_in, gain_in, frequency, order):
    wq, wkv, wo, wg, wu, wd = weights_in
    tokens, width = x.shape
    queries = tokens * LINE
    length = queries * CTX
    heads = wq.shape[1] // HD
    plane = shards * CTX
    full = [struct((width, w.shape[1]), bf16) for w in weights_in]
    outs = full + [
        struct((queries, width), bf16),
        struct((queries, width), bf16),
        struct((queries, width), bf16),
        struct((tokens, width), f32),
        struct((heads, 2 * HD, queries), bf16),
        struct((length, 2 * HD), bf16),
        struct((CTX, 2 * HD, queries), bf16),
        struct((heads * HD, queries), bf16),
        struct((queries, width), bf16),
        struct((heads, 1, queries), f32),
        struct((2, width), f32),
        struct((HD // 2, queries), f32),
        struct((HD // 2, queries), f32),
    ]
    block = (LINE - 1, tokens, width)
    count = 6 + 18 * PIECES + 6 * (4 + 4 * (shards - 1)) + plane - 1 + 21
    return pl.pallas_call(
        functools.partial(forward_kernel, shards),
        out_shape=outs,
        in_specs=[any_spec()] * 8
        + [vmem_spec()] * 2
        + [pl.BlockSpec(memory_space=pltpu.SMEM)],
        out_specs=[any_spec()] * 15 + [vmem_spec()] * 4,
        scratch_shapes=[
            pltpu.VMEM((queries, width), bf16),
            pltpu.VMEM((queries, width), bf16),
            pltpu.VMEM((width, wq.shape[1]), bf16),
            pltpu.VMEM((width, wkv.shape[1]), bf16),
            pltpu.VMEM((width, wo.shape[1]), bf16),
            pltpu.VMEM((plane, 2, width), f32),
            pltpu.VMEM((heads, 2 * HD, queries), bf16),
            pltpu.VMEM((CTX, 2 * HD, queries), bf16),
            pltpu.VMEM((length, 2 * HD), bf16),
            pltpu.VMEM((HD, length), bf16),
            pltpu.VMEM((length, queries // 2), f32),
            pltpu.VMEM((length, queries // 2), bf16),
            pltpu.VMEM((heads * HD, queries), bf16),
            pltpu.VMEM((queries, width), f32),
            pltpu.VMEM(block, bf16),
            pltpu.VMEM(block, bf16),
            pltpu.VMEM((tokens, width), f32),
            pltpu.VMEM((tokens, width), bf16),
            pltpu.VMEM((tokens, width), bf16),
            pltpu.VMEM(wg.shape, bf16),
            pltpu.VMEM(wu.shape, bf16),
            pltpu.VMEM(wd.shape, bf16),
            pltpu.VMEM((2, width), f32),
            pltpu.SemaphoreType.DMA((count,)),
            pltpu.SemaphoreType.DMA((count,)),
            pltpu.SemaphoreType.DMA((32,)),
        ],
        compiler_params=pltpu.CompilerParams(
            collective_id=0, has_side_effects=True, vmem_limit_bytes=60 * 2**20
        ),
        name="forward",
    )(x, og, wq, wkv, wo, wg, wu, wd, gain_in, frequency, order)


def middle_kernel(
    shards, rows,
    n2_in, og_in, wg_in, wu_in, wd_in, mid_in, gains,
    dmid_o, dmid_all_o, gg_o, gd_part_o, gd_x_o, gd_y_o, branch_o, gu_part_o, gain_sum,
    n2, og, wg, wu, wd, mid, hidden, dgate, dup, part, branch,
    left, right, dmid, dsend, gain_rows, up_in,
    *rest,
):
    grads, (send_sems, recv_sems, local_sems) = rest[:-3], rest[-3:]
    tokens, width = mid.shape
    queries = n2.shape[0]
    columns = wg.shape[1]
    links = Links(shards, send_sems, recv_sems, local_sems)
    t = links.t
    links.greet()
    own_rows = pl.ds(pl.multiple_of(place(t) * tokens, tokens), tokens)

    far = pl.multiple_of(jnp.where(t < LINE // 2, tokens, 0), tokens)
    near = pl.multiple_of(jnp.where(t < LINE // 2, 0, tokens), tokens)
    sides = [pl.ds(far, tokens), pl.ds(2 * tokens, 2 * tokens), pl.ds(near, tokens)]
    full, rest_columns = columns // 256, columns % 256
    weights = ((wg_in, wg), (wu_in, wu), (wd_in, wd))

    def fetch(j, start, size, index):
        src, dst = weights[j]
        of = pl.ds(start, size)
        sem = local_sems.at[3 * index + j]
        return pltpu.make_async_copy(src.at[:, of], dst.at[:, of], sem)

    links.local_used = 3 * (full + 1)
    load_n2 = [links.keep(n2_in.at[sides[0]], n2.at[sides[0]])]
    for index in range(full):
        for j in range(3):
            fetch(j, index * 256, 256, index).start()
        if index == 0:
            load_og = [links.keep(og_in.at[sides[0]], og.at[sides[0]])]
    if rest_columns:
        for j in range(3):
            fetch(j, full * 256, rest_columns, full).start()
    load_n2 += [links.keep(n2_in.at[at], n2.at[at]) for at in sides[1:]]
    load_og += [links.keep(og_in.at[at], og.at[at]) for at in sides[1:]]
    load_mid = links.keep(mid_in, mid)
    scatter = LineScatter(links, part, tokens, left, right, PIECES)
    gather = LineGather(links, dsend, dmid_all_o, tokens, PIECES)
    down = PlaneScatter(links, og, hidden, rows, *grads[0:6])
    gate = PlaneScatter(links, n2, dgate, rows, *grads[6:12])
    up = PlaneScatter(links, n2, dup, rows, up_in, None, None, None, None, None)

    def feed_forward(half):
        at = sides[half]
        load_n2[half].wait()
        load_og[half].wait()

        def tile(start, size, index):
            of = pl.ds(start, size)
            if half == 0:
                fetch(0, start, size, index).wait()
                fetch(1, start, size, index).wait()
            gate_act = nn_dot(n2[at, :], wg[:, of])
            up_act = nn_dot(n2[at, :], wu[:, of])
            if half == 0:
                fetch(2, start, size, index).wait()
            d_hidden = nn_dot(og[at, :], wd[:, of])
            sig = jax.nn.sigmoid(gate_act)
            silu = gate_act * sig
            hidden[at, of] = (silu * up_act).astype(bf16)
            d_gate = d_hidden * up_act * sig * (1.0 + gate_act * (1.0 - sig))
            dgate[at, of] = d_gate.astype(bf16)
            dup[at, of] = (d_hidden * silu).astype(bf16)

        @pl.loop(0, full)
        def _(index):
            tile(pl.multiple_of(index * 256, 256), 256, index)

        if rest_columns:
            tile(full * 256, rest_columns, full)

        @pl.loop(0, width // 512)
        def _(j):
            of = pl.ds(pl.multiple_of(j * 512, 512), 512)
            summed = nt_dot(dgate[at, :], wg[of, :]) + nt_dot(dup[at, :], wu[of, :])
            part[at, of] = summed.astype(bf16)

    piece = CTX * rows

    def others(grad, room):
        for step in range(1, shards):
            grad.other(step, room.at[pl.ds((step - 1) * piece, piece)])

    feed_forward(0)
    links.met()
    line_ends(scatter, 0)
    feed_forward(1)
    line_ends(scatter, 1, 2)
    line_steps(scatter, 1)
    feed_forward(2)
    others(gate, wg)
    line_steps(scatter, 2)

    @pl.loop(0, width // 512)
    def _(j):
        of = pl.ds(pl.multiple_of(j * 512, 512), 512)
        branch[:, of] = nt_dot(hidden[...], wd[of, :]).astype(bf16)

    links.keep_later(branch, branch_o)
    gate.own()
    gate.exchange()
    others(down, wd)
    load_mid.wait()
    gain_rows[...] = jnp.zeros_like(gain_rows)

    def finish_rows(r, d_normed):
        at = pl.ds(r, ROWS)
        q = pl.ds(pl.multiple_of(place(t) * tokens + r, ROWS), ROWS)
        middle = mid[at, :]
        inverse = lax.rsqrt(jnp.mean(middle * middle, -1, keepdims=True) + epsilon)
        unit = middle * inverse
        gain_rows[...] += d_normed * unit
        d_unit = d_normed * gains[1:2, :]
        back = inverse * (d_unit - unit * jnp.mean(d_unit * unit, -1, keepdims=True))
        d_middle = og[q, :].astype(f32) + back
        dmid[at, :] = d_middle
        dsend[at, :] = d_middle.astype(bf16)

    line_finish(scatter, finish_rows, gather)
    gate.fold()
    down.own()
    down.exchange()
    links.keep_later(dsend, dmid_all_o.at[own_rows])
    links.keep_later(dmid, dmid_o)
    links.keep_later(down.core_in.at[0], gd_part_o)
    line_spread(gather, 1)
    others(up, wu)
    gain_sum[...] = jnp.sum(gain_rows[...], 0, keepdims=True)
    line_spread(gather, 2)
    up.own()
    links.keep_later(up_in.at[0], gu_part_o)
    gate.total()
    links.keep_later(gate.out, gg_o)
    line_spread(gather, 3)
    down.arrived()
    links.keep_later(down.x_in, gd_x_o)
    links.keep_later(down.y_in, gd_y_o)
    links.finish()


def middle_call(shards, rows, n2, og, wg, wu, wd, mid, gains):
    queries, width = n2.shape
    tokens = mid.shape[0]
    columns = wg.shape[1]
    token = (tokens, width)
    wide = (queries, columns)
    block = (LINE - 1,) + token
    outs = [
        struct(token, f32),
        struct((queries, width), bf16),
        struct((rows, columns), f32),
        struct((CTX * rows, columns), bf16),
        struct((2, rows // 2, columns), bf16),
        struct((2, rows // 2, columns), bf16),
        struct((queries, width), bf16),
        struct((CTX * rows, columns), bf16),
        struct((1, width), f32),
    ]
    count = 12 * PIECES + 3 * (shards - 1 + 6)
    return pl.pallas_call(
        functools.partial(middle_kernel, shards, rows),
        out_shape=outs,
        in_specs=[any_spec()] * 6 + [vmem_spec()],
        out_specs=[any_spec()] * 8 + [vmem_spec()],
        scratch_shapes=[
            pltpu.VMEM((queries, width), bf16),
            pltpu.VMEM((queries, width), bf16),
            pltpu.VMEM((width, columns), bf16),
            pltpu.VMEM((width, columns), bf16),
            pltpu.VMEM((width, columns), bf16),
            pltpu.VMEM(token, f32),
            pltpu.VMEM(wide, bf16),
            pltpu.VMEM(wide, bf16),
            pltpu.VMEM(wide, bf16),
            pltpu.VMEM((queries, width), bf16),
            pltpu.VMEM((queries, width), bf16),
            pltpu.VMEM(block, bf16),
            pltpu.VMEM(block, bf16),
            pltpu.VMEM(token, f32),
            pltpu.VMEM(token, bf16),
            pltpu.VMEM((ROWS, width), f32),
            pltpu.VMEM((shards - 1, CTX * rows, columns), bf16),
            *PlaneScatter.scratch(shards, rows, columns),
            *PlaneScatter.scratch(shards, rows, columns),
            pltpu.SemaphoreType.DMA((count,)),
            pltpu.SemaphoreType.DMA((count,)),
            pltpu.SemaphoreType.DMA((40,)),
        ],
        compiler_params=pltpu.CompilerParams(
            collective_id=1, has_side_effects=True, vmem_limit_bytes=63 * 2**20
        ),
        name="middle",
    )(n2, og, wg, wu, wd, mid, gains)


def backward_kernel(
    shards, rows,
    dmid_all_in, wo_in, wq_in, wkv_in, n1_in, qaug_in, kaug_in, kv_in, att_in, x_in, dmid_in,
    branch_in, gu_part_in, gd_part_in, gd_x_in, gd_y_in, mid_in, lse, gains, gain_mlp, cos, sin,
    in_o, gq_o, gkv_o, go_o, gu_o, gd_o, out_o, gain_o,
    dmid_all, wo, wq, wkv, n1, qaug, kaug, kv, att, x, dmid,
    d_out, attn_rows, v_rows, d_keys, d_values, d_query, d_query_rows, kv_send, kv_recv, d_kv, part,
    left, right, gain_rows, pair, plane_in, line_in, total, stage_o, stage_q, stage_kv,
    branch, left_b, right_b, mid, layer, gain_sum, part_query,
    *rest,
):
    grads, (send_sems, recv_sems, local_sems) = rest[:-3], rest[-3:]
    tokens, width = dmid.shape
    queries = n1.shape[0]
    heads = qaug.shape[0]
    length = kaug.shape[0]
    half = HD // 2
    plane = shards * CTX
    links = Links(shards, send_sems, recv_sems, local_sems)
    s, c, t = links.s, links.c, links.t
    links.greet(whole_line=True)

    scatter = LineScatter(links, part, tokens, left, right, PIECES)
    scatter_out = LineScatter(links, branch, tokens, left_b, right_b)
    g_o = PlaneScatter(links, dmid_all, attn_rows, rows, *grads[0:6])
    g_q = PlaneScatter(links, n1, d_query_rows, rows, *grads[6:12])
    g_kv = PlaneScatter(links, n1, d_kv, rows, *grads[12:18])
    g_u = PlaneScatter(links, None, None, rows, *grads[18:24])
    g_d = PlaneScatter(links, None, None, rows, *grads[24:30])
    kv_slot = links.slots(CTX - 1)
    plane_slot = links.slots(plane - 1)
    line_slot = links.slots(LINE - 1)
    piece = CTX * rows
    loads = [
        links.keep(src, dst)
        for src, dst in (
            (dmid_all_in, dmid_all), (wo_in, wo), (branch_in, branch), (gu_part_in, g_u.core_in.at[0]),
            (att_in, att), (kv_in, kv), (qaug_in, qaug), (kaug_in, kaug),
            (gd_part_in, g_d.core_in.at[0]), (gd_x_in, g_d.x_in), (gd_y_in, g_d.y_in), (n1_in, n1),
            (wq_in, wq), (wkv_in, wkv), (x_in, x), (dmid_in, dmid), (mid_in, mid),
        )
    ]

    def others(grad, stage):
        for step in range(1, shards):
            grad.other(step, stage.at[pl.ds((step - 1) * piece, piece)])

    for load in loads[0:2]:
        load.wait()
    d_out[...] = nn_dot(dmid_all[...], wo[...]).astype(bf16).T
    links.met()
    loads[2].wait()
    line_ends(scatter_out, 0)
    loads[3].wait()
    g_u.exchange()
    for load in loads[4:8]:
        load.wait()
    for other in range(CTX):
        v_rows[other * queries : (other + 1) * queries, :] = kv[other, HD : 2 * HD, :].T
    d_keys[...] = jnp.zeros_like(d_keys)
    d_values[...] = jnp.zeros_like(d_values)

    def head(h):
        at = pl.ds(pl.multiple_of(h * HD, HD), HD)
        query = qaug[h]
        d_head = d_out[at, :]
        delta = jnp.sum(d_head.astype(f32) * att[at, :].astype(f32), 0, keepdims=True)
        log_sum = lse[h]
        d_q = jnp.zeros((HD, queries), f32)
        for b in range(0, length, BLOCK):
            e = b + BLOCK
            probs = jnp.exp(nn_dot(kaug[b:e, :], query) - log_sum)
            d_probs = nn_dot(v_rows[b:e, :], d_head)
            d_scores = (probs * (d_probs - delta)).astype(bf16)
            d_values[b:e, :] += nt_dot(probs.astype(bf16), d_head)
            d_keys[b:e, :] += nt_dot(d_scores, query[0:HD])
            at_b = b % queries
            d_q = d_q + nn_dot(kv[b // queries, 0:HD, at_b : at_b + BLOCK], d_scores)
        d_query[at, :] = d_q * (HD ** (-0.5))

    pl.loop(0, heads // 2)(head)
    line_ends(scatter_out, 1, 2)
    scatter_out.stage(1)
    for load in loads[8:11]:
        load.wait()
    g_d.fold(here=True)
    pl.loop(heads // 2, heads)(head)

    def pack(other):
        block = pl.ds(pl.multiple_of(other * queries, queries), queries)
        both = jnp.concatenate([d_keys[block, :], d_values[block, :]], 1)
        kv_send[other] = both.astype(bf16)

    for step in range(1, CTX):
        peer = lax.rem(c + step, CTX)
        pack(peer)
        links.send(kv_send.at[peer], kv_recv.at[step - 1], (s, peer, t), kv_slot + step - 1)
    pack(c)
    scatter_out.stage(2)
    for load in loads[11:]:
        load.wait()

    cosine, sine = cos[...], sin[...]
    for h in range(heads):
        at = h * HD
        d1, d2 = d_query[at : at + half, :], d_query[at + half : at + HD, :]
        d_query[at : at + half, :] = d1 * cosine + d2 * sine
        d_query[at + half : at + HD, :] = d2 * cosine - d1 * sine
    d_query_rows[...] = d_query[...].astype(bf16).T
    for b in range(0, width, 512):
        part_query[:, b : b + 512] = nt_dot(d_query_rows[...], wq[b : b + 512, :])
    others(g_q, stage_q)
    attn_rows[...] = att[...].T
    others(g_o, stage_o)
    for step in range(1, CTX):
        links.recv(kv_recv.at[step - 1], kv_slot + step - 1)
    d_pair = kv_send[c].astype(f32)
    for step in range(1, CTX):
        d_pair = d_pair + kv_recv[step - 1].astype(f32)
    d_pair = d_pair.T
    d1, d2 = d_pair[0:half], d_pair[half:HD]
    turned = jnp.concatenate(
        [d1 * cosine + d2 * sine, d2 * cosine - d1 * sine, d_pair[HD:]], 0
    )
    d_kv[...] = turned.astype(bf16).T

    for b in range(0, width, 512):
        summed = part_query[:, b : b + 512] + nt_dot(d_kv[...], wkv[b : b + 512, :])
        part[:, b : b + 512] = summed.astype(bf16)

    line_ends(scatter, 0, 1)

    gain_rows[...] = jnp.zeros_like(gain_rows)

    @pl.loop(0, queries // ROWS)
    def _(i):
        r = pl.ds(pl.multiple_of(i * ROWS, ROWS), ROWS)
        v = x[r, :].astype(f32)
        inverse = lax.rsqrt(jnp.mean(v * v, -1, keepdims=True) + epsilon)
        gain_rows[...] += part[r, :].astype(f32) * (v * inverse)

    pair[0:1, :] = jnp.sum(gain_rows[...], 0, keepdims=True)
    pair[1:2, :] = gain_mlp[...]
    for step in range(1, plane):
        links.send(pair, plane_in.at[step - 1], links.plane_peer(step), plane_slot + step - 1)
    g_u.fold()
    line_steps(scatter, 1)
    g_o.own()
    g_o.exchange()
    summed = pair[...]
    for step in range(1, plane):
        links.recv(plane_in.at[step - 1], plane_slot + step - 1)
        summed = summed + plane_in[step - 1]
    total[...] = summed
    for step in range(1, LINE):
        links.send(total, line_in.at[step - 1], links.line_peer(step), line_slot + step - 1)
    line_ends(scatter, 2)
    others(g_kv, stage_kv)
    g_q.own()
    g_q.exchange()
    line_steps(scatter, 2)
    g_kv.own()
    g_kv.exchange()
    g_o.fold()
    scatter_out.arrive()

    def layer_rows(r, total_rows):
        layer[pl.ds(r, ROWS), :] = (mid[pl.ds(r, ROWS), :] + total_rows).astype(bf16)

    scatter_out.owned(0, layer_rows)
    links.keep_later(layer, out_o)
    g_q.fold()
    g_kv.fold()
    g_u.total()
    links.keep_later(g_u.out, gu_o)
    g_o.total()
    links.keep_later(g_o.out, go_o)
    g_d.total(here=True)
    links.keep_later(g_d.out, gd_o)

    def finish_rows(r, d_normed):
        at = pl.ds(r, ROWS)
        q = pl.ds(pl.multiple_of(place(t) * tokens + r, ROWS), ROWS)
        v = x[q, :].astype(f32)
        inverse = lax.rsqrt(jnp.mean(v * v, -1, keepdims=True) + epsilon)
        unit = v * inverse
        d_unit = d_normed * gains[0:1, :]
        back = inverse * (d_unit - unit * jnp.mean(d_unit * unit, -1, keepdims=True))
        dmid[at, :] = dmid[at, :] + back

    scatter.arrive(0)
    scatter.owned(0, finish_rows)
    g_q.total()
    links.keep_later(g_q.out, gq_o)
    g_kv.total()
    links.keep_later(g_kv.out, gkv_o)
    for p in range(1, PIECES):
        scatter.arrive(p)
        scatter.owned(p, finish_rows)
    links.keep_later(dmid, in_o)
    for step in range(1, LINE):
        links.recv(line_in.at[step - 1], line_slot + step - 1)
        summed = summed + line_in[step - 1]
    own_gains = gain_o.shape[1]
    if own_gains == width:
        gain_o[...] = summed
    else:
        gain_sum[...] = summed
        me = s * CTX + c
        gain_o[...] = gain_sum[:, pl.ds(pl.multiple_of(me * own_gains, own_gains), own_gains)]
    links.finish()


def backward_call(
    shards, rows, dmid_all, wo, wq, wkv, n1, qaug, kaug, kv, att, x, dmid, branch, gu_part,
    gd_part, gd_x, gd_y, mid, lse, gains, gain_mlp, cos, sin,
):
    tokens, width = dmid.shape
    queries = n1.shape[0]
    heads = qaug.shape[0]
    length = kaug.shape[0]
    inner = heads * HD
    columns = gu_part.shape[1]
    plane = shards * CTX
    own_gains = width // plane if width // plane % 128 == 0 else width
    piece = CTX * rows * (shards - 1)
    token = (tokens, width)
    block = (LINE - 1,) + token
    outs = [
        struct(token, f32),
        struct((rows, inner), f32),
        struct((rows, 2 * HD), f32),
        struct((rows, inner), f32),
        struct((rows, columns), f32),
        struct((rows, columns), f32),
        struct(token, bf16),
        struct((2, own_gains), f32),
    ]
    count = 6 + 6 * PIECES + 5 * (shards - 1 + 6) + CTX - 1 + plane - 1 + LINE - 1
    return pl.pallas_call(
        functools.partial(backward_kernel, shards, rows),
        out_shape=outs,
        in_specs=[any_spec()] * 17 + [vmem_spec()] * 5,
        out_specs=[any_spec()] * 7 + [vmem_spec()],
        scratch_shapes=[
            pltpu.VMEM((queries, width), bf16),
            pltpu.VMEM((width, inner), bf16),
            pltpu.VMEM((width, inner), bf16),
            pltpu.VMEM((width, 2 * HD), bf16),
            pltpu.VMEM((queries, width), bf16),
            pltpu.VMEM(qaug.shape, bf16),
            pltpu.VMEM(kaug.shape, bf16),
            pltpu.VMEM(kv.shape, bf16),
            pltpu.VMEM((inner, queries), bf16),
            pltpu.VMEM((queries, width), bf16),
            pltpu.VMEM(token, f32),
            pltpu.VMEM((inner, queries), bf16),
            pltpu.VMEM((queries, inner), bf16),
            pltpu.VMEM((length, HD), bf16),
            pltpu.VMEM((length, HD), f32),
            pltpu.VMEM((length, HD), f32),
            pltpu.VMEM((inner, queries), f32),
            pltpu.VMEM((queries, inner), bf16),
            pltpu.VMEM((CTX, queries, 2 * HD), bf16),
            pltpu.VMEM((CTX - 1, queries, 2 * HD), bf16),
            pltpu.VMEM((queries, 2 * HD), bf16),
            pltpu.VMEM((queries, width), bf16),
            pltpu.VMEM(block, bf16),
            pltpu.VMEM(block, bf16),
            pltpu.VMEM((ROWS, width), f32),
            pltpu.VMEM((2, width), f32),
            pltpu.VMEM((plane - 1, 2, width), f32),
            pltpu.VMEM((LINE - 1, 2, width), f32),
            pltpu.VMEM((2, width), f32),
            pltpu.VMEM((piece, inner), bf16),
            pltpu.VMEM((piece, inner), bf16),
            pltpu.VMEM((piece, 2 * HD), bf16),
            pltpu.VMEM((queries, width), bf16),
            pltpu.VMEM(block, bf16),
            pltpu.VMEM(block, bf16),
            pltpu.VMEM(token, f32),
            pltpu.VMEM(token, bf16),
            pltpu.VMEM((2, width), f32),
            pltpu.VMEM((queries, width), f32),
            *PlaneScatter.scratch(shards, rows, inner),
            *PlaneScatter.scratch(shards, rows, inner),
            *PlaneScatter.scratch(shards, rows, 2 * HD),
            *PlaneScatter.scratch(1 + 1, rows, columns),
            *PlaneScatter.scratch(1 + 1, rows, columns),
            pltpu.SemaphoreType.DMA((count,)),
            pltpu.SemaphoreType.DMA((count,)),
            pltpu.SemaphoreType.DMA((32,)),
        ],
        compiler_params=pltpu.CompilerParams(
            collective_id=2, has_side_effects=True, vmem_limit_bytes=60 * 2**20
        ),
        name="backward",
    )(
        dmid_all, wo, wq, wkv, n1, qaug, kaug, kv, att, x, dmid, branch, gu_part,
        gd_part, gd_x, gd_y, mid, lse, gains, gain_mlp, cos, sin,
    )


def finish_kernel(gains, layer_in, *refs):
    count = (len(refs) - 2) // 2
    layer_out = refs[count]
    layer_out[0] = layer_in[...]
    refs[count + 1][0] = refs[0][...]
    for src, dst in zip(refs[1:count], refs[count + 2 : -2]):
        dst[...] = src[...]
    for row, dst in enumerate(refs[-2:]):
        dst[...] = gains[row : row + 1, :]


def finish_call(arrays, gains, steps=2):
    rows = [array.shape[0] // steps for array in arrays]
    wide = [array.shape[1] for array in arrays]
    own = gains.shape[1]
    shapes = [struct((1,) * (i < 2) + array.shape, array.dtype) for i, array in enumerate(arrays)]
    return pl.pallas_call(
        finish_kernel,
        grid=(steps,),
        out_shape=shapes + [struct((1, own), f32)] * 2,
        in_specs=[pl.BlockSpec((2, own), lambda i: (0, 0))]
        + [pl.BlockSpec((r, n), lambda i: (i, 0)) for r, n in zip(rows, wide)],
        out_specs=[
            pl.BlockSpec((1, r, n), lambda i: (0, i, 0))
            if index < 2
            else pl.BlockSpec((r, n), lambda i: (i, 0))
            for index, (r, n) in enumerate(zip(rows, wide))
        ]
        + [pl.BlockSpec((1, own), lambda i: (0, 0))] * 2,
        compiler_params=pltpu.CompilerParams(vmem_limit_bytes=60 * 2**20),
        name="finish",
    )(gains, *arrays)


def body(
    inputs, out_grad, block_order, gain_attn, w_query, w_keyval, w_output, gain_mlp, w_gate, w_up, w_down
):
    shards = lax.axis_size("shard")
    x, og = inputs[0], out_grad[0]
    tokens, width = x.shape
    s, c = lax.axis_index("shard"), lax.axis_index("ctx")
    frequency = np.float32(10000.0) ** (-np.arange(HD // 2, dtype=np.float32)[:, None] * 2.0 / HD)
    own = gain_attn.shape[0]
    start = (s * CTX + c) * own
    row = lax.broadcasted_iota(jnp.int32, (2, own), 0)
    gain_in = jnp.where(row == 0, gain_attn, gain_mlp)
    aligned = own % 128 == 0
    if not aligned:
        gain_in = lax.dynamic_update_slice(jnp.zeros((2, width), bf16), gain_in, (0, start))
    (wq, wkv, wo, wg, wu, wd, n1, og_all, n2, mid, qaug, kaug, kv, att, x_all, lse, gains, cos, sin) = forward_call(
        shards, x, og, (w_query, w_keyval, w_output, w_gate, w_up, w_down), gain_in,
        jnp.asarray(frequency, f32), block_order[0],
    )
    (dmid, dmid_all, grad_gate, gd_part, gd_x, gd_y, branch, gu_part, gm) = middle_call(
        shards, w_gate.shape[0], n2, og_all, wg, wu, wd, mid, gains
    )
    (input_grad, grad_query, grad_keyval, grad_output, grad_up, grad_down, layer_out, both) = backward_call(
        shards, w_query.shape[0], dmid_all, wo, wq, wkv, n1, qaug, kaug, kv, att, x_all, dmid,
        branch, gu_part, gd_part, gd_x, gd_y, mid, lse, gains, gm, cos, sin,
    )
    if not aligned:
        both = lax.dynamic_slice(both, (0, start), (2, own))
    (
        layer_out, input_grad, grad_query, grad_keyval, grad_output, grad_gate, grad_up, grad_down,
        *gain_grads,
    ) = finish_call([
        layer_out, input_grad, grad_query, grad_keyval, grad_output, grad_gate, grad_up, grad_down,
    ], both)
    return (
        layer_out, input_grad, gain_grads[0][0], grad_query, grad_keyval, grad_output,
        gain_grads[1][0], grad_gate, grad_up, grad_down,
    )


def solution(mesh):
    plane = P(("shard", "ctx"), "tensor")
    gain = P(("shard", "ctx"))
    token = P("shard", ("ctx", "tensor"), None)
    return jax.shard_map(
        body,
        mesh=mesh,
        in_specs=(token, token, P("shard", None), gain, plane, plane, plane, gain, plane, plane, plane),
        out_specs=(token, token, gain, plane, plane, plane, gain, plane, plane, plane),
        check_vma=False,
    )
```

```python
import functools

import jax
import jax.numpy as jnp
import numpy as np
from jax import lax
from jax.experimental import pallas as pl
from jax.experimental.pallas import tpu as pltpu
from jax.sharding import PartitionSpec as P

HD = 64
BLOCK = 256
BLOCKS = 8
ROWS = 16
CTX = 4
LINE = 4
PIECES = 2

epsilon = 1e-05
blocked = -1e30

f32 = jnp.float32
bf16 = jnp.bfloat16
MESH = pl.DeviceIdType.MESH


def place(owner):
    return (owner + (owner + 1) // 2) % LINE if isinstance(owner, int) else lax.rem(
        owner + (owner + 1) // 2, LINE
    )


def nn_dot(left, right):
    return jnp.dot(left, right, preferred_element_type=f32)


def nt_dot(left, right):
    return lax.dot_general(left, right, (((1,), (1,)), ((), ())), preferred_element_type=f32)


def tn_dot(left, right):
    return lax.dot_general(left, right, (((0,), (0,)), ((), ())), preferred_element_type=f32)


class Links:
    def __init__(self, shards, send_sems, recv_sems, local_sems):
        self.shards = shards
        self.send_sems, self.recv_sems, self.local_sems = send_sems, recv_sems, local_sems
        self.s = lax.axis_index("shard")
        self.c = lax.axis_index("ctx")
        self.t = lax.axis_index("tensor")
        self.c_x = self.c + 1 - 2 * lax.rem(self.c, 2)
        self.c_y = lax.rem(self.c + 2, CTX)
        self.c_d = CTX - 1 - self.c
        self.x_dev = (self.s, self.c_x, self.t)
        self.y_dev = (self.s, self.c_y, self.t)
        self.right = (self.s, self.c, self.t + 1)
        self.left = (self.s, self.c, self.t - 1)
        self.used = 0
        self.local_used = 0
        self.sends = []
        self.locals = []

    def slots(self, count):
        first = self.used
        self.used += count
        assert self.used <= self.send_sems.shape[0]
        return first

    def plane_peer(self, step):
        index = lax.rem(self.s * CTX + self.c + step, self.shards * CTX)
        return (index // CTX, lax.rem(index, CTX), self.t)

    def core_peer(self, step):
        return (lax.rem(self.s + step, self.shards), self.c, self.t)

    def line_peer(self, step):
        return (self.s, self.c, lax.rem(self.t + step, LINE))

    def greet(self, whole_line=False):
        sem = pltpu.get_barrier_semaphore()
        count = self.shards * CTX - 1
        for step in range(1, count + 1):
            pl.semaphore_signal(
                sem, inc=1, device_id=self.plane_peer(step), device_id_type=MESH
            )
        if whole_line:
            for step in range(1, LINE):
                pl.semaphore_signal(
                    sem, inc=1, device_id=self.line_peer(step), device_id_type=MESH
                )
            self.partners = count + LINE - 1
            return

        @pl.when(self.t > 0)
        def _():
            pl.semaphore_signal(sem, inc=1, device_id=self.left, device_id_type=MESH)

        @pl.when(self.t < LINE - 1)
        def _():
            pl.semaphore_signal(sem, inc=1, device_id=self.right, device_id_type=MESH)

        beside = (self.t + LINE - 1) // LINE + (2 * LINE - 2 - self.t) // LINE
        self.partners = count + beside

    def met(self):
        pl.semaphore_wait(pltpu.get_barrier_semaphore(), self.partners)

    def copy(self, src, dst, device, slot):
        return pltpu.make_async_remote_copy(
            src_ref=src,
            dst_ref=dst,
            send_sem=self.send_sems.at[slot],
            recv_sem=self.recv_sems.at[slot],
            device_id=device,
            device_id_type=MESH,
        )

    def send(self, src, dst, device, slot, cond=None):
        if cond is None:
            self.copy(src, dst, device, slot).start()
        else:

            @pl.when(cond)
            def _():
                self.copy(src, dst, device, slot).start()

        handle = (src, dst, device, slot, cond)
        self.sends.append(handle)
        return handle

    def sent(self, handle):
        self.sends = [other for other in self.sends if other is not handle]
        self.copy(*handle[:4]).wait_send()

    def recv(self, dst, slot):
        self.copy(dst, dst, self.x_dev, slot).wait_recv()

    def keep(self, src, dst):
        copy = pltpu.make_async_copy(src, dst, self.local_sems.at[self.local_used])
        self.local_used += 1
        assert self.local_used <= self.local_sems.shape[0]
        copy.start()
        return copy

    def keep_later(self, src, dst):
        self.locals.append(self.keep(src, dst))

    def finish(self):
        for src, dst, device, slot, cond in self.sends:
            if cond is None:
                self.copy(src, dst, device, slot).wait_send()
            else:

                @pl.when(cond)
                def _():
                    self.copy(src, dst, device, slot).wait_send()

        for copy in self.locals:
            copy.wait()


class PlaneGather:
    def __init__(self, links, src, full, stage=None):
        self.links, self.src, self.full, self.stage = links, src, full, stage
        self.rows = src.shape[0]
        self.first = links.slots(4 + 4 * (links.shards - 1))

    def block(self, s, c):
        start = pl.multiple_of((s * CTX + c) * self.rows, self.rows)
        return self.full.at[pl.ds(start, self.rows)]

    def half(self, s, c, which):
        size = self.rows // 2
        start = pl.multiple_of((s * CTX + c) * self.rows + which * size, size)
        return self.full.at[pl.ds(start, size)]

    def core_slot(self, step, part):
        return self.first + 4 + (step - 1) * 4 + part

    def core_send(self, src, c, part):
        links = self.links
        for step in range(1, links.shards):
            links.send(
                src,
                self.block(links.s, c),
                links.core_peer(step),
                self.core_slot(step, part),
            )

    def start(self):
        links = self.links
        own = self.block(links.s, links.c)
        links.send(self.src, own, links.x_dev, self.first)
        links.send(self.src, own, links.y_dev, self.first + 1)
        self.core_send(self.src, links.c, 0)
        self.local = links.keep(self.src, own if self.stage is None else self.stage)

    def settle(self):
        self.local.wait()
        self.local = self.links.keep(self.stage, self.block(self.links.s, self.links.c))

    def forward(self):
        links = self.links
        links.recv(self.block(links.s, links.c_x), self.first)
        links.recv(self.block(links.s, links.c_y), self.first + 1)
        from_x = self.half(links.s, links.c_x, 0)
        from_y = self.half(links.s, links.c_y, 1)
        links.send(from_x, from_x, links.y_dev, self.first + 2)
        links.send(from_y, from_y, links.x_dev, self.first + 3)
        self.core_send(self.block(links.s, links.c_x), links.c_x, 1)
        self.core_send(self.block(links.s, links.c_y), links.c_y, 2)

    def diagonal(self):
        links = self.links
        links.recv(self.half(links.s, links.c_d, 0), self.first + 2)
        links.recv(self.half(links.s, links.c_d, 1), self.first + 3)
        self.core_send(self.block(links.s, links.c_d), links.c_d, 3)

    def done(self):
        links = self.links
        for step in range(1, links.shards):
            other = lax.rem(links.s + links.shards - step, links.shards)
            for part, c in enumerate((links.c, links.c_x, links.c_y, links.c_d)):
                links.recv(self.block(other, c), self.core_slot(step, part))
        self.local.wait()


class LineGather:
    def __init__(self, links, own, full, tokens, pieces=1):
        self.links, self.own, self.full, self.tokens = links, own, full, tokens
        self.pieces, self.size = pieces, tokens // pieces
        self.first = links.slots(2 * (LINE - 1) * pieces)

    def block(self, owner, p):
        start = pl.multiple_of(place(owner) * self.tokens + p * self.size, self.size)
        return self.full.at[pl.ds(start, self.size)]

    def slot(self, side, k, p):
        return self.first + (side * (LINE - 1) + k - 1) * self.pieces + p

    def send(self, k, p=0):
        links = self.links
        t, u = links.t, LINE - 1 - links.t
        own = self.own.at[pl.ds(p * self.size, self.size)]
        right, left = self.block(t - k + 1, p), self.block(t + k - 1, p)
        links.send(
            own if k == 1 else right,
            right,
            links.right,
            self.slot(0, k, p),
            jnp.logical_and(t >= k - 1, t < LINE - 1),
        )
        links.send(
            own if k == 1 else left,
            left,
            links.left,
            self.slot(1, k, p),
            jnp.logical_and(u >= k - 1, u < LINE - 1),
        )

    def recv(self, k, p=0):
        links = self.links
        t, u = links.t, LINE - 1 - links.t

        @pl.when(t >= k)
        def _():
            links.recv(self.block(t - k, p), self.slot(0, k, p))

        @pl.when(u >= k)
        def _():
            links.recv(self.block(t + k, p), self.slot(1, k, p))


class LineScatter:
    def __init__(self, links, part, tokens, from_left, from_right, pieces=1):
        self.links, self.part, self.tokens = links, part, tokens
        self.from_left, self.from_right = from_left, from_right
        self.pieces, self.size = pieces, tokens // pieces
        self.first = links.slots(2 * (LINE - 1) * pieces)

    def slot(self, side, k, p):
        return self.first + (side * (LINE - 1) + k) * self.pieces + p

    def piece(self, ref, k, p):
        return ref.at[k, pl.ds(p * self.size, self.size)]

    def total(self, owner, k, p, arrived):
        @pl.loop(0, self.size // ROWS)
        def _(i):
            r = pl.multiple_of(p * self.size + i * ROWS, ROWS)
            q = pl.multiple_of(place(owner) * self.tokens + p * self.size + i * ROWS, ROWS)
            mine = self.part[pl.ds(q, ROWS), :].astype(f32)
            summed = mine + arrived[k, pl.ds(r, ROWS), :].astype(f32)
            arrived[k, pl.ds(r, ROWS), :] = summed.astype(arrived.dtype)

    def ends(self, k, p=0):
        links = self.links
        for side, behind, arrived, device in self.sides():
            owner = LINE - 1 - k if side == 0 else k
            piece, slot = self.piece(arrived, k, p), self.slot(side, k, p)

            @pl.when(behind == 0)
            def _():
                self.first_part(owner, k, p, arrived)

            links.send(piece, piece, device, slot, behind == 0)

    def sides(self):
        links = self.links
        return (
            (0, links.t, self.from_left, links.right),
            (1, LINE - 1 - links.t, self.from_right, links.left),
        )

    def stage(self, now, p=0):
        links = self.links
        for side, behind, arrived, device in self.sides():
            k = now - behind
            owner = LINE - 1 - k if side == 0 else k
            piece, slot = self.piece(arrived, k, p), self.slot(side, k, p)
            ready = jnp.logical_and(k >= 0, behind > 0)

            @pl.when(ready)
            def _():
                links.recv(piece, slot)
                self.total(owner, k, p, arrived)

            links.send(piece, piece, device, slot, ready)

    def first_part(self, owner, k, p, out):
        @pl.loop(0, self.size // ROWS)
        def _(i):
            r = pl.multiple_of(p * self.size + i * ROWS, ROWS)
            q = pl.multiple_of(place(owner) * self.tokens + p * self.size + i * ROWS, ROWS)
            out[k, pl.ds(r, ROWS), :] = self.part[pl.ds(q, ROWS), :].astype(out.dtype)

    def arrive(self, p=0):
        links = self.links
        t = links.t

        @pl.when(t > 0)
        def _():
            links.recv(
                self.piece(self.from_left, LINE - 1 - t, p), self.slot(0, LINE - 1 - t, p)
            )

        @pl.when(t < LINE - 1)
        def _():
            links.recv(self.piece(self.from_right, t, p), self.slot(1, t, p))

    def rows(self, r):
        t = self.links.t
        q = pl.multiple_of(place(t) * self.tokens + r, ROWS)
        k_l = jnp.minimum(LINE - 1 - t, LINE - 2)
        k_r = jnp.minimum(t, LINE - 2)
        zero = jnp.zeros((ROWS, self.part.shape[1]), f32)
        return (
            self.part[pl.ds(q, ROWS), :].astype(f32)
            + jnp.where(t > 0, self.from_left[k_l, pl.ds(r, ROWS), :].astype(f32), zero)
            + jnp.where(t < LINE - 1, self.from_right[k_r, pl.ds(r, ROWS), :].astype(f32), zero)
        )

    def owned(self, p, use):
        @pl.loop(0, self.size // ROWS)
        def _(i):
            r = pl.multiple_of(p * self.size + i * ROWS, ROWS)
            use(r, self.rows(r))


def line_ends(scatter, *hops):
    for k in hops:
        for p in range(scatter.pieces):
            scatter.ends(k, p)


def line_steps(scatter, now):
    for p in range(scatter.pieces):
        scatter.stage(now, p)


def line_finish(scatter, use, gather=None):
    for p in range(scatter.pieces):
        scatter.arrive(p)
        scatter.owned(p, use)
        if gather is not None:
            gather.send(1, p)


def line_spread(gather, k):
    for p in range(gather.pieces):
        gather.recv(k, p)
        if k < LINE - 1:
            gather.send(k + 1, p)


class PlaneScatter:
    def __init__(
        self, links, left, right, rows, core_in, x_in, y_in, x_last, y_last, out, parts=1
    ):
        self.links, self.left, self.right, self.rows = links, left, right, rows
        self.core_in, self.x_in, self.y_in = core_in, x_in, y_in
        self.x_last, self.y_last, self.out = x_last, y_last, out
        self.tile = min(256, CTX * rows)
        self.parts = parts if CTX * rows // self.tile % parts == 0 else 1
        self.core_first = links.slots((links.shards - 1) * self.parts)
        self.first = links.slots(6)

    def product(self, shard, i):
        start = pl.multiple_of(shard * (CTX * self.rows) + i * self.tile, self.tile)
        return tn_dot(self.left[:, pl.ds(start, self.tile)], self.right[...])

    def part(self, ref, index):
        size = CTX * self.rows // self.parts
        return ref.at[pl.ds(index * size, size)]

    def each_tile(self, index, body):
        tiles = CTX * self.rows // self.tile // self.parts

        @pl.loop(index * tiles, (index + 1) * tiles)
        def _(i):
            body(i, pl.ds(pl.multiple_of(i * self.tile, self.tile), self.tile))

    def other(self, step, stage):
        links = self.links
        target = lax.rem(links.s + step, links.shards)

        def tile(i, at):
            stage[at, :] = self.product(target, i).astype(bf16)

        for index in range(self.parts):
            self.each_tile(index, tile)
            links.send(
                self.part(stage, index),
                self.part(self.core_in.at[step - 1], index),
                links.core_peer(step),
                self.core_first + (step - 1) * self.parts + index,
            )

    def own(self):
        links = self.links

        def tile(i, at):
            summed = self.product(links.s, i)
            for step in range(1, links.shards):
                summed = summed + self.core_in[step - 1, at, :].astype(f32)
            self.core_in[0, at, :] = summed.astype(bf16)

        for index in range(self.parts):
            for step in range(1, links.shards):
                links.recv(
                    self.part(self.core_in.at[step - 1], index),
                    self.core_first + (step - 1) * self.parts + index,
                )
            self.each_tile(index, tile)

    def half(self, c, which):
        size = self.rows // 2
        start = pl.multiple_of(c * self.rows + which * size, size)
        return self.core_in.at[0, pl.ds(start, size)]

    def exchange(self):
        links, first = self.links, self.first
        links.send(self.half(links.c_d, 0), self.x_in.at[1], links.x_dev, first)
        links.send(self.half(links.c_d, 1), self.y_in.at[1], links.y_dev, first + 1)
        links.send(self.half(links.c_x, 0), self.x_in.at[0], links.x_dev, first + 2)
        links.send(self.half(links.c_y, 1), self.y_in.at[0], links.y_dev, first + 3)

    def add(self, c, which, arrived):
        size = self.rows // 2

        @pl.loop(0, size // ROWS)
        def _(i):
            r = pl.multiple_of(i * ROWS, ROWS)
            q = pl.multiple_of(c * self.rows + which * size + i * ROWS, ROWS)
            mine = self.core_in[0, pl.ds(q, ROWS), :].astype(f32)
            summed = mine + arrived[1, pl.ds(r, ROWS), :].astype(f32)
            self.core_in[0, pl.ds(q, ROWS), :] = summed.astype(bf16)

    def arrived(self):
        links, first = self.links, self.first
        for ref, offset in ((self.x_in, 0), (self.y_in, 1)):
            for part in range(2):
                links.recv(ref.at[1 - part], first + offset + 2 * part)

    def fold(self, here=False):
        links, first = self.links, self.first
        if not here:
            links.recv(self.x_in.at[1], first)
        self.add(links.c_y, 0, self.x_in)
        links.send(self.half(links.c_y, 0), self.y_last, links.y_dev, first + 4)
        if not here:
            links.recv(self.y_in.at[1], first + 1)
        self.add(links.c_x, 1, self.y_in)
        links.send(self.half(links.c_x, 1), self.x_last, links.x_dev, first + 5)

    def total(self, here=False):
        links, first = self.links, self.first
        size = self.rows // 2
        if not here:
            links.recv(self.x_in.at[0], first + 2)
            links.recv(self.y_in.at[0], first + 3)
        links.recv(self.y_last, first + 4)
        links.recv(self.x_last, first + 5)
        for which, arrived, last in ((0, self.x_in, self.y_last), (1, self.y_in, self.x_last)):

            @pl.loop(0, size // ROWS)
            def _(i):
                r = pl.multiple_of(i * ROWS, ROWS)
                q = pl.multiple_of(links.c * self.rows + which * size + i * ROWS, ROWS)
                self.out[pl.ds(which * size + r, ROWS), :] = (
                    self.core_in[0, pl.ds(q, ROWS), :].astype(f32)
                    + arrived[0, pl.ds(r, ROWS), :].astype(f32)
                    + last[pl.ds(r, ROWS), :].astype(f32)
                )

    @staticmethod
    def scratch(shards, rows, columns):
        half = (rows // 2, columns)
        return [
            pltpu.VMEM((shards - 1, CTX * rows, columns), bf16),
            pltpu.VMEM((2,) + half, bf16),
            pltpu.VMEM((2,) + half, bf16),
            pltpu.VMEM(half, bf16),
            pltpu.VMEM(half, bf16),
            pltpu.VMEM((rows, columns), f32),
        ]


def any_spec():
    return pl.BlockSpec(memory_space=pl.ANY)


def vmem_spec():
    return pl.BlockSpec(memory_space=pltpu.VMEM)


def struct(shape, dtype):
    return jax.ShapeDtypeStruct(shape, dtype)


def forward_kernel(
    shards,
    x, og, wq, wkv, wo, wg, wu, wd, gain_in, frequency, order,
    wq_o, wkv_o, wo_o, wg_o, wu_o, wd_o, n1_o, og_o, n2_o, mid_o, qaug_o, kaug_o, kv_o, att_o, x_o,
    lse, gains, cos, sin,
    x_all, n1_all, wq_all, wkv_all, wo_all, gains_all, qaug, kv_all, kaug, v_all, scores, weights,
    attn, part, from_left, from_right, mid, n2, og_stage, wg_stage, wu_stage, wd_stage, gpad,
    send_sems, recv_sems, local_sems,
):
    tokens, width = x.shape
    queries = tokens * LINE
    heads = qaug.shape[0]
    links = Links(shards, send_sems, recv_sems, local_sems)
    s, c, t = links.s, links.c, links.t

    gather_x = LineGather(links, x, x_all, tokens, PIECES)
    gather_og = LineGather(links, og, og_o, tokens)
    gather_n2 = LineGather(links, n2, n2_o, tokens, PIECES)
    small = [PlaneGather(links, *pair) for pair in ((wq, wq_all), (wkv, wkv_all), (wo, wo_all))]
    large = [
        PlaneGather(links, *three)
        for three in ((wg, wg_o, wg_stage), (wu, wu_o, wu_stage), (wd, wd_o, wd_stage))
    ]
    scatter = LineScatter(links, part, tokens, from_left, from_right, PIECES)
    plane = shards * CTX
    gain_slot = links.slots(plane - 1)
    kv_slot = links.slots((CTX - 1) * (2 * LINE - 1))

    links.greet()
    me = s * CTX + c
    own_gains = gain_in.shape[1]
    if own_gains == width:
        gpad[...] = gain_in[...].astype(f32)
    else:
        gpad[...] = jnp.zeros_like(gpad)
        gpad[:, pl.ds(pl.multiple_of(me * own_gains, own_gains), own_gains)] = gain_in[
            ...
        ].astype(f32)
    links.met()
    for step in range(1, plane):
        links.send(gpad, gains_all.at[me], links.plane_peer(step), gain_slot + step - 1)
    own_gain = links.keep(gpad, gains_all.at[me])
    for p in range(PIECES):
        gather_x.send(1, p)
    own_rows = pl.ds(pl.multiple_of(place(t) * tokens, tokens), tokens)
    own_x = links.keep(x, x_all.at[own_rows])
    for gather in small:
        gather.start()

    per = queries // BLOCK
    lane = lax.broadcasted_iota(jnp.int32, (1, queries), 1)
    owner = jnp.zeros((1, queries), jnp.int32)
    for index in range(LINE):
        owner = jnp.where(lane // tokens == place(index), index, owner)
    slot = owner * tokens + lax.rem(lane, tokens)
    block_here = jnp.zeros((1, queries), jnp.int32)
    for index in range(per):
        block_here = jnp.where(slot // BLOCK == index, order[c * per + index], block_here)
    position = (block_here * BLOCK + lax.rem(slot, BLOCK)).astype(f32)
    angles = frequency[...] * position
    cos[...] = jnp.cos(angles)
    sin[...] = jnp.sin(angles)
    row = lax.broadcasted_iota(jnp.int32, (HD, queries), 0)
    bias = jnp.zeros((HD, queries), f32)
    for index in range(BLOCKS):
        barred = jnp.logical_and(row == index, order[index] > block_here)
        bias = jnp.where(barred, blocked, bias)
    bias = bias.astype(bf16)
    for h in range(heads):
        qaug[h, HD:, :] = bias

    own_gain.wait()
    for step in range(1, plane):
        other = lax.rem(me + plane - step, plane)
        links.recv(gains_all.at[other], gain_slot + step - 1)
    total = gains_all[0]
    for index in range(1, plane):
        total = total + gains_all[index]
    gains[...] = total
    own_x.wait()

    def norm_block(owner):
        @pl.loop(0, tokens // ROWS)
        def _(i):
            r = pl.multiple_of(place(owner) * tokens + i * ROWS, ROWS)
            v = x_all[pl.ds(r, ROWS), :].astype(f32)
            inverse = lax.rsqrt(jnp.mean(v * v, -1, keepdims=True) + epsilon)
            n1_all[pl.ds(r, ROWS), :] = (v * inverse * gains[0:1, :]).astype(bf16)

    own_og = links.keep(og, og_stage)
    norm_block(t)
    line_spread(gather_x, 1)
    for gather in small:
        gather.forward()
    norm_pair(gather_x, norm_block, 1)
    line_spread(gather_x, 2)
    gather_og.send(1)
    for gather in small:
        gather.diagonal()
    norm_pair(gather_x, norm_block, 2)
    own_og.wait()
    links.keep_later(og_stage, og_o.at[own_rows])
    for gather in small:
        gather.done()

    half = HD // 2
    scale = HD ** (-0.5)

    def lanes_of(owner):
        return pl.ds(pl.multiple_of(place(owner) * tokens, tokens), tokens)

    def turn(v1, v2, cosine, sine):
        return (v1 * cosine - v2 * sine).astype(bf16), (v2 * cosine + v1 * sine).astype(bf16)

    def project_block(owner):
        at = lanes_of(owner)
        cosine, sine = cos[:, at], sin[:, at]
        kv_t = nn_dot(n1_all[at, :], wkv_all[...]).T
        k1, k2 = turn(kv_t[0:half], kv_t[half:HD], cosine, sine)
        kv_all[c, 0:half, at] = k1
        kv_all[c, half:HD, at] = k2
        kv_all[c, HD : 2 * HD, at] = kv_t[HD:].astype(bf16)
        q_t = nn_dot(n1_all[at, :], wq_all[...]).T
        for h in range(heads):
            b = h * HD
            q1, q2 = turn(q_t[b : b + half], q_t[b + half : b + HD], cosine, sine)
            qaug[h, 0:half, at] = (q1 * scale).astype(bf16)
            qaug[h, half:HD, at] = (q2 * scale).astype(bf16)

    u = LINE - 1 - t
    arrivals = [(t, None)]
    for k in range(1, LINE):
        arrivals += [(t - k, t >= k), (t + k, u >= k)]

    def send_block(index):
        owner, cond = arrivals[index]
        for step in range(1, CTX):
            peer = lax.rem(c + step, CTX)
            ref = kv_all.at[c, :, lanes_of(owner)]
            links.send(ref, ref, (s, peer, t), kv_slot + index * (CTX - 1) + step - 1, cond)

    def recv_block(index):
        owner, cond = arrivals[index]

        def wait():
            for step in range(1, CTX):
                other = lax.rem(c + CTX - step, CTX)
                slot = kv_slot + index * (CTX - 1) + step - 1
                links.recv(kv_all.at[other, :, lanes_of(owner)], slot)

        if cond is None:
            wait()
        else:
            pl.when(cond)(wait)

    project_block(t)
    send_block(0)
    for k in range(1, LINE):
        if k == LINE - 1:
            line_spread(gather_x, k)
            norm_pair(gather_x, norm_block, k)
        norm_pair(gather_x, project_block, k)
        send_block(2 * k - 1)
        send_block(2 * k)
    for gather in large:
        gather.start()
    links.keep_later(n1_all, n1_o)
    links.keep_later(x_all, x_o)
    links.keep_later(wq_all, wq_o)
    links.keep_later(wkv_all, wkv_o)
    links.keep_later(wo_all, wo_o)
    links.keep_later(qaug, qaug_o)
    for index in range(len(arrivals)):
        recv_block(index)
    for other in range(CTX):
        row = lax.broadcasted_iota(jnp.int32, (HD, queries), 0)
        lane = lax.broadcasted_iota(jnp.int32, (HD, queries), 1)
        mark = (row == other * (queries // BLOCK) + lax.rem(lane // tokens, 2)).astype(f32).astype(bf16)
        both = jnp.concatenate([kv_all[other, 0:HD, :], mark], 0)
        kaug[other * queries : (other + 1) * queries, :] = both.T
        v_all[:, other * queries : (other + 1) * queries] = kv_all[other, HD : 2 * HD, :]
    links.keep_later(kaug, kaug_o)
    links.keep_later(kv_all, kv_o)

    length = queries * CTX

    far = pl.multiple_of(jnp.where(t < LINE // 2, tokens, 0), tokens)
    near = pl.multiple_of(jnp.where(t < LINE // 2, 0, tokens), tokens)

    def soften(query):
        size = query.shape[1]
        top = jnp.full((1, size), -jnp.inf, f32)
        for b in range(0, length, BLOCK):
            block_scores = nn_dot(kaug[b : b + BLOCK, :], query)
            scores[b : b + BLOCK, :] = block_scores
            top = jnp.maximum(top, jnp.max(block_scores, 0, keepdims=True))
        norm = jnp.zeros((1, size), f32)
        for b in range(0, length, BLOCK):
            exponent = jnp.exp(scores[b : b + BLOCK, :] - top)
            norm = norm + jnp.sum(exponent, 0, keepdims=True)
            weights[b : b + BLOCK, :] = exponent.astype(bf16)
        out = nn_dot(v_all[...], weights[...]) / norm
        return out.astype(bf16), top + jnp.log(norm)

    def put(h, lanes, out, log_sum):
        attn[pl.ds(pl.multiple_of(h * HD, HD), HD), lanes] = out
        lse[h, :, lanes] = log_sum

    def head(lanes, h):
        put(h, lanes, *soften(qaug[h, :, lanes]))

    def head_pair(lanes, g):
        h = 2 * g
        both = jnp.concatenate([qaug[h, :, lanes], qaug[h + 1, :, lanes]], 1)
        out, log_sum = soften(both)
        put(h, lanes, out[:, 0:tokens], log_sum[:, 0:tokens])
        put(h + 1, lanes, out[:, tokens:], log_sum[:, tokens:])

    def attend(start, size):
        if size == tokens:
            pl.loop(0, heads // 2)(functools.partial(head_pair, pl.ds(start, size)))
        else:
            pl.loop(0, heads)(functools.partial(head, pl.ds(start, size)))
        rows = pl.ds(start, size)
        attn_rows = attn[:, rows].T
        for b in range(0, width, 512):
            part[rows, b : b + 512] = nt_dot(attn_rows, wo_all[b : b + 512, :])

    attend(far, tokens)
    line_ends(scatter, 0)
    gather_og.recv(1)
    gather_og.send(2)
    for gather in large:
        gather.settle()
    attend(2 * tokens, 2 * tokens)
    line_ends(scatter, 1, 2)
    gather_og.recv(2)
    gather_og.send(3)
    line_steps(scatter, 1)
    attend(near, tokens)
    links.keep_later(attn, att_o)

    def finish_rows(r, summed):
        q = pl.multiple_of(place(t) * tokens + r, ROWS)
        middle = x_all[pl.ds(q, ROWS), :].astype(f32) + summed
        mid[pl.ds(r, ROWS), :] = middle
        inverse = lax.rsqrt(jnp.mean(middle * middle, -1, keepdims=True) + epsilon)
        n2[pl.ds(r, ROWS), :] = (middle * inverse * gains[1:2, :]).astype(bf16)

    large[0].forward()
    line_steps(scatter, 2)
    large[1].forward()
    line_finish(scatter, finish_rows, gather_n2)
    large[2].forward()
    links.keep_later(n2, n2_o.at[own_rows])
    links.keep_later(mid, mid_o)
    line_spread(gather_n2, 1)
    large[0].diagonal()
    large[1].diagonal()
    line_spread(gather_n2, 2)
    large[2].diagonal()
    gather_og.recv(3)
    line_spread(gather_n2, 3)
    for gather in large:
        gather.done()
    links.finish()


def norm_pair(gather, norm_block, k):
    t, u = gather.links.t, LINE - 1 - gather.links.t

    @pl.when(t >= k)
    def _():
        norm_block(t - k)

    @pl.when(u >= k)
    def _():
        norm_block(t + k)


def forward_call(shards, x, og, weights_in, gain_in, frequency, order):
    wq, wkv, wo, wg, wu, wd = weights_in
    tokens, width = x.shape
    queries = tokens * LINE
    length = queries * CTX
    heads = wq.shape[1] // HD
    plane = shards * CTX
    full = [struct((width, w.shape[1]), bf16) for w in weights_in]
    outs = full + [
        struct((queries, width), bf16),
        struct((queries, width), bf16),
        struct((queries, width), bf16),
        struct((tokens, width), f32),
        struct((heads, 2 * HD, queries), bf16),
        struct((length, 2 * HD), bf16),
        struct((CTX, 2 * HD, queries), bf16),
        struct((heads * HD, queries), bf16),
        struct((queries, width), bf16),
        struct((heads, 1, queries), f32),
        struct((2, width), f32),
        struct((HD // 2, queries), f32),
        struct((HD // 2, queries), f32),
    ]
    block = (LINE - 1, tokens, width)
    count = 6 + 18 * PIECES + 6 * (4 + 4 * (shards - 1)) + plane - 1 + 21
    return pl.pallas_call(
        functools.partial(forward_kernel, shards),
        out_shape=outs,
        in_specs=[any_spec()] * 8
        + [vmem_spec()] * 2
        + [pl.BlockSpec(memory_space=pltpu.SMEM)],
        out_specs=[any_spec()] * 15 + [vmem_spec()] * 4,
        scratch_shapes=[
            pltpu.VMEM((queries, width), bf16),
            pltpu.VMEM((queries, width), bf16),
            pltpu.VMEM((width, wq.shape[1]), bf16),
            pltpu.VMEM((width, wkv.shape[1]), bf16),
            pltpu.VMEM((width, wo.shape[1]), bf16),
            pltpu.VMEM((plane, 2, width), f32),
            pltpu.VMEM((heads, 2 * HD, queries), bf16),
            pltpu.VMEM((CTX, 2 * HD, queries), bf16),
            pltpu.VMEM((length, 2 * HD), bf16),
            pltpu.VMEM((HD, length), bf16),
            pltpu.VMEM((length, queries // 2), f32),
            pltpu.VMEM((length, queries // 2), bf16),
            pltpu.VMEM((heads * HD, queries), bf16),
            pltpu.VMEM((queries, width), f32),
            pltpu.VMEM(block, bf16),
            pltpu.VMEM(block, bf16),
            pltpu.VMEM((tokens, width), f32),
            pltpu.VMEM((tokens, width), bf16),
            pltpu.VMEM((tokens, width), bf16),
            pltpu.VMEM(wg.shape, bf16),
            pltpu.VMEM(wu.shape, bf16),
            pltpu.VMEM(wd.shape, bf16),
            pltpu.VMEM((2, width), f32),
            pltpu.SemaphoreType.DMA((count,)),
            pltpu.SemaphoreType.DMA((count,)),
            pltpu.SemaphoreType.DMA((32,)),
        ],
        compiler_params=pltpu.CompilerParams(
            collective_id=0, has_side_effects=True, vmem_limit_bytes=60 * 2**20
        ),
        name="forward",
    )(x, og, wq, wkv, wo, wg, wu, wd, gain_in, frequency, order)


def middle_kernel(
    shards, rows,
    n2_in, og_in, wg_in, wu_in, wd_in, mid_in, gains,
    dmid_o, dmid_all_o, gg_o, gd_part_o, gd_x_o, gd_y_o, branch_o, gu_part_o, gain_sum,
    n2, og, wg, wu, wd, mid, hidden, dgate, dup, part, branch,
    left, right, dmid, dsend, gain_rows, up_in, first,
    *rest,
):
    grads, (send_sems, recv_sems, local_sems) = rest[:-3], rest[-3:]
    tokens, width = mid.shape
    queries = n2.shape[0]
    columns = wg.shape[1]
    links = Links(shards, send_sems, recv_sems, local_sems)
    t = links.t
    links.greet()
    own_rows = pl.ds(pl.multiple_of(place(t) * tokens, tokens), tokens)

    far = pl.multiple_of(jnp.where(t < LINE // 2, tokens, 0), tokens)
    near = pl.multiple_of(jnp.where(t < LINE // 2, 0, tokens), tokens)
    sides = [pl.ds(far, tokens), pl.ds(2 * tokens, 2 * tokens), pl.ds(near, tokens)]
    full, rest_columns = columns // 256, columns % 256
    weights = ((wg_in, wg), (wu_in, wu), (wd_in, wd))

    def fetch(j, start, size, index):
        src, dst = weights[j]
        of = pl.ds(start, size)
        sem = local_sems.at[3 * index + j]
        return pltpu.make_async_copy(src.at[:, of], dst.at[:, of], sem)

    links.local_used = 3 * (full + 1)
    load_n2 = [links.keep(n2_in.at[sides[0]], n2.at[sides[0]])]
    for index in range(full):
        for j in range(3):
            fetch(j, index * 256, 256, index).start()
        if index == 0:
            load_og = [links.keep(og_in.at[sides[0]], og.at[sides[0]])]
    if rest_columns:
        for j in range(3):
            fetch(j, full * 256, rest_columns, full).start()
    load_n2 += [links.keep(n2_in.at[at], n2.at[at]) for at in sides[1:]]
    load_og += [links.keep(og_in.at[at], og.at[at]) for at in sides[1:]]
    load_mid = links.keep(mid_in, mid)
    scatter = LineScatter(links, part, tokens, left, right, PIECES)
    gather = LineGather(links, dsend, dmid_all_o, tokens, PIECES)
    down = PlaneScatter(links, og, hidden, rows, *grads[0:6])
    gate = PlaneScatter(links, n2, dgate, rows, *grads[6:12], parts=2)
    up = PlaneScatter(links, n2, dup, rows, up_in, None, None, None, None, None)

    def feed_forward(half):
        at = sides[half]
        load_n2[half].wait()
        load_og[half].wait()

        def tile(start, size, index):
            of = pl.ds(start, size)
            if half == 0:
                fetch(0, start, size, index).wait()
                fetch(1, start, size, index).wait()
            gate_act = nn_dot(n2[at, :], wg[:, of])
            up_act = nn_dot(n2[at, :], wu[:, of])
            if half == 0:
                fetch(2, start, size, index).wait()
            d_hidden = nn_dot(og[at, :], wd[:, of])
            sig = jax.nn.sigmoid(gate_act)
            silu = gate_act * sig
            hidden[at, of] = (silu * up_act).astype(bf16)
            d_gate = d_hidden * up_act * sig * (1.0 + gate_act * (1.0 - sig))
            dgate[at, of] = d_gate.astype(bf16)
            dup[at, of] = (d_hidden * silu).astype(bf16)
            if half == 0:
                for b in range(0, width, 512):
                    e = b + 512
                    summed = nt_dot(dgate[at, of], wg[b:e, of]) + nt_dot(dup[at, of], wu[b:e, of])
                    first[:, b:e] += summed

        @pl.loop(0, full)
        def _(index):
            tile(pl.multiple_of(index * 256, 256), 256, index)

        if rest_columns:
            tile(full * 256, rest_columns, full)
        if half == 0:
            part[at, :] = first[...].astype(bf16)
            return

        @pl.loop(0, width // 512)
        def _(j):
            of = pl.ds(pl.multiple_of(j * 512, 512), 512)
            summed = nt_dot(dgate[at, :], wg[of, :]) + nt_dot(dup[at, :], wu[of, :])
            part[at, of] = summed.astype(bf16)

    piece = CTX * rows

    def others(grad, room):
        for step in range(1, shards):
            grad.other(step, room.at[pl.ds((step - 1) * piece, piece)])

    first[...] = jnp.zeros_like(first)
    feed_forward(0)
    links.met()
    line_ends(scatter, 0)
    feed_forward(1)
    line_ends(scatter, 1, 2)
    line_steps(scatter, 1)
    feed_forward(2)
    others(gate, wg)
    line_steps(scatter, 2)

    gate.own()
    gate.exchange()

    @pl.loop(0, width // 512)
    def _(j):
        of = pl.ds(pl.multiple_of(j * 512, 512), 512)
        branch[:, of] = nt_dot(hidden[...], wd[of, :]).astype(bf16)

    links.keep_later(branch, branch_o)
    others(down, wd)
    load_mid.wait()
    gain_rows[...] = jnp.zeros_like(gain_rows)

    def finish_rows(r, d_normed):
        at = pl.ds(r, ROWS)
        q = pl.ds(pl.multiple_of(place(t) * tokens + r, ROWS), ROWS)
        middle = mid[at, :]
        inverse = lax.rsqrt(jnp.mean(middle * middle, -1, keepdims=True) + epsilon)
        unit = middle * inverse
        gain_rows[...] += d_normed * unit
        d_unit = d_normed * gains[1:2, :]
        back = inverse * (d_unit - unit * jnp.mean(d_unit * unit, -1, keepdims=True))
        d_middle = og[q, :].astype(f32) + back
        dmid[at, :] = d_middle
        dsend[at, :] = d_middle.astype(bf16)

    line_finish(scatter, finish_rows, gather)
    gate.fold()
    down.own()
    down.exchange()
    links.keep_later(dsend, dmid_all_o.at[own_rows])
    links.keep_later(dmid, dmid_o)
    links.keep_later(down.core_in.at[0], gd_part_o)
    line_spread(gather, 1)
    others(up, wu)
    gain_sum[...] = jnp.sum(gain_rows[...], 0, keepdims=True)
    line_spread(gather, 2)
    up.own()
    links.keep_later(up_in.at[0], gu_part_o)
    gate.total()
    links.keep_later(gate.out, gg_o)
    line_spread(gather, 3)
    down.arrived()
    links.keep_later(down.x_in, gd_x_o)
    links.keep_later(down.y_in, gd_y_o)
    links.finish()


def middle_call(shards, rows, n2, og, wg, wu, wd, mid, gains):
    queries, width = n2.shape
    tokens = mid.shape[0]
    columns = wg.shape[1]
    token = (tokens, width)
    wide = (queries, columns)
    block = (LINE - 1,) + token
    outs = [
        struct(token, f32),
        struct((queries, width), bf16),
        struct((rows, columns), f32),
        struct((CTX * rows, columns), bf16),
        struct((2, rows // 2, columns), bf16),
        struct((2, rows // 2, columns), bf16),
        struct((queries, width), bf16),
        struct((CTX * rows, columns), bf16),
        struct((1, width), f32),
    ]
    count = 12 * PIECES + 3 * (2 * (shards - 1) + 6)
    return pl.pallas_call(
        functools.partial(middle_kernel, shards, rows),
        out_shape=outs,
        in_specs=[any_spec()] * 6 + [vmem_spec()],
        out_specs=[any_spec()] * 8 + [vmem_spec()],
        scratch_shapes=[
            pltpu.VMEM((queries, width), bf16),
            pltpu.VMEM((queries, width), bf16),
            pltpu.VMEM((width, columns), bf16),
            pltpu.VMEM((width, columns), bf16),
            pltpu.VMEM((width, columns), bf16),
            pltpu.VMEM(token, f32),
            pltpu.VMEM(wide, bf16),
            pltpu.VMEM(wide, bf16),
            pltpu.VMEM(wide, bf16),
            pltpu.VMEM((queries, width), bf16),
            pltpu.VMEM((queries, width), bf16),
            pltpu.VMEM(block, bf16),
            pltpu.VMEM(block, bf16),
            pltpu.VMEM(token, f32),
            pltpu.VMEM(token, bf16),
            pltpu.VMEM((ROWS, width), f32),
            pltpu.VMEM((shards - 1, CTX * rows, columns), bf16),
            pltpu.VMEM(token, f32),
            *PlaneScatter.scratch(shards, rows, columns),
            *PlaneScatter.scratch(shards, rows, columns),
            pltpu.SemaphoreType.DMA((count,)),
            pltpu.SemaphoreType.DMA((count,)),
            pltpu.SemaphoreType.DMA((40,)),
        ],
        compiler_params=pltpu.CompilerParams(
            collective_id=1, has_side_effects=True, vmem_limit_bytes=63 * 2**20
        ),
        name="middle",
    )(n2, og, wg, wu, wd, mid, gains)


def backward_kernel(
    shards, rows,
    dmid_all_in, wo_in, wq_in, wkv_in, n1_in, qaug_in, kaug_in, kv_in, att_in, x_in, dmid_in,
    branch_in, gu_part_in, gd_part_in, gd_x_in, gd_y_in, mid_in, lse, gains, gain_mlp, cos, sin,
    in_o, gq_o, gkv_o, go_o, gu_o, gd_o, out_o, gain_o,
    dmid_all, wo, wq, wkv, n1, qaug, kaug, kv, att, x, dmid,
    d_out, attn_rows, v_rows, d_keys, d_values, d_query, d_query_rows, kv_send, kv_recv, d_kv, part,
    left, right, gain_rows, pair, plane_in, line_in, total, stage_o, stage_q, stage_kv,
    branch, left_b, right_b, mid, layer, gain_sum, part_query,
    *rest,
):
    grads, (send_sems, recv_sems, local_sems) = rest[:-3], rest[-3:]
    tokens, width = dmid.shape
    queries = n1.shape[0]
    heads = qaug.shape[0]
    length = kaug.shape[0]
    half = HD // 2
    plane = shards * CTX
    links = Links(shards, send_sems, recv_sems, local_sems)
    s, c, t = links.s, links.c, links.t
    links.greet(whole_line=True)

    scatter = LineScatter(links, part, tokens, left, right, PIECES)
    scatter_out = LineScatter(links, branch, tokens, left_b, right_b)
    g_o = PlaneScatter(links, dmid_all, attn_rows, rows, *grads[0:6])
    g_q = PlaneScatter(links, n1, d_query_rows, rows, *grads[6:12])
    g_kv = PlaneScatter(links, n1, d_kv, rows, *grads[12:18])
    g_u = PlaneScatter(links, None, None, rows, *grads[18:24])
    g_d = PlaneScatter(links, None, None, rows, *grads[24:30])
    kv_slot = links.slots(CTX - 1)
    plane_slot = links.slots(plane - 1)
    line_slot = links.slots(LINE - 1)
    piece = CTX * rows
    loads = [
        links.keep(src, dst)
        for src, dst in (
            (dmid_all_in, dmid_all), (wo_in, wo), (branch_in, branch), (gu_part_in, g_u.core_in.at[0]),
            (att_in, att), (kv_in, kv), (qaug_in, qaug), (kaug_in, kaug),
            (gd_part_in, g_d.core_in.at[0]), (gd_x_in, g_d.x_in), (gd_y_in, g_d.y_in), (n1_in, n1),
            (wq_in, wq), (wkv_in, wkv), (x_in, x), (dmid_in, dmid), (mid_in, mid),
        )
    ]

    def others(grad, stage):
        for step in range(1, shards):
            grad.other(step, stage.at[pl.ds((step - 1) * piece, piece)])

    for load in loads[0:2]:
        load.wait()
    d_out[...] = nn_dot(dmid_all[...], wo[...]).astype(bf16).T
    links.met()
    loads[2].wait()
    line_ends(scatter_out, 0)
    loads[3].wait()
    g_u.exchange()
    for load in loads[4:8]:
        load.wait()
    for other in range(CTX):
        v_rows[other * queries : (other + 1) * queries, :] = kv[other, HD : 2 * HD, :].T
    d_keys[...] = jnp.zeros_like(d_keys)
    d_values[...] = jnp.zeros_like(d_values)

    def head(h):
        at = pl.ds(pl.multiple_of(h * HD, HD), HD)
        query = qaug[h]
        d_head = d_out[at, :]
        delta = jnp.sum(d_head.astype(f32) * att[at, :].astype(f32), 0, keepdims=True)
        log_sum = lse[h]
        d_q = jnp.zeros((HD, queries), f32)
        for b in range(0, length, BLOCK):
            e = b + BLOCK
            probs = jnp.exp(nn_dot(kaug[b:e, :], query) - log_sum)
            d_probs = nn_dot(v_rows[b:e, :], d_head)
            d_scores = (probs * (d_probs - delta)).astype(bf16)
            d_values[b:e, :] += nt_dot(probs.astype(bf16), d_head)
            d_keys[b:e, :] += nt_dot(d_scores, query[0:HD])
            at_b = b % queries
            d_q = d_q + nn_dot(kv[b // queries, 0:HD, at_b : at_b + BLOCK], d_scores)
        d_query[at, :] = d_q * (HD ** (-0.5))

    pl.loop(0, heads // 2)(head)
    line_ends(scatter_out, 1, 2)
    scatter_out.stage(1)
    for load in loads[8:11]:
        load.wait()
    g_d.fold(here=True)
    pl.loop(heads // 2, heads)(head)

    def pack(other):
        block = pl.ds(pl.multiple_of(other * queries, queries), queries)
        both = jnp.concatenate([d_keys[block, :], d_values[block, :]], 1)
        kv_send[other] = both.astype(bf16)

    for step in range(1, CTX):
        peer = lax.rem(c + step, CTX)
        pack(peer)
        links.send(kv_send.at[peer], kv_recv.at[step - 1], (s, peer, t), kv_slot + step - 1)
    pack(c)
    scatter_out.stage(2)
    for load in loads[11:]:
        load.wait()

    cosine, sine = cos[...], sin[...]
    for h in range(heads):
        at = h * HD
        d1, d2 = d_query[at : at + half, :], d_query[at + half : at + HD, :]
        d_query[at : at + half, :] = d1 * cosine + d2 * sine
        d_query[at + half : at + HD, :] = d2 * cosine - d1 * sine
    d_query_rows[...] = d_query[...].astype(bf16).T
    for b in range(0, width, 512):
        part_query[:, b : b + 512] = nt_dot(d_query_rows[...], wq[b : b + 512, :])
    others(g_q, stage_q)
    attn_rows[...] = att[...].T
    others(g_o, stage_o)
    for step in range(1, CTX):
        links.recv(kv_recv.at[step - 1], kv_slot + step - 1)
    d_pair = kv_send[c].astype(f32)
    for step in range(1, CTX):
        d_pair = d_pair + kv_recv[step - 1].astype(f32)
    d_pair = d_pair.T
    d1, d2 = d_pair[0:half], d_pair[half:HD]
    turned = jnp.concatenate(
        [d1 * cosine + d2 * sine, d2 * cosine - d1 * sine, d_pair[HD:]], 0
    )
    d_kv[...] = turned.astype(bf16).T

    for b in range(0, width, 512):
        summed = part_query[:, b : b + 512] + nt_dot(d_kv[...], wkv[b : b + 512, :])
        part[:, b : b + 512] = summed.astype(bf16)

    line_ends(scatter, 0, 1)

    gain_rows[...] = jnp.zeros_like(gain_rows)

    @pl.loop(0, queries // ROWS)
    def _(i):
        r = pl.ds(pl.multiple_of(i * ROWS, ROWS), ROWS)
        v = x[r, :].astype(f32)
        inverse = lax.rsqrt(jnp.mean(v * v, -1, keepdims=True) + epsilon)
        gain_rows[...] += part[r, :].astype(f32) * (v * inverse)

    pair[0:1, :] = jnp.sum(gain_rows[...], 0, keepdims=True)
    pair[1:2, :] = gain_mlp[...]
    for step in range(1, plane):
        links.send(pair, plane_in.at[step - 1], links.plane_peer(step), plane_slot + step - 1)
    g_u.fold()
    line_steps(scatter, 1)
    g_o.own()
    g_o.exchange()
    summed = pair[...]
    for step in range(1, plane):
        links.recv(plane_in.at[step - 1], plane_slot + step - 1)
        summed = summed + plane_in[step - 1]
    total[...] = summed
    for step in range(1, LINE):
        links.send(total, line_in.at[step - 1], links.line_peer(step), line_slot + step - 1)
    line_ends(scatter, 2)
    others(g_kv, stage_kv)
    g_q.own()
    g_q.exchange()
    line_steps(scatter, 2)
    g_kv.own()
    g_kv.exchange()
    g_o.fold()
    scatter_out.arrive()

    def layer_rows(r, total_rows):
        layer[pl.ds(r, ROWS), :] = (mid[pl.ds(r, ROWS), :] + total_rows).astype(bf16)

    scatter_out.owned(0, layer_rows)
    links.keep_later(layer, out_o)
    g_q.fold()
    g_kv.fold()
    g_u.total()
    links.keep_later(g_u.out, gu_o)
    g_o.total()
    links.keep_later(g_o.out, go_o)
    g_d.total(here=True)
    links.keep_later(g_d.out, gd_o)

    def finish_rows(r, d_normed):
        at = pl.ds(r, ROWS)
        q = pl.ds(pl.multiple_of(place(t) * tokens + r, ROWS), ROWS)
        v = x[q, :].astype(f32)
        inverse = lax.rsqrt(jnp.mean(v * v, -1, keepdims=True) + epsilon)
        unit = v * inverse
        d_unit = d_normed * gains[0:1, :]
        back = inverse * (d_unit - unit * jnp.mean(d_unit * unit, -1, keepdims=True))
        dmid[at, :] = dmid[at, :] + back

    scatter.arrive(0)
    scatter.owned(0, finish_rows)
    g_q.total()
    links.keep_later(g_q.out, gq_o)
    g_kv.total()
    links.keep_later(g_kv.out, gkv_o)
    for p in range(1, PIECES):
        scatter.arrive(p)
        scatter.owned(p, finish_rows)
    links.keep_later(dmid, in_o)
    for step in range(1, LINE):
        links.recv(line_in.at[step - 1], line_slot + step - 1)
        summed = summed + line_in[step - 1]
    own_gains = gain_o.shape[1]
    if own_gains == width:
        gain_o[...] = summed
    else:
        gain_sum[...] = summed
        me = s * CTX + c
        gain_o[...] = gain_sum[:, pl.ds(pl.multiple_of(me * own_gains, own_gains), own_gains)]
    links.finish()


def backward_call(
    shards, rows, dmid_all, wo, wq, wkv, n1, qaug, kaug, kv, att, x, dmid, branch, gu_part,
    gd_part, gd_x, gd_y, mid, lse, gains, gain_mlp, cos, sin,
):
    tokens, width = dmid.shape
    queries = n1.shape[0]
    heads = qaug.shape[0]
    length = kaug.shape[0]
    inner = heads * HD
    columns = gu_part.shape[1]
    plane = shards * CTX
    own_gains = width // plane if width // plane % 128 == 0 else width
    piece = CTX * rows * (shards - 1)
    token = (tokens, width)
    block = (LINE - 1,) + token
    outs = [
        struct(token, f32),
        struct((rows, inner), f32),
        struct((rows, 2 * HD), f32),
        struct((rows, inner), f32),
        struct((rows, columns), f32),
        struct((rows, columns), f32),
        struct(token, bf16),
        struct((2, own_gains), f32),
    ]
    count = 6 + 6 * PIECES + 5 * (2 * (shards - 1) + 6) + CTX - 1 + plane - 1 + LINE - 1
    return pl.pallas_call(
        functools.partial(backward_kernel, shards, rows),
        out_shape=outs,
        in_specs=[any_spec()] * 17 + [vmem_spec()] * 5,
        out_specs=[any_spec()] * 7 + [vmem_spec()],
        scratch_shapes=[
            pltpu.VMEM((queries, width), bf16),
            pltpu.VMEM((width, inner), bf16),
            pltpu.VMEM((width, inner), bf16),
            pltpu.VMEM((width, 2 * HD), bf16),
            pltpu.VMEM((queries, width), bf16),
            pltpu.VMEM(qaug.shape, bf16),
            pltpu.VMEM(kaug.shape, bf16),
            pltpu.VMEM(kv.shape, bf16),
            pltpu.VMEM((inner, queries), bf16),
            pltpu.VMEM((queries, width), bf16),
            pltpu.VMEM(token, f32),
            pltpu.VMEM((inner, queries), bf16),
            pltpu.VMEM((queries, inner), bf16),
            pltpu.VMEM((length, HD), bf16),
            pltpu.VMEM((length, HD), f32),
            pltpu.VMEM((length, HD), f32),
            pltpu.VMEM((inner, queries), f32),
            pltpu.VMEM((queries, inner), bf16),
            pltpu.VMEM((CTX, queries, 2 * HD), bf16),
            pltpu.VMEM((CTX - 1, queries, 2 * HD), bf16),
            pltpu.VMEM((queries, 2 * HD), bf16),
            pltpu.VMEM((queries, width), bf16),
            pltpu.VMEM(block, bf16),
            pltpu.VMEM(block, bf16),
            pltpu.VMEM((ROWS, width), f32),
            pltpu.VMEM((2, width), f32),
            pltpu.VMEM((plane - 1, 2, width), f32),
            pltpu.VMEM((LINE - 1, 2, width), f32),
            pltpu.VMEM((2, width), f32),
            pltpu.VMEM((piece, inner), bf16),
            pltpu.VMEM((piece, inner), bf16),
            pltpu.VMEM((piece, 2 * HD), bf16),
            pltpu.VMEM((queries, width), bf16),
            pltpu.VMEM(block, bf16),
            pltpu.VMEM(block, bf16),
            pltpu.VMEM(token, f32),
            pltpu.VMEM(token, bf16),
            pltpu.VMEM((2, width), f32),
            pltpu.VMEM((queries, width), f32),
            *PlaneScatter.scratch(shards, rows, inner),
            *PlaneScatter.scratch(shards, rows, inner),
            *PlaneScatter.scratch(shards, rows, 2 * HD),
            *PlaneScatter.scratch(1 + 1, rows, columns),
            *PlaneScatter.scratch(1 + 1, rows, columns),
            pltpu.SemaphoreType.DMA((count,)),
            pltpu.SemaphoreType.DMA((count,)),
            pltpu.SemaphoreType.DMA((32,)),
        ],
        compiler_params=pltpu.CompilerParams(
            collective_id=2, has_side_effects=True, vmem_limit_bytes=60 * 2**20
        ),
        name="backward",
    )(
        dmid_all, wo, wq, wkv, n1, qaug, kaug, kv, att, x, dmid, branch, gu_part,
        gd_part, gd_x, gd_y, mid, lse, gains, gain_mlp, cos, sin,
    )


def finish_kernel(gains, layer_in, *refs):
    count = (len(refs) - 2) // 2
    layer_out = refs[count]
    layer_out[0] = layer_in[...]
    refs[count + 1][0] = refs[0][...]
    for src, dst in zip(refs[1:count], refs[count + 2 : -2]):
        dst[...] = src[...]
    for row, dst in enumerate(refs[-2:]):
        dst[...] = gains[row : row + 1, :]


def finish_call(arrays, gains, steps=2):
    rows = [array.shape[0] // steps for array in arrays]
    wide = [array.shape[1] for array in arrays]
    own = gains.shape[1]
    shapes = [struct((1,) * (i < 2) + array.shape, array.dtype) for i, array in enumerate(arrays)]
    return pl.pallas_call(
        finish_kernel,
        grid=(steps,),
        out_shape=shapes + [struct((1, own), f32)] * 2,
        in_specs=[pl.BlockSpec((2, own), lambda i: (0, 0))]
        + [pl.BlockSpec((r, n), lambda i: (i, 0)) for r, n in zip(rows, wide)],
        out_specs=[
            pl.BlockSpec((1, r, n), lambda i: (0, i, 0))
            if index < 2
            else pl.BlockSpec((r, n), lambda i: (i, 0))
            for index, (r, n) in enumerate(zip(rows, wide))
        ]
        + [pl.BlockSpec((1, own), lambda i: (0, 0))] * 2,
        compiler_params=pltpu.CompilerParams(vmem_limit_bytes=60 * 2**20),
        name="finish",
    )(gains, *arrays)


def body(
    inputs, out_grad, block_order, gain_attn, w_query, w_keyval, w_output, gain_mlp, w_gate, w_up, w_down
):
    shards = lax.axis_size("shard")
    x, og = inputs[0], out_grad[0]
    tokens, width = x.shape
    s, c = lax.axis_index("shard"), lax.axis_index("ctx")
    frequency = np.float32(10000.0) ** (-np.arange(HD // 2, dtype=np.float32)[:, None] * 2.0 / HD)
    own = gain_attn.shape[0]
    start = (s * CTX + c) * own
    row = lax.broadcasted_iota(jnp.int32, (2, own), 0)
    gain_in = jnp.where(row == 0, gain_attn, gain_mlp)
    aligned = own % 128 == 0
    if not aligned:
        gain_in = lax.dynamic_update_slice(jnp.zeros((2, width), bf16), gain_in, (0, start))
    (wq, wkv, wo, wg, wu, wd, n1, og_all, n2, mid, qaug, kaug, kv, att, x_all, lse, gains, cos, sin) = forward_call(
        shards, x, og, (w_query, w_keyval, w_output, w_gate, w_up, w_down), gain_in,
        jnp.asarray(frequency, f32), block_order[0],
    )
    (dmid, dmid_all, grad_gate, gd_part, gd_x, gd_y, branch, gu_part, gm) = middle_call(
        shards, w_gate.shape[0], n2, og_all, wg, wu, wd, mid, gains
    )
    (input_grad, grad_query, grad_keyval, grad_output, grad_up, grad_down, layer_out, both) = backward_call(
        shards, w_query.shape[0], dmid_all, wo, wq, wkv, n1, qaug, kaug, kv, att, x_all, dmid,
        branch, gu_part, gd_part, gd_x, gd_y, mid, lse, gains, gm, cos, sin,
    )
    if not aligned:
        both = lax.dynamic_slice(both, (0, start), (2, own))
    (
        layer_out, input_grad, grad_query, grad_keyval, grad_output, grad_gate, grad_up, grad_down,
        *gain_grads,
    ) = finish_call([
        layer_out, input_grad, grad_query, grad_keyval, grad_output, grad_gate, grad_up, grad_down,
    ], both)
    return (
        layer_out, input_grad, gain_grads[0][0], grad_query, grad_keyval, grad_output,
        gain_grads[1][0], grad_gate, grad_up, grad_down,
    )


def solution(mesh):
    plane = P(("shard", "ctx"), "tensor")
    gain = P(("shard", "ctx"))
    token = P("shard", ("ctx", "tensor"), None)
    return jax.shard_map(
        body,
        mesh=mesh,
        in_specs=(token, token, P("shard", None), gain, plane, plane, plane, gain, plane, plane, plane),
        out_specs=(token, token, gain, plane, plane, plane, gain, plane, plane, plane),
        check_vma=False,
    )
```

```python
import functools

import jax
import jax.numpy as jnp
import numpy as np
from jax import lax
from jax.experimental import pallas as pl
from jax.experimental.pallas import tpu as pltpu
from jax.sharding import PartitionSpec as P

HD = 64
BLOCK = 256
BLOCKS = 8
ROWS = 16
CTX = 4
LINE = 4
PIECES = 2

epsilon = 1e-05
blocked = -1e30

f32 = jnp.float32
bf16 = jnp.bfloat16
MESH = pl.DeviceIdType.MESH


def place(owner):
    return (owner + (owner + 1) // 2) % LINE if isinstance(owner, int) else lax.rem(
        owner + (owner + 1) // 2, LINE
    )


def nn_dot(left, right):
    return jnp.dot(left, right, preferred_element_type=f32)


def nt_dot(left, right):
    return lax.dot_general(left, right, (((1,), (1,)), ((), ())), preferred_element_type=f32)


def tn_dot(left, right):
    return lax.dot_general(left, right, (((0,), (0,)), ((), ())), preferred_element_type=f32)


class Links:
    def __init__(self, shards, send_sems, recv_sems, local_sems):
        self.shards = shards
        self.send_sems, self.recv_sems, self.local_sems = send_sems, recv_sems, local_sems
        self.s = lax.axis_index("shard")
        self.c = lax.axis_index("ctx")
        self.t = lax.axis_index("tensor")
        self.c_x = self.c + 1 - 2 * lax.rem(self.c, 2)
        self.c_y = lax.rem(self.c + 2, CTX)
        self.c_d = CTX - 1 - self.c
        self.x_dev = (self.s, self.c_x, self.t)
        self.y_dev = (self.s, self.c_y, self.t)
        self.right = (self.s, self.c, self.t + 1)
        self.left = (self.s, self.c, self.t - 1)
        self.used = 0
        self.local_used = 0
        self.sends = []
        self.locals = []

    def slots(self, count):
        first = self.used
        self.used += count
        assert self.used <= self.send_sems.shape[0]
        return first

    def plane_peer(self, step):
        index = lax.rem(self.s * CTX + self.c + step, self.shards * CTX)
        return (index // CTX, lax.rem(index, CTX), self.t)

    def core_peer(self, step):
        return (lax.rem(self.s + step, self.shards), self.c, self.t)

    def line_peer(self, step):
        return (self.s, self.c, lax.rem(self.t + step, LINE))

    def greet(self, whole_line=False):
        sem = pltpu.get_barrier_semaphore()
        count = self.shards * CTX - 1
        for step in range(1, count + 1):
            pl.semaphore_signal(
                sem, inc=1, device_id=self.plane_peer(step), device_id_type=MESH
            )
        if whole_line:
            for step in range(1, LINE):
                pl.semaphore_signal(
                    sem, inc=1, device_id=self.line_peer(step), device_id_type=MESH
                )
            self.partners = count + LINE - 1
            return

        @pl.when(self.t > 0)
        def _():
            pl.semaphore_signal(sem, inc=1, device_id=self.left, device_id_type=MESH)

        @pl.when(self.t < LINE - 1)
        def _():
            pl.semaphore_signal(sem, inc=1, device_id=self.right, device_id_type=MESH)

        beside = (self.t + LINE - 1) // LINE + (2 * LINE - 2 - self.t) // LINE
        self.partners = count + beside

    def met(self):
        pl.semaphore_wait(pltpu.get_barrier_semaphore(), self.partners)

    def copy(self, src, dst, device, slot):
        return pltpu.make_async_remote_copy(
            src_ref=src,
            dst_ref=dst,
            send_sem=self.send_sems.at[slot],
            recv_sem=self.recv_sems.at[slot],
            device_id=device,
            device_id_type=MESH,
        )

    def send(self, src, dst, device, slot, cond=None):
        if cond is None:
            self.copy(src, dst, device, slot).start()
        else:

            @pl.when(cond)
            def _():
                self.copy(src, dst, device, slot).start()

        handle = (src, dst, device, slot, cond)
        self.sends.append(handle)
        return handle

    def sent(self, handle):
        self.sends = [other for other in self.sends if other is not handle]
        self.copy(*handle[:4]).wait_send()

    def recv(self, dst, slot):
        self.copy(dst, dst, self.x_dev, slot).wait_recv()

    def keep(self, src, dst):
        copy = pltpu.make_async_copy(src, dst, self.local_sems.at[self.local_used])
        self.local_used += 1
        assert self.local_used <= self.local_sems.shape[0]
        copy.start()
        return copy

    def keep_later(self, src, dst):
        self.locals.append(self.keep(src, dst))

    def finish(self):
        for src, dst, device, slot, cond in self.sends:
            if cond is None:
                self.copy(src, dst, device, slot).wait_send()
            else:

                @pl.when(cond)
                def _():
                    self.copy(src, dst, device, slot).wait_send()

        for copy in self.locals:
            copy.wait()


class PlaneGather:
    def __init__(self, links, src, full, stage=None):
        self.links, self.src, self.full, self.stage = links, src, full, stage
        self.rows = src.shape[0]
        self.first = links.slots(4 + 4 * (links.shards - 1))

    def block(self, s, c):
        start = pl.multiple_of((s * CTX + c) * self.rows, self.rows)
        return self.full.at[pl.ds(start, self.rows)]

    def half(self, s, c, which):
        size = self.rows // 2
        start = pl.multiple_of((s * CTX + c) * self.rows + which * size, size)
        return self.full.at[pl.ds(start, size)]

    def core_slot(self, step, part):
        return self.first + 4 + (step - 1) * 4 + part

    def core_send(self, src, c, part):
        links = self.links
        for step in range(1, links.shards):
            links.send(
                src,
                self.block(links.s, c),
                links.core_peer(step),
                self.core_slot(step, part),
            )

    def start(self):
        links = self.links
        own = self.block(links.s, links.c)
        links.send(self.src, own, links.x_dev, self.first)
        links.send(self.src, own, links.y_dev, self.first + 1)
        self.core_send(self.src, links.c, 0)
        self.local = links.keep(self.src, own if self.stage is None else self.stage)

    def settle(self):
        self.local.wait()
        self.local = self.links.keep(self.stage, self.block(self.links.s, self.links.c))

    def forward(self):
        links = self.links
        links.recv(self.block(links.s, links.c_x), self.first)
        links.recv(self.block(links.s, links.c_y), self.first + 1)
        from_x = self.half(links.s, links.c_x, 0)
        from_y = self.half(links.s, links.c_y, 1)
        links.send(from_x, from_x, links.y_dev, self.first + 2)
        links.send(from_y, from_y, links.x_dev, self.first + 3)
        self.core_send(self.block(links.s, links.c_x), links.c_x, 1)
        self.core_send(self.block(links.s, links.c_y), links.c_y, 2)

    def diagonal(self):
        links = self.links
        links.recv(self.half(links.s, links.c_d, 0), self.first + 2)
        links.recv(self.half(links.s, links.c_d, 1), self.first + 3)
        self.core_send(self.block(links.s, links.c_d), links.c_d, 3)

    def done(self):
        links = self.links
        for step in range(1, links.shards):
            other = lax.rem(links.s + links.shards - step, links.shards)
            for part, c in enumerate((links.c, links.c_x, links.c_y, links.c_d)):
                links.recv(self.block(other, c), self.core_slot(step, part))
        self.local.wait()


class LineGather:
    def __init__(self, links, own, full, tokens, pieces=1):
        self.links, self.own, self.full, self.tokens = links, own, full, tokens
        self.pieces, self.size = pieces, tokens // pieces
        self.first = links.slots(2 * (LINE - 1) * pieces)

    def block(self, owner, p):
        start = pl.multiple_of(place(owner) * self.tokens + p * self.size, self.size)
        return self.full.at[pl.ds(start, self.size)]

    def slot(self, side, k, p):
        return self.first + (side * (LINE - 1) + k - 1) * self.pieces + p

    def send(self, k, p=0):
        links = self.links
        t, u = links.t, LINE - 1 - links.t
        own = self.own.at[pl.ds(p * self.size, self.size)]
        right, left = self.block(t - k + 1, p), self.block(t + k - 1, p)
        links.send(
            own if k == 1 else right,
            right,
            links.right,
            self.slot(0, k, p),
            jnp.logical_and(t >= k - 1, t < LINE - 1),
        )
        links.send(
            own if k == 1 else left,
            left,
            links.left,
            self.slot(1, k, p),
            jnp.logical_and(u >= k - 1, u < LINE - 1),
        )

    def recv(self, k, p=0):
        links = self.links
        t, u = links.t, LINE - 1 - links.t

        @pl.when(t >= k)
        def _():
            links.recv(self.block(t - k, p), self.slot(0, k, p))

        @pl.when(u >= k)
        def _():
            links.recv(self.block(t + k, p), self.slot(1, k, p))


class LineScatter:
    def __init__(self, links, part, tokens, from_left, from_right, pieces=1):
        self.links, self.part, self.tokens = links, part, tokens
        self.from_left, self.from_right = from_left, from_right
        self.pieces, self.size = pieces, tokens // pieces
        self.first = links.slots(2 * (LINE - 1) * pieces)

    def slot(self, side, k, p):
        return self.first + (side * (LINE - 1) + k) * self.pieces + p

    def piece(self, ref, k, p):
        return ref.at[k, pl.ds(p * self.size, self.size)]

    def total(self, owner, k, p, arrived):
        @pl.loop(0, self.size // ROWS)
        def _(i):
            r = pl.multiple_of(p * self.size + i * ROWS, ROWS)
            q = pl.multiple_of(place(owner) * self.tokens + p * self.size + i * ROWS, ROWS)
            mine = self.part[pl.ds(q, ROWS), :].astype(f32)
            summed = mine + arrived[k, pl.ds(r, ROWS), :].astype(f32)
            arrived[k, pl.ds(r, ROWS), :] = summed.astype(arrived.dtype)

    def ends(self, k, p=0):
        links = self.links
        for side, behind, arrived, device in self.sides():
            owner = LINE - 1 - k if side == 0 else k
            piece, slot = self.piece(arrived, k, p), self.slot(side, k, p)

            @pl.when(behind == 0)
            def _():
                self.first_part(owner, k, p, arrived)

            links.send(piece, piece, device, slot, behind == 0)

    def sides(self):
        links = self.links
        return (
            (0, links.t, self.from_left, links.right),
            (1, LINE - 1 - links.t, self.from_right, links.left),
        )

    def stage(self, now, p=0):
        links = self.links
        for side, behind, arrived, device in self.sides():
            k = now - behind
            owner = LINE - 1 - k if side == 0 else k
            piece, slot = self.piece(arrived, k, p), self.slot(side, k, p)
            ready = jnp.logical_and(k >= 0, behind > 0)

            @pl.when(ready)
            def _():
                links.recv(piece, slot)
                self.total(owner, k, p, arrived)

            links.send(piece, piece, device, slot, ready)

    def first_part(self, owner, k, p, out):
        @pl.loop(0, self.size // ROWS)
        def _(i):
            r = pl.multiple_of(p * self.size + i * ROWS, ROWS)
            q = pl.multiple_of(place(owner) * self.tokens + p * self.size + i * ROWS, ROWS)
            out[k, pl.ds(r, ROWS), :] = self.part[pl.ds(q, ROWS), :].astype(out.dtype)

    def arrive(self, p=0):
        links = self.links
        t = links.t

        @pl.when(t > 0)
        def _():
            links.recv(
                self.piece(self.from_left, LINE - 1 - t, p), self.slot(0, LINE - 1 - t, p)
            )

        @pl.when(t < LINE - 1)
        def _():
            links.recv(self.piece(self.from_right, t, p), self.slot(1, t, p))

    def rows(self, r):
        t = self.links.t
        q = pl.multiple_of(place(t) * self.tokens + r, ROWS)
        k_l = jnp.minimum(LINE - 1 - t, LINE - 2)
        k_r = jnp.minimum(t, LINE - 2)
        zero = jnp.zeros((ROWS, self.part.shape[1]), f32)
        return (
            self.part[pl.ds(q, ROWS), :].astype(f32)
            + jnp.where(t > 0, self.from_left[k_l, pl.ds(r, ROWS), :].astype(f32), zero)
            + jnp.where(t < LINE - 1, self.from_right[k_r, pl.ds(r, ROWS), :].astype(f32), zero)
        )

    def owned(self, p, use):
        @pl.loop(0, self.size // ROWS)
        def _(i):
            r = pl.multiple_of(p * self.size + i * ROWS, ROWS)
            use(r, self.rows(r))


def line_ends(scatter, *hops):
    for k in hops:
        for p in range(scatter.pieces):
            scatter.ends(k, p)


def line_steps(scatter, now):
    for p in range(scatter.pieces):
        scatter.stage(now, p)


def line_finish(scatter, use, gather=None):
    for p in range(scatter.pieces):
        scatter.arrive(p)
        scatter.owned(p, use)
        if gather is not None:
            gather.send(1, p)


def line_spread(gather, k):
    for p in range(gather.pieces):
        gather.recv(k, p)
        if k < LINE - 1:
            gather.send(k + 1, p)


class PlaneScatter:
    def __init__(
        self, links, left, right, rows, core_in, x_in, y_in, x_last, y_last, out, parts=1
    ):
        self.links, self.left, self.right, self.rows = links, left, right, rows
        self.core_in, self.x_in, self.y_in = core_in, x_in, y_in
        self.x_last, self.y_last, self.out = x_last, y_last, out
        self.tile = min(256, CTX * rows)
        self.parts = parts if CTX * rows // self.tile % parts == 0 else 1
        self.core_first = links.slots((links.shards - 1) * self.parts)
        self.first = links.slots(6)

    def product(self, shard, i):
        start = pl.multiple_of(shard * (CTX * self.rows) + i * self.tile, self.tile)
        return tn_dot(self.left[:, pl.ds(start, self.tile)], self.right[...])

    def part(self, ref, index):
        size = CTX * self.rows // self.parts
        return ref.at[pl.ds(index * size, size)]

    def each_tile(self, index, body):
        tiles = CTX * self.rows // self.tile // self.parts

        @pl.loop(index * tiles, (index + 1) * tiles)
        def _(i):
            body(i, pl.ds(pl.multiple_of(i * self.tile, self.tile), self.tile))

    def other(self, step, stage):
        links = self.links
        target = lax.rem(links.s + step, links.shards)

        def tile(i, at):
            stage[at, :] = self.product(target, i).astype(bf16)

        for index in range(self.parts):
            self.each_tile(index, tile)
            links.send(
                self.part(stage, index),
                self.part(self.core_in.at[step - 1], index),
                links.core_peer(step),
                self.core_first + (step - 1) * self.parts + index,
            )

    def own(self):
        links = self.links

        def tile(i, at):
            summed = self.product(links.s, i)
            for step in range(1, links.shards):
                summed = summed + self.core_in[step - 1, at, :].astype(f32)
            self.core_in[0, at, :] = summed.astype(bf16)

        for index in range(self.parts):
            for step in range(1, links.shards):
                links.recv(
                    self.part(self.core_in.at[step - 1], index),
                    self.core_first + (step - 1) * self.parts + index,
                )
            self.each_tile(index, tile)

    def half(self, c, which):
        size = self.rows // 2
        start = pl.multiple_of(c * self.rows + which * size, size)
        return self.core_in.at[0, pl.ds(start, size)]

    def exchange(self):
        links, first = self.links, self.first
        links.send(self.half(links.c_d, 0), self.x_in.at[1], links.x_dev, first)
        links.send(self.half(links.c_d, 1), self.y_in.at[1], links.y_dev, first + 1)
        links.send(self.half(links.c_x, 0), self.x_in.at[0], links.x_dev, first + 2)
        links.send(self.half(links.c_y, 1), self.y_in.at[0], links.y_dev, first + 3)

    def add(self, c, which, arrived):
        size = self.rows // 2

        @pl.loop(0, size // ROWS)
        def _(i):
            r = pl.multiple_of(i * ROWS, ROWS)
            q = pl.multiple_of(c * self.rows + which * size + i * ROWS, ROWS)
            mine = self.core_in[0, pl.ds(q, ROWS), :].astype(f32)
            summed = mine + arrived[1, pl.ds(r, ROWS), :].astype(f32)
            self.core_in[0, pl.ds(q, ROWS), :] = summed.astype(bf16)

    def arrived(self):
        links, first = self.links, self.first
        for ref, offset in ((self.x_in, 0), (self.y_in, 1)):
            for part in range(2):
                links.recv(ref.at[1 - part], first + offset + 2 * part)

    def fold(self, here=False):
        links, first = self.links, self.first
        if not here:
            links.recv(self.x_in.at[1], first)
        self.add(links.c_y, 0, self.x_in)
        links.send(self.half(links.c_y, 0), self.y_last, links.y_dev, first + 4)
        if not here:
            links.recv(self.y_in.at[1], first + 1)
        self.add(links.c_x, 1, self.y_in)
        links.send(self.half(links.c_x, 1), self.x_last, links.x_dev, first + 5)

    def total(self, here=False):
        links, first = self.links, self.first
        size = self.rows // 2
        if not here:
            links.recv(self.x_in.at[0], first + 2)
            links.recv(self.y_in.at[0], first + 3)
        links.recv(self.y_last, first + 4)
        links.recv(self.x_last, first + 5)
        for which, arrived, last in ((0, self.x_in, self.y_last), (1, self.y_in, self.x_last)):

            @pl.loop(0, size // ROWS)
            def _(i):
                r = pl.multiple_of(i * ROWS, ROWS)
                q = pl.multiple_of(links.c * self.rows + which * size + i * ROWS, ROWS)
                self.out[pl.ds(which * size + r, ROWS), :] = (
                    self.core_in[0, pl.ds(q, ROWS), :].astype(f32)
                    + arrived[0, pl.ds(r, ROWS), :].astype(f32)
                    + last[pl.ds(r, ROWS), :].astype(f32)
                )

    @staticmethod
    def scratch(shards, rows, columns):
        half = (rows // 2, columns)
        return [
            pltpu.VMEM((shards - 1, CTX * rows, columns), bf16),
            pltpu.VMEM((2,) + half, bf16),
            pltpu.VMEM((2,) + half, bf16),
            pltpu.VMEM(half, bf16),
            pltpu.VMEM(half, bf16),
            pltpu.VMEM((rows, columns), f32),
        ]


def any_spec():
    return pl.BlockSpec(memory_space=pl.ANY)


def vmem_spec():
    return pl.BlockSpec(memory_space=pltpu.VMEM)


def struct(shape, dtype):
    return jax.ShapeDtypeStruct(shape, dtype)


def forward_kernel(
    shards,
    x, og, wq, wkv, wo, wg, wu, wd, gain_a, gain_m, frequency, order,
    wq_o, wkv_o, wo_o, wg_o, wu_o, wd_o, n1_o, og_o, n2_o, mid_o, qaug_o, kaug_o, kv_o, att_o, x_o,
    lse, gains, cos, sin,
    x_all, n1_all, wq_all, wkv_all, wo_all, gains_all, qaug, kv_all, kaug, v_all, scores, weights,
    attn, part, from_left, from_right, mid, n2, og_stage, wg_stage, wu_stage, wd_stage, gpad,
    send_sems, recv_sems, local_sems,
):
    tokens, width = x.shape
    queries = tokens * LINE
    heads = qaug.shape[0]
    links = Links(shards, send_sems, recv_sems, local_sems)
    s, c, t = links.s, links.c, links.t

    gather_x = LineGather(links, x, x_all, tokens, PIECES)
    gather_og = LineGather(links, og, og_o, tokens)
    gather_n2 = LineGather(links, n2, n2_o, tokens, PIECES)
    small = [PlaneGather(links, *pair) for pair in ((wq, wq_all), (wkv, wkv_all), (wo, wo_all))]
    large = [
        PlaneGather(links, *three)
        for three in ((wg, wg_o, wg_stage), (wu, wu_o, wu_stage), (wd, wd_o, wd_stage))
    ]
    scatter = LineScatter(links, part, tokens, from_left, from_right, PIECES)
    plane = shards * CTX
    gain_slot = links.slots(plane - 1)
    kv_slot = links.slots((CTX - 1) * (2 * LINE - 1))

    links.greet()
    me = s * CTX + c
    own_gains = gain_a.shape[0]
    if own_gains == width:
        own_lanes = slice(0, width)
    else:
        gpad[...] = jnp.zeros_like(gpad)
        own_lanes = pl.ds(pl.multiple_of(me * own_gains, own_gains), own_gains)
    for row, gain in enumerate((gain_a, gain_m)):
        gpad[row : row + 1, own_lanes] = gain[...].astype(f32).reshape(1, own_gains)
    links.met()
    for step in range(1, plane):
        links.send(gpad, gains_all.at[me], links.plane_peer(step), gain_slot + step - 1)
    own_gain = links.keep(gpad, gains_all.at[me])
    for p in range(PIECES):
        gather_x.send(1, p)
    own_rows = pl.ds(pl.multiple_of(place(t) * tokens, tokens), tokens)
    own_x = links.keep(x, x_all.at[own_rows])
    for gather in small:
        gather.start()

    per = queries // BLOCK
    lane = lax.broadcasted_iota(jnp.int32, (1, queries), 1)
    owner = jnp.zeros((1, queries), jnp.int32)
    for index in range(LINE):
        owner = jnp.where(lane // tokens == place(index), index, owner)
    slot = owner * tokens + lax.rem(lane, tokens)
    block_here = jnp.zeros((1, queries), jnp.int32)
    for index in range(per):
        block_here = jnp.where(slot // BLOCK == index, order[c * per + index], block_here)
    position = (block_here * BLOCK + lax.rem(slot, BLOCK)).astype(f32)
    angles = frequency[...] * position
    cos[...] = jnp.cos(angles)
    sin[...] = jnp.sin(angles)
    row = lax.broadcasted_iota(jnp.int32, (HD, queries), 0)
    bias = jnp.zeros((HD, queries), f32)
    for index in range(BLOCKS):
        barred = jnp.logical_and(row == index, order[index] > block_here)
        bias = jnp.where(barred, blocked, bias)
    bias = bias.astype(bf16)
    for h in range(heads):
        qaug[h, HD:, :] = bias

    own_gain.wait()
    for step in range(1, plane):
        other = lax.rem(me + plane - step, plane)
        links.recv(gains_all.at[other], gain_slot + step - 1)
    total = gains_all[0]
    for index in range(1, plane):
        total = total + gains_all[index]
    gains[...] = total
    own_x.wait()

    def norm_block(owner):
        @pl.loop(0, tokens // ROWS)
        def _(i):
            r = pl.multiple_of(place(owner) * tokens + i * ROWS, ROWS)
            v = x_all[pl.ds(r, ROWS), :].astype(f32)
            inverse = lax.rsqrt(jnp.mean(v * v, -1, keepdims=True) + epsilon)
            n1_all[pl.ds(r, ROWS), :] = (v * inverse * gains[0:1, :]).astype(bf16)

    own_og = links.keep(og, og_stage)
    norm_block(t)
    line_spread(gather_x, 1)
    for gather in small:
        gather.forward()
    norm_pair(gather_x, norm_block, 1)
    line_spread(gather_x, 2)
    gather_og.send(1)
    for gather in small:
        gather.diagonal()
    norm_pair(gather_x, norm_block, 2)
    own_og.wait()
    links.keep_later(og_stage, og_o.at[own_rows])
    for gather in small:
        gather.done()

    half = HD // 2
    scale = HD ** (-0.5)

    def lanes_of(owner):
        return pl.ds(pl.multiple_of(place(owner) * tokens, tokens), tokens)

    def turn(v1, v2, cosine, sine):
        return (v1 * cosine - v2 * sine).astype(bf16), (v2 * cosine + v1 * sine).astype(bf16)

    def project_block(owner):
        at = lanes_of(owner)
        cosine, sine = cos[:, at], sin[:, at]
        kv_t = nn_dot(n1_all[at, :], wkv_all[...]).T
        k1, k2 = turn(kv_t[0:half], kv_t[half:HD], cosine, sine)
        kv_all[c, 0:half, at] = k1
        kv_all[c, half:HD, at] = k2
        kv_all[c, HD : 2 * HD, at] = kv_t[HD:].astype(bf16)
        q_t = nn_dot(n1_all[at, :], wq_all[...]).T
        for h in range(heads):
            b = h * HD
            q1, q2 = turn(q_t[b : b + half], q_t[b + half : b + HD], cosine, sine)
            qaug[h, 0:half, at] = (q1 * scale).astype(bf16)
            qaug[h, half:HD, at] = (q2 * scale).astype(bf16)

    u = LINE - 1 - t
    arrivals = [(t, None)]
    for k in range(1, LINE):
        arrivals += [(t - k, t >= k), (t + k, u >= k)]

    def send_block(index):
        owner, cond = arrivals[index]
        for step in range(1, CTX):
            peer = lax.rem(c + step, CTX)
            ref = kv_all.at[c, :, lanes_of(owner)]
            links.send(ref, ref, (s, peer, t), kv_slot + index * (CTX - 1) + step - 1, cond)

    def recv_block(index):
        owner, cond = arrivals[index]

        def wait():
            for step in range(1, CTX):
                other = lax.rem(c + CTX - step, CTX)
                slot = kv_slot + index * (CTX - 1) + step - 1
                links.recv(kv_all.at[other, :, lanes_of(owner)], slot)

        if cond is None:
            wait()
        else:
            pl.when(cond)(wait)

    project_block(t)
    send_block(0)
    for k in range(1, LINE):
        if k == LINE - 1:
            line_spread(gather_x, k)
            norm_pair(gather_x, norm_block, k)
        norm_pair(gather_x, project_block, k)
        send_block(2 * k - 1)
        send_block(2 * k)
    for gather in large:
        gather.start()
    links.keep_later(n1_all, n1_o)
    links.keep_later(x_all, x_o)
    links.keep_later(wq_all, wq_o)
    links.keep_later(wkv_all, wkv_o)
    links.keep_later(wo_all, wo_o)
    links.keep_later(qaug, qaug_o)
    for index in range(len(arrivals)):
        recv_block(index)
    for other in range(CTX):
        row = lax.broadcasted_iota(jnp.int32, (HD, queries), 0)
        lane = lax.broadcasted_iota(jnp.int32, (HD, queries), 1)
        mark = (row == other * (queries // BLOCK) + lax.rem(lane // tokens, 2)).astype(f32).astype(bf16)
        both = jnp.concatenate([kv_all[other, 0:HD, :], mark], 0)
        kaug[other * queries : (other + 1) * queries, :] = both.T
        v_all[:, other * queries : (other + 1) * queries] = kv_all[other, HD : 2 * HD, :]
    links.keep_later(kaug, kaug_o)
    links.keep_later(kv_all, kv_o)

    length = queries * CTX

    far = pl.multiple_of(jnp.where(t < LINE // 2, tokens, 0), tokens)
    near = pl.multiple_of(jnp.where(t < LINE // 2, 0, tokens), tokens)

    def soften(query):
        size = query.shape[1]
        top = jnp.full((1, size), -jnp.inf, f32)
        for b in range(0, length, BLOCK):
            block_scores = nn_dot(kaug[b : b + BLOCK, :], query)
            scores[b : b + BLOCK, :] = block_scores
            top = jnp.maximum(top, jnp.max(block_scores, 0, keepdims=True))
        norm = jnp.zeros((1, size), f32)
        for b in range(0, length, BLOCK):
            exponent = jnp.exp(scores[b : b + BLOCK, :] - top)
            norm = norm + jnp.sum(exponent, 0, keepdims=True)
            weights[b : b + BLOCK, :] = exponent.astype(bf16)
        out = nn_dot(v_all[...], weights[...]) / norm
        return out.astype(bf16), top + jnp.log(norm)

    def put(h, lanes, out, log_sum):
        attn[pl.ds(pl.multiple_of(h * HD, HD), HD), lanes] = out
        lse[h, :, lanes] = log_sum

    def head(lanes, h):
        put(h, lanes, *soften(qaug[h, :, lanes]))

    def head_pair(lanes, g):
        h = 2 * g
        both = jnp.concatenate([qaug[h, :, lanes], qaug[h + 1, :, lanes]], 1)
        out, log_sum = soften(both)
        put(h, lanes, out[:, 0:tokens], log_sum[:, 0:tokens])
        put(h + 1, lanes, out[:, tokens:], log_sum[:, tokens:])

    def attend(start, size):
        if size == tokens:
            pl.loop(0, heads // 2)(functools.partial(head_pair, pl.ds(start, size)))
        else:
            pl.loop(0, heads)(functools.partial(head, pl.ds(start, size)))
        rows = pl.ds(start, size)
        attn_rows = attn[:, rows].T
        for b in range(0, width, 512):
            part[rows, b : b + 512] = nt_dot(attn_rows, wo_all[b : b + 512, :])

    attend(far, tokens)
    line_ends(scatter, 0)
    gather_og.recv(1)
    gather_og.send(2)
    for gather in large:
        gather.settle()
    attend(2 * tokens, 2 * tokens)
    line_ends(scatter, 1, 2)
    gather_og.recv(2)
    gather_og.send(3)
    line_steps(scatter, 1)
    attend(near, tokens)
    links.keep_later(attn, att_o)

    def finish_rows(r, summed):
        q = pl.multiple_of(place(t) * tokens + r, ROWS)
        middle = x_all[pl.ds(q, ROWS), :].astype(f32) + summed
        mid[pl.ds(r, ROWS), :] = middle
        inverse = lax.rsqrt(jnp.mean(middle * middle, -1, keepdims=True) + epsilon)
        n2[pl.ds(r, ROWS), :] = (middle * inverse * gains[1:2, :]).astype(bf16)

    large[0].forward()
    line_steps(scatter, 2)
    large[1].forward()
    line_finish(scatter, finish_rows, gather_n2)
    large[2].forward()
    links.keep_later(n2, n2_o.at[own_rows])
    links.keep_later(mid, mid_o)
    line_spread(gather_n2, 1)
    large[0].diagonal()
    large[1].diagonal()
    line_spread(gather_n2, 2)
    large[2].diagonal()
    gather_og.recv(3)
    line_spread(gather_n2, 3)
    for gather in large:
        gather.done()
    links.finish()


def norm_pair(gather, norm_block, k):
    t, u = gather.links.t, LINE - 1 - gather.links.t

    @pl.when(t >= k)
    def _():
        norm_block(t - k)

    @pl.when(u >= k)
    def _():
        norm_block(t + k)


def forward_call(shards, x, og, weights_in, gain_a, gain_m, frequency, order):
    wq, wkv, wo, wg, wu, wd = weights_in
    tokens, width = x.shape
    queries = tokens * LINE
    length = queries * CTX
    heads = wq.shape[1] // HD
    plane = shards * CTX
    full = [struct((width, w.shape[1]), bf16) for w in weights_in]
    outs = full + [
        struct((queries, width), bf16),
        struct((queries, width), bf16),
        struct((queries, width), bf16),
        struct((tokens, width), f32),
        struct((heads, 2 * HD, queries), bf16),
        struct((length, 2 * HD), bf16),
        struct((CTX, 2 * HD, queries), bf16),
        struct((heads * HD, queries), bf16),
        struct((queries, width), bf16),
        struct((heads, 1, queries), f32),
        struct((2, width), f32),
        struct((HD // 2, queries), f32),
        struct((HD // 2, queries), f32),
    ]
    block = (LINE - 1, tokens, width)
    count = 6 + 18 * PIECES + 6 * (4 + 4 * (shards - 1)) + plane - 1 + 21
    return pl.pallas_call(
        functools.partial(forward_kernel, shards),
        out_shape=outs,
        in_specs=[any_spec()] * 8
        + [vmem_spec()] * 3
        + [pl.BlockSpec(memory_space=pltpu.SMEM)],
        out_specs=[any_spec()] * 15 + [vmem_spec()] * 4,
        scratch_shapes=[
            pltpu.VMEM((queries, width), bf16),
            pltpu.VMEM((queries, width), bf16),
            pltpu.VMEM((width, wq.shape[1]), bf16),
            pltpu.VMEM((width, wkv.shape[1]), bf16),
            pltpu.VMEM((width, wo.shape[1]), bf16),
            pltpu.VMEM((plane, 2, width), f32),
            pltpu.VMEM((heads, 2 * HD, queries), bf16),
            pltpu.VMEM((CTX, 2 * HD, queries), bf16),
            pltpu.VMEM((length, 2 * HD), bf16),
            pltpu.VMEM((HD, length), bf16),
            pltpu.VMEM((length, queries // 2), f32),
            pltpu.VMEM((length, queries // 2), bf16),
            pltpu.VMEM((heads * HD, queries), bf16),
            pltpu.VMEM((queries, width), f32),
            pltpu.VMEM(block, bf16),
            pltpu.VMEM(block, bf16),
            pltpu.VMEM((tokens, width), f32),
            pltpu.VMEM((tokens, width), bf16),
            pltpu.VMEM((tokens, width), bf16),
            pltpu.VMEM(wg.shape, bf16),
            pltpu.VMEM(wu.shape, bf16),
            pltpu.VMEM(wd.shape, bf16),
            pltpu.VMEM((2, width), f32),
            pltpu.SemaphoreType.DMA((count,)),
            pltpu.SemaphoreType.DMA((count,)),
            pltpu.SemaphoreType.DMA((32,)),
        ],
        compiler_params=pltpu.CompilerParams(
            collective_id=0, has_side_effects=True, vmem_limit_bytes=60 * 2**20
        ),
        name="forward",
    )(x, og, wq, wkv, wo, wg, wu, wd, gain_a, gain_m, frequency, order)


def middle_kernel(
    shards, rows,
    n2_in, og_in, wg_in, wu_in, wd_in, mid_in, gains,
    dmid_o, dmid_all_o, gg_o, gd_part_o, gd_x_o, gd_y_o, branch_o, gu_part_o, gain_sum,
    n2, og, wg, wu, wd, mid, hidden, dgate, dup, part, branch,
    left, right, dmid, dsend, gain_rows, up_in, first,
    *rest,
):
    grads, (send_sems, recv_sems, local_sems) = rest[:-3], rest[-3:]
    tokens, width = mid.shape
    queries = n2.shape[0]
    columns = wg.shape[1]
    links = Links(shards, send_sems, recv_sems, local_sems)
    t = links.t
    links.greet()
    own_rows = pl.ds(pl.multiple_of(place(t) * tokens, tokens), tokens)

    far = pl.multiple_of(jnp.where(t < LINE // 2, tokens, 0), tokens)
    near = pl.multiple_of(jnp.where(t < LINE // 2, 0, tokens), tokens)
    sides = [pl.ds(far, tokens), pl.ds(2 * tokens, 2 * tokens), pl.ds(near, tokens)]
    full, rest_columns = columns // 256, columns % 256
    weights = ((wg_in, wg), (wu_in, wu), (wd_in, wd))

    def fetch(j, start, size, index):
        src, dst = weights[j]
        of = pl.ds(start, size)
        sem = local_sems.at[3 * index + j]
        return pltpu.make_async_copy(src.at[:, of], dst.at[:, of], sem)

    links.local_used = 3 * (full + 1)
    load_n2 = [links.keep(n2_in.at[sides[0]], n2.at[sides[0]])]
    for index in range(full):
        for j in range(3):
            fetch(j, index * 256, 256, index).start()
        if index == 0:
            load_og = [links.keep(og_in.at[sides[0]], og.at[sides[0]])]
    if rest_columns:
        for j in range(3):
            fetch(j, full * 256, rest_columns, full).start()
    load_n2 += [links.keep(n2_in.at[at], n2.at[at]) for at in sides[1:]]
    load_og += [links.keep(og_in.at[at], og.at[at]) for at in sides[1:]]
    load_mid = links.keep(mid_in, mid)
    scatter = LineScatter(links, part, tokens, left, right, PIECES)
    gather = LineGather(links, dsend, dmid_all_o, tokens, PIECES)
    down = PlaneScatter(links, og, hidden, rows, *grads[0:6])
    gate = PlaneScatter(links, n2, dgate, rows, *grads[6:12], parts=2)
    up = PlaneScatter(links, n2, dup, rows, up_in, None, None, None, None, None)

    def feed_forward(half):
        at = sides[half]
        load_n2[half].wait()
        load_og[half].wait()

        def tile(start, size, index):
            of = pl.ds(start, size)
            if half == 0:
                fetch(0, start, size, index).wait()
                fetch(1, start, size, index).wait()
            gate_act = nn_dot(n2[at, :], wg[:, of])
            up_act = nn_dot(n2[at, :], wu[:, of])
            if half == 0:
                fetch(2, start, size, index).wait()
            d_hidden = nn_dot(og[at, :], wd[:, of])
            sig = jax.nn.sigmoid(gate_act)
            silu = gate_act * sig
            hidden[at, of] = (silu * up_act).astype(bf16)
            d_gate = d_hidden * up_act * sig * (1.0 + gate_act * (1.0 - sig))
            dgate[at, of] = d_gate.astype(bf16)
            dup[at, of] = (d_hidden * silu).astype(bf16)
            if half == 0:
                for b in range(0, width, 512):
                    e = b + 512
                    summed = nt_dot(dgate[at, of], wg[b:e, of]) + nt_dot(dup[at, of], wu[b:e, of])
                    first[:, b:e] += summed

        @pl.loop(0, full)
        def _(index):
            tile(pl.multiple_of(index * 256, 256), 256, index)

        if rest_columns:
            tile(full * 256, rest_columns, full)
        if half == 0:
            part[at, :] = first[...].astype(bf16)
            return

        @pl.loop(0, width // 512)
        def _(j):
            of = pl.ds(pl.multiple_of(j * 512, 512), 512)
            summed = nt_dot(dgate[at, :], wg[of, :]) + nt_dot(dup[at, :], wu[of, :])
            part[at, of] = summed.astype(bf16)

    piece = CTX * rows

    def others(grad, room):
        for step in range(1, shards):
            grad.other(step, room.at[pl.ds((step - 1) * piece, piece)])

    first[...] = jnp.zeros_like(first)
    feed_forward(0)
    links.met()
    line_ends(scatter, 0)
    feed_forward(1)
    line_ends(scatter, 1, 2)
    line_steps(scatter, 1)
    feed_forward(2)
    others(gate, wg)
    line_steps(scatter, 2)

    gate.own()
    gate.exchange()

    @pl.loop(0, width // 512)
    def _(j):
        of = pl.ds(pl.multiple_of(j * 512, 512), 512)
        branch[:, of] = nt_dot(hidden[...], wd[of, :]).astype(bf16)

    links.keep_later(branch, branch_o)
    others(down, wd)
    load_mid.wait()
    gain_rows[...] = jnp.zeros_like(gain_rows)

    def finish_rows(r, d_normed):
        at = pl.ds(r, ROWS)
        q = pl.ds(pl.multiple_of(place(t) * tokens + r, ROWS), ROWS)
        middle = mid[at, :]
        inverse = lax.rsqrt(jnp.mean(middle * middle, -1, keepdims=True) + epsilon)
        unit = middle * inverse
        gain_rows[...] += d_normed * unit
        d_unit = d_normed * gains[1:2, :]
        back = inverse * (d_unit - unit * jnp.mean(d_unit * unit, -1, keepdims=True))
        d_middle = og[q, :].astype(f32) + back
        dmid[at, :] = d_middle
        dsend[at, :] = d_middle.astype(bf16)

    line_finish(scatter, finish_rows, gather)
    gate.fold()
    down.own()
    down.exchange()
    links.keep_later(dsend, dmid_all_o.at[own_rows])
    links.keep_later(dmid, dmid_o)
    links.keep_later(down.core_in.at[0], gd_part_o)
    line_spread(gather, 1)
    others(up, wu)
    gain_sum[...] = jnp.sum(gain_rows[...], 0, keepdims=True)
    line_spread(gather, 2)
    up.own()
    links.keep_later(up_in.at[0], gu_part_o)
    gate.total()
    links.keep_later(gate.out, gg_o)
    line_spread(gather, 3)
    down.arrived()
    links.keep_later(down.x_in, gd_x_o)
    links.keep_later(down.y_in, gd_y_o)
    links.finish()


def middle_call(shards, rows, n2, og, wg, wu, wd, mid, gains):
    queries, width = n2.shape
    tokens = mid.shape[0]
    columns = wg.shape[1]
    token = (tokens, width)
    wide = (queries, columns)
    block = (LINE - 1,) + token
    outs = [
        struct(token, f32),
        struct((queries, width), bf16),
        struct((rows, columns), f32),
        struct((CTX * rows, columns), bf16),
        struct((2, rows // 2, columns), bf16),
        struct((2, rows // 2, columns), bf16),
        struct((queries, width), bf16),
        struct((CTX * rows, columns), bf16),
        struct((1, width), f32),
    ]
    count = 12 * PIECES + 3 * (2 * (shards - 1) + 6)
    return pl.pallas_call(
        functools.partial(middle_kernel, shards, rows),
        out_shape=outs,
        in_specs=[any_spec()] * 6 + [vmem_spec()],
        out_specs=[any_spec()] * 8 + [vmem_spec()],
        scratch_shapes=[
            pltpu.VMEM((queries, width), bf16),
            pltpu.VMEM((queries, width), bf16),
            pltpu.VMEM((width, columns), bf16),
            pltpu.VMEM((width, columns), bf16),
            pltpu.VMEM((width, columns), bf16),
            pltpu.VMEM(token, f32),
            pltpu.VMEM(wide, bf16),
            pltpu.VMEM(wide, bf16),
            pltpu.VMEM(wide, bf16),
            pltpu.VMEM((queries, width), bf16),
            pltpu.VMEM((queries, width), bf16),
            pltpu.VMEM(block, bf16),
            pltpu.VMEM(block, bf16),
            pltpu.VMEM(token, f32),
            pltpu.VMEM(token, bf16),
            pltpu.VMEM((ROWS, width), f32),
            pltpu.VMEM((shards - 1, CTX * rows, columns), bf16),
            pltpu.VMEM(token, f32),
            *PlaneScatter.scratch(shards, rows, columns),
            *PlaneScatter.scratch(shards, rows, columns),
            pltpu.SemaphoreType.DMA((count,)),
            pltpu.SemaphoreType.DMA((count,)),
            pltpu.SemaphoreType.DMA((40,)),
        ],
        compiler_params=pltpu.CompilerParams(
            collective_id=1, has_side_effects=True, vmem_limit_bytes=63 * 2**20
        ),
        name="middle",
    )(n2, og, wg, wu, wd, mid, gains)


def backward_kernel(
    shards, rows,
    dmid_all_in, wo_in, wq_in, wkv_in, n1_in, qaug_in, kaug_in, kv_in, att_in, x_in, dmid_in,
    branch_in, gu_part_in, gd_part_in, gd_x_in, gd_y_in, mid_in, lse, gains, gain_mlp, cos, sin,
    in_o, gq_o, gkv_o, go_o, gu_o, gd_o, out_o, gain_o,
    dmid_all, wo, wq, wkv, n1, qaug, kaug, kv, att, x, dmid,
    d_out, attn_rows, v_rows, d_keys, d_values, d_query, d_query_rows, kv_send, kv_recv, d_kv, part,
    left, right, gain_rows, pair, plane_in, line_in, total, stage_o, stage_q, stage_kv,
    branch, left_b, right_b, mid, layer, gain_sum, part_query,
    *rest,
):
    grads, (send_sems, recv_sems, local_sems) = rest[:-3], rest[-3:]
    tokens, width = dmid.shape
    queries = n1.shape[0]
    heads = qaug.shape[0]
    length = kaug.shape[0]
    half = HD // 2
    plane = shards * CTX
    links = Links(shards, send_sems, recv_sems, local_sems)
    s, c, t = links.s, links.c, links.t
    links.greet(whole_line=True)

    scatter = LineScatter(links, part, tokens, left, right, PIECES)
    scatter_out = LineScatter(links, branch, tokens, left_b, right_b)
    g_o = PlaneScatter(links, dmid_all, attn_rows, rows, *grads[0:6])
    g_q = PlaneScatter(links, n1, d_query_rows, rows, *grads[6:12])
    g_kv = PlaneScatter(links, n1, d_kv, rows, *grads[12:18])
    g_u = PlaneScatter(links, None, None, rows, *grads[18:24])
    g_d = PlaneScatter(links, None, None, rows, *grads[24:30])
    kv_slot = links.slots(CTX - 1)
    plane_slot = links.slots(plane - 1)
    line_slot = links.slots(LINE - 1)
    piece = CTX * rows
    loads = [
        links.keep(src, dst)
        for src, dst in (
            (dmid_all_in, dmid_all), (wo_in, wo), (branch_in, branch), (gu_part_in, g_u.core_in.at[0]),
            (att_in, att), (kv_in, kv), (qaug_in, qaug), (kaug_in, kaug),
            (gd_part_in, g_d.core_in.at[0]), (gd_x_in, g_d.x_in), (gd_y_in, g_d.y_in), (n1_in, n1),
            (wq_in, wq), (wkv_in, wkv), (x_in, x), (dmid_in, dmid), (mid_in, mid),
        )
    ]

    def others(grad, stage):
        for step in range(1, shards):
            grad.other(step, stage.at[pl.ds((step - 1) * piece, piece)])

    for load in loads[0:2]:
        load.wait()
    d_out[...] = nn_dot(dmid_all[...], wo[...]).astype(bf16).T
    links.met()
    loads[2].wait()
    line_ends(scatter_out, 0)
    loads[3].wait()
    g_u.exchange()
    for load in loads[4:8]:
        load.wait()
    for other in range(CTX):
        v_rows[other * queries : (other + 1) * queries, :] = kv[other, HD : 2 * HD, :].T
    d_keys[...] = jnp.zeros_like(d_keys)
    d_values[...] = jnp.zeros_like(d_values)

    def head(h):
        at = pl.ds(pl.multiple_of(h * HD, HD), HD)
        query = qaug[h]
        d_head = d_out[at, :]
        delta = jnp.sum(d_head.astype(f32) * att[at, :].astype(f32), 0, keepdims=True)
        log_sum = lse[h]
        d_q = jnp.zeros((HD, queries), f32)
        for b in range(0, length, BLOCK):
            e = b + BLOCK
            probs = jnp.exp(nn_dot(kaug[b:e, :], query) - log_sum)
            d_probs = nn_dot(v_rows[b:e, :], d_head)
            d_scores = (probs * (d_probs - delta)).astype(bf16)
            d_values[b:e, :] += nt_dot(probs.astype(bf16), d_head)
            d_keys[b:e, :] += nt_dot(d_scores, query[0:HD])
            at_b = b % queries
            d_q = d_q + nn_dot(kv[b // queries, 0:HD, at_b : at_b + BLOCK], d_scores)
        d_query[at, :] = d_q * (HD ** (-0.5))

    pl.loop(0, heads // 2)(head)
    line_ends(scatter_out, 1, 2)
    scatter_out.stage(1)
    for load in loads[8:11]:
        load.wait()
    g_d.fold(here=True)
    pl.loop(heads // 2, heads)(head)

    def pack(other):
        block = pl.ds(pl.multiple_of(other * queries, queries), queries)
        both = jnp.concatenate([d_keys[block, :], d_values[block, :]], 1)
        kv_send[other] = both.astype(bf16)

    for step in range(1, CTX):
        peer = lax.rem(c + step, CTX)
        pack(peer)
        links.send(kv_send.at[peer], kv_recv.at[step - 1], (s, peer, t), kv_slot + step - 1)
    pack(c)
    scatter_out.stage(2)
    for load in loads[11:]:
        load.wait()

    cosine, sine = cos[...], sin[...]
    for h in range(heads):
        at = h * HD
        d1, d2 = d_query[at : at + half, :], d_query[at + half : at + HD, :]
        d_query[at : at + half, :] = d1 * cosine + d2 * sine
        d_query[at + half : at + HD, :] = d2 * cosine - d1 * sine
    d_query_rows[...] = d_query[...].astype(bf16).T
    for b in range(0, width, 512):
        part_query[:, b : b + 512] = nt_dot(d_query_rows[...], wq[b : b + 512, :])
    others(g_q, stage_q)
    attn_rows[...] = att[...].T
    others(g_o, stage_o)
    for step in range(1, CTX):
        links.recv(kv_recv.at[step - 1], kv_slot + step - 1)
    d_pair = kv_send[c].astype(f32)
    for step in range(1, CTX):
        d_pair = d_pair + kv_recv[step - 1].astype(f32)
    d_pair = d_pair.T
    d1, d2 = d_pair[0:half], d_pair[half:HD]
    turned = jnp.concatenate(
        [d1 * cosine + d2 * sine, d2 * cosine - d1 * sine, d_pair[HD:]], 0
    )
    d_kv[...] = turned.astype(bf16).T

    for b in range(0, width, 512):
        summed = part_query[:, b : b + 512] + nt_dot(d_kv[...], wkv[b : b + 512, :])
        part[:, b : b + 512] = summed.astype(bf16)

    line_ends(scatter, 0, 1)

    gain_rows[...] = jnp.zeros_like(gain_rows)

    @pl.loop(0, queries // ROWS)
    def _(i):
        r = pl.ds(pl.multiple_of(i * ROWS, ROWS), ROWS)
        v = x[r, :].astype(f32)
        inverse = lax.rsqrt(jnp.mean(v * v, -1, keepdims=True) + epsilon)
        gain_rows[...] += part[r, :].astype(f32) * (v * inverse)

    pair[0:1, :] = jnp.sum(gain_rows[...], 0, keepdims=True)
    pair[1:2, :] = gain_mlp[...]
    for step in range(1, plane):
        links.send(pair, plane_in.at[step - 1], links.plane_peer(step), plane_slot + step - 1)
    g_u.fold()
    line_steps(scatter, 1)
    g_o.own()
    g_o.exchange()
    summed = pair[...]
    for step in range(1, plane):
        links.recv(plane_in.at[step - 1], plane_slot + step - 1)
        summed = summed + plane_in[step - 1]
    total[...] = summed
    for step in range(1, LINE):
        links.send(total, line_in.at[step - 1], links.line_peer(step), line_slot + step - 1)
    line_ends(scatter, 2)
    others(g_kv, stage_kv)
    g_q.own()
    g_q.exchange()
    line_steps(scatter, 2)
    g_kv.own()
    g_kv.exchange()
    g_o.fold()
    scatter_out.arrive()

    def layer_rows(r, total_rows):
        layer[pl.ds(r, ROWS), :] = (mid[pl.ds(r, ROWS), :] + total_rows).astype(bf16)

    scatter_out.owned(0, layer_rows)
    links.keep_later(layer, out_o)
    g_q.fold()
    g_kv.fold()
    g_u.total()
    links.keep_later(g_u.out, gu_o)
    g_o.total()
    links.keep_later(g_o.out, go_o)
    g_d.total(here=True)
    links.keep_later(g_d.out, gd_o)

    def finish_rows(r, d_normed):
        at = pl.ds(r, ROWS)
        q = pl.ds(pl.multiple_of(place(t) * tokens + r, ROWS), ROWS)
        v = x[q, :].astype(f32)
        inverse = lax.rsqrt(jnp.mean(v * v, -1, keepdims=True) + epsilon)
        unit = v * inverse
        d_unit = d_normed * gains[0:1, :]
        back = inverse * (d_unit - unit * jnp.mean(d_unit * unit, -1, keepdims=True))
        dmid[at, :] = dmid[at, :] + back

    scatter.arrive(0)
    scatter.owned(0, finish_rows)
    g_q.total()
    links.keep_later(g_q.out, gq_o)
    g_kv.total()
    links.keep_later(g_kv.out, gkv_o)
    for p in range(1, PIECES):
        scatter.arrive(p)
        scatter.owned(p, finish_rows)
    links.keep_later(dmid, in_o)
    for step in range(1, LINE):
        links.recv(line_in.at[step - 1], line_slot + step - 1)
        summed = summed + line_in[step - 1]
    own_gains = gain_o.shape[1]
    if own_gains == width:
        gain_o[...] = summed
    else:
        gain_sum[...] = summed
        me = s * CTX + c
        gain_o[...] = gain_sum[:, pl.ds(pl.multiple_of(me * own_gains, own_gains), own_gains)]
    links.finish()


def backward_call(
    shards, rows, dmid_all, wo, wq, wkv, n1, qaug, kaug, kv, att, x, dmid, branch, gu_part,
    gd_part, gd_x, gd_y, mid, lse, gains, gain_mlp, cos, sin,
):
    tokens, width = dmid.shape
    queries = n1.shape[0]
    heads = qaug.shape[0]
    length = kaug.shape[0]
    inner = heads * HD
    columns = gu_part.shape[1]
    plane = shards * CTX
    own_gains = width // plane if width // plane % 128 == 0 else width
    piece = CTX * rows * (shards - 1)
    token = (tokens, width)
    block = (LINE - 1,) + token
    outs = [
        struct(token, f32),
        struct((rows, inner), f32),
        struct((rows, 2 * HD), f32),
        struct((rows, inner), f32),
        struct((rows, columns), f32),
        struct((rows, columns), f32),
        struct(token, bf16),
        struct((2, own_gains), f32),
    ]
    count = 6 + 6 * PIECES + 5 * (2 * (shards - 1) + 6) + CTX - 1 + plane - 1 + LINE - 1
    return pl.pallas_call(
        functools.partial(backward_kernel, shards, rows),
        out_shape=outs,
        in_specs=[any_spec()] * 17 + [vmem_spec()] * 5,
        out_specs=[any_spec()] * 7 + [vmem_spec()],
        scratch_shapes=[
            pltpu.VMEM((queries, width), bf16),
            pltpu.VMEM((width, inner), bf16),
            pltpu.VMEM((width, inner), bf16),
            pltpu.VMEM((width, 2 * HD), bf16),
            pltpu.VMEM((queries, width), bf16),
            pltpu.VMEM(qaug.shape, bf16),
            pltpu.VMEM(kaug.shape, bf16),
            pltpu.VMEM(kv.shape, bf16),
            pltpu.VMEM((inner, queries), bf16),
            pltpu.VMEM((queries, width), bf16),
            pltpu.VMEM(token, f32),
            pltpu.VMEM((inner, queries), bf16),
            pltpu.VMEM((queries, inner), bf16),
            pltpu.VMEM((length, HD), bf16),
            pltpu.VMEM((length, HD), f32),
            pltpu.VMEM((length, HD), f32),
            pltpu.VMEM((inner, queries), f32),
            pltpu.VMEM((queries, inner), bf16),
            pltpu.VMEM((CTX, queries, 2 * HD), bf16),
            pltpu.VMEM((CTX - 1, queries, 2 * HD), bf16),
            pltpu.VMEM((queries, 2 * HD), bf16),
            pltpu.VMEM((queries, width), bf16),
            pltpu.VMEM(block, bf16),
            pltpu.VMEM(block, bf16),
            pltpu.VMEM((ROWS, width), f32),
            pltpu.VMEM((2, width), f32),
            pltpu.VMEM((plane - 1, 2, width), f32),
            pltpu.VMEM((LINE - 1, 2, width), f32),
            pltpu.VMEM((2, width), f32),
            pltpu.VMEM((piece, inner), bf16),
            pltpu.VMEM((piece, inner), bf16),
            pltpu.VMEM((piece, 2 * HD), bf16),
            pltpu.VMEM((queries, width), bf16),
            pltpu.VMEM(block, bf16),
            pltpu.VMEM(block, bf16),
            pltpu.VMEM(token, f32),
            pltpu.VMEM(token, bf16),
            pltpu.VMEM((2, width), f32),
            pltpu.VMEM((queries, width), f32),
            *PlaneScatter.scratch(shards, rows, inner),
            *PlaneScatter.scratch(shards, rows, inner),
            *PlaneScatter.scratch(shards, rows, 2 * HD),
            *PlaneScatter.scratch(1 + 1, rows, columns),
            *PlaneScatter.scratch(1 + 1, rows, columns),
            pltpu.SemaphoreType.DMA((count,)),
            pltpu.SemaphoreType.DMA((count,)),
            pltpu.SemaphoreType.DMA((32,)),
        ],
        compiler_params=pltpu.CompilerParams(
            collective_id=2, has_side_effects=True, vmem_limit_bytes=60 * 2**20
        ),
        name="backward",
    )(
        dmid_all, wo, wq, wkv, n1, qaug, kaug, kv, att, x, dmid, branch, gu_part,
        gd_part, gd_x, gd_y, mid, lse, gains, gain_mlp, cos, sin,
    )


def finish_kernel(gains, layer_in, *refs):
    count = (len(refs) - 2) // 2
    layer_out = refs[count]
    layer_out[0] = layer_in[...]
    refs[count + 1][0] = refs[0][...]
    for src, dst in zip(refs[1:count], refs[count + 2 : -2]):
        dst[...] = src[...]
    for row, dst in enumerate(refs[-2:]):
        dst[...] = gains[row : row + 1, :]


def finish_call(arrays, gains, steps=2):
    rows = [array.shape[0] // steps for array in arrays]
    wide = [array.shape[1] for array in arrays]
    own = gains.shape[1]
    shapes = [struct((1,) * (i < 2) + array.shape, array.dtype) for i, array in enumerate(arrays)]
    return pl.pallas_call(
        finish_kernel,
        grid=(steps,),
        out_shape=shapes + [struct((1, own), f32)] * 2,
        in_specs=[pl.BlockSpec((2, own), lambda i: (0, 0))]
        + [pl.BlockSpec((r, n), lambda i: (i, 0)) for r, n in zip(rows, wide)],
        out_specs=[
            pl.BlockSpec((1, r, n), lambda i: (0, i, 0))
            if index < 2
            else pl.BlockSpec((r, n), lambda i: (i, 0))
            for index, (r, n) in enumerate(zip(rows, wide))
        ]
        + [pl.BlockSpec((1, own), lambda i: (0, 0))] * 2,
        compiler_params=pltpu.CompilerParams(vmem_limit_bytes=60 * 2**20),
        name="finish",
    )(gains, *arrays)


def body(
    inputs, out_grad, block_order, gain_attn, w_query, w_keyval, w_output, gain_mlp, w_gate, w_up, w_down
):
    shards = lax.axis_size("shard")
    x, og = inputs[0], out_grad[0]
    tokens, width = x.shape
    s, c = lax.axis_index("shard"), lax.axis_index("ctx")
    frequency = np.float32(10000.0) ** (-np.arange(HD // 2, dtype=np.float32)[:, None] * 2.0 / HD)
    own = gain_attn.shape[0]
    start = (s * CTX + c) * own
    gain_a, gain_m = gain_attn, gain_mlp
    aligned = own % 128 == 0
    if not aligned:
        gain_a, gain_m = (
            lax.dynamic_update_slice(jnp.zeros((width,), bf16), gain, (start,))
            for gain in (gain_attn, gain_mlp)
        )
    (wq, wkv, wo, wg, wu, wd, n1, og_all, n2, mid, qaug, kaug, kv, att, x_all, lse, gains, cos, sin) = forward_call(
        shards, x, og, (w_query, w_keyval, w_output, w_gate, w_up, w_down), gain_a, gain_m,
        jnp.asarray(frequency, f32), block_order[0],
    )
    (dmid, dmid_all, grad_gate, gd_part, gd_x, gd_y, branch, gu_part, gm) = middle_call(
        shards, w_gate.shape[0], n2, og_all, wg, wu, wd, mid, gains
    )
    (input_grad, grad_query, grad_keyval, grad_output, grad_up, grad_down, layer_out, both) = backward_call(
        shards, w_query.shape[0], dmid_all, wo, wq, wkv, n1, qaug, kaug, kv, att, x_all, dmid,
        branch, gu_part, gd_part, gd_x, gd_y, mid, lse, gains, gm, cos, sin,
    )
    if not aligned:
        both = lax.dynamic_slice(both, (0, start), (2, own))
    (
        layer_out, input_grad, grad_query, grad_keyval, grad_output, grad_gate, grad_up, grad_down,
        *gain_grads,
    ) = finish_call([
        layer_out, input_grad, grad_query, grad_keyval, grad_output, grad_gate, grad_up, grad_down,
    ], both)
    return (
        layer_out, input_grad, gain_grads[0][0], grad_query, grad_keyval, grad_output,
        gain_grads[1][0], grad_gate, grad_up, grad_down,
    )


def solution(mesh):
    plane = P(("shard", "ctx"), "tensor")
    gain = P(("shard", "ctx"))
    token = P("shard", ("ctx", "tensor"), None)
    return jax.shard_map(
        body,
        mesh=mesh,
        in_specs=(token, token, P("shard", None), gain, plane, plane, plane, gain, plane, plane, plane),
        out_specs=(token, token, gain, plane, plane, plane, gain, plane, plane, plane),
        check_vma=False,
    )
```

```python
import functools

import jax
import jax.numpy as jnp
import numpy as np
from jax import lax
from jax.experimental import pallas as pl
from jax.experimental.pallas import tpu as pltpu
from jax.sharding import PartitionSpec as P

HD = 64
BLOCK = 256
BLOCKS = 8
ROWS = 16
CTX = 4
LINE = 4
PIECES = 2

epsilon = 1e-05
blocked = -1e30

f32 = jnp.float32
bf16 = jnp.bfloat16
MESH = pl.DeviceIdType.MESH


def place(owner):
    return (owner + (owner + 1) // 2) % LINE if isinstance(owner, int) else lax.rem(
        owner + (owner + 1) // 2, LINE
    )


def nn_dot(left, right):
    return jnp.dot(left, right, preferred_element_type=f32)


def nt_dot(left, right):
    return lax.dot_general(left, right, (((1,), (1,)), ((), ())), preferred_element_type=f32)


def tn_dot(left, right):
    return lax.dot_general(left, right, (((0,), (0,)), ((), ())), preferred_element_type=f32)


class Links:
    def __init__(self, shards, send_sems, recv_sems, local_sems):
        self.shards = shards
        self.send_sems, self.recv_sems, self.local_sems = send_sems, recv_sems, local_sems
        self.s = lax.axis_index("shard")
        self.c = lax.axis_index("ctx")
        self.t = lax.axis_index("tensor")
        self.c_x = self.c + 1 - 2 * lax.rem(self.c, 2)
        self.c_y = lax.rem(self.c + 2, CTX)
        self.c_d = CTX - 1 - self.c
        self.x_dev = (self.s, self.c_x, self.t)
        self.y_dev = (self.s, self.c_y, self.t)
        self.right = (self.s, self.c, self.t + 1)
        self.left = (self.s, self.c, self.t - 1)
        self.used = 0
        self.local_used = 0
        self.sends = []
        self.locals = []

    def slots(self, count):
        first = self.used
        self.used += count
        assert self.used <= self.send_sems.shape[0]
        return first

    def plane_peer(self, step):
        index = lax.rem(self.s * CTX + self.c + step, self.shards * CTX)
        return (index // CTX, lax.rem(index, CTX), self.t)

    def core_peer(self, step):
        return (lax.rem(self.s + step, self.shards), self.c, self.t)

    def line_peer(self, step):
        return (self.s, self.c, lax.rem(self.t + step, LINE))

    def greet(self, whole_line=False):
        sem = pltpu.get_barrier_semaphore()
        count = self.shards * CTX - 1
        for step in range(1, count + 1):
            pl.semaphore_signal(
                sem, inc=1, device_id=self.plane_peer(step), device_id_type=MESH
            )
        if whole_line:
            for step in range(1, LINE):
                pl.semaphore_signal(
                    sem, inc=1, device_id=self.line_peer(step), device_id_type=MESH
                )
            self.partners = count + LINE - 1
            return

        @pl.when(self.t > 0)
        def _():
            pl.semaphore_signal(sem, inc=1, device_id=self.left, device_id_type=MESH)

        @pl.when(self.t < LINE - 1)
        def _():
            pl.semaphore_signal(sem, inc=1, device_id=self.right, device_id_type=MESH)

        beside = (self.t + LINE - 1) // LINE + (2 * LINE - 2 - self.t) // LINE
        self.partners = count + beside

    def met(self):
        pl.semaphore_wait(pltpu.get_barrier_semaphore(), self.partners)

    def copy(self, src, dst, device, slot):
        return pltpu.make_async_remote_copy(
            src_ref=src,
            dst_ref=dst,
            send_sem=self.send_sems.at[slot],
            recv_sem=self.recv_sems.at[slot],
            device_id=device,
            device_id_type=MESH,
        )

    def send(self, src, dst, device, slot, cond=None):
        if cond is None:
            self.copy(src, dst, device, slot).start()
        else:

            @pl.when(cond)
            def _():
                self.copy(src, dst, device, slot).start()

        handle = (src, dst, device, slot, cond)
        self.sends.append(handle)
        return handle

    def sent(self, handle):
        self.sends = [other for other in self.sends if other is not handle]
        self.copy(*handle[:4]).wait_send()

    def recv(self, dst, slot):
        self.copy(dst, dst, self.x_dev, slot).wait_recv()

    def keep(self, src, dst):
        copy = pltpu.make_async_copy(src, dst, self.local_sems.at[self.local_used])
        self.local_used += 1
        assert self.local_used <= self.local_sems.shape[0]
        copy.start()
        return copy

    def keep_later(self, src, dst):
        self.locals.append(self.keep(src, dst))

    def finish(self):
        for src, dst, device, slot, cond in self.sends:
            if cond is None:
                self.copy(src, dst, device, slot).wait_send()
            else:

                @pl.when(cond)
                def _():
                    self.copy(src, dst, device, slot).wait_send()

        for copy in self.locals:
            copy.wait()


class PlaneGather:
    def __init__(self, links, src, full, stage=None):
        self.links, self.src, self.full, self.stage = links, src, full, stage
        self.rows = src.shape[0]
        self.first = links.slots(4 + 4 * (links.shards - 1))

    def block(self, s, c):
        start = pl.multiple_of((s * CTX + c) * self.rows, self.rows)
        return self.full.at[pl.ds(start, self.rows)]

    def half(self, s, c, which):
        size = self.rows // 2
        start = pl.multiple_of((s * CTX + c) * self.rows + which * size, size)
        return self.full.at[pl.ds(start, size)]

    def core_slot(self, step, part):
        return self.first + 4 + (step - 1) * 4 + part

    def core_send(self, src, c, part):
        links = self.links
        for step in range(1, links.shards):
            links.send(
                src,
                self.block(links.s, c),
                links.core_peer(step),
                self.core_slot(step, part),
            )

    def start(self):
        links = self.links
        own = self.block(links.s, links.c)
        links.send(self.src, own, links.x_dev, self.first)
        links.send(self.src, own, links.y_dev, self.first + 1)
        self.core_send(self.src, links.c, 0)
        self.local = links.keep(self.src, own if self.stage is None else self.stage)

    def settle(self):
        self.local.wait()
        self.local = self.links.keep(self.stage, self.block(self.links.s, self.links.c))

    def forward(self):
        links = self.links
        links.recv(self.block(links.s, links.c_x), self.first)
        links.recv(self.block(links.s, links.c_y), self.first + 1)
        from_x = self.half(links.s, links.c_x, 0)
        from_y = self.half(links.s, links.c_y, 1)
        links.send(from_x, from_x, links.y_dev, self.first + 2)
        links.send(from_y, from_y, links.x_dev, self.first + 3)
        self.core_send(self.block(links.s, links.c_x), links.c_x, 1)
        self.core_send(self.block(links.s, links.c_y), links.c_y, 2)

    def diagonal(self):
        links = self.links
        links.recv(self.half(links.s, links.c_d, 0), self.first + 2)
        links.recv(self.half(links.s, links.c_d, 1), self.first + 3)
        self.core_send(self.block(links.s, links.c_d), links.c_d, 3)

    def done(self):
        links = self.links
        for step in range(1, links.shards):
            other = lax.rem(links.s + links.shards - step, links.shards)
            for part, c in enumerate((links.c, links.c_x, links.c_y, links.c_d)):
                links.recv(self.block(other, c), self.core_slot(step, part))
        self.local.wait()


class LineGather:
    def __init__(self, links, own, full, tokens, pieces=1):
        self.links, self.own, self.full, self.tokens = links, own, full, tokens
        self.pieces, self.size = pieces, tokens // pieces
        self.first = links.slots(2 * (LINE - 1) * pieces)

    def block(self, owner, p):
        start = pl.multiple_of(place(owner) * self.tokens + p * self.size, self.size)
        return self.full.at[pl.ds(start, self.size)]

    def slot(self, side, k, p):
        return self.first + (side * (LINE - 1) + k - 1) * self.pieces + p

    def send(self, k, p=0):
        links = self.links
        t, u = links.t, LINE - 1 - links.t
        own = self.own.at[pl.ds(p * self.size, self.size)]
        right, left = self.block(t - k + 1, p), self.block(t + k - 1, p)
        links.send(
            own if k == 1 else right,
            right,
            links.right,
            self.slot(0, k, p),
            jnp.logical_and(t >= k - 1, t < LINE - 1),
        )
        links.send(
            own if k == 1 else left,
            left,
            links.left,
            self.slot(1, k, p),
            jnp.logical_and(u >= k - 1, u < LINE - 1),
        )

    def recv(self, k, p=0):
        links = self.links
        t, u = links.t, LINE - 1 - links.t

        @pl.when(t >= k)
        def _():
            links.recv(self.block(t - k, p), self.slot(0, k, p))

        @pl.when(u >= k)
        def _():
            links.recv(self.block(t + k, p), self.slot(1, k, p))


class LineScatter:
    def __init__(self, links, part, tokens, from_left, from_right, pieces=1):
        self.links, self.part, self.tokens = links, part, tokens
        self.from_left, self.from_right = from_left, from_right
        self.pieces, self.size = pieces, tokens // pieces
        self.first = links.slots(2 * (LINE - 1) * pieces)

    def slot(self, side, k, p):
        return self.first + (side * (LINE - 1) + k) * self.pieces + p

    def piece(self, ref, k, p):
        return ref.at[k, pl.ds(p * self.size, self.size)]

    def total(self, owner, k, p, arrived):
        @pl.loop(0, self.size // ROWS)
        def _(i):
            r = pl.multiple_of(p * self.size + i * ROWS, ROWS)
            q = pl.multiple_of(place(owner) * self.tokens + p * self.size + i * ROWS, ROWS)
            mine = self.part[pl.ds(q, ROWS), :].astype(f32)
            summed = mine + arrived[k, pl.ds(r, ROWS), :].astype(f32)
            arrived[k, pl.ds(r, ROWS), :] = summed.astype(arrived.dtype)

    def ends(self, k, p=0):
        links = self.links
        for side, behind, arrived, device in self.sides():
            owner = LINE - 1 - k if side == 0 else k
            piece, slot = self.piece(arrived, k, p), self.slot(side, k, p)

            @pl.when(behind == 0)
            def _():
                self.first_part(owner, k, p, arrived)

            links.send(piece, piece, device, slot, behind == 0)

    def sides(self):
        links = self.links
        return (
            (0, links.t, self.from_left, links.right),
            (1, LINE - 1 - links.t, self.from_right, links.left),
        )

    def stage(self, now, p=0):
        links = self.links
        for side, behind, arrived, device in self.sides():
            k = now - behind
            owner = LINE - 1 - k if side == 0 else k
            piece, slot = self.piece(arrived, k, p), self.slot(side, k, p)
            ready = jnp.logical_and(k >= 0, behind > 0)

            @pl.when(ready)
            def _():
                links.recv(piece, slot)
                self.total(owner, k, p, arrived)

            links.send(piece, piece, device, slot, ready)

    def first_part(self, owner, k, p, out):
        @pl.loop(0, self.size // ROWS)
        def _(i):
            r = pl.multiple_of(p * self.size + i * ROWS, ROWS)
            q = pl.multiple_of(place(owner) * self.tokens + p * self.size + i * ROWS, ROWS)
            out[k, pl.ds(r, ROWS), :] = self.part[pl.ds(q, ROWS), :].astype(out.dtype)

    def arrive(self, p=0):
        links = self.links
        t = links.t

        @pl.when(t > 0)
        def _():
            links.recv(
                self.piece(self.from_left, LINE - 1 - t, p), self.slot(0, LINE - 1 - t, p)
            )

        @pl.when(t < LINE - 1)
        def _():
            links.recv(self.piece(self.from_right, t, p), self.slot(1, t, p))

    def rows(self, r):
        t = self.links.t
        q = pl.multiple_of(place(t) * self.tokens + r, ROWS)
        k_l = jnp.minimum(LINE - 1 - t, LINE - 2)
        k_r = jnp.minimum(t, LINE - 2)
        zero = jnp.zeros((ROWS, self.part.shape[1]), f32)
        return (
            self.part[pl.ds(q, ROWS), :].astype(f32)
            + jnp.where(t > 0, self.from_left[k_l, pl.ds(r, ROWS), :].astype(f32), zero)
            + jnp.where(t < LINE - 1, self.from_right[k_r, pl.ds(r, ROWS), :].astype(f32), zero)
        )

    def owned(self, p, use):
        @pl.loop(0, self.size // ROWS)
        def _(i):
            r = pl.multiple_of(p * self.size + i * ROWS, ROWS)
            use(r, self.rows(r))


def line_ends(scatter, *hops):
    for k in hops:
        for p in range(scatter.pieces):
            scatter.ends(k, p)


def line_steps(scatter, now):
    for p in range(scatter.pieces):
        scatter.stage(now, p)


def line_finish(scatter, use, gather=None):
    for p in range(scatter.pieces):
        scatter.arrive(p)
        scatter.owned(p, use)
        if gather is not None:
            gather.send(1, p)


def line_spread(gather, k):
    for p in range(gather.pieces):
        gather.recv(k, p)
        if k < LINE - 1:
            gather.send(k + 1, p)


class PlaneScatter:
    def __init__(
        self, links, left, right, rows, core_in, x_in, y_in, x_last, y_last, out, parts=1
    ):
        self.links, self.left, self.right, self.rows = links, left, right, rows
        self.core_in, self.x_in, self.y_in = core_in, x_in, y_in
        self.x_last, self.y_last, self.out = x_last, y_last, out
        self.tile = min(256, CTX * rows)
        self.parts = parts if CTX * rows // self.tile % parts == 0 else 1
        self.core_first = links.slots((links.shards - 1) * self.parts)
        self.first = links.slots(6)

    def product(self, shard, i):
        start = pl.multiple_of(shard * (CTX * self.rows) + i * self.tile, self.tile)
        return tn_dot(self.left[:, pl.ds(start, self.tile)], self.right[...])

    def part(self, ref, index):
        size = CTX * self.rows // self.parts
        return ref.at[pl.ds(index * size, size)]

    def each_tile(self, index, body):
        tiles = CTX * self.rows // self.tile // self.parts

        @pl.loop(index * tiles, (index + 1) * tiles)
        def _(i):
            body(i, pl.ds(pl.multiple_of(i * self.tile, self.tile), self.tile))

    def other(self, step, stage):
        links = self.links
        target = lax.rem(links.s + step, links.shards)

        def tile(i, at):
            stage[at, :] = self.product(target, i).astype(bf16)

        for index in range(self.parts):
            self.each_tile(index, tile)
            links.send(
                self.part(stage, index),
                self.part(self.core_in.at[step - 1], index),
                links.core_peer(step),
                self.core_first + (step - 1) * self.parts + index,
            )

    def own(self):
        links = self.links

        def tile(i, at):
            summed = self.product(links.s, i)
            for step in range(1, links.shards):
                summed = summed + self.core_in[step - 1, at, :].astype(f32)
            self.core_in[0, at, :] = summed.astype(bf16)

        for index in range(self.parts):
            for step in range(1, links.shards):
                links.recv(
                    self.part(self.core_in.at[step - 1], index),
                    self.core_first + (step - 1) * self.parts + index,
                )
            self.each_tile(index, tile)

    def half(self, c, which):
        size = self.rows // 2
        start = pl.multiple_of(c * self.rows + which * size, size)
        return self.core_in.at[0, pl.ds(start, size)]

    def exchange(self):
        links, first = self.links, self.first
        links.send(self.half(links.c_d, 0), self.x_in.at[1], links.x_dev, first)
        links.send(self.half(links.c_d, 1), self.y_in.at[1], links.y_dev, first + 1)
        links.send(self.half(links.c_x, 0), self.x_in.at[0], links.x_dev, first + 2)
        links.send(self.half(links.c_y, 1), self.y_in.at[0], links.y_dev, first + 3)

    def add(self, c, which, arrived):
        size = self.rows // 2

        @pl.loop(0, size // ROWS)
        def _(i):
            r = pl.multiple_of(i * ROWS, ROWS)
            q = pl.multiple_of(c * self.rows + which * size + i * ROWS, ROWS)
            mine = self.core_in[0, pl.ds(q, ROWS), :].astype(f32)
            summed = mine + arrived[1, pl.ds(r, ROWS), :].astype(f32)
            self.core_in[0, pl.ds(q, ROWS), :] = summed.astype(bf16)

    def arrived(self):
        links, first = self.links, self.first
        for ref, offset in ((self.x_in, 0), (self.y_in, 1)):
            for part in range(2):
                links.recv(ref.at[1 - part], first + offset + 2 * part)

    def fold(self, here=False):
        links, first = self.links, self.first
        if not here:
            links.recv(self.x_in.at[1], first)
        self.add(links.c_y, 0, self.x_in)
        links.send(self.half(links.c_y, 0), self.y_last, links.y_dev, first + 4)
        if not here:
            links.recv(self.y_in.at[1], first + 1)
        self.add(links.c_x, 1, self.y_in)
        links.send(self.half(links.c_x, 1), self.x_last, links.x_dev, first + 5)

    def total(self, here=False):
        links, first = self.links, self.first
        size = self.rows // 2
        if not here:
            links.recv(self.x_in.at[0], first + 2)
            links.recv(self.y_in.at[0], first + 3)
        links.recv(self.y_last, first + 4)
        links.recv(self.x_last, first + 5)
        for which, arrived, last in ((0, self.x_in, self.y_last), (1, self.y_in, self.x_last)):

            @pl.loop(0, size // ROWS)
            def _(i):
                r = pl.multiple_of(i * ROWS, ROWS)
                q = pl.multiple_of(links.c * self.rows + which * size + i * ROWS, ROWS)
                self.out[pl.ds(which * size + r, ROWS), :] = (
                    self.core_in[0, pl.ds(q, ROWS), :].astype(f32)
                    + arrived[0, pl.ds(r, ROWS), :].astype(f32)
                    + last[pl.ds(r, ROWS), :].astype(f32)
                )

    @staticmethod
    def scratch(shards, rows, columns):
        half = (rows // 2, columns)
        return [
            pltpu.VMEM((shards - 1, CTX * rows, columns), bf16),
            pltpu.VMEM((2,) + half, bf16),
            pltpu.VMEM((2,) + half, bf16),
            pltpu.VMEM(half, bf16),
            pltpu.VMEM(half, bf16),
            pltpu.VMEM((rows, columns), f32),
        ]


def any_spec():
    return pl.BlockSpec(memory_space=pl.ANY)


def vmem_spec():
    return pl.BlockSpec(memory_space=pltpu.VMEM)


def struct(shape, dtype):
    return jax.ShapeDtypeStruct(shape, dtype)


def forward_kernel(
    shards,
    x, og, wq, wkv, wo, wg, wu, wd, gain_a, gain_m, frequency, order,
    wq_o, wkv_o, wo_o, wg_o, wu_o, wd_o, n1_o, og_o, n2_o, mid_o, qaug_o, kaug_o, kv_o, att_o, x_o,
    lse, gains, cos, sin,
    x_all, n1_all, wq_all, wkv_all, wo_all, gains_all, qaug, kv_all, kaug, v_all, scores, weights,
    attn, part, from_left, from_right, mid, n2, og_stage, wg_stage, wu_stage, wd_stage, gpad,
    send_sems, recv_sems, local_sems,
):
    tokens, width = x.shape
    queries = tokens * LINE
    heads = qaug.shape[0]
    links = Links(shards, send_sems, recv_sems, local_sems)
    s, c, t = links.s, links.c, links.t

    gather_x = LineGather(links, x, x_all, tokens, PIECES)
    gather_og = LineGather(links, og, og_o, tokens)
    gather_n2 = LineGather(links, n2, n2_o, tokens, PIECES)
    small = [PlaneGather(links, *pair) for pair in ((wq, wq_all), (wkv, wkv_all), (wo, wo_all))]
    large = [
        PlaneGather(links, *three)
        for three in ((wg, wg_o, wg_stage), (wu, wu_o, wu_stage), (wd, wd_o, wd_stage))
    ]
    scatter = LineScatter(links, part, tokens, from_left, from_right, PIECES)
    plane = shards * CTX
    gain_slot = links.slots(plane - 1)
    kv_slot = links.slots((CTX - 1) * (2 * LINE - 1))

    links.greet()
    me = s * CTX + c
    own_gains = gain_a.shape[0]
    if own_gains == width:
        own_lanes = slice(0, width)
    else:
        gpad[...] = jnp.zeros_like(gpad)
        own_lanes = pl.ds(pl.multiple_of(me * own_gains, own_gains), own_gains)
    for row, gain in enumerate((gain_a, gain_m)):
        gpad[row : row + 1, own_lanes] = gain[...].astype(f32).reshape(1, own_gains)
    links.met()
    for step in range(1, plane):
        links.send(gpad, gains_all.at[me], links.plane_peer(step), gain_slot + step - 1)
    own_gain = links.keep(gpad, gains_all.at[me])
    for p in range(PIECES):
        gather_x.send(1, p)
    own_rows = pl.ds(pl.multiple_of(place(t) * tokens, tokens), tokens)
    own_x = links.keep(x, x_all.at[own_rows])
    for gather in small:
        gather.start()

    per = queries // BLOCK
    lane = lax.broadcasted_iota(jnp.int32, (1, queries), 1)
    owner = jnp.zeros((1, queries), jnp.int32)
    for index in range(LINE):
        owner = jnp.where(lane // tokens == place(index), index, owner)
    slot = owner * tokens + lax.rem(lane, tokens)
    block_here = jnp.zeros((1, queries), jnp.int32)
    for index in range(per):
        block_here = jnp.where(slot // BLOCK == index, order[c * per + index], block_here)
    position = (block_here * BLOCK + lax.rem(slot, BLOCK)).astype(f32)
    angles = frequency[...] * position
    cos[...] = jnp.cos(angles)
    sin[...] = jnp.sin(angles)
    row = lax.broadcasted_iota(jnp.int32, (HD, queries), 0)
    bias = jnp.zeros((HD, queries), f32)
    for index in range(BLOCKS):
        barred = jnp.logical_and(row == index, order[index] > block_here)
        bias = jnp.where(barred, blocked, bias)
    bias = bias.astype(bf16)
    for h in range(heads):
        qaug[h, HD:, :] = bias

    own_gain.wait()
    for step in range(1, plane):
        other = lax.rem(me + plane - step, plane)
        links.recv(gains_all.at[other], gain_slot + step - 1)
    total = gains_all[0]
    for index in range(1, plane):
        total = total + gains_all[index]
    gains[...] = total
    own_x.wait()

    def norm_block(owner):
        @pl.loop(0, tokens // ROWS)
        def _(i):
            r = pl.multiple_of(place(owner) * tokens + i * ROWS, ROWS)
            v = x_all[pl.ds(r, ROWS), :].astype(f32)
            inverse = lax.rsqrt(jnp.mean(v * v, -1, keepdims=True) + epsilon)
            n1_all[pl.ds(r, ROWS), :] = (v * inverse * gains[0:1, :]).astype(bf16)

    own_og = links.keep(og, og_stage)
    norm_block(t)
    line_spread(gather_x, 1)
    for gather in small:
        gather.forward()
    norm_pair(gather_x, norm_block, 1)
    line_spread(gather_x, 2)
    gather_og.send(1)
    for gather in small:
        gather.diagonal()
    norm_pair(gather_x, norm_block, 2)
    own_og.wait()
    links.keep_later(og_stage, og_o.at[own_rows])
    for gather in small:
        gather.done()

    half = HD // 2
    scale = HD ** (-0.5)

    def lanes_of(owner):
        return pl.ds(pl.multiple_of(place(owner) * tokens, tokens), tokens)

    def turn(v1, v2, cosine, sine):
        return (v1 * cosine - v2 * sine).astype(bf16), (v2 * cosine + v1 * sine).astype(bf16)

    def project_block(owner):
        at = lanes_of(owner)
        cosine, sine = cos[:, at], sin[:, at]
        kv_t = nn_dot(n1_all[at, :], wkv_all[...]).T
        k1, k2 = turn(kv_t[0:half], kv_t[half:HD], cosine, sine)
        kv_all[c, 0:half, at] = k1
        kv_all[c, half:HD, at] = k2
        kv_all[c, HD : 2 * HD, at] = kv_t[HD:].astype(bf16)
        q_t = nn_dot(n1_all[at, :], wq_all[...]).T
        for h in range(heads):
            b = h * HD
            q1, q2 = turn(q_t[b : b + half], q_t[b + half : b + HD], cosine, sine)
            qaug[h, 0:half, at] = (q1 * scale).astype(bf16)
            qaug[h, half:HD, at] = (q2 * scale).astype(bf16)

    u = LINE - 1 - t
    arrivals = [(t, None)]
    for k in range(1, LINE):
        arrivals += [(t - k, t >= k), (t + k, u >= k)]

    def send_block(index):
        owner, cond = arrivals[index]
        for step in range(1, CTX):
            peer = lax.rem(c + step, CTX)
            ref = kv_all.at[c, :, lanes_of(owner)]
            links.send(ref, ref, (s, peer, t), kv_slot + index * (CTX - 1) + step - 1, cond)

    def recv_block(index):
        owner, cond = arrivals[index]

        def wait():
            for step in range(1, CTX):
                other = lax.rem(c + CTX - step, CTX)
                slot = kv_slot + index * (CTX - 1) + step - 1
                links.recv(kv_all.at[other, :, lanes_of(owner)], slot)

        if cond is None:
            wait()
        else:
            pl.when(cond)(wait)

    project_block(t)
    send_block(0)
    for k in range(1, LINE):
        if k == LINE - 1:
            line_spread(gather_x, k)
            norm_pair(gather_x, norm_block, k)
        norm_pair(gather_x, project_block, k)
        send_block(2 * k - 1)
        send_block(2 * k)
    for gather in large:
        gather.start()
    links.keep_later(n1_all, n1_o)
    links.keep_later(x_all, x_o)
    links.keep_later(wq_all, wq_o)
    links.keep_later(wkv_all, wkv_o)
    links.keep_later(wo_all, wo_o)
    links.keep_later(qaug, qaug_o)
    for index in range(len(arrivals)):
        recv_block(index)
    for other in range(CTX):
        row = lax.broadcasted_iota(jnp.int32, (HD, queries), 0)
        lane = lax.broadcasted_iota(jnp.int32, (HD, queries), 1)
        mark = (row == other * (queries // BLOCK) + lax.rem(lane // tokens, 2)).astype(f32).astype(bf16)
        both = jnp.concatenate([kv_all[other, 0:HD, :], mark], 0)
        kaug[other * queries : (other + 1) * queries, :] = both.T
        v_all[:, other * queries : (other + 1) * queries] = kv_all[other, HD : 2 * HD, :]
    links.keep_later(kaug, kaug_o)
    links.keep_later(kv_all, kv_o)

    length = queries * CTX

    far = pl.multiple_of(jnp.where(t < LINE // 2, tokens, 0), tokens)
    near = pl.multiple_of(jnp.where(t < LINE // 2, 0, tokens), tokens)

    def soften(query):
        size = query.shape[1]
        top = jnp.full((1, size), -jnp.inf, f32)
        for b in range(0, length, BLOCK):
            block_scores = nn_dot(kaug[b : b + BLOCK, :], query)
            scores[b : b + BLOCK, :] = block_scores
            top = jnp.maximum(top, jnp.max(block_scores, 0, keepdims=True))
        norm = jnp.zeros((1, size), f32)
        for b in range(0, length, BLOCK):
            exponent = jnp.exp(scores[b : b + BLOCK, :] - top)
            norm = norm + jnp.sum(exponent, 0, keepdims=True)
            weights[b : b + BLOCK, :] = exponent.astype(bf16)
        out = nn_dot(v_all[...], weights[...]) / norm
        return out.astype(bf16), top + jnp.log(norm)

    def put(h, lanes, out, log_sum):
        attn[pl.ds(pl.multiple_of(h * HD, HD), HD), lanes] = out
        lse[h, :, lanes] = log_sum

    def head(lanes, h):
        put(h, lanes, *soften(qaug[h, :, lanes]))

    def head_pair(lanes, g):
        h = 2 * g
        both = jnp.concatenate([qaug[h, :, lanes], qaug[h + 1, :, lanes]], 1)
        out, log_sum = soften(both)
        put(h, lanes, out[:, 0:tokens], log_sum[:, 0:tokens])
        put(h + 1, lanes, out[:, tokens:], log_sum[:, tokens:])

    def attend(start, size):
        if size == tokens:
            pl.loop(0, heads // 2)(functools.partial(head_pair, pl.ds(start, size)))
        else:
            pl.loop(0, heads)(functools.partial(head, pl.ds(start, size)))
        rows = pl.ds(start, size)
        attn_rows = attn[:, rows].T
        for b in range(0, width, 512):
            part[rows, b : b + 512] = nt_dot(attn_rows, wo_all[b : b + 512, :])

    attend(far, tokens)
    line_ends(scatter, 0)
    gather_og.recv(1)
    gather_og.send(2)
    for gather in large:
        gather.settle()
    attend(2 * tokens, 2 * tokens)
    line_ends(scatter, 1, 2)
    gather_og.recv(2)
    gather_og.send(3)
    line_steps(scatter, 1)
    attend(near, tokens)
    links.keep_later(attn, att_o)

    def finish_rows(r, summed):
        q = pl.multiple_of(place(t) * tokens + r, ROWS)
        middle = x_all[pl.ds(q, ROWS), :].astype(f32) + summed
        mid[pl.ds(r, ROWS), :] = middle
        inverse = lax.rsqrt(jnp.mean(middle * middle, -1, keepdims=True) + epsilon)
        n2[pl.ds(r, ROWS), :] = (middle * inverse * gains[1:2, :]).astype(bf16)

    large[0].forward()
    line_steps(scatter, 2)
    large[1].forward()
    line_finish(scatter, finish_rows, gather_n2)
    large[2].forward()
    links.keep_later(n2, n2_o.at[own_rows])
    links.keep_later(mid, mid_o)
    line_spread(gather_n2, 1)
    large[0].diagonal()
    large[1].diagonal()
    line_spread(gather_n2, 2)
    large[2].diagonal()
    gather_og.recv(3)
    line_spread(gather_n2, 3)
    for gather in large:
        gather.done()
    links.finish()


def norm_pair(gather, norm_block, k):
    t, u = gather.links.t, LINE - 1 - gather.links.t

    @pl.when(t >= k)
    def _():
        norm_block(t - k)

    @pl.when(u >= k)
    def _():
        norm_block(t + k)


def forward_call(shards, x, og, weights_in, gain_a, gain_m, frequency, order):
    wq, wkv, wo, wg, wu, wd = weights_in
    tokens, width = x.shape
    queries = tokens * LINE
    length = queries * CTX
    heads = wq.shape[1] // HD
    plane = shards * CTX
    full = [struct((width, w.shape[1]), bf16) for w in weights_in]
    outs = full + [
        struct((queries, width), bf16),
        struct((queries, width), bf16),
        struct((queries, width), bf16),
        struct((tokens, width), f32),
        struct((heads, 2 * HD, queries), bf16),
        struct((length, 2 * HD), bf16),
        struct((CTX, 2 * HD, queries), bf16),
        struct((heads * HD, queries), bf16),
        struct((queries, width), bf16),
        struct((heads, 1, queries), f32),
        struct((2, width), f32),
        struct((HD // 2, queries), f32),
        struct((HD // 2, queries), f32),
    ]
    block = (LINE - 1, tokens, width)
    count = 6 + 18 * PIECES + 6 * (4 + 4 * (shards - 1)) + plane - 1 + 21
    return pl.pallas_call(
        functools.partial(forward_kernel, shards),
        out_shape=outs,
        in_specs=[any_spec()] * 8
        + [vmem_spec()] * 3
        + [pl.BlockSpec(memory_space=pltpu.SMEM)],
        out_specs=[any_spec()] * 15 + [vmem_spec()] * 4,
        scratch_shapes=[
            pltpu.VMEM((queries, width), bf16),
            pltpu.VMEM((queries, width), bf16),
            pltpu.VMEM((width, wq.shape[1]), bf16),
            pltpu.VMEM((width, wkv.shape[1]), bf16),
            pltpu.VMEM((width, wo.shape[1]), bf16),
            pltpu.VMEM((plane, 2, width), f32),
            pltpu.VMEM((heads, 2 * HD, queries), bf16),
            pltpu.VMEM((CTX, 2 * HD, queries), bf16),
            pltpu.VMEM((length, 2 * HD), bf16),
            pltpu.VMEM((HD, length), bf16),
            pltpu.VMEM((length, queries // 2), f32),
            pltpu.VMEM((length, queries // 2), bf16),
            pltpu.VMEM((heads * HD, queries), bf16),
            pltpu.VMEM((queries, width), f32),
            pltpu.VMEM(block, bf16),
            pltpu.VMEM(block, bf16),
            pltpu.VMEM((tokens, width), f32),
            pltpu.VMEM((tokens, width), bf16),
            pltpu.VMEM((tokens, width), bf16),
            pltpu.VMEM(wg.shape, bf16),
            pltpu.VMEM(wu.shape, bf16),
            pltpu.VMEM(wd.shape, bf16),
            pltpu.VMEM((2, width), f32),
            pltpu.SemaphoreType.DMA((count,)),
            pltpu.SemaphoreType.DMA((count,)),
            pltpu.SemaphoreType.DMA((32,)),
        ],
        compiler_params=pltpu.CompilerParams(
            collective_id=0, has_side_effects=True, vmem_limit_bytes=60 * 2**20
        ),
        name="forward",
    )(x, og, wq, wkv, wo, wg, wu, wd, gain_a, gain_m, frequency, order)


def middle_kernel(
    shards, rows,
    n2_in, og_in, wg_in, wu_in, wd_in, mid_in, gains,
    dmid_o, dmid_all_o, gg_o, gd_part_o, gd_x_o, gd_y_o, branch_o, gu_part_o, gain_sum,
    n2, og, wg, wu, wd, mid, hidden, dgate, dup, part, branch,
    left, right, dmid, dsend, gain_rows, up_in, first,
    *rest,
):
    grads, (send_sems, recv_sems, local_sems) = rest[:-3], rest[-3:]
    tokens, width = mid.shape
    queries = n2.shape[0]
    columns = wg.shape[1]
    links = Links(shards, send_sems, recv_sems, local_sems)
    t = links.t
    links.greet()
    own_rows = pl.ds(pl.multiple_of(place(t) * tokens, tokens), tokens)

    far = pl.multiple_of(jnp.where(t < LINE // 2, tokens, 0), tokens)
    near = pl.multiple_of(jnp.where(t < LINE // 2, 0, tokens), tokens)
    sides = [pl.ds(far, tokens), pl.ds(2 * tokens, 2 * tokens), pl.ds(near, tokens)]
    full, rest_columns = columns // 256, columns % 256
    weights = ((wg_in, wg), (wu_in, wu), (wd_in, wd))

    def fetch(j, start, size, index):
        src, dst = weights[j]
        of = pl.ds(start, size)
        sem = local_sems.at[3 * index + j]
        return pltpu.make_async_copy(src.at[:, of], dst.at[:, of], sem)

    links.local_used = 3 * (full + 1)
    load_n2 = [links.keep(n2_in.at[sides[0]], n2.at[sides[0]])]
    for index in range(full):
        for j in range(3):
            fetch(j, index * 256, 256, index).start()
        if index == 0:
            load_og = [links.keep(og_in.at[sides[0]], og.at[sides[0]])]
    if rest_columns:
        for j in range(3):
            fetch(j, full * 256, rest_columns, full).start()
    load_n2 += [links.keep(n2_in.at[at], n2.at[at]) for at in sides[1:]]
    load_og += [links.keep(og_in.at[at], og.at[at]) for at in sides[1:]]
    load_mid = links.keep(mid_in, mid)
    scatter = LineScatter(links, part, tokens, left, right, PIECES)
    gather = LineGather(links, dsend, dmid_all_o, tokens, PIECES)
    down = PlaneScatter(links, og, hidden, rows, *grads[0:6])
    gate = PlaneScatter(links, n2, dgate, rows, *grads[6:12], parts=2)
    up = PlaneScatter(links, n2, dup, rows, up_in, None, None, None, None, None)

    def feed_forward(half):
        at = sides[half]
        load_n2[half].wait()
        load_og[half].wait()

        def tile(start, size, index):
            of = pl.ds(start, size)
            if half == 0:
                fetch(0, start, size, index).wait()
                fetch(1, start, size, index).wait()
            gate_act = nn_dot(n2[at, :], wg[:, of])
            up_act = nn_dot(n2[at, :], wu[:, of])
            if half == 0:
                fetch(2, start, size, index).wait()
            d_hidden = nn_dot(og[at, :], wd[:, of])
            sig = jax.nn.sigmoid(gate_act)
            silu = gate_act * sig
            hidden[at, of] = (silu * up_act).astype(bf16)
            d_gate = d_hidden * up_act * sig * (1.0 + gate_act * (1.0 - sig))
            dgate[at, of] = d_gate.astype(bf16)
            dup[at, of] = (d_hidden * silu).astype(bf16)
            if half == 0:
                for b in range(0, width, 512):
                    e = b + 512
                    summed = nt_dot(dgate[at, of], wg[b:e, of]) + nt_dot(dup[at, of], wu[b:e, of])
                    first[:, b:e] += summed

        @pl.loop(0, full)
        def _(index):
            tile(pl.multiple_of(index * 256, 256), 256, index)

        if rest_columns:
            tile(full * 256, rest_columns, full)
        if half == 0:
            part[at, :] = first[...].astype(bf16)
            return

        @pl.loop(0, width // 512)
        def _(j):
            of = pl.ds(pl.multiple_of(j * 512, 512), 512)
            summed = nt_dot(dgate[at, :], wg[of, :]) + nt_dot(dup[at, :], wu[of, :])
            part[at, of] = summed.astype(bf16)

    piece = CTX * rows

    def others(grad, room):
        for step in range(1, shards):
            grad.other(step, room.at[pl.ds((step - 1) * piece, piece)])

    first[...] = jnp.zeros_like(first)
    feed_forward(0)
    links.met()
    line_ends(scatter, 0)
    feed_forward(1)
    line_ends(scatter, 1, 2)
    line_steps(scatter, 1)
    feed_forward(2)
    others(gate, wg)
    line_steps(scatter, 2)

    gate.own()
    gate.exchange()

    @pl.loop(0, width // 512)
    def _(j):
        of = pl.ds(pl.multiple_of(j * 512, 512), 512)
        branch[:, of] = nt_dot(hidden[...], wd[of, :]).astype(bf16)

    links.keep_later(branch, branch_o)
    others(down, wd)
    load_mid.wait()
    gain_rows[...] = jnp.zeros_like(gain_rows)

    def finish_rows(r, d_normed):
        at = pl.ds(r, ROWS)
        q = pl.ds(pl.multiple_of(place(t) * tokens + r, ROWS), ROWS)
        middle = mid[at, :]
        inverse = lax.rsqrt(jnp.mean(middle * middle, -1, keepdims=True) + epsilon)
        unit = middle * inverse
        gain_rows[...] += d_normed * unit
        d_unit = d_normed * gains[1:2, :]
        back = inverse * (d_unit - unit * jnp.mean(d_unit * unit, -1, keepdims=True))
        d_middle = og[q, :].astype(f32) + back
        dmid[at, :] = d_middle
        dsend[at, :] = d_middle.astype(bf16)

    line_finish(scatter, finish_rows, gather)
    gate.fold()
    down.own()
    down.exchange()
    links.keep_later(dsend, dmid_all_o.at[own_rows])
    links.keep_later(dmid, dmid_o)
    links.keep_later(down.core_in.at[0], gd_part_o)
    line_spread(gather, 1)
    others(up, wu)
    gain_sum[...] = jnp.sum(gain_rows[...], 0, keepdims=True)
    line_spread(gather, 2)
    up.own()
    links.keep_later(up_in.at[0], gu_part_o)
    gate.total()
    links.keep_later(gate.out, gg_o)
    line_spread(gather, 3)
    down.arrived()
    links.keep_later(down.x_in, gd_x_o)
    links.keep_later(down.y_in, gd_y_o)
    links.finish()


def middle_call(shards, rows, n2, og, wg, wu, wd, mid, gains):
    queries, width = n2.shape
    tokens = mid.shape[0]
    columns = wg.shape[1]
    token = (tokens, width)
    wide = (queries, columns)
    block = (LINE - 1,) + token
    outs = [
        struct(token, f32),
        struct((queries, width), bf16),
        struct((rows, columns), f32),
        struct((CTX * rows, columns), bf16),
        struct((2, rows // 2, columns), bf16),
        struct((2, rows // 2, columns), bf16),
        struct((queries, width), bf16),
        struct((CTX * rows, columns), bf16),
        struct((1, width), f32),
    ]
    count = 12 * PIECES + 3 * (2 * (shards - 1) + 6)
    return pl.pallas_call(
        functools.partial(middle_kernel, shards, rows),
        out_shape=outs,
        in_specs=[any_spec()] * 6 + [vmem_spec()],
        out_specs=[any_spec()] * 8 + [vmem_spec()],
        scratch_shapes=[
            pltpu.VMEM((queries, width), bf16),
            pltpu.VMEM((queries, width), bf16),
            pltpu.VMEM((width, columns), bf16),
            pltpu.VMEM((width, columns), bf16),
            pltpu.VMEM((width, columns), bf16),
            pltpu.VMEM(token, f32),
            pltpu.VMEM(wide, bf16),
            pltpu.VMEM(wide, bf16),
            pltpu.VMEM(wide, bf16),
            pltpu.VMEM((queries, width), bf16),
            pltpu.VMEM((queries, width), bf16),
            pltpu.VMEM(block, bf16),
            pltpu.VMEM(block, bf16),
            pltpu.VMEM(token, f32),
            pltpu.VMEM(token, bf16),
            pltpu.VMEM((ROWS, width), f32),
            pltpu.VMEM((shards - 1, CTX * rows, columns), bf16),
            pltpu.VMEM(token, f32),
            *PlaneScatter.scratch(shards, rows, columns),
            *PlaneScatter.scratch(shards, rows, columns),
            pltpu.SemaphoreType.DMA((count,)),
            pltpu.SemaphoreType.DMA((count,)),
            pltpu.SemaphoreType.DMA((40,)),
        ],
        compiler_params=pltpu.CompilerParams(
            collective_id=1, has_side_effects=True, vmem_limit_bytes=63 * 2**20
        ),
        name="middle",
    )(n2, og, wg, wu, wd, mid, gains)


def backward_kernel(
    shards, rows,
    dmid_all_in, wo_in, wq_in, wkv_in, n1_in, qaug_in, kaug_in, kv_in, att_in, x_in, dmid_in,
    branch_in, gu_part_in, gd_part_in, gd_x_in, gd_y_in, mid_in, lse, gains, gain_mlp, cos, sin,
    in_o, gq_o, gkv_o, go_o, gu_o, gd_o, out_o, gain_o,
    dmid_all, wo, wq, wkv, n1, qaug, kaug, kv, att, x, dmid,
    d_out, attn_rows, v_rows, d_keys, d_values, d_query, d_query_rows, kv_send, kv_recv, d_kv, part,
    left, right, gain_rows, pair, plane_in, line_in, total, stage_o, stage_q, stage_kv,
    branch, left_b, right_b, mid, layer, gain_sum, part_query,
    *rest,
):
    grads, (send_sems, recv_sems, local_sems) = rest[:-3], rest[-3:]
    tokens, width = dmid.shape
    queries = n1.shape[0]
    heads = qaug.shape[0]
    length = kaug.shape[0]
    half = HD // 2
    plane = shards * CTX
    links = Links(shards, send_sems, recv_sems, local_sems)
    s, c, t = links.s, links.c, links.t
    links.greet(whole_line=True)

    scatter = LineScatter(links, part, tokens, left, right, PIECES)
    scatter_out = LineScatter(links, branch, tokens, left_b, right_b)
    g_o = PlaneScatter(links, dmid_all, attn_rows, rows, *grads[0:6])
    g_q = PlaneScatter(links, n1, d_query_rows, rows, *grads[6:12])
    g_kv = PlaneScatter(links, n1, d_kv, rows, *grads[12:18])
    g_u = PlaneScatter(links, None, None, rows, *grads[18:24])
    g_d = PlaneScatter(links, None, None, rows, *grads[24:30])
    kv_slot = links.slots(CTX - 1)
    plane_slot = links.slots(plane - 1)
    line_slot = links.slots(LINE - 1)
    piece = CTX * rows
    loads = [
        links.keep(src, dst)
        for src, dst in (
            (dmid_all_in, dmid_all), (wo_in, wo), (branch_in, branch), (gu_part_in, g_u.core_in.at[0]),
            (att_in, att), (kv_in, kv), (qaug_in, qaug), (kaug_in, kaug),
            (gd_part_in, g_d.core_in.at[0]), (gd_x_in, g_d.x_in), (gd_y_in, g_d.y_in), (n1_in, n1),
            (wq_in, wq), (wkv_in, wkv), (x_in, x), (dmid_in, dmid), (mid_in, mid),
        )
    ]

    def others(grad, stage):
        for step in range(1, shards):
            grad.other(step, stage.at[pl.ds((step - 1) * piece, piece)])

    for load in loads[0:2]:
        load.wait()
    d_out[...] = nn_dot(dmid_all[...], wo[...]).astype(bf16).T
    links.met()
    loads[2].wait()
    line_ends(scatter_out, 0)
    loads[3].wait()
    g_u.exchange()
    for load in loads[4:8]:
        load.wait()
    for other in range(CTX):
        v_rows[other * queries : (other + 1) * queries, :] = kv[other, HD : 2 * HD, :].T
    d_keys[...] = jnp.zeros_like(d_keys)
    d_values[...] = jnp.zeros_like(d_values)

    def head(h):
        at = pl.ds(pl.multiple_of(h * HD, HD), HD)
        query = qaug[h]
        d_head = d_out[at, :]
        delta = jnp.sum(d_head.astype(f32) * att[at, :].astype(f32), 0, keepdims=True)
        log_sum = lse[h]
        d_q = jnp.zeros((HD, queries), f32)
        for b in range(0, length, BLOCK):
            e = b + BLOCK
            probs = jnp.exp(nn_dot(kaug[b:e, :], query) - log_sum)
            d_probs = nn_dot(v_rows[b:e, :], d_head)
            d_scores = (probs * (d_probs - delta)).astype(bf16)
            d_values[b:e, :] += nt_dot(probs.astype(bf16), d_head)
            d_keys[b:e, :] += nt_dot(d_scores, query[0:HD])
            at_b = b % queries
            d_q = d_q + nn_dot(kv[b // queries, 0:HD, at_b : at_b + BLOCK], d_scores)
        d_query[at, :] = d_q * (HD ** (-0.5))

    pl.loop(0, heads // 2)(head)
    line_ends(scatter_out, 1, 2)
    scatter_out.stage(1)
    for load in loads[8:11]:
        load.wait()
    g_d.fold(here=True)
    pl.loop(heads // 2, heads)(head)

    def pack(other):
        block = pl.ds(pl.multiple_of(other * queries, queries), queries)
        both = jnp.concatenate([d_keys[block, :], d_values[block, :]], 1)
        kv_send[other] = both.astype(bf16)

    for step in range(1, CTX):
        peer = lax.rem(c + step, CTX)
        pack(peer)
        links.send(kv_send.at[peer], kv_recv.at[step - 1], (s, peer, t), kv_slot + step - 1)
    pack(c)
    scatter_out.stage(2)
    for load in loads[11:]:
        load.wait()

    cosine, sine = cos[...], sin[...]
    for h in range(heads):
        at = h * HD
        d1, d2 = d_query[at : at + half, :], d_query[at + half : at + HD, :]
        d_query[at : at + half, :] = d1 * cosine + d2 * sine
        d_query[at + half : at + HD, :] = d2 * cosine - d1 * sine
    d_query_rows[...] = d_query[...].astype(bf16).T
    for b in range(0, width, 512):
        part_query[:, b : b + 512] = nt_dot(d_query_rows[...], wq[b : b + 512, :])
    others(g_q, stage_q)
    attn_rows[...] = att[...].T
    others(g_o, stage_o)
    for step in range(1, CTX):
        links.recv(kv_recv.at[step - 1], kv_slot + step - 1)
    d_pair = kv_send[c].astype(f32)
    for step in range(1, CTX):
        d_pair = d_pair + kv_recv[step - 1].astype(f32)
    d_pair = d_pair.T
    d1, d2 = d_pair[0:half], d_pair[half:HD]
    turned = jnp.concatenate(
        [d1 * cosine + d2 * sine, d2 * cosine - d1 * sine, d_pair[HD:]], 0
    )
    d_kv[...] = turned.astype(bf16).T

    for b in range(0, width, 512):
        summed = part_query[:, b : b + 512] + nt_dot(d_kv[...], wkv[b : b + 512, :])
        part[:, b : b + 512] = summed.astype(bf16)

    line_ends(scatter, 0, 1)

    gain_rows[...] = jnp.zeros_like(gain_rows)

    @pl.loop(0, queries // ROWS)
    def _(i):
        r = pl.ds(pl.multiple_of(i * ROWS, ROWS), ROWS)
        v = x[r, :].astype(f32)
        inverse = lax.rsqrt(jnp.mean(v * v, -1, keepdims=True) + epsilon)
        gain_rows[...] += part[r, :].astype(f32) * (v * inverse)

    pair[0:1, :] = jnp.sum(gain_rows[...], 0, keepdims=True)
    pair[1:2, :] = gain_mlp[...]
    for step in range(1, plane):
        links.send(pair, plane_in.at[step - 1], links.plane_peer(step), plane_slot + step - 1)
    g_u.fold()
    line_steps(scatter, 1)
    g_o.own()
    g_o.exchange()
    summed = pair[...]
    for step in range(1, plane):
        links.recv(plane_in.at[step - 1], plane_slot + step - 1)
        summed = summed + plane_in[step - 1]
    total[...] = summed
    for step in range(1, LINE):
        links.send(total, line_in.at[step - 1], links.line_peer(step), line_slot + step - 1)
    line_ends(scatter, 2)
    others(g_kv, stage_kv)
    g_q.own()
    g_q.exchange()
    line_steps(scatter, 2)
    g_kv.own()
    g_kv.exchange()
    g_o.fold()
    scatter_out.arrive()

    def layer_rows(r, total_rows):
        layer[pl.ds(r, ROWS), :] = (mid[pl.ds(r, ROWS), :] + total_rows).astype(bf16)

    scatter_out.owned(0, layer_rows)
    links.keep_later(layer, out_o)
    g_u.total()
    links.keep_later(g_u.out, gu_o)
    g_q.fold()
    g_d.total(here=True)
    links.keep_later(g_d.out, gd_o)
    g_kv.fold()
    g_o.total()
    links.keep_later(g_o.out, go_o)

    def finish_rows(r, d_normed):
        at = pl.ds(r, ROWS)
        q = pl.ds(pl.multiple_of(place(t) * tokens + r, ROWS), ROWS)
        v = x[q, :].astype(f32)
        inverse = lax.rsqrt(jnp.mean(v * v, -1, keepdims=True) + epsilon)
        unit = v * inverse
        d_unit = d_normed * gains[0:1, :]
        back = inverse * (d_unit - unit * jnp.mean(d_unit * unit, -1, keepdims=True))
        dmid[at, :] = dmid[at, :] + back

    scatter.arrive(0)
    scatter.owned(0, finish_rows)
    g_q.total()
    links.keep_later(g_q.out, gq_o)
    g_kv.total()
    links.keep_later(g_kv.out, gkv_o)
    for p in range(1, PIECES):
        scatter.arrive(p)
        scatter.owned(p, finish_rows)
    links.keep_later(dmid, in_o)
    for step in range(1, LINE):
        links.recv(line_in.at[step - 1], line_slot + step - 1)
        summed = summed + line_in[step - 1]
    own_gains = gain_o.shape[1]
    if own_gains == width:
        gain_o[...] = summed
    else:
        gain_sum[...] = summed
        me = s * CTX + c
        gain_o[...] = gain_sum[:, pl.ds(pl.multiple_of(me * own_gains, own_gains), own_gains)]
    links.finish()


def backward_call(
    shards, rows, dmid_all, wo, wq, wkv, n1, qaug, kaug, kv, att, x, dmid, branch, gu_part,
    gd_part, gd_x, gd_y, mid, lse, gains, gain_mlp, cos, sin,
):
    tokens, width = dmid.shape
    queries = n1.shape[0]
    heads = qaug.shape[0]
    length = kaug.shape[0]
    inner = heads * HD
    columns = gu_part.shape[1]
    plane = shards * CTX
    own_gains = width // plane if width // plane % 128 == 0 else width
    piece = CTX * rows * (shards - 1)
    token = (tokens, width)
    block = (LINE - 1,) + token
    outs = [
        struct(token, f32),
        struct((rows, inner), f32),
        struct((rows, 2 * HD), f32),
        struct((rows, inner), f32),
        struct((rows, columns), f32),
        struct((rows, columns), f32),
        struct(token, bf16),
        struct((2, own_gains), f32),
    ]
    count = 6 + 6 * PIECES + 5 * (2 * (shards - 1) + 6) + CTX - 1 + plane - 1 + LINE - 1
    return pl.pallas_call(
        functools.partial(backward_kernel, shards, rows),
        out_shape=outs,
        in_specs=[any_spec()] * 17 + [vmem_spec()] * 5,
        out_specs=[any_spec()] * 7 + [vmem_spec()],
        scratch_shapes=[
            pltpu.VMEM((queries, width), bf16),
            pltpu.VMEM((width, inner), bf16),
            pltpu.VMEM((width, inner), bf16),
            pltpu.VMEM((width, 2 * HD), bf16),
            pltpu.VMEM((queries, width), bf16),
            pltpu.VMEM(qaug.shape, bf16),
            pltpu.VMEM(kaug.shape, bf16),
            pltpu.VMEM(kv.shape, bf16),
            pltpu.VMEM((inner, queries), bf16),
            pltpu.VMEM((queries, width), bf16),
            pltpu.VMEM(token, f32),
            pltpu.VMEM((inner, queries), bf16),
            pltpu.VMEM((queries, inner), bf16),
            pltpu.VMEM((length, HD), bf16),
            pltpu.VMEM((length, HD), f32),
            pltpu.VMEM((length, HD), f32),
            pltpu.VMEM((inner, queries), f32),
            pltpu.VMEM((queries, inner), bf16),
            pltpu.VMEM((CTX, queries, 2 * HD), bf16),
            pltpu.VMEM((CTX - 1, queries, 2 * HD), bf16),
            pltpu.VMEM((queries, 2 * HD), bf16),
            pltpu.VMEM((queries, width), bf16),
            pltpu.VMEM(block, bf16),
            pltpu.VMEM(block, bf16),
            pltpu.VMEM((ROWS, width), f32),
            pltpu.VMEM((2, width), f32),
            pltpu.VMEM((plane - 1, 2, width), f32),
            pltpu.VMEM((LINE - 1, 2, width), f32),
            pltpu.VMEM((2, width), f32),
            pltpu.VMEM((piece, inner), bf16),
            pltpu.VMEM((piece, inner), bf16),
            pltpu.VMEM((piece, 2 * HD), bf16),
            pltpu.VMEM((queries, width), bf16),
            pltpu.VMEM(block, bf16),
            pltpu.VMEM(block, bf16),
            pltpu.VMEM(token, f32),
            pltpu.VMEM(token, bf16),
            pltpu.VMEM((2, width), f32),
            pltpu.VMEM((queries, width), f32),
            *PlaneScatter.scratch(shards, rows, inner),
            *PlaneScatter.scratch(shards, rows, inner),
            *PlaneScatter.scratch(shards, rows, 2 * HD),
            *PlaneScatter.scratch(1 + 1, rows, columns),
            *PlaneScatter.scratch(1 + 1, rows, columns),
            pltpu.SemaphoreType.DMA((count,)),
            pltpu.SemaphoreType.DMA((count,)),
            pltpu.SemaphoreType.DMA((32,)),
        ],
        compiler_params=pltpu.CompilerParams(
            collective_id=2, has_side_effects=True, vmem_limit_bytes=60 * 2**20
        ),
        name="backward",
    )(
        dmid_all, wo, wq, wkv, n1, qaug, kaug, kv, att, x, dmid, branch, gu_part,
        gd_part, gd_x, gd_y, mid, lse, gains, gain_mlp, cos, sin,
    )


def finish_kernel(gains, layer_in, *refs):
    count = (len(refs) - 2) // 2
    layer_out = refs[count]
    layer_out[0] = layer_in[...]
    refs[count + 1][0] = refs[0][...]
    for src, dst in zip(refs[1:count], refs[count + 2 : -2]):
        dst[...] = src[...]
    for row, dst in enumerate(refs[-2:]):
        dst[...] = gains[row : row + 1, :]


def finish_call(arrays, gains, steps=2):
    rows = [array.shape[0] // steps for array in arrays]
    wide = [array.shape[1] for array in arrays]
    own = gains.shape[1]
    shapes = [struct((1,) * (i < 2) + array.shape, array.dtype) for i, array in enumerate(arrays)]
    return pl.pallas_call(
        finish_kernel,
        grid=(steps,),
        out_shape=shapes + [struct((1, own), f32)] * 2,
        in_specs=[pl.BlockSpec((2, own), lambda i: (0, 0))]
        + [pl.BlockSpec((r, n), lambda i: (i, 0)) for r, n in zip(rows, wide)],
        out_specs=[
            pl.BlockSpec((1, r, n), lambda i: (0, i, 0))
            if index < 2
            else pl.BlockSpec((r, n), lambda i: (i, 0))
            for index, (r, n) in enumerate(zip(rows, wide))
        ]
        + [pl.BlockSpec((1, own), lambda i: (0, 0))] * 2,
        compiler_params=pltpu.CompilerParams(vmem_limit_bytes=60 * 2**20),
        name="finish",
    )(gains, *arrays)


def body(
    inputs, out_grad, block_order, gain_attn, w_query, w_keyval, w_output, gain_mlp, w_gate, w_up, w_down
):
    shards = lax.axis_size("shard")
    x, og = inputs[0], out_grad[0]
    tokens, width = x.shape
    s, c = lax.axis_index("shard"), lax.axis_index("ctx")
    frequency = np.float32(10000.0) ** (-np.arange(HD // 2, dtype=np.float32)[:, None] * 2.0 / HD)
    own = gain_attn.shape[0]
    start = (s * CTX + c) * own
    gain_a, gain_m = gain_attn, gain_mlp
    aligned = own % 128 == 0
    if not aligned:
        gain_a, gain_m = (
            lax.dynamic_update_slice(jnp.zeros((width,), bf16), gain, (start,))
            for gain in (gain_attn, gain_mlp)
        )
    (wq, wkv, wo, wg, wu, wd, n1, og_all, n2, mid, qaug, kaug, kv, att, x_all, lse, gains, cos, sin) = forward_call(
        shards, x, og, (w_query, w_keyval, w_output, w_gate, w_up, w_down), gain_a, gain_m,
        jnp.asarray(frequency, f32), block_order[0],
    )
    (dmid, dmid_all, grad_gate, gd_part, gd_x, gd_y, branch, gu_part, gm) = middle_call(
        shards, w_gate.shape[0], n2, og_all, wg, wu, wd, mid, gains
    )
    (input_grad, grad_query, grad_keyval, grad_output, grad_up, grad_down, layer_out, both) = backward_call(
        shards, w_query.shape[0], dmid_all, wo, wq, wkv, n1, qaug, kaug, kv, att, x_all, dmid,
        branch, gu_part, gd_part, gd_x, gd_y, mid, lse, gains, gm, cos, sin,
    )
    if not aligned:
        both = lax.dynamic_slice(both, (0, start), (2, own))
    (
        layer_out, input_grad, grad_query, grad_keyval, grad_output, grad_gate, grad_up, grad_down,
        *gain_grads,
    ) = finish_call([
        layer_out, input_grad, grad_query, grad_keyval, grad_output, grad_gate, grad_up, grad_down,
    ], both)
    return (
        layer_out, input_grad, gain_grads[0][0], grad_query, grad_keyval, grad_output,
        gain_grads[1][0], grad_gate, grad_up, grad_down,
    )


def solution(mesh):
    plane = P(("shard", "ctx"), "tensor")
    gain = P(("shard", "ctx"))
    token = P("shard", ("ctx", "tensor"), None)
    return jax.shard_map(
        body,
        mesh=mesh,
        in_specs=(token, token, P("shard", None), gain, plane, plane, plane, gain, plane, plane, plane),
        out_specs=(token, token, gain, plane, plane, plane, gain, plane, plane, plane),
        check_vma=False,
    )
```

```python
import functools

import jax
import jax.numpy as jnp
import numpy as np
from jax import lax
from jax.experimental import pallas as pl
from jax.experimental.pallas import tpu as pltpu
from jax.sharding import PartitionSpec as P

HD = 64
BLOCK = 256
BLOCKS = 8
ROWS = 16
CTX = 4
LINE = 4
PIECES = 2

epsilon = 1e-05
blocked = -1e30

f32 = jnp.float32
bf16 = jnp.bfloat16
MESH = pl.DeviceIdType.MESH


def place(owner):
    return (owner + (owner + 1) // 2) % LINE if isinstance(owner, int) else lax.rem(
        owner + (owner + 1) // 2, LINE
    )


def nn_dot(left, right):
    return jnp.dot(left, right, preferred_element_type=f32)


def nt_dot(left, right):
    return lax.dot_general(left, right, (((1,), (1,)), ((), ())), preferred_element_type=f32)


def tn_dot(left, right):
    return lax.dot_general(left, right, (((0,), (0,)), ((), ())), preferred_element_type=f32)


class Links:
    def __init__(self, shards, send_sems, recv_sems, local_sems):
        self.shards = shards
        self.send_sems, self.recv_sems, self.local_sems = send_sems, recv_sems, local_sems
        self.s = lax.axis_index("shard")
        self.c = lax.axis_index("ctx")
        self.t = lax.axis_index("tensor")
        self.c_x = self.c + 1 - 2 * lax.rem(self.c, 2)
        self.c_y = lax.rem(self.c + 2, CTX)
        self.c_d = CTX - 1 - self.c
        self.x_dev = (self.s, self.c_x, self.t)
        self.y_dev = (self.s, self.c_y, self.t)
        self.right = (self.s, self.c, self.t + 1)
        self.left = (self.s, self.c, self.t - 1)
        self.used = 0
        self.local_used = 0
        self.sends = []
        self.locals = []

    def slots(self, count):
        first = self.used
        self.used += count
        assert self.used <= self.send_sems.shape[0]
        return first

    def plane_peer(self, step):
        index = lax.rem(self.s * CTX + self.c + step, self.shards * CTX)
        return (index // CTX, lax.rem(index, CTX), self.t)

    def core_peer(self, step):
        return (lax.rem(self.s + step, self.shards), self.c, self.t)

    def line_peer(self, step):
        return (self.s, self.c, lax.rem(self.t + step, LINE))

    def greet(self, whole_line=False):
        sem = pltpu.get_barrier_semaphore()
        count = self.shards * CTX - 1
        for step in range(1, count + 1):
            pl.semaphore_signal(
                sem, inc=1, device_id=self.plane_peer(step), device_id_type=MESH
            )
        if whole_line:
            for step in range(1, LINE):
                pl.semaphore_signal(
                    sem, inc=1, device_id=self.line_peer(step), device_id_type=MESH
                )
            self.partners = count + LINE - 1
            return

        @pl.when(self.t > 0)
        def _():
            pl.semaphore_signal(sem, inc=1, device_id=self.left, device_id_type=MESH)

        @pl.when(self.t < LINE - 1)
        def _():
            pl.semaphore_signal(sem, inc=1, device_id=self.right, device_id_type=MESH)

        beside = (self.t + LINE - 1) // LINE + (2 * LINE - 2 - self.t) // LINE
        self.partners = count + beside

    def met(self):
        pl.semaphore_wait(pltpu.get_barrier_semaphore(), self.partners)

    def copy(self, src, dst, device, slot):
        return pltpu.make_async_remote_copy(
            src_ref=src,
            dst_ref=dst,
            send_sem=self.send_sems.at[slot],
            recv_sem=self.recv_sems.at[slot],
            device_id=device,
            device_id_type=MESH,
        )

    def send(self, src, dst, device, slot, cond=None):
        if cond is None:
            self.copy(src, dst, device, slot).start()
        else:

            @pl.when(cond)
            def _():
                self.copy(src, dst, device, slot).start()

        handle = (src, dst, device, slot, cond)
        self.sends.append(handle)
        return handle

    def sent(self, handle):
        self.sends = [other for other in self.sends if other is not handle]
        self.copy(*handle[:4]).wait_send()

    def recv(self, dst, slot):
        self.copy(dst, dst, self.x_dev, slot).wait_recv()

    def keep(self, src, dst):
        copy = pltpu.make_async_copy(src, dst, self.local_sems.at[self.local_used])
        self.local_used += 1
        assert self.local_used <= self.local_sems.shape[0]
        copy.start()
        return copy

    def keep_later(self, src, dst):
        self.locals.append(self.keep(src, dst))

    def finish(self):
        for src, dst, device, slot, cond in self.sends:
            if cond is None:
                self.copy(src, dst, device, slot).wait_send()
            else:

                @pl.when(cond)
                def _():
                    self.copy(src, dst, device, slot).wait_send()

        for copy in self.locals:
            copy.wait()


class PlaneGather:
    def __init__(self, links, src, full, stage=None):
        self.links, self.src, self.full, self.stage = links, src, full, stage
        self.rows = src.shape[0]
        self.first = links.slots(4 + 4 * (links.shards - 1))

    def block(self, s, c):
        start = pl.multiple_of((s * CTX + c) * self.rows, self.rows)
        return self.full.at[pl.ds(start, self.rows)]

    def half(self, s, c, which):
        size = self.rows // 2
        start = pl.multiple_of((s * CTX + c) * self.rows + which * size, size)
        return self.full.at[pl.ds(start, size)]

    def core_slot(self, step, part):
        return self.first + 4 + (step - 1) * 4 + part

    def core_send(self, src, c, part):
        links = self.links
        for step in range(1, links.shards):
            links.send(
                src,
                self.block(links.s, c),
                links.core_peer(step),
                self.core_slot(step, part),
            )

    def start(self):
        links = self.links
        own = self.block(links.s, links.c)
        links.send(self.src, own, links.x_dev, self.first)
        links.send(self.src, own, links.y_dev, self.first + 1)
        self.core_send(self.src, links.c, 0)
        self.local = links.keep(self.src, own if self.stage is None else self.stage)

    def settle(self):
        self.local.wait()
        self.local = self.links.keep(self.stage, self.block(self.links.s, self.links.c))

    def forward(self):
        links = self.links
        links.recv(self.block(links.s, links.c_x), self.first)
        links.recv(self.block(links.s, links.c_y), self.first + 1)
        from_x = self.half(links.s, links.c_x, 0)
        from_y = self.half(links.s, links.c_y, 1)
        links.send(from_x, from_x, links.y_dev, self.first + 2)
        links.send(from_y, from_y, links.x_dev, self.first + 3)
        self.core_send(self.block(links.s, links.c_x), links.c_x, 1)
        self.core_send(self.block(links.s, links.c_y), links.c_y, 2)

    def diagonal(self):
        links = self.links
        links.recv(self.half(links.s, links.c_d, 0), self.first + 2)
        links.recv(self.half(links.s, links.c_d, 1), self.first + 3)
        self.core_send(self.block(links.s, links.c_d), links.c_d, 3)

    def done(self):
        links = self.links
        for step in range(1, links.shards):
            other = lax.rem(links.s + links.shards - step, links.shards)
            for part, c in enumerate((links.c, links.c_x, links.c_y, links.c_d)):
                links.recv(self.block(other, c), self.core_slot(step, part))
        self.local.wait()


class LineGather:
    def __init__(self, links, own, full, tokens, pieces=1):
        self.links, self.own, self.full, self.tokens = links, own, full, tokens
        self.pieces, self.size = pieces, tokens // pieces
        self.first = links.slots(2 * (LINE - 1) * pieces)

    def block(self, owner, p):
        start = pl.multiple_of(place(owner) * self.tokens + p * self.size, self.size)
        return self.full.at[pl.ds(start, self.size)]

    def slot(self, side, k, p):
        return self.first + (side * (LINE - 1) + k - 1) * self.pieces + p

    def send(self, k, p=0):
        links = self.links
        t, u = links.t, LINE - 1 - links.t
        own = self.own.at[pl.ds(p * self.size, self.size)]
        right, left = self.block(t - k + 1, p), self.block(t + k - 1, p)
        links.send(
            own if k == 1 else right,
            right,
            links.right,
            self.slot(0, k, p),
            jnp.logical_and(t >= k - 1, t < LINE - 1),
        )
        links.send(
            own if k == 1 else left,
            left,
            links.left,
            self.slot(1, k, p),
            jnp.logical_and(u >= k - 1, u < LINE - 1),
        )

    def recv(self, k, p=0):
        links = self.links
        t, u = links.t, LINE - 1 - links.t

        @pl.when(t >= k)
        def _():
            links.recv(self.block(t - k, p), self.slot(0, k, p))

        @pl.when(u >= k)
        def _():
            links.recv(self.block(t + k, p), self.slot(1, k, p))


class LineScatter:
    def __init__(self, links, part, tokens, from_left, from_right, pieces=1):
        self.links, self.part, self.tokens = links, part, tokens
        self.from_left, self.from_right = from_left, from_right
        self.pieces, self.size = pieces, tokens // pieces
        self.first = links.slots(2 * (LINE - 1) * pieces)

    def slot(self, side, k, p):
        return self.first + (side * (LINE - 1) + k) * self.pieces + p

    def piece(self, ref, k, p):
        return ref.at[k, pl.ds(p * self.size, self.size)]

    def total(self, owner, k, p, arrived):
        @pl.loop(0, self.size // ROWS)
        def _(i):
            r = pl.multiple_of(p * self.size + i * ROWS, ROWS)
            q = pl.multiple_of(place(owner) * self.tokens + p * self.size + i * ROWS, ROWS)
            mine = self.part[pl.ds(q, ROWS), :].astype(f32)
            summed = mine + arrived[k, pl.ds(r, ROWS), :].astype(f32)
            arrived[k, pl.ds(r, ROWS), :] = summed.astype(arrived.dtype)

    def ends(self, k, p=0):
        links = self.links
        for side, behind, arrived, device in self.sides():
            owner = LINE - 1 - k if side == 0 else k
            piece, slot = self.piece(arrived, k, p), self.slot(side, k, p)

            @pl.when(behind == 0)
            def _():
                self.first_part(owner, k, p, arrived)

            links.send(piece, piece, device, slot, behind == 0)

    def sides(self):
        links = self.links
        return (
            (0, links.t, self.from_left, links.right),
            (1, LINE - 1 - links.t, self.from_right, links.left),
        )

    def stage(self, now, p=0):
        links = self.links
        for side, behind, arrived, device in self.sides():
            k = now - behind
            owner = LINE - 1 - k if side == 0 else k
            piece, slot = self.piece(arrived, k, p), self.slot(side, k, p)
            ready = jnp.logical_and(k >= 0, behind > 0)

            @pl.when(ready)
            def _():
                links.recv(piece, slot)
                self.total(owner, k, p, arrived)

            links.send(piece, piece, device, slot, ready)

    def first_part(self, owner, k, p, out):
        @pl.loop(0, self.size // ROWS)
        def _(i):
            r = pl.multiple_of(p * self.size + i * ROWS, ROWS)
            q = pl.multiple_of(place(owner) * self.tokens + p * self.size + i * ROWS, ROWS)
            out[k, pl.ds(r, ROWS), :] = self.part[pl.ds(q, ROWS), :].astype(out.dtype)

    def arrive(self, p=0):
        links = self.links
        t = links.t

        @pl.when(t > 0)
        def _():
            links.recv(
                self.piece(self.from_left, LINE - 1 - t, p), self.slot(0, LINE - 1 - t, p)
            )

        @pl.when(t < LINE - 1)
        def _():
            links.recv(self.piece(self.from_right, t, p), self.slot(1, t, p))

    def rows(self, r):
        t = self.links.t
        q = pl.multiple_of(place(t) * self.tokens + r, ROWS)
        k_l = jnp.minimum(LINE - 1 - t, LINE - 2)
        k_r = jnp.minimum(t, LINE - 2)
        zero = jnp.zeros((ROWS, self.part.shape[1]), f32)
        return (
            self.part[pl.ds(q, ROWS), :].astype(f32)
            + jnp.where(t > 0, self.from_left[k_l, pl.ds(r, ROWS), :].astype(f32), zero)
            + jnp.where(t < LINE - 1, self.from_right[k_r, pl.ds(r, ROWS), :].astype(f32), zero)
        )

    def owned(self, p, use):
        @pl.loop(0, self.size // ROWS)
        def _(i):
            r = pl.multiple_of(p * self.size + i * ROWS, ROWS)
            use(r, self.rows(r))


def line_ends(scatter, *hops):
    for k in hops:
        for p in range(scatter.pieces):
            scatter.ends(k, p)


def line_steps(scatter, now):
    for p in range(scatter.pieces):
        scatter.stage(now, p)


def line_finish(scatter, use, gather=None):
    for p in range(scatter.pieces):
        scatter.arrive(p)
        scatter.owned(p, use)
        if gather is not None:
            gather.send(1, p)


def line_spread(gather, k):
    for p in range(gather.pieces):
        gather.recv(k, p)
        if k < LINE - 1:
            gather.send(k + 1, p)


class PlaneScatter:
    def __init__(
        self, links, left, right, rows, core_in, x_in, y_in, x_last, y_last, out, parts=1
    ):
        self.links, self.left, self.right, self.rows = links, left, right, rows
        self.core_in, self.x_in, self.y_in = core_in, x_in, y_in
        self.x_last, self.y_last, self.out = x_last, y_last, out
        self.tile = min(256, CTX * rows)
        self.parts = parts if CTX * rows // self.tile % parts == 0 else 1
        self.core_first = links.slots((links.shards - 1) * self.parts)
        self.first = links.slots(6)

    def product(self, shard, i):
        start = pl.multiple_of(shard * (CTX * self.rows) + i * self.tile, self.tile)
        return tn_dot(self.left[:, pl.ds(start, self.tile)], self.right[...])

    def part(self, ref, index):
        size = CTX * self.rows // self.parts
        return ref.at[pl.ds(index * size, size)]

    def each_tile(self, index, body):
        tiles = CTX * self.rows // self.tile // self.parts

        @pl.loop(index * tiles, (index + 1) * tiles)
        def _(i):
            body(i, pl.ds(pl.multiple_of(i * self.tile, self.tile), self.tile))

    def other(self, step, stage):
        links = self.links
        target = lax.rem(links.s + step, links.shards)

        def tile(i, at):
            stage[at, :] = self.product(target, i).astype(bf16)

        for index in range(self.parts):
            self.each_tile(index, tile)
            links.send(
                self.part(stage, index),
                self.part(self.core_in.at[step - 1], index),
                links.core_peer(step),
                self.core_first + (step - 1) * self.parts + index,
            )

    def own(self):
        links = self.links

        def tile(i, at):
            summed = self.product(links.s, i)
            for step in range(1, links.shards):
                summed = summed + self.core_in[step - 1, at, :].astype(f32)
            self.core_in[0, at, :] = summed.astype(bf16)

        for index in range(self.parts):
            for step in range(1, links.shards):
                links.recv(
                    self.part(self.core_in.at[step - 1], index),
                    self.core_first + (step - 1) * self.parts + index,
                )
            self.each_tile(index, tile)

    def half(self, c, which):
        size = self.rows // 2
        start = pl.multiple_of(c * self.rows + which * size, size)
        return self.core_in.at[0, pl.ds(start, size)]

    def exchange(self):
        links, first = self.links, self.first
        links.send(self.half(links.c_d, 0), self.x_in.at[1], links.x_dev, first)
        links.send(self.half(links.c_d, 1), self.y_in.at[1], links.y_dev, first + 1)
        links.send(self.half(links.c_x, 0), self.x_in.at[0], links.x_dev, first + 2)
        links.send(self.half(links.c_y, 1), self.y_in.at[0], links.y_dev, first + 3)

    def add(self, c, which, arrived):
        size = self.rows // 2

        @pl.loop(0, size // ROWS)
        def _(i):
            r = pl.multiple_of(i * ROWS, ROWS)
            q = pl.multiple_of(c * self.rows + which * size + i * ROWS, ROWS)
            mine = self.core_in[0, pl.ds(q, ROWS), :].astype(f32)
            summed = mine + arrived[1, pl.ds(r, ROWS), :].astype(f32)
            self.core_in[0, pl.ds(q, ROWS), :] = summed.astype(bf16)

    def arrived(self, part):
        links, first = self.links, self.first
        for ref, offset in ((self.x_in, 0), (self.y_in, 1)):
            links.recv(ref.at[1 - part], first + offset + 2 * part)

    def fold(self, here=False):
        links, first = self.links, self.first
        if not here:
            links.recv(self.x_in.at[1], first)
        self.add(links.c_y, 0, self.x_in)
        links.send(self.half(links.c_y, 0), self.y_last, links.y_dev, first + 4)
        if not here:
            links.recv(self.y_in.at[1], first + 1)
        self.add(links.c_x, 1, self.y_in)
        links.send(self.half(links.c_x, 1), self.x_last, links.x_dev, first + 5)

    def total(self, here=False):
        links, first = self.links, self.first
        size = self.rows // 2
        if not here:
            links.recv(self.x_in.at[0], first + 2)
            links.recv(self.y_in.at[0], first + 3)
        links.recv(self.y_last, first + 4)
        links.recv(self.x_last, first + 5)
        for which, arrived, last in ((0, self.x_in, self.y_last), (1, self.y_in, self.x_last)):

            @pl.loop(0, size // ROWS)
            def _(i):
                r = pl.multiple_of(i * ROWS, ROWS)
                q = pl.multiple_of(links.c * self.rows + which * size + i * ROWS, ROWS)
                self.out[pl.ds(which * size + r, ROWS), :] = (
                    self.core_in[0, pl.ds(q, ROWS), :].astype(f32)
                    + arrived[0, pl.ds(r, ROWS), :].astype(f32)
                    + last[pl.ds(r, ROWS), :].astype(f32)
                )

    @staticmethod
    def scratch(shards, rows, columns):
        half = (rows // 2, columns)
        return [
            pltpu.VMEM((shards - 1, CTX * rows, columns), bf16),
            pltpu.VMEM((2,) + half, bf16),
            pltpu.VMEM((2,) + half, bf16),
            pltpu.VMEM(half, bf16),
            pltpu.VMEM(half, bf16),
            pltpu.VMEM((rows, columns), f32),
        ]


def any_spec():
    return pl.BlockSpec(memory_space=pl.ANY)


def vmem_spec():
    return pl.BlockSpec(memory_space=pltpu.VMEM)


def struct(shape, dtype):
    return jax.ShapeDtypeStruct(shape, dtype)


def forward_kernel(
    shards,
    x, og, wq, wkv, wo, wg, wu, wd, gain_a, gain_m, frequency, order,
    wq_o, wkv_o, wo_o, wg_o, wu_o, wd_o, n1_o, og_o, n2_o, mid_o, qaug_o, kaug_o, kv_o, att_o, x_o,
    lse, gains, cos, sin,
    x_all, n1_all, wq_all, wkv_all, wo_all, gains_all, qaug, kv_all, kaug, v_all, scores, weights,
    attn, part, from_left, from_right, mid, n2, og_stage, wg_stage, wu_stage, wd_stage, gpad,
    send_sems, recv_sems, local_sems,
):
    tokens, width = x.shape
    queries = tokens * LINE
    heads = qaug.shape[0]
    links = Links(shards, send_sems, recv_sems, local_sems)
    s, c, t = links.s, links.c, links.t

    gather_x = LineGather(links, x, x_all, tokens, PIECES)
    gather_og = LineGather(links, og, og_o, tokens)
    gather_n2 = LineGather(links, n2, n2_o, tokens, PIECES)
    small = [PlaneGather(links, *pair) for pair in ((wq, wq_all), (wkv, wkv_all), (wo, wo_all))]
    large = [
        PlaneGather(links, *three)
        for three in ((wg, wg_o, wg_stage), (wu, wu_o, wu_stage), (wd, wd_o, wd_stage))
    ]
    scatter = LineScatter(links, part, tokens, from_left, from_right, PIECES)
    plane = shards * CTX
    gain_slot = links.slots(plane - 1)
    kv_slot = links.slots((CTX - 1) * (2 * LINE - 1))

    links.greet()
    me = s * CTX + c
    own_gains = gain_a.shape[0]
    if own_gains == width:
        own_lanes = slice(0, width)
    else:
        gpad[...] = jnp.zeros_like(gpad)
        own_lanes = pl.ds(pl.multiple_of(me * own_gains, own_gains), own_gains)
    for row, gain in enumerate((gain_a, gain_m)):
        gpad[row : row + 1, own_lanes] = gain[...].astype(f32).reshape(1, own_gains)
    links.met()
    for step in range(1, plane):
        links.send(gpad, gains_all.at[me], links.plane_peer(step), gain_slot + step - 1)
    own_gain = links.keep(gpad, gains_all.at[me])
    for p in range(PIECES):
        gather_x.send(1, p)
    own_rows = pl.ds(pl.multiple_of(place(t) * tokens, tokens), tokens)
    own_x = links.keep(x, x_all.at[own_rows])
    for gather in small:
        gather.start()

    per = queries // BLOCK
    lane = lax.broadcasted_iota(jnp.int32, (1, queries), 1)
    owner = jnp.zeros((1, queries), jnp.int32)
    for index in range(LINE):
        owner = jnp.where(lane // tokens == place(index), index, owner)
    slot = owner * tokens + lax.rem(lane, tokens)
    block_here = jnp.zeros((1, queries), jnp.int32)
    for index in range(per):
        block_here = jnp.where(slot // BLOCK == index, order[c * per + index], block_here)
    position = (block_here * BLOCK + lax.rem(slot, BLOCK)).astype(f32)
    angles = frequency[...] * position
    cos[...] = jnp.cos(angles)
    sin[...] = jnp.sin(angles)
    row = lax.broadcasted_iota(jnp.int32, (HD, queries), 0)
    bias = jnp.zeros((HD, queries), f32)
    for index in range(BLOCKS):
        barred = jnp.logical_and(row == index, order[index] > block_here)
        bias = jnp.where(barred, blocked, bias)
    bias = bias.astype(bf16)
    for h in range(heads):
        qaug[h, HD:, :] = bias

    own_gain.wait()
    for step in range(1, plane):
        other = lax.rem(me + plane - step, plane)
        links.recv(gains_all.at[other], gain_slot + step - 1)
    total = gains_all[0]
    for index in range(1, plane):
        total = total + gains_all[index]
    gains[...] = total
    own_x.wait()

    def norm_block(owner):
        @pl.loop(0, tokens // ROWS)
        def _(i):
            r = pl.multiple_of(place(owner) * tokens + i * ROWS, ROWS)
            v = x_all[pl.ds(r, ROWS), :].astype(f32)
            inverse = lax.rsqrt(jnp.mean(v * v, -1, keepdims=True) + epsilon)
            n1_all[pl.ds(r, ROWS), :] = (v * inverse * gains[0:1, :]).astype(bf16)

    own_og = links.keep(og, og_stage)
    norm_block(t)
    line_spread(gather_x, 1)
    for gather in small:
        gather.forward()
    norm_pair(gather_x, norm_block, 1)
    line_spread(gather_x, 2)
    gather_og.send(1)
    for gather in small:
        gather.diagonal()
    norm_pair(gather_x, norm_block, 2)
    own_og.wait()
    links.keep_later(og_stage, og_o.at[own_rows])
    for gather in small:
        gather.done()

    half = HD // 2
    scale = HD ** (-0.5)

    def lanes_of(owner):
        return pl.ds(pl.multiple_of(place(owner) * tokens, tokens), tokens)

    def turn(v1, v2, cosine, sine):
        return (v1 * cosine - v2 * sine).astype(bf16), (v2 * cosine + v1 * sine).astype(bf16)

    def project_block(owner):
        at = lanes_of(owner)
        cosine, sine = cos[:, at], sin[:, at]
        kv_t = nn_dot(n1_all[at, :], wkv_all[...]).T
        k1, k2 = turn(kv_t[0:half], kv_t[half:HD], cosine, sine)
        kv_all[c, 0:half, at] = k1
        kv_all[c, half:HD, at] = k2
        kv_all[c, HD : 2 * HD, at] = kv_t[HD:].astype(bf16)
        q_t = nn_dot(n1_all[at, :], wq_all[...]).T
        for h in range(heads):
            b = h * HD
            q1, q2 = turn(q_t[b : b + half], q_t[b + half : b + HD], cosine, sine)
            qaug[h, 0:half, at] = (q1 * scale).astype(bf16)
            qaug[h, half:HD, at] = (q2 * scale).astype(bf16)

    u = LINE - 1 - t
    arrivals = [(t, None)]
    for k in range(1, LINE):
        arrivals += [(t - k, t >= k), (t + k, u >= k)]

    def send_block(index):
        owner, cond = arrivals[index]
        for step in range(1, CTX):
            peer = lax.rem(c + step, CTX)
            ref = kv_all.at[c, :, lanes_of(owner)]
            links.send(ref, ref, (s, peer, t), kv_slot + index * (CTX - 1) + step - 1, cond)

    def recv_block(index):
        owner, cond = arrivals[index]

        def wait():
            for step in range(1, CTX):
                other = lax.rem(c + CTX - step, CTX)
                slot = kv_slot + index * (CTX - 1) + step - 1
                links.recv(kv_all.at[other, :, lanes_of(owner)], slot)

        if cond is None:
            wait()
        else:
            pl.when(cond)(wait)

    project_block(t)
    send_block(0)
    for k in range(1, LINE):
        if k == LINE - 1:
            line_spread(gather_x, k)
            norm_pair(gather_x, norm_block, k)
        norm_pair(gather_x, project_block, k)
        send_block(2 * k - 1)
        send_block(2 * k)
    for gather in large:
        gather.start()
    links.keep_later(n1_all, n1_o)
    links.keep_later(x_all, x_o)
    links.keep_later(wq_all, wq_o)
    links.keep_later(wkv_all, wkv_o)
    links.keep_later(wo_all, wo_o)
    links.keep_later(qaug, qaug_o)
    for index in range(len(arrivals)):
        recv_block(index)
    for other in range(CTX):
        row = lax.broadcasted_iota(jnp.int32, (HD, queries), 0)
        lane = lax.broadcasted_iota(jnp.int32, (HD, queries), 1)
        mark = (row == other * (queries // BLOCK) + lax.rem(lane // tokens, 2)).astype(f32).astype(bf16)
        both = jnp.concatenate([kv_all[other, 0:HD, :], mark], 0)
        kaug[other * queries : (other + 1) * queries, :] = both.T
        v_all[:, other * queries : (other + 1) * queries] = kv_all[other, HD : 2 * HD, :]
    links.keep_later(kaug, kaug_o)
    links.keep_later(kv_all, kv_o)

    length = queries * CTX

    far = pl.multiple_of(jnp.where(t < LINE // 2, tokens, 0), tokens)
    near = pl.multiple_of(jnp.where(t < LINE // 2, 0, tokens), tokens)

    def soften(query):
        size = query.shape[1]
        top = jnp.full((1, size), -jnp.inf, f32)
        for b in range(0, length, BLOCK):
            block_scores = nn_dot(kaug[b : b + BLOCK, :], query)
            scores[b : b + BLOCK, :] = block_scores
            top = jnp.maximum(top, jnp.max(block_scores, 0, keepdims=True))
        norm = jnp.zeros((1, size), f32)
        for b in range(0, length, BLOCK):
            exponent = jnp.exp(scores[b : b + BLOCK, :] - top)
            norm = norm + jnp.sum(exponent, 0, keepdims=True)
            weights[b : b + BLOCK, :] = exponent.astype(bf16)
        out = nn_dot(v_all[...], weights[...]) / norm
        return out.astype(bf16), top + jnp.log(norm)

    def put(h, lanes, out, log_sum):
        attn[pl.ds(pl.multiple_of(h * HD, HD), HD), lanes] = out
        lse[h, :, lanes] = log_sum

    def head(lanes, h):
        put(h, lanes, *soften(qaug[h, :, lanes]))

    def head_pair(lanes, g):
        h = 2 * g
        both = jnp.concatenate([qaug[h, :, lanes], qaug[h + 1, :, lanes]], 1)
        out, log_sum = soften(both)
        put(h, lanes, out[:, 0:tokens], log_sum[:, 0:tokens])
        put(h + 1, lanes, out[:, tokens:], log_sum[:, tokens:])

    def attend(start, size):
        if size == tokens:
            pl.loop(0, heads // 2)(functools.partial(head_pair, pl.ds(start, size)))
        else:
            pl.loop(0, heads)(functools.partial(head, pl.ds(start, size)))
        rows = pl.ds(start, size)
        attn_rows = attn[:, rows].T
        for b in range(0, width, 512):
            part[rows, b : b + 512] = nt_dot(attn_rows, wo_all[b : b + 512, :])

    attend(far, tokens)
    line_ends(scatter, 0)
    gather_og.recv(1)
    gather_og.send(2)
    for gather in large:
        gather.settle()
    attend(2 * tokens, 2 * tokens)
    line_ends(scatter, 1, 2)
    gather_og.recv(2)
    gather_og.send(3)
    line_steps(scatter, 1)
    attend(near, tokens)
    links.keep_later(attn, att_o)

    def finish_rows(r, summed):
        q = pl.multiple_of(place(t) * tokens + r, ROWS)
        middle = x_all[pl.ds(q, ROWS), :].astype(f32) + summed
        mid[pl.ds(r, ROWS), :] = middle
        inverse = lax.rsqrt(jnp.mean(middle * middle, -1, keepdims=True) + epsilon)
        n2[pl.ds(r, ROWS), :] = (middle * inverse * gains[1:2, :]).astype(bf16)

    large[0].forward()
    line_steps(scatter, 2)
    large[1].forward()
    line_finish(scatter, finish_rows, gather_n2)
    large[2].forward()
    links.keep_later(n2, n2_o.at[own_rows])
    links.keep_later(mid, mid_o)
    line_spread(gather_n2, 1)
    large[0].diagonal()
    large[1].diagonal()
    line_spread(gather_n2, 2)
    large[2].diagonal()
    gather_og.recv(3)
    line_spread(gather_n2, 3)
    for gather in large:
        gather.done()
    links.finish()


def norm_pair(gather, norm_block, k):
    t, u = gather.links.t, LINE - 1 - gather.links.t

    @pl.when(t >= k)
    def _():
        norm_block(t - k)

    @pl.when(u >= k)
    def _():
        norm_block(t + k)


def forward_call(shards, x, og, weights_in, gain_a, gain_m, frequency, order):
    wq, wkv, wo, wg, wu, wd = weights_in
    tokens, width = x.shape
    queries = tokens * LINE
    length = queries * CTX
    heads = wq.shape[1] // HD
    plane = shards * CTX
    full = [struct((width, w.shape[1]), bf16) for w in weights_in]
    outs = full + [
        struct((queries, width), bf16),
        struct((queries, width), bf16),
        struct((queries, width), bf16),
        struct((tokens, width), f32),
        struct((heads, 2 * HD, queries), bf16),
        struct((length, 2 * HD), bf16),
        struct((CTX, 2 * HD, queries), bf16),
        struct((heads * HD, queries), bf16),
        struct((queries, width), bf16),
        struct((heads, 1, queries), f32),
        struct((2, width), f32),
        struct((HD // 2, queries), f32),
        struct((HD // 2, queries), f32),
    ]
    block = (LINE - 1, tokens, width)
    count = 6 + 18 * PIECES + 6 * (4 + 4 * (shards - 1)) + plane - 1 + 21
    return pl.pallas_call(
        functools.partial(forward_kernel, shards),
        out_shape=outs,
        in_specs=[any_spec()] * 8
        + [vmem_spec()] * 3
        + [pl.BlockSpec(memory_space=pltpu.SMEM)],
        out_specs=[any_spec()] * 15 + [vmem_spec()] * 4,
        scratch_shapes=[
            pltpu.VMEM((queries, width), bf16),
            pltpu.VMEM((queries, width), bf16),
            pltpu.VMEM((width, wq.shape[1]), bf16),
            pltpu.VMEM((width, wkv.shape[1]), bf16),
            pltpu.VMEM((width, wo.shape[1]), bf16),
            pltpu.VMEM((plane, 2, width), f32),
            pltpu.VMEM((heads, 2 * HD, queries), bf16),
            pltpu.VMEM((CTX, 2 * HD, queries), bf16),
            pltpu.VMEM((length, 2 * HD), bf16),
            pltpu.VMEM((HD, length), bf16),
            pltpu.VMEM((length, queries // 2), f32),
            pltpu.VMEM((length, queries // 2), bf16),
            pltpu.VMEM((heads * HD, queries), bf16),
            pltpu.VMEM((queries, width), f32),
            pltpu.VMEM(block, bf16),
            pltpu.VMEM(block, bf16),
            pltpu.VMEM((tokens, width), f32),
            pltpu.VMEM((tokens, width), bf16),
            pltpu.VMEM((tokens, width), bf16),
            pltpu.VMEM(wg.shape, bf16),
            pltpu.VMEM(wu.shape, bf16),
            pltpu.VMEM(wd.shape, bf16),
            pltpu.VMEM((2, width), f32),
            pltpu.SemaphoreType.DMA((count,)),
            pltpu.SemaphoreType.DMA((count,)),
            pltpu.SemaphoreType.DMA((32,)),
        ],
        compiler_params=pltpu.CompilerParams(
            collective_id=0, has_side_effects=True, vmem_limit_bytes=60 * 2**20
        ),
        name="forward",
    )(x, og, wq, wkv, wo, wg, wu, wd, gain_a, gain_m, frequency, order)


def middle_kernel(
    shards, rows,
    n2_in, og_in, wg_in, wu_in, wd_in, mid_in, gains,
    dmid_o, dmid_all_o, gg_o, gd_part_o, gd_x_o, gd_y_o, branch_o, gu_part_o, gain_sum,
    n2, og, wg, wu, wd, mid, hidden, dgate, dup, part, branch,
    left, right, dmid, dsend, gain_rows, up_in, first,
    *rest,
):
    grads, (send_sems, recv_sems, local_sems) = rest[:-3], rest[-3:]
    tokens, width = mid.shape
    queries = n2.shape[0]
    columns = wg.shape[1]
    links = Links(shards, send_sems, recv_sems, local_sems)
    t = links.t
    links.greet()
    own_rows = pl.ds(pl.multiple_of(place(t) * tokens, tokens), tokens)

    far = pl.multiple_of(jnp.where(t < LINE // 2, tokens, 0), tokens)
    near = pl.multiple_of(jnp.where(t < LINE // 2, 0, tokens), tokens)
    sides = [pl.ds(far, tokens), pl.ds(2 * tokens, 2 * tokens), pl.ds(near, tokens)]
    full, rest_columns = columns // 256, columns % 256
    weights = ((wg_in, wg), (wu_in, wu), (wd_in, wd))

    def fetch(j, start, size, index):
        src, dst = weights[j]
        of = pl.ds(start, size)
        sem = local_sems.at[3 * index + j]
        return pltpu.make_async_copy(src.at[:, of], dst.at[:, of], sem)

    links.local_used = 3 * (full + 1)
    load_n2 = [links.keep(n2_in.at[sides[0]], n2.at[sides[0]])]
    for index in range(full):
        for j in range(3):
            fetch(j, index * 256, 256, index).start()
        if index == 0:
            load_og = [links.keep(og_in.at[sides[0]], og.at[sides[0]])]
    if rest_columns:
        for j in range(3):
            fetch(j, full * 256, rest_columns, full).start()
    load_n2 += [links.keep(n2_in.at[at], n2.at[at]) for at in sides[1:]]
    load_og += [links.keep(og_in.at[at], og.at[at]) for at in sides[1:]]
    load_mid = links.keep(mid_in, mid)
    scatter = LineScatter(links, part, tokens, left, right, PIECES)
    gather = LineGather(links, dsend, dmid_all_o, tokens, PIECES)
    down = PlaneScatter(links, og, hidden, rows, *grads[0:6])
    gate = PlaneScatter(links, n2, dgate, rows, *grads[6:12], parts=2)
    up = PlaneScatter(links, n2, dup, rows, up_in, None, None, None, None, None)

    def feed_forward(half):
        at = sides[half]
        load_n2[half].wait()
        load_og[half].wait()

        def tile(start, size, index):
            of = pl.ds(start, size)
            if half == 0:
                fetch(0, start, size, index).wait()
                fetch(1, start, size, index).wait()
            gate_act = nn_dot(n2[at, :], wg[:, of])
            up_act = nn_dot(n2[at, :], wu[:, of])
            if half == 0:
                fetch(2, start, size, index).wait()
            d_hidden = nn_dot(og[at, :], wd[:, of])
            sig = jax.nn.sigmoid(gate_act)
            silu = gate_act * sig
            hidden[at, of] = (silu * up_act).astype(bf16)
            d_gate = d_hidden * up_act * sig * (1.0 + gate_act * (1.0 - sig))
            dgate[at, of] = d_gate.astype(bf16)
            dup[at, of] = (d_hidden * silu).astype(bf16)
            if half == 0:
                for b in range(0, width, 512):
                    e = b + 512
                    summed = nt_dot(dgate[at, of], wg[b:e, of]) + nt_dot(dup[at, of], wu[b:e, of])
                    first[:, b:e] += summed

        @pl.loop(0, full)
        def _(index):
            tile(pl.multiple_of(index * 256, 256), 256, index)

        if rest_columns:
            tile(full * 256, rest_columns, full)
        if half == 0:
            part[at, :] = first[...].astype(bf16)
            return

        @pl.loop(0, width // 512)
        def _(j):
            of = pl.ds(pl.multiple_of(j * 512, 512), 512)
            summed = nt_dot(dgate[at, :], wg[of, :]) + nt_dot(dup[at, :], wu[of, :])
            part[at, of] = summed.astype(bf16)

    piece = CTX * rows

    def others(grad, room):
        for step in range(1, shards):
            grad.other(step, room.at[pl.ds((step - 1) * piece, piece)])

    first[...] = jnp.zeros_like(first)
    feed_forward(0)
    links.met()
    line_ends(scatter, 0)
    feed_forward(1)
    line_ends(scatter, 1, 2)
    line_steps(scatter, 1)
    feed_forward(2)
    others(gate, wg)
    line_steps(scatter, 2)

    gate.own()
    gate.exchange()

    @pl.loop(0, width // 512)
    def _(j):
        of = pl.ds(pl.multiple_of(j * 512, 512), 512)
        branch[:, of] = nt_dot(hidden[...], wd[of, :]).astype(bf16)

    links.keep_later(branch, branch_o)
    others(down, wd)
    load_mid.wait()
    gain_rows[...] = jnp.zeros_like(gain_rows)

    def finish_rows(r, d_normed):
        at = pl.ds(r, ROWS)
        q = pl.ds(pl.multiple_of(place(t) * tokens + r, ROWS), ROWS)
        middle = mid[at, :]
        inverse = lax.rsqrt(jnp.mean(middle * middle, -1, keepdims=True) + epsilon)
        unit = middle * inverse
        gain_rows[...] += d_normed * unit
        d_unit = d_normed * gains[1:2, :]
        back = inverse * (d_unit - unit * jnp.mean(d_unit * unit, -1, keepdims=True))
        d_middle = og[q, :].astype(f32) + back
        dmid[at, :] = d_middle
        dsend[at, :] = d_middle.astype(bf16)

    line_finish(scatter, finish_rows, gather)
    gate.fold()
    down.own()
    down.exchange()
    links.keep_later(dsend, dmid_all_o.at[own_rows])
    links.keep_later(dmid, dmid_o)
    links.keep_later(down.core_in.at[0], gd_part_o)
    line_spread(gather, 1)
    others(up, wu)
    gain_sum[...] = jnp.sum(gain_rows[...], 0, keepdims=True)
    line_spread(gather, 2)
    up.own()
    links.keep_later(up_in.at[0], gu_part_o)
    gate.total()
    links.keep_later(gate.out, gg_o)
    down.arrived(0)
    links.keep_later(down.x_in.at[1], gd_x_o.at[1])
    links.keep_later(down.y_in.at[1], gd_y_o.at[1])
    line_spread(gather, 3)
    down.arrived(1)
    links.keep_later(down.x_in.at[0], gd_x_o.at[0])
    links.keep_later(down.y_in.at[0], gd_y_o.at[0])
    links.finish()


def middle_call(shards, rows, n2, og, wg, wu, wd, mid, gains):
    queries, width = n2.shape
    tokens = mid.shape[0]
    columns = wg.shape[1]
    token = (tokens, width)
    wide = (queries, columns)
    block = (LINE - 1,) + token
    outs = [
        struct(token, f32),
        struct((queries, width), bf16),
        struct((rows, columns), f32),
        struct((CTX * rows, columns), bf16),
        struct((2, rows // 2, columns), bf16),
        struct((2, rows // 2, columns), bf16),
        struct((queries, width), bf16),
        struct((CTX * rows, columns), bf16),
        struct((1, width), f32),
    ]
    count = 12 * PIECES + 3 * (2 * (shards - 1) + 6)
    return pl.pallas_call(
        functools.partial(middle_kernel, shards, rows),
        out_shape=outs,
        in_specs=[any_spec()] * 6 + [vmem_spec()],
        out_specs=[any_spec()] * 8 + [vmem_spec()],
        scratch_shapes=[
            pltpu.VMEM((queries, width), bf16),
            pltpu.VMEM((queries, width), bf16),
            pltpu.VMEM((width, columns), bf16),
            pltpu.VMEM((width, columns), bf16),
            pltpu.VMEM((width, columns), bf16),
            pltpu.VMEM(token, f32),
            pltpu.VMEM(wide, bf16),
            pltpu.VMEM(wide, bf16),
            pltpu.VMEM(wide, bf16),
            pltpu.VMEM((queries, width), bf16),
            pltpu.VMEM((queries, width), bf16),
            pltpu.VMEM(block, bf16),
            pltpu.VMEM(block, bf16),
            pltpu.VMEM(token, f32),
            pltpu.VMEM(token, bf16),
            pltpu.VMEM((ROWS, width), f32),
            pltpu.VMEM((shards - 1, CTX * rows, columns), bf16),
            pltpu.VMEM(token, f32),
            *PlaneScatter.scratch(shards, rows, columns),
            *PlaneScatter.scratch(shards, rows, columns),
            pltpu.SemaphoreType.DMA((count,)),
            pltpu.SemaphoreType.DMA((count,)),
            pltpu.SemaphoreType.DMA((40,)),
        ],
        compiler_params=pltpu.CompilerParams(
            collective_id=1, has_side_effects=True, vmem_limit_bytes=63 * 2**20
        ),
        name="middle",
    )(n2, og, wg, wu, wd, mid, gains)


def backward_kernel(
    shards, rows,
    dmid_all_in, wo_in, wq_in, wkv_in, n1_in, qaug_in, kaug_in, kv_in, att_in, x_in, dmid_in,
    branch_in, gu_part_in, gd_part_in, gd_x_in, gd_y_in, mid_in, lse, gains, gain_mlp, cos, sin,
    in_o, gq_o, gkv_o, go_o, gu_o, gd_o, out_o, gain_o,
    dmid_all, wo, wq, wkv, n1, qaug, kaug, kv, att, x, dmid,
    d_out, attn_rows, v_rows, d_keys, d_values, d_query, d_query_rows, kv_send, kv_recv, d_kv, part,
    left, right, gain_rows, pair, plane_in, line_in, total, stage_o, stage_q, stage_kv,
    branch, left_b, right_b, mid, layer, gain_sum, part_query,
    *rest,
):
    grads, (send_sems, recv_sems, local_sems) = rest[:-3], rest[-3:]
    tokens, width = dmid.shape
    queries = n1.shape[0]
    heads = qaug.shape[0]
    length = kaug.shape[0]
    half = HD // 2
    plane = shards * CTX
    links = Links(shards, send_sems, recv_sems, local_sems)
    s, c, t = links.s, links.c, links.t
    links.greet(whole_line=True)

    scatter = LineScatter(links, part, tokens, left, right, PIECES)
    scatter_out = LineScatter(links, branch, tokens, left_b, right_b)
    g_o = PlaneScatter(links, dmid_all, attn_rows, rows, *grads[0:6])
    g_q = PlaneScatter(links, n1, d_query_rows, rows, *grads[6:12])
    g_kv = PlaneScatter(links, n1, d_kv, rows, *grads[12:18])
    g_u = PlaneScatter(links, None, None, rows, *grads[18:24])
    g_d = PlaneScatter(links, None, None, rows, *grads[24:30])
    kv_slot = links.slots(CTX - 1)
    plane_slot = links.slots(plane - 1)
    line_slot = links.slots(LINE - 1)
    piece = CTX * rows
    loads = [
        links.keep(src, dst)
        for src, dst in (
            (dmid_all_in, dmid_all), (wo_in, wo), (branch_in, branch), (gu_part_in, g_u.core_in.at[0]),
            (att_in, att), (kv_in, kv), (qaug_in, qaug), (kaug_in, kaug),
            (gd_part_in, g_d.core_in.at[0]), (gd_x_in, g_d.x_in), (gd_y_in, g_d.y_in), (n1_in, n1),
            (wq_in, wq), (wkv_in, wkv), (x_in, x), (dmid_in, dmid), (mid_in, mid),
        )
    ]

    def others(grad, stage):
        for step in range(1, shards):
            grad.other(step, stage.at[pl.ds((step - 1) * piece, piece)])

    for load in loads[0:2]:
        load.wait()
    d_out[...] = nn_dot(dmid_all[...], wo[...]).astype(bf16).T
    links.met()
    loads[2].wait()
    line_ends(scatter_out, 0)
    loads[3].wait()
    g_u.exchange()
    for load in loads[4:8]:
        load.wait()
    for other in range(CTX):
        v_rows[other * queries : (other + 1) * queries, :] = kv[other, HD : 2 * HD, :].T
    d_keys[...] = jnp.zeros_like(d_keys)
    d_values[...] = jnp.zeros_like(d_values)

    def head(h):
        at = pl.ds(pl.multiple_of(h * HD, HD), HD)
        query = qaug[h]
        d_head = d_out[at, :]
        delta = jnp.sum(d_head.astype(f32) * att[at, :].astype(f32), 0, keepdims=True)
        log_sum = lse[h]
        d_q = jnp.zeros((HD, queries), f32)
        for b in range(0, length, BLOCK):
            e = b + BLOCK
            probs = jnp.exp(nn_dot(kaug[b:e, :], query) - log_sum)
            d_probs = nn_dot(v_rows[b:e, :], d_head)
            d_scores = (probs * (d_probs - delta)).astype(bf16)
            d_values[b:e, :] += nt_dot(probs.astype(bf16), d_head)
            d_keys[b:e, :] += nt_dot(d_scores, query[0:HD])
            at_b = b % queries
            d_q = d_q + nn_dot(kv[b // queries, 0:HD, at_b : at_b + BLOCK], d_scores)
        d_query[at, :] = d_q * (HD ** (-0.5))

    pl.loop(0, heads // 2)(head)
    line_ends(scatter_out, 1, 2)
    scatter_out.stage(1)
    for load in loads[8:11]:
        load.wait()
    g_d.fold(here=True)
    pl.loop(heads // 2, heads)(head)

    def pack(other):
        block = pl.ds(pl.multiple_of(other * queries, queries), queries)
        both = jnp.concatenate([d_keys[block, :], d_values[block, :]], 1)
        kv_send[other] = both.astype(bf16)

    for step in range(1, CTX):
        peer = lax.rem(c + step, CTX)
        pack(peer)
        links.send(kv_send.at[peer], kv_recv.at[step - 1], (s, peer, t), kv_slot + step - 1)
    pack(c)
    scatter_out.stage(2)
    for load in loads[11:]:
        load.wait()

    cosine, sine = cos[...], sin[...]
    for h in range(heads):
        at = h * HD
        d1, d2 = d_query[at : at + half, :], d_query[at + half : at + HD, :]
        d_query[at : at + half, :] = d1 * cosine + d2 * sine
        d_query[at + half : at + HD, :] = d2 * cosine - d1 * sine
    d_query_rows[...] = d_query[...].astype(bf16).T
    for b in range(0, width, 512):
        part_query[:, b : b + 512] = nt_dot(d_query_rows[...], wq[b : b + 512, :])
    others(g_q, stage_q)
    attn_rows[...] = att[...].T
    others(g_o, stage_o)
    for step in range(1, CTX):
        links.recv(kv_recv.at[step - 1], kv_slot + step - 1)
    d_pair = kv_send[c].astype(f32)
    for step in range(1, CTX):
        d_pair = d_pair + kv_recv[step - 1].astype(f32)
    d_pair = d_pair.T
    d1, d2 = d_pair[0:half], d_pair[half:HD]
    turned = jnp.concatenate(
        [d1 * cosine + d2 * sine, d2 * cosine - d1 * sine, d_pair[HD:]], 0
    )
    d_kv[...] = turned.astype(bf16).T

    for b in range(0, width, 512):
        summed = part_query[:, b : b + 512] + nt_dot(d_kv[...], wkv[b : b + 512, :])
        part[:, b : b + 512] = summed.astype(bf16)

    line_ends(scatter, 0, 1)

    gain_rows[...] = jnp.zeros_like(gain_rows)

    @pl.loop(0, queries // ROWS)
    def _(i):
        r = pl.ds(pl.multiple_of(i * ROWS, ROWS), ROWS)
        v = x[r, :].astype(f32)
        inverse = lax.rsqrt(jnp.mean(v * v, -1, keepdims=True) + epsilon)
        gain_rows[...] += part[r, :].astype(f32) * (v * inverse)

    pair[0:1, :] = jnp.sum(gain_rows[...], 0, keepdims=True)
    pair[1:2, :] = gain_mlp[...]
    for step in range(1, plane):
        links.send(pair, plane_in.at[step - 1], links.plane_peer(step), plane_slot + step - 1)
    g_u.fold()
    line_steps(scatter, 1)
    g_o.own()
    g_o.exchange()
    summed = pair[...]
    for step in range(1, plane):
        links.recv(plane_in.at[step - 1], plane_slot + step - 1)
        summed = summed + plane_in[step - 1]
    total[...] = summed
    for step in range(1, LINE):
        links.send(total, line_in.at[step - 1], links.line_peer(step), line_slot + step - 1)
    line_ends(scatter, 2)
    others(g_kv, stage_kv)
    g_q.own()
    g_q.exchange()
    line_steps(scatter, 2)
    g_kv.own()
    g_kv.exchange()
    g_o.fold()
    scatter_out.arrive()

    def layer_rows(r, total_rows):
        layer[pl.ds(r, ROWS), :] = (mid[pl.ds(r, ROWS), :] + total_rows).astype(bf16)

    scatter_out.owned(0, layer_rows)
    links.keep_later(layer, out_o)
    g_u.total()
    links.keep_later(g_u.out, gu_o)
    g_q.fold()
    g_d.total(here=True)
    links.keep_later(g_d.out, gd_o)
    g_kv.fold()
    g_o.total()
    links.keep_later(g_o.out, go_o)

    def finish_rows(r, d_normed):
        at = pl.ds(r, ROWS)
        q = pl.ds(pl.multiple_of(place(t) * tokens + r, ROWS), ROWS)
        v = x[q, :].astype(f32)
        inverse = lax.rsqrt(jnp.mean(v * v, -1, keepdims=True) + epsilon)
        unit = v * inverse
        d_unit = d_normed * gains[0:1, :]
        back = inverse * (d_unit - unit * jnp.mean(d_unit * unit, -1, keepdims=True))
        dmid[at, :] = dmid[at, :] + back

    scatter.arrive(0)
    scatter.owned(0, finish_rows)
    g_q.total()
    links.keep_later(g_q.out, gq_o)
    g_kv.total()
    links.keep_later(g_kv.out, gkv_o)
    for p in range(1, PIECES):
        scatter.arrive(p)
        scatter.owned(p, finish_rows)
    links.keep_later(dmid, in_o)
    for step in range(1, LINE):
        links.recv(line_in.at[step - 1], line_slot + step - 1)
        summed = summed + line_in[step - 1]
    own_gains = gain_o.shape[1]
    if own_gains == width:
        gain_o[...] = summed
    else:
        gain_sum[...] = summed
        me = s * CTX + c
        gain_o[...] = gain_sum[:, pl.ds(pl.multiple_of(me * own_gains, own_gains), own_gains)]
    links.finish()


def backward_call(
    shards, rows, dmid_all, wo, wq, wkv, n1, qaug, kaug, kv, att, x, dmid, branch, gu_part,
    gd_part, gd_x, gd_y, mid, lse, gains, gain_mlp, cos, sin,
):
    tokens, width = dmid.shape
    queries = n1.shape[0]
    heads = qaug.shape[0]
    length = kaug.shape[0]
    inner = heads * HD
    columns = gu_part.shape[1]
    plane = shards * CTX
    own_gains = width // plane if width // plane % 128 == 0 else width
    piece = CTX * rows * (shards - 1)
    token = (tokens, width)
    block = (LINE - 1,) + token
    outs = [
        struct(token, f32),
        struct((rows, inner), f32),
        struct((rows, 2 * HD), f32),
        struct((rows, inner), f32),
        struct((rows, columns), f32),
        struct((rows, columns), f32),
        struct(token, bf16),
        struct((2, own_gains), f32),
    ]
    count = 6 + 6 * PIECES + 5 * (2 * (shards - 1) + 6) + CTX - 1 + plane - 1 + LINE - 1
    return pl.pallas_call(
        functools.partial(backward_kernel, shards, rows),
        out_shape=outs,
        in_specs=[any_spec()] * 17 + [vmem_spec()] * 5,
        out_specs=[any_spec()] * 7 + [vmem_spec()],
        scratch_shapes=[
            pltpu.VMEM((queries, width), bf16),
            pltpu.VMEM((width, inner), bf16),
            pltpu.VMEM((width, inner), bf16),
            pltpu.VMEM((width, 2 * HD), bf16),
            pltpu.VMEM((queries, width), bf16),
            pltpu.VMEM(qaug.shape, bf16),
            pltpu.VMEM(kaug.shape, bf16),
            pltpu.VMEM(kv.shape, bf16),
            pltpu.VMEM((inner, queries), bf16),
            pltpu.VMEM((queries, width), bf16),
            pltpu.VMEM(token, f32),
            pltpu.VMEM((inner, queries), bf16),
            pltpu.VMEM((queries, inner), bf16),
            pltpu.VMEM((length, HD), bf16),
            pltpu.VMEM((length, HD), f32),
            pltpu.VMEM((length, HD), f32),
            pltpu.VMEM((inner, queries), f32),
            pltpu.VMEM((queries, inner), bf16),
            pltpu.VMEM((CTX, queries, 2 * HD), bf16),
            pltpu.VMEM((CTX - 1, queries, 2 * HD), bf16),
            pltpu.VMEM((queries, 2 * HD), bf16),
            pltpu.VMEM((queries, width), bf16),
            pltpu.VMEM(block, bf16),
            pltpu.VMEM(block, bf16),
            pltpu.VMEM((ROWS, width), f32),
            pltpu.VMEM((2, width), f32),
            pltpu.VMEM((plane - 1, 2, width), f32),
            pltpu.VMEM((LINE - 1, 2, width), f32),
            pltpu.VMEM((2, width), f32),
            pltpu.VMEM((piece, inner), bf16),
            pltpu.VMEM((piece, inner), bf16),
            pltpu.VMEM((piece, 2 * HD), bf16),
            pltpu.VMEM((queries, width), bf16),
            pltpu.VMEM(block, bf16),
            pltpu.VMEM(block, bf16),
            pltpu.VMEM(token, f32),
            pltpu.VMEM(token, bf16),
            pltpu.VMEM((2, width), f32),
            pltpu.VMEM((queries, width), f32),
            *PlaneScatter.scratch(shards, rows, inner),
            *PlaneScatter.scratch(shards, rows, inner),
            *PlaneScatter.scratch(shards, rows, 2 * HD),
            *PlaneScatter.scratch(1 + 1, rows, columns),
            *PlaneScatter.scratch(1 + 1, rows, columns),
            pltpu.SemaphoreType.DMA((count,)),
            pltpu.SemaphoreType.DMA((count,)),
            pltpu.SemaphoreType.DMA((32,)),
        ],
        compiler_params=pltpu.CompilerParams(
            collective_id=2, has_side_effects=True, vmem_limit_bytes=60 * 2**20
        ),
        name="backward",
    )(
        dmid_all, wo, wq, wkv, n1, qaug, kaug, kv, att, x, dmid, branch, gu_part,
        gd_part, gd_x, gd_y, mid, lse, gains, gain_mlp, cos, sin,
    )


def finish_kernel(gains, layer_in, *refs):
    count = (len(refs) - 2) // 2
    layer_out = refs[count]
    layer_out[0] = layer_in[...]
    refs[count + 1][0] = refs[0][...]
    for src, dst in zip(refs[1:count], refs[count + 2 : -2]):
        dst[...] = src[...]
    for row, dst in enumerate(refs[-2:]):
        dst[...] = gains[row : row + 1, :]


def finish_call(arrays, gains, steps=1):
    rows = [array.shape[0] // steps for array in arrays]
    wide = [array.shape[1] for array in arrays]
    own = gains.shape[1]
    shapes = [struct((1,) * (i < 2) + array.shape, array.dtype) for i, array in enumerate(arrays)]
    return pl.pallas_call(
        finish_kernel,
        grid=(steps,),
        out_shape=shapes + [struct((1, own), f32)] * 2,
        in_specs=[pl.BlockSpec((2, own), lambda i: (0, 0))]
        + [pl.BlockSpec((r, n), lambda i: (i, 0)) for r, n in zip(rows, wide)],
        out_specs=[
            pl.BlockSpec((1, r, n), lambda i: (0, i, 0))
            if index < 2
            else pl.BlockSpec((r, n), lambda i: (i, 0))
            for index, (r, n) in enumerate(zip(rows, wide))
        ]
        + [pl.BlockSpec((1, own), lambda i: (0, 0))] * 2,
        compiler_params=pltpu.CompilerParams(vmem_limit_bytes=60 * 2**20),
        name="finish",
    )(gains, *arrays)


def body(
    inputs, out_grad, block_order, gain_attn, w_query, w_keyval, w_output, gain_mlp, w_gate, w_up, w_down
):
    shards = lax.axis_size("shard")
    x, og = inputs[0], out_grad[0]
    tokens, width = x.shape
    s, c = lax.axis_index("shard"), lax.axis_index("ctx")
    frequency = np.float32(10000.0) ** (-np.arange(HD // 2, dtype=np.float32)[:, None] * 2.0 / HD)
    own = gain_attn.shape[0]
    start = (s * CTX + c) * own
    gain_a, gain_m = gain_attn, gain_mlp
    aligned = own % 128 == 0
    if not aligned:
        gain_a, gain_m = (
            lax.dynamic_update_slice(jnp.zeros((width,), bf16), gain, (start,))
            for gain in (gain_attn, gain_mlp)
        )
    (wq, wkv, wo, wg, wu, wd, n1, og_all, n2, mid, qaug, kaug, kv, att, x_all, lse, gains, cos, sin) = forward_call(
        shards, x, og, (w_query, w_keyval, w_output, w_gate, w_up, w_down), gain_a, gain_m,
        jnp.asarray(frequency, f32), block_order[0],
    )
    (dmid, dmid_all, grad_gate, gd_part, gd_x, gd_y, branch, gu_part, gm) = middle_call(
        shards, w_gate.shape[0], n2, og_all, wg, wu, wd, mid, gains
    )
    (input_grad, grad_query, grad_keyval, grad_output, grad_up, grad_down, layer_out, both) = backward_call(
        shards, w_query.shape[0], dmid_all, wo, wq, wkv, n1, qaug, kaug, kv, att, x_all, dmid,
        branch, gu_part, gd_part, gd_x, gd_y, mid, lse, gains, gm, cos, sin,
    )
    if not aligned:
        both = lax.dynamic_slice(both, (0, start), (2, own))
    (
        layer_out, input_grad, grad_query, grad_keyval, grad_output, grad_gate, grad_up, grad_down,
        *gain_grads,
    ) = finish_call([
        layer_out, input_grad, grad_query, grad_keyval, grad_output, grad_gate, grad_up, grad_down,
    ], both)
    return (
        layer_out, input_grad, gain_grads[0][0], grad_query, grad_keyval, grad_output,
        gain_grads[1][0], grad_gate, grad_up, grad_down,
    )


def solution(mesh):
    plane = P(("shard", "ctx"), "tensor")
    gain = P(("shard", "ctx"))
    token = P("shard", ("ctx", "tensor"), None)
    return jax.shard_map(
        body,
        mesh=mesh,
        in_specs=(token, token, P("shard", None), gain, plane, plane, plane, gain, plane, plane, plane),
        out_specs=(token, token, gain, plane, plane, plane, gain, plane, plane, plane),
        check_vma=False,
    )
```
